32 devices in a mesh: dp: 16 (over z, x, core), tensor: 2 (over y).
Axes of the slice: x: 2, y: 2, z: 4, core: 2. Of those that a mesh axis runs over, the one named last changes fastest.
Arguments:
- tokens: bfloat16 [8192, 2048], P('dp'), may hold values from -6 to 6
- seg_ids: int32 [32, 256], P('dp'), may hold values from 0 to 3, as said below
- q_weight: bfloat16 [2048, 2048], P('dp', 'tensor'), may hold values from -0.125 to 0.125
- k_weight: bfloat16 [2048, 256], P('dp', 'tensor'), may hold values from -0.125 to 0.125
- v_weight: bfloat16 [2048, 256], P('dp', 'tensor'), may hold values from -0.125 to 0.125
- o_weight: bfloat16 [2048, 2048], P('tensor', 'dp'), may hold values from -0.5 to 0.5
- attn_gain: bfloat16 [2048], P('dp'), may hold values from 0.5 to 1.5
- gate_weight: bfloat16 [2048, 5632], P('dp', 'tensor'), may hold values from -0.125 to 0.125
- up_weight: bfloat16 [2048, 5632], P('dp', 'tensor'), may hold values from -0.125 to 0.125
- down_weight: bfloat16 [5632, 2048], P('tensor', 'dp'), may hold values from -0.078125 to 0.078125
- mlp_gain: bfloat16 [2048], P('dp'), may hold values from 0.5 to 1.5
- out_grad: bfloat16 [8192, 2048], P('dp'), may hold values from -6 to 6
Outputs:
- out: bfloat16 [8192, 2048], P('dp')
- in_grad: bfloat16 [8192, 2048], P('dp')
- grad_q_weight: float32 [2048, 2048], P('dp', 'tensor')
- grad_k_weight: float32 [2048, 256], P('dp', 'tensor')
- grad_v_weight: float32 [2048, 256], P('dp', 'tensor')
- grad_o_weight: float32 [2048, 2048], P('tensor', 'dp')
- grad_attn_gain: float32 [2048], P('dp')
- grad_gate_weight: float32 [2048, 5632], P('dp', 'tensor')
- grad_up_weight: float32 [2048, 5632], P('dp', 'tensor')
- grad_down_weight: float32 [5632, 2048], P('tensor', 'dp')
- grad_mlp_gain: float32 [2048], P('dp')
The draws below stay inside these ranges and needn't reach their ends.
Inputs may be any that keep to these rules, and one draw needn't show every extreme that they name: `seg_ids`: along each row segment numbers never fall; a sequence is the tokens of one number in one row. Row 0 holds a single sequence of 256 tokens.
All inputs are finite; a program needn't handle non-finite values.
Results may differ from the reference program's by a relative error of at most 0.014.
Values may be sent and summed in bfloat16 or wider, within the bound.
A program may use at most 152 MiB of HBM per device.

```python
import jax
import jax.numpy as jnp
from jax import lax

D = 2048
HEADS = 32
KV_HEADS = 4
HEAD_DIM = 64
FF = 5632
MB_TOK = 256
TOKENS = 8192


def draw_seg_ids(key, part):
    buffers = TOKENS // MB_TOK
    key_count, key_points = jax.random.split(key)
    cut_count = jax.random.randint(key_count, (buffers, 1), 0, 4)
    cut_count = cut_count * (jnp.arange(buffers)[:, None] > 0).astype(jnp.int32)
    cut_points = jax.random.randint(key_points, (buffers, 3), 1, MB_TOK)
    active = jnp.arange(3)[None, :] < cut_count
    position_row = jnp.arange(MB_TOK)[None, None, :]
    segment = jnp.sum((active[:, :, None] & (position_row >= cut_points[:, :, None])).astype(jnp.int32), axis=1)
    return segment.astype(jnp.int32)


def with_spikes(entries, key, source, target, blocks, factor):
    owner, partner = [(jnp.arange(entries.shape[axis_at]) // (entries.shape[axis_at] // blocks)).reshape([-1 if axis == axis_at else 1 for axis in range(entries.ndim)]) for axis_at in (source, target)]
    chosen = jax.random.permutation(key, blocks)[partner]
    strong = (owner == chosen) | (owner == (partner + blocks // 2) % blocks)
    return jnp.where(strong, factor * entries, entries)


def level_of(stream_key, dims, cuts, least, top_value):
    level = 1.0
    for dim, blocks in cuts:
        steps = jax.random.uniform(jax.random.fold_in(jax.random.fold_in(stream_key, 6), dim), (blocks,), jnp.float32, least / len(cuts), top_value / len(cuts))
        level = level * jnp.repeat(jnp.exp(steps), dims[dim] // blocks).reshape((-1,) + (1,) * (len(dims) - 1 - dim))
    return level


def scatter_about(stream_key, shape, width, most, cuts=(), kind=jnp.bfloat16):
    level = level_of(stream_key, shape, cuts, -0.22, 0.18) if cuts else 1.0
    entries = jax.random.normal(stream_key, shape, jnp.float32) * width * level
    return jnp.minimum(jnp.maximum(entries, -most), most).astype(kind)


def bell_draw_with(key, dims, deviation, limit, cuts, heavy, held_as=jnp.bfloat16):
    values = deviation * jax.random.normal(key, dims, jnp.float32)
    if cuts:
        values = values * level_of(key, dims, cuts, -0.22, 0.18)
    return jnp.clip(with_spikes(values, jax.random.fold_in(key, 3), *heavy), -limit, limit).astype(held_as)


def setup_inputs(seed: int = 0) -> dict:
    splits = jax.random.split(jax.random.key(seed), 13)
    tokens = scatter_about(splits[0], (TOKENS, D), 1.0, 6.0, ((0, 16),))
    seg_ids = draw_seg_ids(jax.random.fold_in(splits[12], 71), 0)
    q_weight = scatter_about(splits[2], (D, HEADS * HEAD_DIM), D ** -0.5, 0.125, ((0, 16), (1, 2)))
    k_weight = scatter_about(splits[3], (D, KV_HEADS * HEAD_DIM), D ** -0.5, 0.125, ((0, 16), (1, 2)))
    v_weight = scatter_about(splits[4], (D, KV_HEADS * HEAD_DIM), D ** -0.5, 0.125, ((0, 16), (1, 2)))
    o_weight = scatter_about(splits[5], (HEADS * HEAD_DIM, D), (HEADS * HEAD_DIM // 16) ** -0.5, 0.5, ((0, 2), (1, 16)))
    attn_gain = jnp.clip(1.0 + 0.1 * jax.random.normal(splits[6], (D,), jnp.float32), 0.5, 1.5).astype(jnp.bfloat16)
    gate_weight = scatter_about(splits[7], (D, FF), D ** -0.5, 0.125, ((0, 16), (1, 2)))
    up_weight = scatter_about(splits[8], (D, FF), D ** -0.5, 0.125, ((0, 16), (1, 2)))
    down_weight = scatter_about(splits[9], (FF, D), FF ** -0.5, 0.078125, ((0, 2), (1, 16)))
    mlp_gain = jnp.clip(1.0 + 0.1 * jax.random.normal(splits[10], (D,), jnp.float32), 0.5, 1.5).astype(jnp.bfloat16)
    out_grad = bell_draw_with(splits[11], (TOKENS, D), 1.0, 6.0, ((0, 16),), (0, 1, 16, 2.0))
    return dict(tokens=tokens, seg_ids=seg_ids, q_weight=q_weight, k_weight=k_weight, v_weight=v_weight, o_weight=o_weight, attn_gain=attn_gain, gate_weight=gate_weight, up_weight=up_weight, down_weight=down_weight, mlp_gain=mlp_gain, out_grad=out_grad)


@jax.custom_vjp
def low(v):
    return lax.optimization_barrier(v.astype(jnp.bfloat16)).astype(jnp.float32)

@jax.custom_vjp
def low_back(v):
    return v

def low_keep(v):
    return (low(v), None)

def low_pass(kept, grad):
    return (grad,)

def back_keep(v):
    return (v, None)

def back_low(kept, grad):
    return (low(grad),)
low.defvjp(low_keep, low_pass)
low_back.defvjp(back_keep, back_low)
norm_eps = 1e-05
highest = lax.Precision.HIGHEST

def positions(segment):
    token_count = segment.shape[0]
    order_ids = jnp.arange(token_count, dtype=jnp.int32)
    same_seg = segment[:, None] == segment[None, :]
    before = order_ids[None, :] < order_ids[:, None]
    position = lax.optimization_barrier(jnp.sum((same_seg & before).astype(jnp.int32), axis=1)).astype(jnp.int32)
    allowed = same_seg & (order_ids[None, :] <= order_ids[:, None])
    return (position, allowed)

def rotary_tables(position):
    inverse = 1.0 / 10000.0 ** (jnp.arange(0, HEAD_DIM, 2, dtype=jnp.float32) / HEAD_DIM)
    angles = position.astype(jnp.float32)[:, None] * inverse[None, :]
    return (jnp.cos(angles), jnp.sin(angles))

def rotate(vectors, cosine, sine_rows):
    half_dim = vectors.shape[-1] // 2
    first_half = vectors[..., :half_dim]
    second = vectors[..., half_dim:]
    cos_rows = cosine[:, None, :]
    sin_rows = sine_rows[:, None, :]
    return jnp.concatenate([first_half * cos_rows - second * sin_rows, second * cos_rows + first_half * sin_rows], axis=-1)

def matmul(operand_one, operand_two):
    return jnp.dot(operand_one, operand_two, precision=highest, preferred_element_type=jnp.float32)

def rms_scale(vectors, gain):
    factor = lax.rsqrt(lax.optimization_barrier(jnp.mean(vectors * vectors, axis=-1, keepdims=True)) + norm_eps)
    return vectors * factor * gain

def layer_forward(params, inputs, position, allowed):
    q_weight, k_weight, v_weight, o_weight, attn_gain, gate_weight, up_weight, down_weight, mlp_gain = params
    token_count = inputs.shape[0]
    group_size = HEADS // KV_HEADS
    score_scale = HEAD_DIM ** (-0.5)
    normed = low(rms_scale(inputs, attn_gain))
    query_raw = low_back(matmul(normed, q_weight)).reshape(token_count, HEADS, HEAD_DIM)
    key_raw = low_back(matmul(normed, k_weight)).reshape(token_count, KV_HEADS, HEAD_DIM)
    values = low(low_back(matmul(normed, v_weight))).reshape(token_count, KV_HEADS, HEAD_DIM)
    cosine, sine_rows = rotary_tables(position)
    queries = low(rotate(query_raw, cosine, sine_rows)).reshape(token_count, KV_HEADS, group_size, HEAD_DIM)
    keys_rot = low(rotate(key_raw, cosine, sine_rows))
    scores = low_back(jnp.einsum('qkgd,skd->kgqs', queries, keys_rot, precision=highest) * score_scale)
    scores = jnp.where(allowed[None, None], scores, -1e+30)
    attention = jax.nn.softmax(scores, axis=-1)
    combined = jnp.einsum('kgqs,skd->qkgd', low(attention), values, precision=highest)
    context = low(low_back(combined.reshape(token_count, HEADS * HEAD_DIM)))
    attended = low_back(matmul(context, o_weight))
    hidden_mid = inputs + attended
    normed_two = low(rms_scale(hidden_mid, mlp_gain))
    gate_raw = low_back(matmul(normed_two, gate_weight))
    upward = low_back(matmul(normed_two, up_weight))
    activated = low(jax.nn.silu(gate_raw) * upward)
    return hidden_mid + low_back(matmul(activated, down_weight))

def reference(tokens, seg_ids, q_weight, k_weight, v_weight, o_weight, attn_gain, gate_weight, up_weight, down_weight, mlp_gain, out_grad):
    params = tuple((weight.astype(jnp.float32) for weight in (q_weight, k_weight, v_weight, o_weight, attn_gain, gate_weight, up_weight, down_weight, mlp_gain)))
    token_blocks = tokens.astype(jnp.float32).reshape(-1, MB_TOK, D)
    grad_blocks = out_grad.astype(jnp.float32).reshape(-1, MB_TOK, D)

    def one_block(totals, block_item):
        block_tokens, segment, block_grad = block_item
        position, allowed = positions(segment)

        def forward_run(weights, inputs):
            return layer_forward(weights, inputs, position, allowed)
        result, pullback = jax.vjp(forward_run, params, block_tokens)
        weight_grads, input_grad = pullback(block_grad)
        totals = jax.tree.map(lambda carried, added: carried + added, totals, weight_grads)
        return (totals, (result.astype(jnp.bfloat16), input_grad.astype(jnp.bfloat16)))
    zero_grads = tuple((jnp.zeros_like(weight) for weight in params))
    totals, (results, input_grads) = lax.scan(one_block, zero_grads, (token_blocks, seg_ids, grad_blocks))
    return (results.reshape(-1, D), input_grads.reshape(-1, D), totals[0], totals[1], totals[2], totals[3], totals[4], totals[5], totals[6], totals[7], totals[8])
```

```python
import functools

import jax
import jax.numpy as jnp
from jax import lax
from jax.experimental import pallas as pl
from jax.experimental.pallas import tpu as pltpu
from jax.sharding import PartitionSpec as P

HEAD_DIM = 64
norm_eps = 1e-05
MESH = pl.DeviceIdType.MESH
ANY = pl.BlockSpec(memory_space=pl.ANY)
VMEM = pl.BlockSpec(memory_space=pltpu.VMEM)
DMA = pltpu.SemaphoreType.DMA
F32 = jnp.float32
BF16 = jnp.bfloat16


def place():
    d = lax.axis_index("dp")
    t = lax.axis_index("tensor")
    return d, t, d // 4, lax.rem(d // 2, 2), lax.rem(d, 2)


def enter(zn, here):
    d, t, z, x, c = here
    bar = pltpu.get_barrier_semaphore()

    def hail(device):
        pl.semaphore_signal(bar, inc=1, device_id=device, device_id_type=MESH)

    hail((d + 1 - 2 * c, t))
    hail((d + 2 - 4 * x, t))
    hail((d, 1 - t))

    @pl.when(z > 0)
    def _():
        hail((d - 4, t))

    @pl.when(z < zn - 1)
    def _():
        hail((d + 4, t))

    pl.semaphore_wait(bar, 5 - (z == 0).astype(jnp.int32) - (z == zn - 1).astype(jnp.int32))


def farthest_first(zn, z, i):
    up = 1 - (2 * z) // zn
    longer = up * (zn - 1 - z) + (1 - up) * z
    shorter = zn - 1 - longer
    rest = i - (longer - shorter)
    return jnp.where(
        rest < 0,
        z + (2 * up - 1) * (longer - i),
        z + (1 - 2 * lax.rem(jnp.maximum(rest, 0), 2)) * (shorter - jnp.maximum(rest, 0) // 2),
    )


def loop(count, body):
    def step(i, carry):
        body(i)
        return carry

    lax.fori_loop(0, count, step, 0)


def remote(src, dst, send, recv, device):
    return pltpu.make_async_remote_copy(
        src_ref=src, dst_ref=dst, send_sem=send, recv_sem=recv, device_id=device, device_id_type=MESH
    )


def by_rows(count, body, block=16):
    def step(i, carry):
        body(pl.ds(pl.multiple_of(i * block, block), block))
        return carry

    lax.fori_loop(0, count // block, step, 0)


def gather_sems(n, sources, zn):
    return [
        DMA((sources,)),
        DMA((sources,)),
        DMA((sources,)),
        DMA((n, zn)),
        DMA((n, zn)),
        DMA((n,)),
        DMA((n,)),
        DMA((n, 2, zn)),
        DMA((n, zn)),
        DMA((n, 2, zn)),
        DMA((n, zn)),
    ]


def part(ref, core, paired):
    if paired:
        return ref.at[core]
    columns = ref.shape[1] // 2
    return ref.at[:, pl.ds(pl.multiple_of(core * columns, columns), columns)]


class Gather:
    def __init__(self, zn, here, arrays, sems):
        self.zn, self.here = zn, here
        self.full = [full for _, full, _ in arrays]
        self.early = [early for _, _, early in arrays]
        self.sources = [
            (j, i) + source for j, (sources, _, _) in enumerate(arrays) for i, source in enumerate(sources)
        ]
        (
            self.loc,
            self.cs,
            self.cr,
            self.xs,
            self.xr,
            self.es,
            self.er,
            self.zs,
            self.zr,
            self.bs,
            self.br,
        ) = sems

    def unit(self, j, unit, first, count):
        rows = self.full[j].shape[0] // (2 * self.zn)
        return pl.ds(pl.multiple_of(unit * rows + first, 8), count)

    def rows(self, j, unit, early):
        rows = self.full[j].shape[0] // (2 * self.zn)
        late = rows - self.early[j]
        first, count = {None: (0, rows), True: (late, rows - late), False: (0, late)}[early]
        return self.full[j].at[self.unit(j, unit, first, count)]

    def mine(self, s):
        d, t, z, x, c = self.here
        j, _, shard, paired, first, columns = self.sources[s]
        rows = self.full[j].shape[0] // (4 * self.zn)
        return self.full[j].at[self.unit(j, z * 2 + x, c * rows, rows), pl.ds(first, columns)]

    def keep(self, s):
        _, _, shard, paired, _, _ = self.sources[s]
        return pltpu.make_async_copy(part(shard, self.here[4], paired), self.mine(s), self.loc.at[s])

    def give(self, s):
        d, t, z, x, c = self.here
        _, _, shard, paired, _, _ = self.sources[s]
        return remote(
            part(shard, 1 - c, paired), self.mine(s), self.cs.at[s], self.cr.at[s], (d + 1 - 2 * c, t)
        )

    def x_late(self, j, o):
        d, t, z, x, c = self.here
        ref = self.rows(j, o * 2 + x, False)
        return remote(ref, ref, self.xs.at[j, o], self.xr.at[j, o], (d + 2 - 4 * x, t))

    def x_early(self, j):
        d, t, z, x, c = self.here
        ref = self.rows(j, z * 2 + x, True)
        return remote(ref, ref, self.es.at[j], self.er.at[j], (d + 2 - 4 * x, t))

    def along(self, j, o, down):
        d, t, z, x, c = self.here
        ref = self.rows(j, o * 2 + x, None)
        return remote(ref, ref, self.zs.at[j, down, o], self.zr.at[j, o], (d + 4 - 8 * down, t))

    def along_early(self, j, o, down):
        d, t, z, x, c = self.here
        ref = self.rows(j, o * 2 + 1 - x, True)
        return remote(ref, ref, self.bs.at[j, down, o], self.br.at[j, o], (d + 4 - 8 * down, t))

    def start(self):
        for s in range(len(self.sources)):
            self.give(s).start()
            self.keep(s).start()

    def ready(self, arrays):
        for j in arrays:
            for s, source in enumerate(self.sources):
                if source[0] == j:
                    self.keep(s).wait()
                    self.give(s).wait_recv()
            if self.early[j]:
                self.x_early(j).start()

    def start_own(self, arrays):
        z, zn = self.here[2], self.zn
        for j in arrays:
            self.x_late(j, z).start()

            @pl.when(z < zn - 1)
            def _():
                self.along(j, z, 0).start()

            @pl.when(z > 0)
            def _():
                self.along(j, z, 1).start()

    def start_early(self, arrays):
        z, zn = self.here[2], self.zn
        for j in arrays:
            if self.early[j]:
                self.x_early(j).wait_recv()

                @pl.when(z < zn - 1)
                def _():
                    self.along_early(j, z, 0).start()

                @pl.when(z > 0)
                def _():
                    self.along_early(j, z, 1).start()

    def relay(self, k, arrays):
        z, zn = self.here[2], self.zn
        o = farthest_first(zn, z, zn - 1 - k)
        down = (o > z).astype(jnp.int32)
        more = ((o < z) & (z < zn - 1)) | ((o > z) & (z > 0))
        for j in arrays:
            self.along(j, o, down).wait_recv()

            @pl.when(more)
            def _():
                self.along(j, o, down).start()

            self.x_late(j, o).start()
            if self.early[j]:
                self.along_early(j, o, down).wait_recv()

                @pl.when(more)
                def _():
                    self.along_early(j, o, down).start()

    def relays(self, first, arrays):
        loop(max(self.zn - first, 0), lambda i: self.relay(first + i, arrays))

    def arrived(self, j):
        loop(self.zn, lambda o: self.x_late(j, o).wait_recv())

    def finish(self):
        z, zn = self.here[2], self.zn
        for s in range(len(self.sources)):
            self.give(s).wait_send()
        for j in range(len(self.full)):
            if self.early[j]:
                self.x_early(j).wait_send()

            def step(o, j=j):
                self.x_late(j, o).wait_send()

                def sent(down):
                    self.along(j, o, down).wait_send()
                    if self.early[j]:
                        self.along_early(j, o, down).wait_send()

                @pl.when((o <= z) & (z < zn - 1))
                def _():
                    sent(0)

                @pl.when((o >= z) & (z > 0))
                def _():
                    sent(1)

            loop(zn, step)


def scatter_sems(n, outs, zn):
    return [
        DMA((n, zn)),
        DMA((n, zn)),
        DMA((n, zn)),
        DMA((n, zn)),
        DMA((n, zn)),
        DMA((n, zn + 1)),
        DMA((n, 2, zn)),
        DMA((n, zn)),
        DMA((n, zn + 1)),
        DMA((n,)),
        DMA((n,)),
        DMA((outs,)),
        DMA((outs,)),
        DMA((outs,)),
    ]


def scatter_buffers(shapes, early, zn):
    out = []
    for rows, columns in shapes:
        late = rows - early
        out += [
            pltpu.VMEM((zn, late, columns), BF16),
            pltpu.VMEM((zn, late, columns), BF16),
            pltpu.VMEM((zn + 1, late, columns), BF16),
            pltpu.VMEM((zn, 2, early, columns), BF16),
            pltpu.VMEM((zn + 1, 2, early, columns), BF16),
            pltpu.VMEM((early, columns), BF16),
            pltpu.VMEM((rows, columns), F32),
        ]
    return out


SCATTER_BUFFERS = 7


class Scatter:
    def __init__(self, zn, here, early, arrays, sems):
        self.zn, self.here, self.early = zn, here, early
        self.term = [term for term, _, _ in arrays]
        self.buffers = [buffers for _, buffers, _ in arrays]
        self.results = [(j,) + result for j, (_, _, results) in enumerate(arrays) for result in results]
        (
            self.st,
            self.ls,
            self.xs,
            self.xr,
            self.zs,
            self.zr,
            self.bls,
            self.bs,
            self.br,
            self.es,
            self.er,
            self.cs,
            self.cr,
            self.loc,
        ) = sems

    def unit(self, j, o, x, first, count):
        rows = self.term[j].shape[1] // 2
        return self.term[j].at[o, pl.ds(pl.multiple_of(x * rows + first, 16), count)]

    def late(self, j):
        return self.buffers[j][0].shape[1]

    def load(self, j, o):
        return pltpu.make_async_copy(
            self.unit(j, o, self.here[3], 0, self.late(j)), self.buffers[j][0].at[o], self.ls.at[j, o]
        )

    def load_early(self, j, o, other):
        x = self.here[3]
        return pltpu.make_async_copy(
            self.unit(j, o, 1 - x if other else x, self.late(j), self.early),
            self.buffers[j][3].at[o, other],
            self.bls.at[j, other, o],
        )

    def across(self, j, o):
        d, t, z, x, c = self.here
        return remote(
            self.unit(j, o, 1 - x, 0, self.late(j)),
            self.buffers[j][1].at[o],
            self.xs.at[j, o],
            self.xr.at[j, o],
            (d + 2 - 4 * x, t),
        )

    def across_early(self, j):
        d, t, z, x, c = self.here
        return remote(
            self.buffers[j][3].at[z, 1], self.buffers[j][5], self.es.at[j], self.er.at[j], (d + 2 - 4 * x, t)
        )

    def along(self, j, o, slot, down):
        d, t, z, x, c = self.here
        own, line = self.buffers[j][0], self.buffers[j][2]
        return remote(own.at[o], line.at[slot], self.zs.at[j, o], self.zr.at[j, slot], (d + 4 - 8 * down, t))

    def along_early(self, j, o, slot, down):
        d, t, z, x, c = self.here
        own, line = self.buffers[j][3], self.buffers[j][4]
        return remote(own.at[o], line.at[slot], self.bs.at[j, o], self.br.at[j, slot], (d + 4 - 8 * down, t))

    def give(self, r):
        d, t, z, x, c = self.here
        j, out, paired, first, columns = self.results[r]
        rows = out.shape[-2]
        ref = self.buffers[j][6].at[
            pl.ds(pl.multiple_of((1 - c) * rows, rows), rows), pl.ds(first, columns)
        ]
        return remote(ref, part(out, c, paired), self.cs.at[r], self.cr.at[r], (d + 1 - 2 * c, t))

    def keep(self, r):
        c = self.here[4]
        j, out, paired, first, columns = self.results[r]
        rows = out.shape[-2]
        ref = self.buffers[j][6].at[pl.ds(pl.multiple_of(c * rows, rows), rows), pl.ds(first, columns)]
        return pltpu.make_async_copy(ref, part(out, c, paired), self.loc.at[r])

    def store(self, j, o, stage, slot):
        columns = self.term[j].shape[2]
        return pltpu.make_async_copy(
            stage.at[slot, :, pl.ds(0, columns)], self.term[j].at[o], self.st.at[j, o]
        )

    def make(self, j, left, right, stage, between=None):
        z, zn = self.here[2], self.zn
        wide, columns = self.term[j].shape[1:]
        block = min(256, wide)

        def send(i):
            o = farthest_first(zn, z, i)
            self.store(j, o, stage, lax.rem(i, 2)).wait()
            self.across(j, o).start()
            for other in range(2):
                self.load_early(j, o, other).start()
            self.load(j, o).start()

        def compute(i):
            o = farthest_first(zn, z, i)
            slot = lax.rem(i, 2)

            def body(m):
                at = pl.multiple_of(o * wide + m * block, block)
                value = inner_rows(left[:, pl.ds(at, block)], right[...])
                stage[slot, pl.ds(pl.multiple_of(m * block, block), block), pl.ds(0, columns)] = value.astype(
                    BF16
                )

            loop(wide // block, body)
            self.store(j, o, stage, slot).start()

        def both(i):
            compute(i)
            send(i - 1)
            self.hop_early(j, i - 1)

        compute(0)
        if between is not None:
            between()
        loop(zn - 1, lambda i: both(i + 1))
        send(zn - 1)

    def add(self, j, o, slots):
        own, got, line = self.buffers[j][:3]

        def body(at):
            value = own[o, at].astype(F32) + got[o, at].astype(F32)
            for slot in slots:
                value = value + line[slot, at].astype(F32)
            own[o, at] = value.astype(BF16)

        by_rows(own.shape[1], body)

    def add_early(self, j, o, slots):
        own, line = self.buffers[j][3:5]
        for other in range(2):

            def body(at):
                value = own[o, other, at].astype(F32)
                for slot in slots:
                    value = value + line[slot, other, at].astype(F32)
                own[o, other, at] = value.astype(BF16)

            by_rows(own.shape[2], body)

    def route(self, i):
        z, zn = self.here[2], self.zn
        o = farthest_first(zn, z, i)
        down = (o < z).astype(jnp.int32)
        distance = jnp.maximum((o - z) * (1 - 2 * down), 1)
        slot = o + (zn - o) * down * (1 // distance)
        inner = ((o > z) & (z > 0)) | ((o < z) & (z < zn - 1))
        return o, slot, down, inner

    def hop_early(self, j, i):
        o, slot, down, inner = self.route(i)
        for other in range(2):
            self.load_early(j, o, other).wait()

        @pl.when(inner)
        def _():
            self.along_early(j, o, o, down).wait_recv()
            self.add_early(j, o, [o])

        self.along_early(j, o, slot, down).start()

    def hop(self, j, i):
        o, slot, down, inner = self.route(i)
        self.load(j, o).wait()
        self.across(j, o).wait_recv()

        @pl.when(inner)
        def _():
            self.along(j, o, o, down).wait_recv()
            self.add(j, o, [o])

        @pl.when(jnp.logical_not(inner))
        def _():
            self.add(j, o, [])

        self.along(j, o, slot, down).start()

    def late_hops(self, j):
        self.early_home(j)
        loop(self.zn - 1, lambda i: self.hop(j, i))

    def share_of_hops(self, j, i, shares):
        hops = self.zn - 1
        first = i * hops // (shares - 1)
        last = jnp.minimum((i + 1) * hops // (shares - 1), hops)

        def step(hop, carry):
            self.hop(j, hop)
            return carry

        lax.fori_loop(first, last, step, 0)

    def at_home(self, action):
        z, zn = self.here[2], self.zn

        @pl.when((z > 0) & (z < zn - 1))
        def _():
            action([z, zn])

        @pl.when(z == 0)
        def _():
            action([zn])

        @pl.when(z == zn - 1)
        def _():
            action([z])

    def early_home(self, j):
        z = self.here[2]
        for other in range(2):
            self.load_early(j, z, other).wait()

        def home(slots):
            for slot in slots:
                self.along_early(j, z, slot, 0).wait_recv()
            self.add_early(j, z, slots)

        self.at_home(home)
        self.across_early(j).start()

    def finish(self):
        z, zn = self.here[2], self.zn
        n = len(self.term)
        for j in range(n):
            own, got, line, early, _, other_early, total = self.buffers[j]
            late = self.late(j)
            self.load(j, z).wait()
            self.across(j, z).wait_recv()

            def home(slots):
                for slot in slots:
                    self.along(j, z, slot, 0).wait_recv()

                def body(at):
                    value = own[z, at].astype(F32) + got[z, at].astype(F32)
                    for slot in slots:
                        value = value + line[slot, at].astype(F32)
                    total[at] = value

                by_rows(late, body)

            self.at_home(home)
            self.across_early(j).wait_recv()
            for i in range(self.early // 16):
                at = pl.ds(16 * i, 16)
                total[pl.ds(late + 16 * i, 16)] = early[z, 0, at].astype(F32) + other_early[at].astype(F32)
            for r, result in enumerate(self.results):
                if result[0] == j:
                    self.give(r).start()
                    self.keep(r).start()
        for r in range(len(self.results)):
            self.give(r).wait()
            self.keep(r).wait()
        for j in range(n):
            self.across_early(j).wait_send()

            def sent(o, j=j):
                self.across(j, o).wait_send()

                @pl.when(o != z)
                def _():
                    self.along(j, o, 0, 0).wait_send()
                    self.along_early(j, o, 0, 0).wait_send()

            loop(zn, sent)


class Gains:
    def __init__(self, zn, here, own, got, line, sems):
        self.zn, self.here, self.own, self.got, self.line, self.sems = zn, here, own, got, line, sems

    def swap(self, i):
        d, t, z, x, c = self.here
        device = ((d + 1 - 2 * c, t), (d + 2 - 4 * x, t), (d, 1 - t))[i]
        return remote(self.own, self.got.at[i], self.sems.at[0, i], self.sems.at[1, i], device)

    def along(self, o, slot, down):
        d, t, z, x, c = self.here
        return remote(
            self.own.at[o], self.line.at[slot], self.sems.at[2, o], self.sems.at[3, slot], (d + 4 - 8 * down, t)
        )

    def start(self, rows):
        wide = self.own.shape[2]
        for o in range(self.zn):
            for i, row in enumerate(rows):
                self.own[o, pl.ds(i, 1)] = row[:, pl.ds(o * wide, wide)]
        self.swap(0).start()

    def swapped(self, i):
        self.swap(i).wait()
        self.own[...] += self.got[i]
        if i < 2:
            self.swap(i + 1).start()

    def hop(self, o, slot, down, inner):
        @pl.when(inner)
        def _():
            self.along(o, o, down).wait_recv()
            self.own[o] += self.line[o]

        self.along(o, slot, down).start()

    def steps(self, k, nearest):
        z, zn = self.here[2], self.zn

        @pl.when(z + k < zn)
        def _():
            self.hop(z + k, z + k, 0, z > 0)

        @pl.when(z - k >= 0)
        def _():
            self.hop(z - k, zn if nearest else z - k, 1, z < zn - 1)

    def run(self):
        zn = self.zn

        def step(i, carry):
            self.steps(zn - 1 - i, False)
            return carry

        lax.fori_loop(0, zn - 2, step, 0)
        self.steps(1, True)

    def finish(self, out):
        z, zn = self.here[2], self.zn
        value = self.own[z]

        @pl.when(z > 0)
        def _():
            self.along(z, z, 0).wait_recv()
            self.own[z] += self.line[z]

        @pl.when(z < zn - 1)
        def _():
            self.along(z, zn, 1).wait_recv()
            self.own[z] += self.line[zn]

        out[...] = self.own[z]

        def step(o, carry):
            @pl.when(o != z)
            def _():
                self.along(o, 0, 0).wait_send()

            return carry

        lax.fori_loop(0, zn, step, 0)


def gain_buffers(zn, wide):
    return [
        pltpu.VMEM((zn, 8, wide), F32),
        pltpu.VMEM((3, zn, 8, wide), F32),
        pltpu.VMEM((zn + 1, 8, wide), F32),
        DMA((4, zn + 1)),
    ]


class Total:
    def __init__(self, here, term, from_core, half, from_pair, sems):
        self.here, self.term, self.from_core, self.half, self.from_pair = here, term, from_core, half, from_pair
        self.sems = sems

    def core(self):
        d, t, z, x, c = self.here
        return remote(self.term.at[1 - c], self.from_core, self.sems.at[0], self.sems.at[1], (d + 1 - 2 * c, t))

    def load(self):
        return pltpu.make_async_copy(self.term.at[self.here[4]], self.half, self.sems.at[4])

    def start(self):
        self.core().start()
        self.load().start()

    def pair(self):
        d, t, z, x, c = self.here
        return remote(self.half, self.from_pair, self.sems.at[2], self.sems.at[3], (d, 1 - t))

    def meet(self, loaded=True):
        if loaded:
            self.load().wait()
        self.core().wait_recv()
        block = 16

        def body(i, carry):
            at = pl.ds(pl.multiple_of(i * block, block), block)
            self.half[at] = (self.half[at].astype(F32) + self.from_core[at].astype(F32)).astype(BF16)
            return carry

        lax.fori_loop(0, self.half.shape[0] // block, body, 0)
        self.pair().start()

    def rows(self, at):
        return self.half[at].astype(F32) + self.from_pair[at].astype(F32)

    def finish(self):
        self.core().wait_send()
        self.pair().wait_send()


def total_buffers(tokens, width):
    return [pltpu.VMEM((tokens, width), BF16)] * 3 + [DMA((5,))]


def share(here, src, dst, sems):
    d, t, z, x, c = here
    return (
        pltpu.make_async_copy(src, dst.at[c], sems.at[0]),
        remote(src, dst.at[c], sems.at[1], sems.at[2], (d + 1 - 2 * c, t)),
    )


def gather_attention(zn, early, *refs):
    q, kv, o, gains, tokens, grads, seg = refs[:7]
    qkv_all, o_all, gains_all, tokens_two, grads_two, seg_two = refs[7:13]
    pair_sems = refs[13:16]
    here = place()
    enter(zn, here)
    shared = [
        share(here, src, dst, sems)
        for src, dst, sems in zip((tokens, grads, seg), (tokens_two, grads_two, seg_two), pair_sems)
    ]
    q_half = q.shape[1] // 2
    work = Gather(
        zn,
        here,
        [
            ([(gains, True, 0, gains.shape[2])], gains_all, 0),
            ([(q, False, 0, q_half), (kv, True, q_half, kv.shape[2])], qkv_all, early),
            ([(o, False, 0, o.shape[1] // 2)], o_all, early),
        ],
        refs[16:],
    )
    work.start()
    work.ready(range(3))
    work.start_own(range(3))
    for copies in shared:
        for copy in copies:
            copy.start()
    work.start_early(range(3))
    work.relays(1, range(3))
    for j in range(3):
        work.arrived(j)
    work.finish()
    for copies in shared:
        for copy in copies:
            copy.wait()


def lanes(shape):
    return lax.broadcasted_iota(jnp.int32, shape, 1)


def partner(value):
    half = HEAD_DIM // 2
    wide = 2 * HEAD_DIM
    lower = lax.rem(lanes(value.shape), HEAD_DIM) < half
    return jnp.where(lower, pltpu.roll(value, wide - half, 1), pltpu.roll(value, half, 1))


def allowed_in(column, row):
    shape = (column.shape[0], row.shape[1])
    earlier = lax.broadcasted_iota(jnp.int32, shape, 1) <= lax.broadcasted_iota(jnp.int32, shape, 0)
    return (column == row) & earlier


def softmax_of(queries, keys, allowed):
    scores = jnp.where(allowed, times_transposed(queries, keys) * HEAD_DIM ** (-0.5), -1e30)
    shifted = jnp.exp(scores - jnp.max(scores, axis=-1, keepdims=True))
    return shifted / jnp.sum(shifted, axis=-1, keepdims=True)


def key_value_pairs(pair):
    pair = pair.astype(F32)
    first = lanes(pair.shape) < HEAD_DIM
    key, value = jnp.where(first, pair, 0.0), jnp.where(first, 0.0, pair)
    return [
        part.astype(BF16)
        for part in (key, pltpu.roll(key, HEAD_DIM, 1), pltpu.roll(value, HEAD_DIM, 1), value)
    ]


def attention_block(turned, context, queries_wide, column, row):
    wide = 2 * HEAD_DIM
    allowed = allowed_in(column, row)
    key_one, key_two, value_one, value_two = key_value_pairs(turned[:, queries_wide:])

    def heads(p):
        at = pl.ds(pl.multiple_of(p * wide, wide), wide)
        queries = turned[:, at]
        one = softmax_of(queries, key_one, allowed).astype(BF16)
        two = softmax_of(queries, key_two, allowed).astype(BF16)
        context[:, at] = (product(one, value_one) + product(two, value_two)).astype(BF16)

    loop(queries_wide // wide, heads)


def attention_block_back(turned, grads, back, sums, queries_wide, column, row, cosine, sine):
    wide = 2 * HEAD_DIM
    scale = HEAD_DIM ** (-0.5)
    allowed = allowed_in(column, row)
    key_one, key_two, value_one, value_two = key_value_pairs(turned[:, queries_wide:])
    sums[...] = jnp.zeros_like(sums)

    def heads(p):
        at = pl.ds(pl.multiple_of(p * wide, wide), wide)
        queries, grad = turned[:, at], grads[:, at]
        total = None
        for i, (key, value) in enumerate(((key_one, value_one), (key_two, value_two))):
            probs = softmax_of(queries, key, allowed)
            sums[i] += inner_rows(probs.astype(BF16), grad)
            prob_grad = times_transposed(grad, value)
            delta = jnp.sum(probs * prob_grad, axis=-1, keepdims=True)
            score_grad = (probs * (prob_grad - delta)).astype(BF16)
            term = product(score_grad, key)
            total = term if total is None else total + term
            sums[2 + i] += inner_rows(score_grad, queries)
        total = total * scale
        back[:, at] = (total * cosine - partner(total) * sine).astype(BF16)

    loop(queries_wide // wide, heads)
    value_grad = pltpu.roll(sums[0], HEAD_DIM, 1) + sums[1]
    key_grad = (sums[2] + pltpu.roll(sums[3], HEAD_DIM, 1)) * scale
    turned_back = key_grad * cosine - partner(key_grad) * sine
    back[:, pl.ds(queries_wide, wide)] = jnp.where(
        lanes(value_grad.shape) < HEAD_DIM, turned_back, value_grad
    ).astype(BF16)


def feedforward(zn, early, *refs):
    gate, up, down, tokens, gain, chip_grads = refs[:6]
    chip_tokens, gain_one, qkv_all, o_all, cosines, sines, columns_of, rows_of = refs[6:14]
    gate_all, up_all, down_all, mid_out, normed_out, act_out, gate_grad_out, up_grad_out, back_out = refs[14:23]
    term, normed_one_out, turned_out, context_out = refs[23:27]
    total_refs = refs[27:31]
    normed, out_sems, pair_sems, load_sems, grad_sems, stage_sems, block_sems = refs[31:38]
    here = place()
    c = here[4]
    enter(zn, here)
    total = Total(here, term, *total_refs)
    work = Gather(
        zn,
        here,
        [
            ([(shard, False, 0, shard.shape[1] // 2)], full, early)
            for shard, full in ((down, down_all), (gate, gate_all), (up, up_all))
        ],
        refs[38:],
    )
    count, width = tokens.shape
    columns = gate_all.shape[1]
    block = 256
    blocks = 2 * count // block
    per = count // block
    half = total_refs[1]

    def attention(qkv, o, inputs, normed_one, turned, context, attended):
        queries_wide = context.shape[2]
        wide = 2 * HEAD_DIM

        def place_of(i):
            return lax.rem((1 - c) * per + i, blocks)

        def rows_at(i):
            return pl.ds(pl.multiple_of(place_of(i) * block, block), block)

        def fetch_inputs(i, slot):
            return pltpu.make_async_copy(chip_tokens.at[rows_at(i)], inputs.at[slot], grad_sems.at[slot])

        def stores(i, slot):
            return [
                pltpu.make_async_copy(buffer.at[slot], out.at[rows_at(i)], stage_sems.at[slot, n])
                for n, (buffer, out) in enumerate(
                    ((normed_one, normed_one_out), (turned, turned_out), (context, context_out))
                )
            ]

        def store_term(i, slot):
            return pltpu.make_async_copy(
                attended.at[slot],
                term.at[1 - c, pl.ds(pl.multiple_of(i * block, block), block)],
                block_sems.at[slot],
            )

        fetch_inputs(0, 0).start()
        loads = [
            pltpu.make_async_copy(qkv_all, qkv, load_sems.at[0]),
            pltpu.make_async_copy(o_all, o, load_sems.at[1]),
        ]
        for load in loads:
            load.start()
        for load in loads:
            load.wait()

        def one_block(i):
            slot = lax.rem(i, 2)
            to = rows_at(i)
            fetch_inputs(i, slot).wait()

            @pl.when(i + 1 < blocks)
            def _():
                fetch_inputs(i + 1, 1 - slot).start()

            @pl.when(i > 1)
            def _():
                for copy in stores(i - 2, slot):
                    copy.wait()

            def norm(at):
                value = inputs[slot, at].astype(F32)
                factor = lax.rsqrt(jnp.mean(value * value, axis=-1, keepdims=True) + norm_eps)
                normed_one[slot, at] = (value * factor * gain_one[...]).astype(BF16)

            by_rows(block, norm)
            cosine, sine = cosines[to], sines[to]
            raw = product(normed_one[slot], qkv[...])
            for first in range(0, queries_wide, wide):
                value = raw[:, first : first + wide]
                turned[slot, :, pl.ds(first, wide)] = (value * cosine + partner(value) * sine).astype(BF16)
            value = raw[:, queries_wide:]
            is_key = lanes(value.shape) < HEAD_DIM
            turned[slot, :, pl.ds(queries_wide, wide)] = jnp.where(
                is_key, value * cosine + partner(value) * sine, value
            ).astype(BF16)
            which = place_of(i)
            attention_block(
                turned.at[slot], context.at[slot], queries_wide, columns_of[which], rows_of[which]
            )
            for copy in stores(i, slot):
                copy.start()
            return slot

        def other(i):
            slot = one_block(i)
            attended[slot] = times_transposed(context[slot], o[...]).astype(BF16)
            store_term(i, slot).start()

        def own(i):
            slot = one_block(per + i)
            half[pl.ds(pl.multiple_of(i * block, block), block)] = times_transposed(
                context[slot], o[...]
            ).astype(BF16)

        loop(per, other)
        for i in range(per):
            store_term(i, i % 2).wait()
        total.core().start()
        work.start_early(range(3))
        loop(per, own)
        for i in range(blocks - 2, blocks):
            for copy in stores(i, i % 2):
                copy.wait()

    work.start()
    work.ready(range(3))
    work.start_own([0, 1])
    pl.run_scoped(
        attention,
        pltpu.VMEM(qkv_all.shape, BF16),
        pltpu.VMEM(o_all.shape, BF16),
        pltpu.VMEM((2, block, width), BF16),
        pltpu.VMEM((2, block, width), BF16),
        pltpu.VMEM((2, block, qkv_all.shape[1]), BF16),
        pltpu.VMEM((2, block, o_all.shape[1]), BF16),
        pltpu.VMEM((2, block, width), BF16),
    )
    total.meet(False)
    work.relay(1, [0, 1])
    work.start_own([2])

    def sums(mid):
        total.pair().wait_recv()

        def body(at):
            value = tokens[at].astype(F32) + total.rows(at)
            mid[at] = value
            factor = lax.rsqrt(jnp.mean(value * value, axis=-1, keepdims=True) + norm_eps)
            normed[c, at] = (value * factor * gain[...]).astype(BF16)

        by_rows(count, body)
        save = pltpu.make_async_copy(mid, mid_out, out_sems.at[0])
        save.start()
        for copy in share(here, normed.at[c], normed, pair_sems)[1:]:
            copy.start()
        save.wait()

    def hidden(first, second, silu, slope, up_grad, grads, result, stages, back_stage):
        def fetch_grads(i, slot):
            return pltpu.make_async_copy(
                chip_grads.at[pl.ds(pl.multiple_of(i * block, block), block)], grads.at[slot], grad_sems.at[slot]
            )

        def at_block(i):
            return pl.ds(pl.multiple_of(i * block, block), block)

        fetch_grads(0, 0).start()
        work.arrived(0)
        load = pltpu.make_async_copy(down_all, first, load_sems.at[0])
        load.start()
        load.wait()

        def hidden_block(i):
            slot = lax.rem(i, 2)
            fetch_grads(i, slot).wait()

            @pl.when(i + 1 < blocks)
            def _():
                fetch_grads(i + 1, 1 - slot).start()

            slope[at_block(i)] = product(grads[slot], first[...])

        loop(blocks, hidden_block)
        work.arrived(1)
        load = pltpu.make_async_copy(gate_all, second, load_sems.at[1])
        load.start()
        share(here, normed.at[c], normed, pair_sems)[1].wait()
        save = pltpu.make_async_copy(normed, normed_out, out_sems.at[1])
        save.start()
        load.wait()

        def gate_block(i):
            result[...] = product(normed[i // per, at_block(lax.rem(i, per))], second[...])

            def body(at):
                to = pl.ds(pl.multiple_of(i * block + at.start, 16), at.size)
                gated = result[at]
                grad = slope[to]
                sigmoid = 1.0 / (1.0 + jnp.exp(-gated))
                silu[to] = gated * sigmoid
                up_grad[to] = (grad * gated * sigmoid).astype(BF16)
                slope[to] = grad * (sigmoid * (1.0 + gated * (1.0 - sigmoid)))

            by_rows(block, body)

        loop(blocks, gate_block)
        save_up = pltpu.make_async_copy(up_grad, up_grad_out, out_sems.at[2])
        save_up.start()
        work.relays(3, [2])
        work.arrived(2)
        load = pltpu.make_async_copy(up_all, first, load_sems.at[0])
        load.start()
        load.wait()

        def stores(i, slot):
            to = at_block(i)
            return (
                pltpu.make_async_copy(stages.at[slot, 0], act_out.at[to], stage_sems.at[slot, 0]),
                pltpu.make_async_copy(stages.at[slot, 1], gate_grad_out.at[to], stage_sems.at[slot, 1]),
                pltpu.make_async_copy(
                    back_stage.at[slot], back_out.at[i // per, at_block(lax.rem(i, per))], stage_sems.at[slot, 2]
                ),
            )

        def up_block(i):
            slot = lax.rem(i, 2)

            @pl.when(i > 1)
            def _():
                for copy in stores(i - 2, slot):
                    copy.wait()

            result[...] = product(normed[i // per, at_block(lax.rem(i, per))], first[...])

            def body(at):
                to = pl.ds(pl.multiple_of(i * block + at.start, 16), at.size)
                upward = result[at]
                stages[slot, 0, at] = (silu[to] * upward).astype(BF16)
                stages[slot, 1, at] = (slope[to] * upward).astype(BF16)

            by_rows(block, body)
            value = times_transposed(stages[slot, 1], second[...]) + times_transposed(
                up_grad[at_block(i)], first[...]
            )
            back_stage[slot] = value.astype(BF16)
            for copy in stores(i, slot):
                copy.start()

        loop(blocks, up_block)
        for i in range(max(blocks - 2, 0), blocks):
            for copy in stores(i, i % 2):
                copy.wait()
        save.wait()
        save_up.wait()

    work.relay(2, [0, 1])
    work.relay(1, [2])
    pl.run_scoped(sums, pltpu.VMEM((count, width), F32))
    work.relays(3, [0, 1])
    work.relay(2, [2])
    pl.run_scoped(
        hidden,
        pltpu.VMEM((width, columns), BF16),
        pltpu.VMEM((width, columns), BF16),
        pltpu.VMEM((2 * count, columns), F32),
        pltpu.VMEM((2 * count, columns), F32),
        pltpu.VMEM((2 * count, columns), BF16),
        pltpu.VMEM((2, block, width), BF16),
        pltpu.VMEM((block, columns), F32),
        pltpu.VMEM((2, 2, block, columns), BF16),
        pltpu.VMEM((2, block, width), BF16),
    )
    work.finish()
    total.finish()


def fetch(pairs, sems):
    copies = [pltpu.make_async_copy(src, dst, sems.at[i]) for i, (src, dst) in enumerate(pairs)]
    for copy in copies:
        copy.start()
    return copies


def scatter_feedforward(zn, early, *refs):
    normed, gate_grad, chip_grads, activated, back_term, down_all, mid_in, gain = refs[:8]
    turned_all, o_all, qkv_all, cosines, sines, columns_of, rows_of = refs[8:15]
    gate_out, down_out, out, mid_grad_out, branch_out, gain_out, qkv_back, in_term = refs[15:23]
    gate, down, out_term = refs[23:26]
    buffers, refs = refs[26 : 26 + 2 * SCATTER_BUFFERS], refs[26 + 2 * SCATTER_BUFFERS :]
    back_refs, out_refs = refs[:4], refs[4:8]
    fetch_sems, out_sems, pair_sems, weight_sems, stage_sems, block_sems, back_sems = refs[8:15]
    branch, out_rows = back_refs[0], out_refs[0]
    here = place()
    c = here[4]
    chip, width = chip_grads.shape
    enter(zn, here)
    back = Total(here, back_term, *back_refs)
    front = Total(here, out_term, *out_refs)
    work = Scatter(
        zn,
        here,
        early,
        [
            (
                term,
                buffers[SCATTER_BUFFERS * j : SCATTER_BUFFERS * (j + 1)],
                [(result, False, 0, result.shape[1] // 2)],
            )
            for j, (term, result) in enumerate(((down, down_out), (gate, gate_out)))
        ],
        refs[15:],
    )
    back.start()

    def out_terms(right_one, weights, stages):
        block = weights.shape[1]

        def fetch_weights(i, slot):
            return pltpu.make_async_copy(
                down_all.at[pl.ds(pl.multiple_of(i * block, block), block)], weights.at[slot], weight_sems.at[slot]
            )

        def stores(i, slot):
            to = pl.ds(pl.multiple_of(i * block, block), block)
            return [
                pltpu.make_async_copy(
                    stages.at[slot, pl.ds(half * (chip // 2), chip // 2)],
                    out_term.at[half, :, to],
                    stage_sems.at[slot, half],
                )
                for half in range(2)
            ]

        fetch_weights(0, 0).start()

        def step(i):
            slot = lax.rem(i, 2)
            fetch_weights(i, slot).wait()

            @pl.when(i + 1 < width // block)
            def _():
                fetch_weights(i + 1, 1 - slot).start()

            @pl.when(i > 1)
            def _():
                for copy in stores(i - 2, slot):
                    copy.wait()

            stages[slot] = times_transposed(right_one[...], weights[slot]).astype(BF16)
            for copy in stores(i, slot):
                copy.start()

        loop(width // block, step)
        for i in range(width // block - 2, width // block):
            for copy in stores(i, i % 2):
                copy.wait()

    def terms(left_one, right_one, left_two, right_two, stage, weights, stages):
        copies = fetch(
            (
                (chip_grads, left_one),
                (activated, right_one),
                (normed, left_two),
                (gate_grad, right_two),
            ),
            fetch_sems,
        )
        copies[0].wait()
        copies[1].wait()
        work.make(0, left_one, right_one, stage, back.meet)
        copies[2].wait()
        copies[3].wait()
        work.make(1, left_two, right_two, stage)
        out_terms(right_one, weights, stages)
        front.start()

    pl.run_scoped(
        terms,
        pltpu.VMEM(chip_grads.shape, BF16),
        pltpu.VMEM(activated.shape, BF16),
        pltpu.VMEM(normed.shape, BF16),
        pltpu.VMEM(gate_grad.shape, BF16),
        pltpu.VMEM((2,) + down.shape[1:], BF16),
        pltpu.VMEM((2, 256, down.shape[2]), BF16),
        pltpu.VMEM((2, chip, 256), BF16),
    )

    def sums(mid, mid_grad, grads):
        copies = fetch(
            (
                (mid_in, mid),
                (chip_grads.at[pl.ds(pl.multiple_of(c * (chip // 2), 16), chip // 2)], grads),
            ),
            fetch_sems,
        )
        work.late_hops(0)
        front.meet()
        for copy in copies:
            copy.wait()
        gain_out[...] = jnp.zeros_like(gain_out)

        def body_gain(at):
            value = mid[at]
            factor = lax.rsqrt(jnp.mean(value * value, axis=-1, keepdims=True) + norm_eps)
            gain_out[...] += jnp.sum(back.half[at].astype(F32) * (value * factor), axis=0, keepdims=True)

        by_rows(chip // 2, body_gain)
        back.pair().wait_recv()

        def body(at):
            value = mid[at]
            factor = lax.rsqrt(jnp.mean(value * value, axis=-1, keepdims=True) + norm_eps)
            scaled = back.rows(at) * gain[...]
            result = (
                grads[at].astype(F32)
                + factor * scaled
                - value * (factor * factor * factor) * jnp.mean(scaled * value, axis=-1, keepdims=True)
            )
            mid_grad[at] = result
            branch[at] = result.astype(BF16)

        by_rows(chip // 2, body)
        save = pltpu.make_async_copy(mid_grad, mid_grad_out, out_sems.at[0])
        save.start()
        for copy in share(here, branch, branch_out, pair_sems):
            copy.start()
        work.early_home(1)
        save.wait()

    pl.run_scoped(
        sums,
        pltpu.VMEM((chip // 2, width), F32),
        pltpu.VMEM((chip // 2, width), F32),
        pltpu.VMEM((chip // 2, width), BF16),
    )

    def attention(o, qkv, inputs, turned, grads, backs, terms_out, cosine, sine, accumulators):
        block = inputs.shape[1]
        blocks = chip // block
        per = blocks // 2
        queries_wide = o.shape[1]

        def rows_at(i):
            return pl.ds(pl.multiple_of(i * block, block), block)

        def fetches(i, slot):
            sources = (
                (branch_out.at[i // per, rows_at(lax.rem(i, per))], inputs),
                (turned_all.at[rows_at(i)], turned),
                (cosines.at[rows_at(i)], cosine),
                (sines.at[rows_at(i)], sine),
            )
            return [
                pltpu.make_async_copy(source, buffer.at[slot], block_sems.at[slot, n])
                for n, (source, buffer) in enumerate(sources)
            ]

        def stores(i, slot):
            return [
                pltpu.make_async_copy(backs.at[slot], qkv_back.at[rows_at(i)], back_sems.at[slot, 0]),
                pltpu.make_async_copy(
                    terms_out.at[slot], in_term.at[i // per, rows_at(lax.rem(i, per))], back_sems.at[slot, 1]
                ),
            ]

        loads = fetch(((o_all, o), (qkv_all, qkv)), fetch_sems)
        for copy in share(here, branch, branch_out, pair_sems):
            copy.wait()
        for copy in fetches(0, 0):
            copy.start()
        for load in loads:
            load.wait()

        def step(i):
            slot = lax.rem(i, 2)
            work.share_of_hops(1, i, blocks)
            for copy in fetches(i, slot):
                copy.wait()

            @pl.when(i + 1 < blocks)
            def _():
                for copy in fetches(i + 1, 1 - slot):
                    copy.start()

            @pl.when(i > 1)
            def _():
                for copy in stores(i - 2, slot):
                    copy.wait()

            grads[...] = product(inputs[slot], o[...]).astype(BF16)
            attention_block_back(
                turned.at[slot],
                grads,
                backs.at[slot],
                accumulators,
                queries_wide,
                columns_of[i],
                rows_of[i],
                cosine[slot],
                sine[slot],
            )
            terms_out[slot] = times_transposed(backs[slot], qkv[...]).astype(BF16)
            for copy in stores(i, slot):
                copy.start()

        loop(blocks, step)
        for i in range(blocks - 2, blocks):
            for copy in stores(i, i % 2):
                copy.wait()

    block = rows_of.shape[2]
    qkv_wide = qkv_all.shape[1]
    pl.run_scoped(
        attention,
        pltpu.VMEM(o_all.shape, BF16),
        pltpu.VMEM(qkv_all.shape, BF16),
        pltpu.VMEM((2, block, width), BF16),
        pltpu.VMEM((2, block, qkv_wide), BF16),
        pltpu.VMEM((block, o_all.shape[1]), BF16),
        pltpu.VMEM((2, block, qkv_wide), BF16),
        pltpu.VMEM((2, block, width), BF16),
        pltpu.VMEM((2, block, 2 * HEAD_DIM), F32),
        pltpu.VMEM((2, block, 2 * HEAD_DIM), F32),
        pltpu.VMEM((4, block, 2 * HEAD_DIM), F32),
    )

    def output(mid):
        load = fetch(((mid_in, mid),), fetch_sems)[0]
        front.pair().wait_recv()
        load.wait()

        def body_out(at):
            out_rows[at] = (mid[at] + front.rows(at)).astype(BF16)

        by_rows(chip // 2, body_out)

    pl.run_scoped(output, pltpu.VMEM((chip // 2, width), F32))
    save_out = pltpu.make_async_copy(out_rows, out, out_sems.at[1])
    save_out.start()
    work.finish()
    back.finish()
    front.finish()
    save_out.wait()


def scatter_attention(zn, early, *refs):
    normed, qkv_grad, branch, context, normed_two, up_grad, term, mid_grad_in, tokens, gain, two_sum = refs[:11]
    q_out, kv_out, o_out, up_out, in_grad, gain_out, qkv, o, up = refs[11:20]
    buffers, refs = refs[20 : 20 + 3 * SCATTER_BUFFERS], refs[20 + 3 * SCATTER_BUFFERS :]
    total_refs, gain_refs = refs[:4], refs[4:8]
    fetch_sems, out_sems, one_sum = refs[8:11]
    rows_out = total_refs[0]
    here = place()
    enter(zn, here)
    total = Total(here, term, *total_refs)
    q_half = q_out.shape[1] // 2
    work = Scatter(
        zn,
        here,
        early,
        [
            (up, buffers[:SCATTER_BUFFERS], [(up_out, False, 0, up_out.shape[1] // 2)]),
            (o, buffers[SCATTER_BUFFERS : 2 * SCATTER_BUFFERS], [(o_out, False, 0, o_out.shape[1] // 2)]),
            (
                qkv,
                buffers[2 * SCATTER_BUFFERS :],
                [(q_out, False, 0, q_half), (kv_out, True, q_half, kv_out.shape[2])],
            ),
        ],
        refs[11:],
    )
    gains = Gains(zn, here, *gain_refs)
    total.start()

    def terms(left_one, right_one, left_two, right_two, right_three, stage):
        copies = fetch(
            (
                (normed_two, left_one),
                (up_grad, right_one),
                (branch, left_two),
                (context, right_two),
                (qkv_grad, right_three),
            ),
            fetch_sems,
        )
        copies[0].wait()
        copies[1].wait()
        work.make(0, left_one, right_one, stage, total.meet)
        last = pltpu.make_async_copy(normed, left_one, fetch_sems.at[5])
        last.start()
        one_sum[...] = jnp.zeros_like(one_sum)

        def body_gain(at):
            value = tokens[at].astype(F32)
            factor = lax.rsqrt(jnp.mean(value * value, axis=-1, keepdims=True) + norm_eps)
            one_sum[...] += jnp.sum(total.half[at].astype(F32) * (value * factor), axis=0, keepdims=True)

        by_rows(tokens.shape[0], body_gain)
        gains.start([one_sum, two_sum])
        gains.swapped(0)
        copies[2].wait()
        copies[3].wait()
        work.make(1, left_two, right_two, stage)
        copies[4].wait()
        last.wait()
        work.make(2, left_one, right_three, stage)

    pl.run_scoped(
        terms,
        pltpu.VMEM(normed.shape, BF16),
        pltpu.VMEM(up_grad.shape, BF16),
        pltpu.VMEM(branch.shape, BF16),
        pltpu.VMEM(context.shape, BF16),
        pltpu.VMEM(qkv_grad.shape, BF16),
        pltpu.VMEM((2,) + up.shape[1:], BF16),
    )

    def sums(mid_grad):
        copies = fetch(((mid_grad_in, mid_grad),), fetch_sems)
        work.late_hops(0)
        gains.swapped(1)
        work.late_hops(1)
        gains.swapped(2)
        gains.run()
        work.late_hops(2)
        gains.finish(gain_out)
        for copy in copies:
            copy.wait()
        total.pair().wait_recv()

        def body(at):
            value = tokens[at].astype(F32)
            factor = lax.rsqrt(jnp.mean(value * value, axis=-1, keepdims=True) + norm_eps)
            scaled = total.rows(at) * gain[...]
            rows_out[at] = (
                mid_grad[at]
                + factor * scaled
                - value * (factor * factor * factor) * jnp.mean(scaled * value, axis=-1, keepdims=True)
            ).astype(BF16)

        by_rows(tokens.shape[0], body)
        save = pltpu.make_async_copy(rows_out, in_grad, out_sems.at[0])
        save.start()
        save.wait()

    pl.run_scoped(sums, pltpu.VMEM(mid_grad_in.shape, F32))
    work.finish()
    total.finish()


def call(kernel, name, collective_id, operands, specs, outs, out_specs, scratch, order=None):
    results = pl.pallas_call(
        kernel,
        out_shape=[jax.ShapeDtypeStruct(shape, dtype) for shape, dtype in outs],
        in_specs=specs,
        out_specs=out_specs,
        scratch_shapes=scratch,
        name=name,
        compiler_params=pltpu.CompilerParams(
            collective_id=collective_id, has_side_effects=True, vmem_limit_bytes=58 << 20
        ),
    )(*operands)
    return results if order is None else [results[i] for i in order]


def rotate(vectors, cosine, sine_rows):
    half = vectors.shape[-1] // 2
    first, second = vectors[..., :half], vectors[..., half:]
    return jnp.concatenate(
        [first * cosine - second * sine_rows, second * cosine + first * sine_rows], axis=-1
    )


def product(one, two):
    return jnp.dot(one, two, preferred_element_type=F32)


def times_transposed(one, two):
    return lax.dot_general(one, two, (((1,), (1,)), ((), ())), preferred_element_type=F32)


def inner_rows(one, two):
    return lax.dot_general(one, two, (((0,), (0,)), ((), ())), preferred_element_type=F32)


def einsum(form, one, two):
    return jnp.einsum(form, one, two, preferred_element_type=F32)


def halves(weight):
    rows, columns = weight.shape
    return weight.reshape(rows, 2, columns // 2).transpose(1, 0, 2)


def joined(pair):
    return jnp.concatenate([pair[0], pair[1]], axis=1)


def local(
    dp,
    tokens,
    seg_ids,
    q_weight,
    k_weight,
    v_weight,
    o_weight,
    attn_gain,
    gate_weight,
    up_weight,
    down_weight,
    mlp_gain,
    out_grad,
):
    zn = dp // 4
    units = zn * 2
    count, width = tokens.shape
    rows = q_weight.shape[0]
    blocks, block_rows = 2 * seg_ids.shape[0], seg_ids.shape[1]
    q_half, kv_half = q_weight.shape[1] // 2, k_weight.shape[1] // 2
    ff_half = gate_weight.shape[1] // 2
    qkv_half = q_half + 2 * kv_half
    heads, groups = q_half // HEAD_DIM, kv_half // HEAD_DIM
    early = 2 * rows // 48 * 8
    early_sums = max(16, 2 * rows // 128 * 16)

    kv_shard = jnp.concatenate([halves(k_weight), halves(v_weight)], axis=2)
    gain_rows = jnp.zeros((8, 128), F32)
    gain_rows = gain_rows.at[0, :rows].set(attn_gain.astype(F32)).at[1, :rows].set(mlp_gain.astype(F32))
    gain_shard = jnp.stack([gain_rows, gain_rows])

    qkv_full, o_full, gains, tokens_two, grads_two, seg_two = call(
        functools.partial(gather_attention, zn, early),
        "gather_attention",
        0,
        (q_weight, kv_shard, o_weight.T, gain_shard, tokens, out_grad, seg_ids),
        [VMEM] * 7,
        [
            ((width, qkv_half), BF16),
            ((width, q_half), BF16),
            ((units * 16, 128), F32),
            ((2, count, width), BF16),
            ((2, count, width), BF16),
            ((2,) + seg_ids.shape, jnp.int32),
        ],
        [ANY] * 6,
        [DMA((3,))] * 3 + gather_sems(3, 4, zn),
    )
    gains = gains.reshape(dp, 8, 128)[:, :, :rows]
    gain_one, gain_two = gains[:, 0].reshape(1, width), gains[:, 1].reshape(1, width)
    chip = 2 * count
    tokens_chip = tokens_two.reshape(chip, width)
    grads_chip = grads_two.reshape(chip, width)
    segment = seg_two.reshape(blocks, block_rows)

    order = jnp.arange(block_rows, dtype=jnp.int32)
    same = segment[:, :, None] == segment[:, None, :]
    position = jnp.sum((same & (order[None, :] < order[:, None])).astype(jnp.int32), axis=2)
    inverse = 1.0 / 10000.0 ** (jnp.arange(0, HEAD_DIM, 2, dtype=F32) / HEAD_DIM)
    angles = position.astype(F32).reshape(chip, 1) * jnp.tile(inverse, 4)
    sign = jnp.tile(jnp.repeat(jnp.array([-1.0, 1.0], F32), HEAD_DIM // 2), 2)
    cosines, sines = jnp.cos(angles), jnp.sin(angles) * sign

    mid, normed_two, activated, gate_grad, up_grad, back_term, down_full, normed, turned, context = call(
        functools.partial(feedforward, zn, early),
        "feedforward",
        1,
        (
            gate_weight,
            up_weight,
            down_weight.T,
            tokens,
            gain_two,
            grads_chip,
            tokens_chip,
            gain_one,
            qkv_full,
            o_full,
            cosines,
            sines,
            segment[:, :, None],
            segment[:, None, :],
        ),
        [VMEM] * 5 + [ANY] * 2 + [VMEM] + [ANY] * 2 + [VMEM] * 4,
        [((width, ff_half), BF16)] * 3
        + [((count, width), F32), ((2, count, width), BF16)]
        + [((chip, ff_half), BF16)] * 3
        + [((2, count, width), BF16)] * 2
        + [((chip, width), BF16), ((chip, qkv_half), BF16), ((chip, q_half), BF16)],
        [ANY] * 13,
        total_buffers(count, width)
        + [pltpu.VMEM((2, count, width), BF16), DMA((3,)), DMA((3,)), DMA((2,)), DMA((2,)), DMA((2, 3)), DMA((2,))]
        + gather_sems(3, 3, zn),
        order=(3, 4, 5, 6, 7, 8, 2, 10, 11, 12),
    )
    normed_two = normed_two.reshape(chip, width)

    gate_sum, down_sum, out, mid_grad, branch, gain_two_grad, qkv_back, in_term = call(
        functools.partial(scatter_feedforward, zn, early_sums),
        "scatter_feedforward",
        2,
        (
            normed_two,
            gate_grad,
            grads_chip,
            activated,
            back_term,
            down_full,
            mid,
            gain_two,
            turned,
            o_full,
            qkv_full,
            cosines,
            sines,
            segment[:, :, None],
            segment[:, None, :],
        ),
        [ANY] * 7 + [VMEM] + [ANY] * 5 + [VMEM] * 2,
        [((rows, 2 * ff_half), F32)] * 2
        + [
            ((count, width), BF16),
            ((count, width), F32),
            ((2, count, width), BF16),
            ((1, width), F32),
            ((chip, qkv_half), BF16),
            ((2, count, width), BF16),
        ]
        + [((zn, 4 * rows, ff_half), BF16)] * 2
        + [((2, count, width), BF16)],
        [ANY] * 5 + [VMEM] + [ANY] * 5,
        scatter_buffers([(2 * rows, ff_half)] * 2, early_sums, zn)
        + total_buffers(count, width) * 2
        + [DMA((4,)), DMA((2,)), DMA((3,)), DMA((2,)), DMA((2, 2)), DMA((2, 4)), DMA((2, 2))]
        + scatter_sems(2, 2, zn),
        order=range(8),
    )
    branch = branch.reshape(chip, width)

    q_sum, kv_sum, o_sum, up_sum, in_grad, gain_sums = call(
        functools.partial(scatter_attention, zn, early_sums),
        "scatter_attention",
        3,
        (
            normed,
            qkv_back,
            branch,
            context,
            normed_two,
            up_grad,
            in_term,
            mid_grad,
            tokens,
            gain_one,
            gain_two_grad,
        ),
        [ANY] * 8 + [VMEM] * 3,
        [
            ((rows, 2 * q_half), F32),
            ((2, rows, 2 * kv_half), F32),
            ((rows, 2 * q_half), F32),
            ((rows, 2 * ff_half), F32),
            ((count, width), BF16),
            ((8, 4 * rows), F32),
            ((zn, 4 * rows, qkv_half), BF16),
            ((zn, 4 * rows, q_half), BF16),
            ((zn, 4 * rows, ff_half), BF16),
        ],
        [ANY] * 5 + [VMEM] + [ANY] * 3,
        scatter_buffers([(2 * rows, ff_half), (2 * rows, q_half), (2 * rows, qkv_half)], early_sums, zn)
        + total_buffers(count, width)
        + gain_buffers(zn, 4 * rows)
        + [DMA((6,)), DMA((1,)), pltpu.VMEM((1, width), F32)]
        + scatter_sems(3, 4, zn),
        order=range(6),
    )
    gain_grads = lax.dynamic_slice_in_dim(gain_sums, lax.rem(lax.axis_index("dp"), 4) * rows, rows, 1)
    return (
        out,
        in_grad,
        q_sum,
        joined(kv_sum[:, :, :kv_half]),
        joined(kv_sum[:, :, kv_half:]),
        o_sum.T,
        gain_grads[0],
        gate_sum,
        up_sum,
        down_sum.T,
        gain_grads[1],
    )


def solution(mesh):
    arguments = (
        P("dp", None),
        P("dp", None),
        P("dp", "tensor"),
        P("dp", "tensor"),
        P("dp", "tensor"),
        P("tensor", "dp"),
        P("dp"),
        P("dp", "tensor"),
        P("dp", "tensor"),
        P("tensor", "dp"),
        P("dp"),
        P("dp", None),
    )
    results = (
        P("dp", None),
        P("dp", None),
        P("dp", "tensor"),
        P("dp", "tensor"),
        P("dp", "tensor"),
        P("tensor", "dp"),
        P("dp"),
        P("dp", "tensor"),
        P("dp", "tensor"),
        P("tensor", "dp"),
        P("dp"),
    )
    return jax.shard_map(
        functools.partial(local, mesh.shape["dp"]),
        mesh=mesh,
        in_specs=arguments,
        out_specs=results,
        check_vma=False,
    )
```

```python
import functools

import jax
import jax.numpy as jnp
from jax import lax
from jax.experimental import pallas as pl
from jax.experimental.pallas import tpu as pltpu
from jax.sharding import PartitionSpec as P

HEAD_DIM = 64
norm_eps = 1e-05
MESH = pl.DeviceIdType.MESH
ANY = pl.BlockSpec(memory_space=pl.ANY)
VMEM = pl.BlockSpec(memory_space=pltpu.VMEM)
DMA = pltpu.SemaphoreType.DMA
F32 = jnp.float32
BF16 = jnp.bfloat16


def place():
    d = lax.axis_index("dp")
    t = lax.axis_index("tensor")
    return d, t, d // 4, lax.rem(d // 2, 2), lax.rem(d, 2)


def enter(zn, here):
    d, t, z, x, c = here
    bar = pltpu.get_barrier_semaphore()

    def hail(device):
        pl.semaphore_signal(bar, inc=1, device_id=device, device_id_type=MESH)

    hail((d + 1 - 2 * c, t))
    hail((d + 2 - 4 * x, t))
    hail((d, 1 - t))

    @pl.when(z > 0)
    def _():
        hail((d - 4, t))

    @pl.when(z < zn - 1)
    def _():
        hail((d + 4, t))

    pl.semaphore_wait(bar, 5 - (z == 0).astype(jnp.int32) - (z == zn - 1).astype(jnp.int32))


def farthest_first(zn, z, i):
    up = 1 - (2 * z) // zn
    longer = up * (zn - 1 - z) + (1 - up) * z
    shorter = zn - 1 - longer
    rest = i - (longer - shorter)
    return jnp.where(
        rest < 0,
        z + (2 * up - 1) * (longer - i),
        z + (1 - 2 * lax.rem(jnp.maximum(rest, 0), 2)) * (shorter - jnp.maximum(rest, 0) // 2),
    )


def loop(count, body):
    def step(i, carry):
        body(i)
        return carry

    lax.fori_loop(0, count, step, 0)


def remote(src, dst, send, recv, device):
    return pltpu.make_async_remote_copy(
        src_ref=src, dst_ref=dst, send_sem=send, recv_sem=recv, device_id=device, device_id_type=MESH
    )


def by_rows(count, body, block=16):
    def step(i, carry):
        body(pl.ds(pl.multiple_of(i * block, block), block))
        return carry

    lax.fori_loop(0, count // block, step, 0)


def gather_sems(n, sources, zn):
    return [
        DMA((sources,)),
        DMA((sources,)),
        DMA((sources,)),
        DMA((n, zn)),
        DMA((n, zn)),
        DMA((n,)),
        DMA((n,)),
        DMA((n, 2, zn)),
        DMA((n, zn)),
        DMA((n, 2, zn)),
        DMA((n, zn)),
    ]


def part(ref, core, paired):
    if paired:
        return ref.at[core]
    columns = ref.shape[1] // 2
    return ref.at[:, pl.ds(pl.multiple_of(core * columns, columns), columns)]


class Gather:
    def __init__(self, zn, here, arrays, sems):
        self.zn, self.here = zn, here
        self.full = [full for _, full, _ in arrays]
        self.early = [early for _, _, early in arrays]
        self.sources = [
            (j, i) + source for j, (sources, _, _) in enumerate(arrays) for i, source in enumerate(sources)
        ]
        (
            self.loc,
            self.cs,
            self.cr,
            self.xs,
            self.xr,
            self.es,
            self.er,
            self.zs,
            self.zr,
            self.bs,
            self.br,
        ) = sems

    def unit(self, j, unit, first, count):
        rows = self.full[j].shape[0] // (2 * self.zn)
        return pl.ds(pl.multiple_of(unit * rows + first, 8), count)

    def rows(self, j, unit, early):
        rows = self.full[j].shape[0] // (2 * self.zn)
        late = rows - self.early[j]
        first, count = {None: (0, rows), True: (late, rows - late), False: (0, late)}[early]
        return self.full[j].at[self.unit(j, unit, first, count)]

    def mine(self, s):
        d, t, z, x, c = self.here
        j, _, shard, paired, first, columns = self.sources[s]
        rows = self.full[j].shape[0] // (4 * self.zn)
        return self.full[j].at[self.unit(j, z * 2 + x, c * rows, rows), pl.ds(first, columns)]

    def keep(self, s):
        _, _, shard, paired, _, _ = self.sources[s]
        return pltpu.make_async_copy(part(shard, self.here[4], paired), self.mine(s), self.loc.at[s])

    def give(self, s):
        d, t, z, x, c = self.here
        _, _, shard, paired, _, _ = self.sources[s]
        return remote(
            part(shard, 1 - c, paired), self.mine(s), self.cs.at[s], self.cr.at[s], (d + 1 - 2 * c, t)
        )

    def x_late(self, j, o):
        d, t, z, x, c = self.here
        ref = self.rows(j, o * 2 + x, False)
        return remote(ref, ref, self.xs.at[j, o], self.xr.at[j, o], (d + 2 - 4 * x, t))

    def x_early(self, j):
        d, t, z, x, c = self.here
        ref = self.rows(j, z * 2 + x, True)
        return remote(ref, ref, self.es.at[j], self.er.at[j], (d + 2 - 4 * x, t))

    def along(self, j, o, down):
        d, t, z, x, c = self.here
        ref = self.rows(j, o * 2 + x, None)
        return remote(ref, ref, self.zs.at[j, down, o], self.zr.at[j, o], (d + 4 - 8 * down, t))

    def along_early(self, j, o, down):
        d, t, z, x, c = self.here
        ref = self.rows(j, o * 2 + 1 - x, True)
        return remote(ref, ref, self.bs.at[j, down, o], self.br.at[j, o], (d + 4 - 8 * down, t))

    def start(self):
        for s in range(len(self.sources)):
            self.give(s).start()
            self.keep(s).start()

    def ready(self, arrays):
        for j in arrays:
            for s, source in enumerate(self.sources):
                if source[0] == j:
                    self.keep(s).wait()
                    self.give(s).wait_recv()
            if self.early[j]:
                self.x_early(j).start()

    def start_own(self, arrays):
        z, zn = self.here[2], self.zn
        for j in arrays:
            self.x_late(j, z).start()

            @pl.when(z < zn - 1)
            def _():
                self.along(j, z, 0).start()

            @pl.when(z > 0)
            def _():
                self.along(j, z, 1).start()

    def start_early(self, arrays):
        z, zn = self.here[2], self.zn
        for j in arrays:
            if self.early[j]:
                self.x_early(j).wait_recv()

                @pl.when(z < zn - 1)
                def _():
                    self.along_early(j, z, 0).start()

                @pl.when(z > 0)
                def _():
                    self.along_early(j, z, 1).start()

    def relay(self, k, arrays):
        z, zn = self.here[2], self.zn
        o = farthest_first(zn, z, zn - 1 - k)
        down = (o > z).astype(jnp.int32)
        more = ((o < z) & (z < zn - 1)) | ((o > z) & (z > 0))
        for j in arrays:
            self.along(j, o, down).wait_recv()

            @pl.when(more)
            def _():
                self.along(j, o, down).start()

            self.x_late(j, o).start()
            if self.early[j]:
                self.along_early(j, o, down).wait_recv()

                @pl.when(more)
                def _():
                    self.along_early(j, o, down).start()

    def relays(self, first, arrays):
        loop(max(self.zn - first, 0), lambda i: self.relay(first + i, arrays))

    def arrived(self, j):
        loop(self.zn, lambda o: self.x_late(j, o).wait_recv())

    def finish(self):
        z, zn = self.here[2], self.zn
        for s in range(len(self.sources)):
            self.give(s).wait_send()
        for j in range(len(self.full)):
            if self.early[j]:
                self.x_early(j).wait_send()

            def step(o, j=j):
                self.x_late(j, o).wait_send()

                def sent(down):
                    self.along(j, o, down).wait_send()
                    if self.early[j]:
                        self.along_early(j, o, down).wait_send()

                @pl.when((o <= z) & (z < zn - 1))
                def _():
                    sent(0)

                @pl.when((o >= z) & (z > 0))
                def _():
                    sent(1)

            loop(zn, step)


def scatter_sems(n, outs, zn):
    return [
        DMA((n, zn)),
        DMA((n, zn)),
        DMA((n, zn)),
        DMA((n, zn)),
        DMA((n, zn)),
        DMA((n, zn + 1)),
        DMA((n, 2, zn)),
        DMA((n, zn)),
        DMA((n, zn + 1)),
        DMA((n,)),
        DMA((n,)),
        DMA((outs,)),
        DMA((outs,)),
        DMA((outs,)),
    ]


def scatter_buffers(shapes, early, zn):
    out = []
    for rows, columns in shapes:
        late = rows - early
        out += [
            pltpu.VMEM((zn, late, columns), BF16),
            pltpu.VMEM((zn, late, columns), BF16),
            pltpu.VMEM((zn + 1, late, columns), BF16),
            pltpu.VMEM((zn, 2, early, columns), BF16),
            pltpu.VMEM((zn + 1, 2, early, columns), BF16),
            pltpu.VMEM((early, columns), BF16),
            pltpu.VMEM((rows, columns), F32),
        ]
    return out


SCATTER_BUFFERS = 7


class Scatter:
    def __init__(self, zn, here, early, arrays, sems):
        self.zn, self.here, self.early = zn, here, early
        self.term = [term for term, _, _ in arrays]
        self.buffers = [buffers for _, buffers, _ in arrays]
        self.results = [(j,) + result for j, (_, _, results) in enumerate(arrays) for result in results]
        (
            self.st,
            self.ls,
            self.xs,
            self.xr,
            self.zs,
            self.zr,
            self.bls,
            self.bs,
            self.br,
            self.es,
            self.er,
            self.cs,
            self.cr,
            self.loc,
        ) = sems

    def unit(self, j, o, x, first, count):
        rows = self.term[j].shape[1] // 2
        return self.term[j].at[o, pl.ds(pl.multiple_of(x * rows + first, 16), count)]

    def late(self, j):
        return self.buffers[j][0].shape[1]

    def load(self, j, o):
        return pltpu.make_async_copy(
            self.unit(j, o, self.here[3], 0, self.late(j)), self.buffers[j][0].at[o], self.ls.at[j, o]
        )

    def load_early(self, j, o, other):
        x = self.here[3]
        return pltpu.make_async_copy(
            self.unit(j, o, 1 - x if other else x, self.late(j), self.early),
            self.buffers[j][3].at[o, other],
            self.bls.at[j, other, o],
        )

    def across(self, j, o):
        d, t, z, x, c = self.here
        return remote(
            self.unit(j, o, 1 - x, 0, self.late(j)),
            self.buffers[j][1].at[o],
            self.xs.at[j, o],
            self.xr.at[j, o],
            (d + 2 - 4 * x, t),
        )

    def across_early(self, j):
        d, t, z, x, c = self.here
        return remote(
            self.buffers[j][3].at[z, 1], self.buffers[j][5], self.es.at[j], self.er.at[j], (d + 2 - 4 * x, t)
        )

    def along(self, j, o, slot, down):
        d, t, z, x, c = self.here
        own, line = self.buffers[j][0], self.buffers[j][2]
        return remote(own.at[o], line.at[slot], self.zs.at[j, o], self.zr.at[j, slot], (d + 4 - 8 * down, t))

    def along_early(self, j, o, slot, down):
        d, t, z, x, c = self.here
        own, line = self.buffers[j][3], self.buffers[j][4]
        return remote(own.at[o], line.at[slot], self.bs.at[j, o], self.br.at[j, slot], (d + 4 - 8 * down, t))

    def give(self, r):
        d, t, z, x, c = self.here
        j, out, paired, first, columns = self.results[r]
        rows = out.shape[-2]
        ref = self.buffers[j][6].at[
            pl.ds(pl.multiple_of((1 - c) * rows, rows), rows), pl.ds(first, columns)
        ]
        return remote(ref, part(out, c, paired), self.cs.at[r], self.cr.at[r], (d + 1 - 2 * c, t))

    def keep(self, r):
        c = self.here[4]
        j, out, paired, first, columns = self.results[r]
        rows = out.shape[-2]
        ref = self.buffers[j][6].at[pl.ds(pl.multiple_of(c * rows, rows), rows), pl.ds(first, columns)]
        return pltpu.make_async_copy(ref, part(out, c, paired), self.loc.at[r])

    def store(self, j, o, stage, slot):
        columns = self.term[j].shape[2]
        return pltpu.make_async_copy(
            stage.at[slot, :, pl.ds(0, columns)], self.term[j].at[o], self.st.at[j, o]
        )

    def make(self, j, left, right, stage, between=None):
        z, zn = self.here[2], self.zn
        wide, columns = self.term[j].shape[1:]
        block = min(256, wide)

        def send(i):
            o = farthest_first(zn, z, i)
            self.store(j, o, stage, lax.rem(i, 2)).wait()
            self.across(j, o).start()
            for other in range(2):
                self.load_early(j, o, other).start()
            self.load(j, o).start()

        def compute(i):
            o = farthest_first(zn, z, i)
            slot = lax.rem(i, 2)

            def body(m):
                at = pl.multiple_of(o * wide + m * block, block)
                value = inner_rows(left[:, pl.ds(at, block)], right[...])
                stage[slot, pl.ds(pl.multiple_of(m * block, block), block), pl.ds(0, columns)] = value.astype(
                    BF16
                )

            loop(wide // block, body)
            self.store(j, o, stage, slot).start()

        def both(i):
            compute(i)
            send(i - 1)
            self.hop_early(j, i - 1)

        compute(0)
        if between is not None:
            between()
        loop(zn - 1, lambda i: both(i + 1))
        send(zn - 1)

    def add(self, j, o, slots):
        own, got, line = self.buffers[j][:3]

        def body(at):
            value = own[o, at].astype(F32) + got[o, at].astype(F32)
            for slot in slots:
                value = value + line[slot, at].astype(F32)
            own[o, at] = value.astype(BF16)

        by_rows(own.shape[1], body)

    def add_early(self, j, o, slots):
        own, line = self.buffers[j][3:5]
        for other in range(2):

            def body(at):
                value = own[o, other, at].astype(F32)
                for slot in slots:
                    value = value + line[slot, other, at].astype(F32)
                own[o, other, at] = value.astype(BF16)

            by_rows(own.shape[2], body)

    def route(self, i):
        z, zn = self.here[2], self.zn
        o = farthest_first(zn, z, i)
        down = (o < z).astype(jnp.int32)
        distance = jnp.maximum((o - z) * (1 - 2 * down), 1)
        slot = o + (zn - o) * down * (1 // distance)
        inner = ((o > z) & (z > 0)) | ((o < z) & (z < zn - 1))
        return o, slot, down, inner

    def hop_early(self, j, i):
        o, slot, down, inner = self.route(i)
        for other in range(2):
            self.load_early(j, o, other).wait()

        @pl.when(inner)
        def _():
            self.along_early(j, o, o, down).wait_recv()
            self.add_early(j, o, [o])

        self.along_early(j, o, slot, down).start()

    def hop(self, j, i):
        o, slot, down, inner = self.route(i)
        self.load(j, o).wait()
        self.across(j, o).wait_recv()

        @pl.when(inner)
        def _():
            self.along(j, o, o, down).wait_recv()
            self.add(j, o, [o])

        @pl.when(jnp.logical_not(inner))
        def _():
            self.add(j, o, [])

        self.along(j, o, slot, down).start()

    def late_hops(self, j):
        self.early_home(j)
        loop(self.zn - 1, lambda i: self.hop(j, i))

    def share_of_hops(self, j, i, shares):
        hops = self.zn - 1
        first = i * hops // (shares - 1)
        last = jnp.minimum((i + 1) * hops // (shares - 1), hops)

        def step(hop, carry):
            self.hop(j, hop)
            return carry

        lax.fori_loop(first, last, step, 0)

    def at_home(self, action):
        z, zn = self.here[2], self.zn

        @pl.when((z > 0) & (z < zn - 1))
        def _():
            action([z, zn])

        @pl.when(z == 0)
        def _():
            action([zn])

        @pl.when(z == zn - 1)
        def _():
            action([z])

    def early_home(self, j):
        z = self.here[2]
        for other in range(2):
            self.load_early(j, z, other).wait()

        def home(slots):
            for slot in slots:
                self.along_early(j, z, slot, 0).wait_recv()
            self.add_early(j, z, slots)

        self.at_home(home)
        self.across_early(j).start()

    def finish(self):
        z, zn = self.here[2], self.zn
        n = len(self.term)
        for j in range(n):
            own, got, line, early, _, other_early, total = self.buffers[j]
            late = self.late(j)
            self.load(j, z).wait()
            self.across(j, z).wait_recv()

            def home(slots):
                for slot in slots:
                    self.along(j, z, slot, 0).wait_recv()

                def body(at):
                    value = own[z, at].astype(F32) + got[z, at].astype(F32)
                    for slot in slots:
                        value = value + line[slot, at].astype(F32)
                    total[at] = value

                by_rows(late, body)

            self.at_home(home)
            self.across_early(j).wait_recv()
            for i in range(self.early // 16):
                at = pl.ds(16 * i, 16)
                total[pl.ds(late + 16 * i, 16)] = early[z, 0, at].astype(F32) + other_early[at].astype(F32)
            for r, result in enumerate(self.results):
                if result[0] == j:
                    self.give(r).start()
                    self.keep(r).start()
        for r in range(len(self.results)):
            self.give(r).wait()
            self.keep(r).wait()
        for j in range(n):
            self.across_early(j).wait_send()

            def sent(o, j=j):
                self.across(j, o).wait_send()

                @pl.when(o != z)
                def _():
                    self.along(j, o, 0, 0).wait_send()
                    self.along_early(j, o, 0, 0).wait_send()

            loop(zn, sent)


class Gains:
    def __init__(self, zn, here, own, got, line, sems):
        self.zn, self.here, self.own, self.got, self.line, self.sems = zn, here, own, got, line, sems

    def swap(self, i):
        d, t, z, x, c = self.here
        device = ((d + 1 - 2 * c, t), (d + 2 - 4 * x, t), (d, 1 - t))[i]
        return remote(self.own, self.got.at[i], self.sems.at[0, i], self.sems.at[1, i], device)

    def along(self, o, slot, down):
        d, t, z, x, c = self.here
        return remote(
            self.own.at[o], self.line.at[slot], self.sems.at[2, o], self.sems.at[3, slot], (d + 4 - 8 * down, t)
        )

    def start(self, rows):
        wide = self.own.shape[2]
        for o in range(self.zn):
            for i, row in enumerate(rows):
                self.own[o, pl.ds(i, 1)] = row[:, pl.ds(o * wide, wide)]
        self.swap(0).start()

    def swapped(self, i):
        self.swap(i).wait()
        self.own[...] += self.got[i]
        if i < 2:
            self.swap(i + 1).start()

    def hop(self, o, slot, down, inner):
        @pl.when(inner)
        def _():
            self.along(o, o, down).wait_recv()
            self.own[o] += self.line[o]

        self.along(o, slot, down).start()

    def steps(self, k, nearest):
        z, zn = self.here[2], self.zn

        @pl.when(z + k < zn)
        def _():
            self.hop(z + k, z + k, 0, z > 0)

        @pl.when(z - k >= 0)
        def _():
            self.hop(z - k, zn if nearest else z - k, 1, z < zn - 1)

    def run(self):
        zn = self.zn

        def step(i, carry):
            self.steps(zn - 1 - i, False)
            return carry

        lax.fori_loop(0, zn - 2, step, 0)
        self.steps(1, True)

    def finish(self, out):
        z, zn = self.here[2], self.zn
        value = self.own[z]

        @pl.when(z > 0)
        def _():
            self.along(z, z, 0).wait_recv()
            self.own[z] += self.line[z]

        @pl.when(z < zn - 1)
        def _():
            self.along(z, zn, 1).wait_recv()
            self.own[z] += self.line[zn]

        out[...] = self.own[z]

        def step(o, carry):
            @pl.when(o != z)
            def _():
                self.along(o, 0, 0).wait_send()

            return carry

        lax.fori_loop(0, zn, step, 0)


def gain_buffers(zn, wide):
    return [
        pltpu.VMEM((zn, 8, wide), F32),
        pltpu.VMEM((3, zn, 8, wide), F32),
        pltpu.VMEM((zn + 1, 8, wide), F32),
        DMA((4, zn + 1)),
    ]


class Total:
    def __init__(self, here, term, from_core, half, from_pair, sems):
        self.here, self.term, self.from_core, self.half, self.from_pair = here, term, from_core, half, from_pair
        self.sems = sems

    def core(self):
        d, t, z, x, c = self.here
        return remote(self.term.at[1 - c], self.from_core, self.sems.at[0], self.sems.at[1], (d + 1 - 2 * c, t))

    def load(self):
        return pltpu.make_async_copy(self.term.at[self.here[4]], self.half, self.sems.at[4])

    def start(self):
        self.core().start()
        self.load().start()

    def pair(self):
        d, t, z, x, c = self.here
        return remote(self.half, self.from_pair, self.sems.at[2], self.sems.at[3], (d, 1 - t))

    def meet(self, loaded=True):
        if loaded:
            self.load().wait()
        self.core().wait_recv()
        block = 16

        def body(i, carry):
            at = pl.ds(pl.multiple_of(i * block, block), block)
            self.half[at] = (self.half[at].astype(F32) + self.from_core[at].astype(F32)).astype(BF16)
            return carry

        lax.fori_loop(0, self.half.shape[0] // block, body, 0)
        self.pair().start()

    def rows(self, at):
        return self.half[at].astype(F32) + self.from_pair[at].astype(F32)

    def finish(self):
        self.core().wait_send()
        self.pair().wait_send()


def total_buffers(tokens, width):
    return [pltpu.VMEM((tokens, width), BF16)] * 3 + [DMA((5,))]


def share(here, src, dst, sems):
    d, t, z, x, c = here
    return (
        pltpu.make_async_copy(src, dst.at[c], sems.at[0]),
        remote(src, dst.at[c], sems.at[1], sems.at[2], (d + 1 - 2 * c, t)),
    )


def lanes(shape):
    return lax.broadcasted_iota(jnp.int32, shape, 1)


def partner(value):
    half = HEAD_DIM // 2
    wide = 2 * HEAD_DIM
    lower = lax.rem(lanes(value.shape), HEAD_DIM) < half
    return jnp.where(lower, pltpu.roll(value, wide - half, 1), pltpu.roll(value, half, 1))


def same_segment(row):
    count = row.shape[1]
    wide = jnp.broadcast_to(row, (count, count))
    before = lax.broadcasted_iota(jnp.int32, wide.shape, 1) < lax.broadcasted_iota(jnp.int32, wide.shape, 0)
    return wide == wide.T, before


def allowed_in(row):
    same, before = same_segment(row)
    here = lax.broadcasted_iota(jnp.int32, same.shape, 1) == lax.broadcasted_iota(jnp.int32, same.shape, 0)
    return same & (before | here)


def softmax_of(queries, keys, allowed):
    scores = jnp.where(allowed, times_transposed(queries, keys) * HEAD_DIM ** (-0.5), -1e30)
    shifted = jnp.exp(scores - jnp.max(scores, axis=-1, keepdims=True))
    return shifted / jnp.sum(shifted, axis=-1, keepdims=True)


def key_value_pairs(pair):
    pair = pair.astype(F32)
    first = lanes(pair.shape) < HEAD_DIM
    key, value = jnp.where(first, pair, 0.0), jnp.where(first, 0.0, pair)
    return [
        part.astype(BF16)
        for part in (key, pltpu.roll(key, HEAD_DIM, 1), pltpu.roll(value, HEAD_DIM, 1), value)
    ]


def attention_block(turned, context, queries_wide, row):
    wide = 2 * HEAD_DIM
    allowed = allowed_in(row)
    key_one, key_two, value_one, value_two = key_value_pairs(turned[:, queries_wide:])

    def heads(p):
        at = pl.ds(pl.multiple_of(p * wide, wide), wide)
        queries = turned[:, at]
        one = softmax_of(queries, key_one, allowed).astype(BF16)
        two = softmax_of(queries, key_two, allowed).astype(BF16)
        context[:, at] = (product(one, value_one) + product(two, value_two)).astype(BF16)

    loop(queries_wide // wide, heads)


def attention_block_back(turned, grads, back, sums, queries_wide, row, cosine, sine):
    wide = 2 * HEAD_DIM
    scale = HEAD_DIM ** (-0.5)
    allowed = allowed_in(row)
    key_one, key_two, value_one, value_two = key_value_pairs(turned[:, queries_wide:])
    sums[...] = jnp.zeros_like(sums)

    def heads(p):
        at = pl.ds(pl.multiple_of(p * wide, wide), wide)
        queries, grad = turned[:, at], grads[:, at]
        total = None
        for i, (key, value) in enumerate(((key_one, value_one), (key_two, value_two))):
            probs = softmax_of(queries, key, allowed)
            sums[i] += inner_rows(probs.astype(BF16), grad)
            prob_grad = times_transposed(grad, value)
            delta = jnp.sum(probs * prob_grad, axis=-1, keepdims=True)
            score_grad = (probs * (prob_grad - delta)).astype(BF16)
            term = product(score_grad, key)
            total = term if total is None else total + term
            sums[2 + i] += inner_rows(score_grad, queries)
        total = total * scale
        back[:, at] = (total * cosine - partner(total) * sine).astype(BF16)

    loop(queries_wide // wide, heads)
    value_grad = pltpu.roll(sums[0], HEAD_DIM, 1) + sums[1]
    key_grad = (sums[2] + pltpu.roll(sums[3], HEAD_DIM, 1)) * scale
    turned_back = key_grad * cosine - partner(key_grad) * sine
    back[:, pl.ds(queries_wide, wide)] = jnp.where(
        lanes(value_grad.shape) < HEAD_DIM, turned_back, value_grad
    ).astype(BF16)


def forward(zn, early, *refs):
    q, kv, o_shard, gains, tokens, grads, seg, gate, up, down, inverse, sign = refs[:12]
    qkv_all, o_all, gains_all, chip_tokens, chip_grads, seg_all = refs[12:18]
    gate_all, up_all, down_all, mid_out, normed_out, act_out, gate_grad_out, up_grad_out, back_out = refs[18:27]
    term, normed_one_out, turned_out, context_out, cosines_out, sines_out, gain_out = refs[27:34]
    total_refs = refs[34:38]
    normed, out_sems, pair_sems, load_sems, grad_sems, stage_sems, block_sems = refs[38:45]
    cosines, sines, seg_pair, gain_tiles, gain_rows, swap_sems, seg_sems = refs[45:52]
    here = place()
    c = here[4]
    enter(zn, here)
    total = Total(here, term, *total_refs)
    q_half = q.shape[1] // 2
    work = Gather(
        zn,
        here,
        [
            ([(gains, True, 0, gains.shape[2])], gains_all, 0),
            ([(q, False, 0, q_half), (kv, True, q_half, kv.shape[2])], qkv_all, early),
            ([(o_shard, False, 0, o_shard.shape[1] // 2)], o_all, early),
        ]
        + [
            ([(shard, False, 0, shard.shape[1] // 2)], full, early)
            for shard, full in ((down, down_all), (gate, gate_all), (up, up_all))
        ],
        refs[52:],
    )
    count, width = tokens.shape
    columns = gate_all.shape[1]
    block = seg.shape[1]
    blocks = 2 * count // block
    per = count // block
    attention_set = [0, 1, 2]
    swap = remote(seg, seg_pair.at[c], seg_sems.at[0], seg_sems.at[1], (here[0] + 1 - 2 * c, here[1]))
    swap.start()
    seg_pair[c] = seg[...]
    work.start()
    work.ready(attention_set)
    work.start_own(attention_set)
    shared = [
        share(here, src, dst, swap_sems.at[n])
        for n, (src, dst) in enumerate(((tokens, chip_tokens), (grads, chip_grads)))
    ]
    for copies in shared:
        for copy in copies:
            copy.start()
    work.ready([5])
    work.start_own([5])
    swap.wait()
    for i in range(blocks):
        row = seg_pair[i // per, pl.ds(i % per, 1)]
        same, before = same_segment(row)
        position = jnp.sum(jnp.where(same & before, 1.0, 0.0), axis=-1, keepdims=True)
        angles = position * inverse[...]
        cosines[pl.ds(i * block, block)] = jnp.cos(angles)
        sines[pl.ds(i * block, block)] = jnp.sin(angles) * sign[...]
    saves = [
        pltpu.make_async_copy(src, dst, seg_sems.at[2 + n])
        for n, (src, dst) in enumerate(((cosines, cosines_out), (sines, sines_out), (seg_pair, seg_all)))
    ]
    for copy in saves:
        copy.start()
    work.start_early([1, 2])
    work.relay(1, attention_set)
    work.start_early([5])
    work.ready([3])
    work.start_own([3])
    work.relay(2, attention_set)
    work.relays(3, attention_set)
    work.start_early([3])
    work.ready([4])
    work.start_own([4])
    work.arrived(0)
    load = pltpu.make_async_copy(gains_all, gain_tiles, load_sems.at[0])
    load.start()
    load.wait()
    features = width // (4 * zn)
    for owner in range(4 * zn):
        for i in range(2):
            gain_rows[pl.ds(i, 1), pl.ds(owner * features, features)] = gain_tiles[
                pl.ds(owner * 8 + i, 1), :features
            ]
    save_gains = pltpu.make_async_copy(gain_rows, gain_out, load_sems.at[1])
    save_gains.start()
    gain_one, gain = gain_rows[pl.ds(0, 1)], gain_rows[pl.ds(1, 1)]
    for copies in shared:
        for copy in copies:
            copy.wait()
    work.arrived(1)
    work.arrived(2)
    save_gains.wait()
    half = total_refs[1]

    def attention(qkv, o, inputs, normed_one, turned, context, attended):
        queries_wide = context.shape[2]
        wide = 2 * HEAD_DIM

        def place_of(i):
            return lax.rem((1 - c) * per + i, blocks)

        def rows_at(i):
            return pl.ds(pl.multiple_of(place_of(i) * block, block), block)

        def fetch_inputs(i, slot):
            which = place_of(i)
            return pltpu.make_async_copy(
                chip_tokens.at[which // per, pl.ds(pl.multiple_of(lax.rem(which, per) * block, block), block)],
                inputs.at[slot],
                grad_sems.at[slot],
            )

        def stores(i, slot):
            return [
                pltpu.make_async_copy(buffer.at[slot], out.at[rows_at(i)], stage_sems.at[slot, n])
                for n, (buffer, out) in enumerate(
                    ((normed_one, normed_one_out), (turned, turned_out), (context, context_out))
                )
            ]

        def store_term(i, slot):
            return pltpu.make_async_copy(
                attended.at[slot],
                term.at[1 - c, pl.ds(pl.multiple_of(i * block, block), block)],
                block_sems.at[slot],
            )

        fetch_inputs(0, 0).start()
        loads = [
            pltpu.make_async_copy(qkv_all, qkv, load_sems.at[0]),
            pltpu.make_async_copy(o_all, o, load_sems.at[1]),
        ]
        for load in loads:
            load.start()
        for load in loads:
            load.wait()

        def one_block(i):
            slot = lax.rem(i, 2)
            to = rows_at(i)
            fetch_inputs(i, slot).wait()

            @pl.when(i + 1 < blocks)
            def _():
                fetch_inputs(i + 1, 1 - slot).start()

            @pl.when(i > 1)
            def _():
                for copy in stores(i - 2, slot):
                    copy.wait()

            def norm(at):
                value = inputs[slot, at].astype(F32)
                factor = lax.rsqrt(jnp.mean(value * value, axis=-1, keepdims=True) + norm_eps)
                normed_one[slot, at] = (value * factor * gain_one).astype(BF16)

            by_rows(block, norm)
            cosine, sine = cosines[to], sines[to]
            raw = product(normed_one[slot], qkv[...])
            for first in range(0, queries_wide, wide):
                value = raw[:, first : first + wide]
                turned[slot, :, pl.ds(first, wide)] = (value * cosine + partner(value) * sine).astype(BF16)
            value = raw[:, queries_wide:]
            is_key = lanes(value.shape) < HEAD_DIM
            turned[slot, :, pl.ds(queries_wide, wide)] = jnp.where(
                is_key, value * cosine + partner(value) * sine, value
            ).astype(BF16)
            which = place_of(i)
            row = seg_pair[which // per, pl.ds(lax.rem(which, per), 1)]
            attention_block(turned.at[slot], context.at[slot], queries_wide, row)
            for copy in stores(i, slot):
                copy.start()
            return slot

        def other(i):
            slot = one_block(i)
            attended[slot] = times_transposed(context[slot], o[...]).astype(BF16)
            store_term(i, slot).start()

        def own(i):
            slot = one_block(per + i)
            half[pl.ds(pl.multiple_of(i * block, block), block)] = times_transposed(
                context[slot], o[...]
            ).astype(BF16)

        loop(per, other)
        for i in range(per):
            store_term(i, i % 2).wait()
        total.core().start()
        work.relay(1, [3])
        work.relay(2, [3])
        work.relay(1, [5])
        work.relay(2, [5])
        loop(per, own)
        for i in range(blocks - 2, blocks):
            for copy in stores(i, i % 2):
                copy.wait()

    pl.run_scoped(
        attention,
        pltpu.VMEM(qkv_all.shape, BF16),
        pltpu.VMEM(o_all.shape, BF16),
        pltpu.VMEM((2, block, width), BF16),
        pltpu.VMEM((2, block, width), BF16),
        pltpu.VMEM((2, block, qkv_all.shape[1]), BF16),
        pltpu.VMEM((2, block, o_all.shape[1]), BF16),
        pltpu.VMEM((2, block, width), BF16),
    )
    total.meet(False)
    work.start_early([4])
    work.relays(3, [3])
    work.relay(1, [4])
    work.relay(2, [4])

    def sums(mid):
        total.pair().wait_recv()

        def body(at):
            value = tokens[at].astype(F32) + total.rows(at)
            mid[at] = value
            factor = lax.rsqrt(jnp.mean(value * value, axis=-1, keepdims=True) + norm_eps)
            normed[c, at] = (value * factor * gain).astype(BF16)

        by_rows(count, body)
        save = pltpu.make_async_copy(mid, mid_out, out_sems.at[0])
        save.start()
        for copy in share(here, normed.at[c], normed, pair_sems)[1:]:
            copy.start()
        save.wait()

    def hidden(first, second, silu, slope, up_grad, inputs, result, stages, back_stage):
        def fetch_grads(i, slot):
            return pltpu.make_async_copy(
                chip_grads.at[i // per, pl.ds(pl.multiple_of(lax.rem(i, per) * block, block), block)],
                inputs.at[slot],
                grad_sems.at[slot],
            )

        def at_block(i):
            return pl.ds(pl.multiple_of(i * block, block), block)

        fetch_grads(0, 0).start()
        work.arrived(3)
        load = pltpu.make_async_copy(down_all, first, load_sems.at[0])
        load.start()
        load.wait()

        def hidden_block(i):
            slot = lax.rem(i, 2)
            fetch_grads(i, slot).wait()

            @pl.when(i + 1 < blocks)
            def _():
                fetch_grads(i + 1, 1 - slot).start()

            slope[at_block(i)] = product(inputs[slot], first[...])

        loop(blocks, hidden_block)
        work.relays(3, [4])
        pl.run_scoped(sums, pltpu.VMEM((count, width), F32))
        work.relays(3, [5])
        work.arrived(4)
        load = pltpu.make_async_copy(gate_all, second, load_sems.at[1])
        load.start()
        share(here, normed.at[c], normed, pair_sems)[1].wait()
        save = pltpu.make_async_copy(normed, normed_out, out_sems.at[1])
        save.start()
        load.wait()

        def gate_block(i):
            result[...] = product(normed[i // per, at_block(lax.rem(i, per))], second[...])

            def body(at):
                to = pl.ds(pl.multiple_of(i * block + at.start, 16), at.size)
                gated = result[at]
                grad = slope[to]
                sigmoid = 1.0 / (1.0 + jnp.exp(-gated))
                silu[to] = gated * sigmoid
                up_grad[to] = (grad * gated * sigmoid).astype(BF16)
                slope[to] = grad * (sigmoid * (1.0 + gated * (1.0 - sigmoid)))

            by_rows(block, body)

        loop(blocks, gate_block)
        save_up = pltpu.make_async_copy(up_grad, up_grad_out, out_sems.at[2])
        save_up.start()
        work.arrived(5)
        load = pltpu.make_async_copy(up_all, first, load_sems.at[0])
        load.start()
        load.wait()

        def stores(i, slot):
            to = at_block(i)
            return (
                pltpu.make_async_copy(stages.at[slot, 0], act_out.at[to], stage_sems.at[slot, 0]),
                pltpu.make_async_copy(stages.at[slot, 1], gate_grad_out.at[to], stage_sems.at[slot, 1]),
                pltpu.make_async_copy(
                    back_stage.at[slot], back_out.at[i // per, at_block(lax.rem(i, per))], stage_sems.at[slot, 2]
                ),
            )

        def up_block(i):
            slot = lax.rem(i, 2)

            @pl.when(i > 1)
            def _():
                for copy in stores(i - 2, slot):
                    copy.wait()

            result[...] = product(normed[i // per, at_block(lax.rem(i, per))], first[...])

            def body(at):
                to = pl.ds(pl.multiple_of(i * block + at.start, 16), at.size)
                upward = result[at]
                stages[slot, 0, at] = (silu[to] * upward).astype(BF16)
                stages[slot, 1, at] = (slope[to] * upward).astype(BF16)

            by_rows(block, body)
            value = times_transposed(stages[slot, 1], second[...]) + times_transposed(
                up_grad[at_block(i)], first[...]
            )
            back_stage[slot] = value.astype(BF16)
            for copy in stores(i, slot):
                copy.start()

        loop(blocks, up_block)
        for i in range(max(blocks - 2, 0), blocks):
            for copy in stores(i, i % 2):
                copy.wait()
        save.wait()
        save_up.wait()

    pl.run_scoped(
        hidden,
        pltpu.VMEM((width, columns), BF16),
        pltpu.VMEM((width, columns), BF16),
        pltpu.VMEM((2 * count, columns), F32),
        pltpu.VMEM((2 * count, columns), F32),
        pltpu.VMEM((2 * count, columns), BF16),
        pltpu.VMEM((2, block, width), BF16),
        pltpu.VMEM((block, columns), F32),
        pltpu.VMEM((2, 2, block, columns), BF16),
        pltpu.VMEM((2, block, width), BF16),
    )
    work.finish()
    total.finish()
    for copy in saves:
        copy.wait()


def fetch(pairs, sems):
    copies = [pltpu.make_async_copy(src, dst, sems.at[i]) for i, (src, dst) in enumerate(pairs)]
    for copy in copies:
        copy.start()
    return copies


def scatter_feedforward(zn, early, *refs):
    normed, gate_grad, chip_grads, activated, back_term, down_all, mid_in, gain = refs[:8]
    turned_all, o_all, qkv_all, cosines, sines, rows_of = refs[8:14]
    gate_out, down_out, out, mid_grad_out, branch_out, gain_out, qkv_back, in_term = refs[14:22]
    gate, down, out_term = refs[22:25]
    buffers, refs = refs[25 : 25 + 2 * SCATTER_BUFFERS], refs[25 + 2 * SCATTER_BUFFERS :]
    back_refs, out_refs = refs[:4], refs[4:8]
    fetch_sems, out_sems, pair_sems, weight_sems, stage_sems, block_sems, back_sems = refs[8:15]
    branch, out_rows = back_refs[0], out_refs[0]
    here = place()
    c = here[4]
    chip, width = chip_grads.shape
    enter(zn, here)
    back = Total(here, back_term, *back_refs)
    front = Total(here, out_term, *out_refs)
    work = Scatter(
        zn,
        here,
        early,
        [
            (
                term,
                buffers[SCATTER_BUFFERS * j : SCATTER_BUFFERS * (j + 1)],
                [(result, False, 0, result.shape[1] // 2)],
            )
            for j, (term, result) in enumerate(((down, down_out), (gate, gate_out)))
        ],
        refs[15:],
    )
    back.start()

    def out_terms(right_one, weights, stages):
        block = weights.shape[1]

        def fetch_weights(i, slot):
            return pltpu.make_async_copy(
                down_all.at[pl.ds(pl.multiple_of(i * block, block), block)], weights.at[slot], weight_sems.at[slot]
            )

        def stores(i, slot):
            to = pl.ds(pl.multiple_of(i * block, block), block)
            return [
                pltpu.make_async_copy(
                    stages.at[slot, pl.ds(half * (chip // 2), chip // 2)],
                    out_term.at[half, :, to],
                    stage_sems.at[slot, half],
                )
                for half in range(2)
            ]

        fetch_weights(0, 0).start()

        def step(i):
            slot = lax.rem(i, 2)
            fetch_weights(i, slot).wait()

            @pl.when(i + 1 < width // block)
            def _():
                fetch_weights(i + 1, 1 - slot).start()

            @pl.when(i > 1)
            def _():
                for copy in stores(i - 2, slot):
                    copy.wait()

            stages[slot] = times_transposed(right_one[...], weights[slot]).astype(BF16)
            for copy in stores(i, slot):
                copy.start()

        loop(width // block, step)
        for i in range(width // block - 2, width // block):
            for copy in stores(i, i % 2):
                copy.wait()

    def terms(left_one, right_one, left_two, right_two, stage, weights, stages):
        copies = fetch(
            (
                (chip_grads, left_one),
                (activated, right_one),
                (normed, left_two),
                (gate_grad, right_two),
            ),
            fetch_sems,
        )
        copies[0].wait()
        copies[1].wait()
        work.make(0, left_one, right_one, stage, back.meet)
        copies[2].wait()
        copies[3].wait()
        work.make(1, left_two, right_two, stage)
        out_terms(right_one, weights, stages)
        front.start()

    pl.run_scoped(
        terms,
        pltpu.VMEM(chip_grads.shape, BF16),
        pltpu.VMEM(activated.shape, BF16),
        pltpu.VMEM(normed.shape, BF16),
        pltpu.VMEM(gate_grad.shape, BF16),
        pltpu.VMEM((2,) + down.shape[1:], BF16),
        pltpu.VMEM((2, 256, down.shape[2]), BF16),
        pltpu.VMEM((2, chip, 256), BF16),
    )

    def sums(mid, mid_grad, grads):
        copies = fetch(
            (
                (mid_in, mid),
                (chip_grads.at[pl.ds(pl.multiple_of(c * (chip // 2), 16), chip // 2)], grads),
            ),
            fetch_sems,
        )
        work.late_hops(0)
        front.meet()
        for copy in copies:
            copy.wait()
        gain_out[...] = jnp.zeros_like(gain_out)

        def body_gain(at):
            value = mid[at]
            factor = lax.rsqrt(jnp.mean(value * value, axis=-1, keepdims=True) + norm_eps)
            gain_out[...] += jnp.sum(back.half[at].astype(F32) * (value * factor), axis=0, keepdims=True)

        by_rows(chip // 2, body_gain)
        back.pair().wait_recv()

        def body(at):
            value = mid[at]
            factor = lax.rsqrt(jnp.mean(value * value, axis=-1, keepdims=True) + norm_eps)
            scaled = back.rows(at) * gain[...]
            result = (
                grads[at].astype(F32)
                + factor * scaled
                - value * (factor * factor * factor) * jnp.mean(scaled * value, axis=-1, keepdims=True)
            )
            mid_grad[at] = result
            branch[at] = result.astype(BF16)

        by_rows(chip // 2, body)
        save = pltpu.make_async_copy(mid_grad, mid_grad_out, out_sems.at[0])
        save.start()
        for copy in share(here, branch, branch_out, pair_sems):
            copy.start()
        work.early_home(1)
        save.wait()

    pl.run_scoped(
        sums,
        pltpu.VMEM((chip // 2, width), F32),
        pltpu.VMEM((chip // 2, width), F32),
        pltpu.VMEM((chip // 2, width), BF16),
    )

    def attention(o, qkv, inputs, turned, grads, backs, terms_out, cosine, sine, accumulators):
        block = inputs.shape[1]
        blocks = chip // block
        per = blocks // 2
        queries_wide = o.shape[1]

        def rows_at(i):
            return pl.ds(pl.multiple_of(i * block, block), block)

        def fetches(i, slot):
            sources = (
                (branch_out.at[i // per, rows_at(lax.rem(i, per))], inputs),
                (turned_all.at[rows_at(i)], turned),
                (cosines.at[rows_at(i)], cosine),
                (sines.at[rows_at(i)], sine),
            )
            return [
                pltpu.make_async_copy(source, buffer.at[slot], block_sems.at[slot, n])
                for n, (source, buffer) in enumerate(sources)
            ]

        def stores(i, slot):
            return [
                pltpu.make_async_copy(backs.at[slot], qkv_back.at[rows_at(i)], back_sems.at[slot, 0]),
                pltpu.make_async_copy(
                    terms_out.at[slot], in_term.at[i // per, rows_at(lax.rem(i, per))], back_sems.at[slot, 1]
                ),
            ]

        loads = fetch(((o_all, o), (qkv_all, qkv)), fetch_sems)
        for copy in share(here, branch, branch_out, pair_sems):
            copy.wait()
        for copy in fetches(0, 0):
            copy.start()
        for load in loads:
            load.wait()

        def step(i):
            slot = lax.rem(i, 2)
            work.share_of_hops(1, i, blocks)
            for copy in fetches(i, slot):
                copy.wait()

            @pl.when(i + 1 < blocks)
            def _():
                for copy in fetches(i + 1, 1 - slot):
                    copy.start()

            @pl.when(i > 1)
            def _():
                for copy in stores(i - 2, slot):
                    copy.wait()

            grads[...] = product(inputs[slot], o[...]).astype(BF16)
            attention_block_back(
                turned.at[slot],
                grads,
                backs.at[slot],
                accumulators,
                queries_wide,
                rows_of[i],
                cosine[slot],
                sine[slot],
            )
            terms_out[slot] = times_transposed(backs[slot], qkv[...]).astype(BF16)
            for copy in stores(i, slot):
                copy.start()

        loop(blocks, step)
        for i in range(blocks - 2, blocks):
            for copy in stores(i, i % 2):
                copy.wait()

    block = rows_of.shape[2]
    qkv_wide = qkv_all.shape[1]
    pl.run_scoped(
        attention,
        pltpu.VMEM(o_all.shape, BF16),
        pltpu.VMEM(qkv_all.shape, BF16),
        pltpu.VMEM((2, block, width), BF16),
        pltpu.VMEM((2, block, qkv_wide), BF16),
        pltpu.VMEM((block, o_all.shape[1]), BF16),
        pltpu.VMEM((2, block, qkv_wide), BF16),
        pltpu.VMEM((2, block, width), BF16),
        pltpu.VMEM((2, block, 2 * HEAD_DIM), F32),
        pltpu.VMEM((2, block, 2 * HEAD_DIM), F32),
        pltpu.VMEM((4, block, 2 * HEAD_DIM), F32),
    )

    def output(mid):
        load = fetch(((mid_in, mid),), fetch_sems)[0]
        front.pair().wait_recv()
        load.wait()

        def body_out(at):
            out_rows[at] = (mid[at] + front.rows(at)).astype(BF16)

        by_rows(chip // 2, body_out)

    pl.run_scoped(output, pltpu.VMEM((chip // 2, width), F32))
    save_out = pltpu.make_async_copy(out_rows, out, out_sems.at[1])
    save_out.start()
    work.finish()
    back.finish()
    front.finish()
    save_out.wait()


def scatter_attention(zn, early, *refs):
    normed, qkv_grad, branch, context, normed_two, up_grad, term, mid_grad_in, tokens, gain, two_sum = refs[:11]
    q_out, kv_out, o_out, up_out, in_grad, gain_out, qkv, o, up = refs[11:20]
    buffers, refs = refs[20 : 20 + 3 * SCATTER_BUFFERS], refs[20 + 3 * SCATTER_BUFFERS :]
    total_refs, gain_refs = refs[:4], refs[4:8]
    fetch_sems, out_sems, one_sum = refs[8:11]
    rows_out = total_refs[0]
    here = place()
    enter(zn, here)
    total = Total(here, term, *total_refs)
    q_half = q_out.shape[1] // 2
    work = Scatter(
        zn,
        here,
        early,
        [
            (up, buffers[:SCATTER_BUFFERS], [(up_out, False, 0, up_out.shape[1] // 2)]),
            (o, buffers[SCATTER_BUFFERS : 2 * SCATTER_BUFFERS], [(o_out, False, 0, o_out.shape[1] // 2)]),
            (
                qkv,
                buffers[2 * SCATTER_BUFFERS :],
                [(q_out, False, 0, q_half), (kv_out, True, q_half, kv_out.shape[2])],
            ),
        ],
        refs[11:],
    )
    gains = Gains(zn, here, *gain_refs)
    total.start()

    def terms(left_one, right_one, left_two, right_two, right_three, stage):
        copies = fetch(
            (
                (normed_two, left_one),
                (up_grad, right_one),
                (branch, left_two),
                (context, right_two),
                (qkv_grad, right_three),
            ),
            fetch_sems,
        )
        copies[0].wait()
        copies[1].wait()
        work.make(0, left_one, right_one, stage, total.meet)
        last = pltpu.make_async_copy(normed, left_one, fetch_sems.at[5])
        last.start()
        one_sum[...] = jnp.zeros_like(one_sum)

        def body_gain(at):
            value = tokens[at].astype(F32)
            factor = lax.rsqrt(jnp.mean(value * value, axis=-1, keepdims=True) + norm_eps)
            one_sum[...] += jnp.sum(total.half[at].astype(F32) * (value * factor), axis=0, keepdims=True)

        by_rows(tokens.shape[0], body_gain)
        gains.start([one_sum, two_sum])
        gains.swapped(0)
        copies[2].wait()
        copies[3].wait()
        work.make(1, left_two, right_two, stage)
        copies[4].wait()
        last.wait()
        work.make(2, left_one, right_three, stage)

    pl.run_scoped(
        terms,
        pltpu.VMEM(normed.shape, BF16),
        pltpu.VMEM(up_grad.shape, BF16),
        pltpu.VMEM(branch.shape, BF16),
        pltpu.VMEM(context.shape, BF16),
        pltpu.VMEM(qkv_grad.shape, BF16),
        pltpu.VMEM((2,) + up.shape[1:], BF16),
    )

    def sums(mid_grad):
        copies = fetch(((mid_grad_in, mid_grad),), fetch_sems)
        work.late_hops(0)
        gains.swapped(1)
        work.late_hops(1)
        gains.swapped(2)
        gains.run()
        work.late_hops(2)
        gains.finish(gain_out)
        for copy in copies:
            copy.wait()
        total.pair().wait_recv()

        def body(at):
            value = tokens[at].astype(F32)
            factor = lax.rsqrt(jnp.mean(value * value, axis=-1, keepdims=True) + norm_eps)
            scaled = total.rows(at) * gain[...]
            rows_out[at] = (
                mid_grad[at]
                + factor * scaled
                - value * (factor * factor * factor) * jnp.mean(scaled * value, axis=-1, keepdims=True)
            ).astype(BF16)

        by_rows(tokens.shape[0], body)
        save = pltpu.make_async_copy(rows_out, in_grad, out_sems.at[0])
        save.start()
        save.wait()

    pl.run_scoped(sums, pltpu.VMEM(mid_grad_in.shape, F32))
    work.finish()
    total.finish()


def call(kernel, name, collective_id, operands, specs, outs, out_specs, scratch, order=None):
    results = pl.pallas_call(
        kernel,
        out_shape=[jax.ShapeDtypeStruct(shape, dtype) for shape, dtype in outs],
        in_specs=specs,
        out_specs=out_specs,
        scratch_shapes=scratch,
        name=name,
        compiler_params=pltpu.CompilerParams(
            collective_id=collective_id, has_side_effects=True, vmem_limit_bytes=58 << 20
        ),
    )(*operands)
    return results if order is None else [results[i] for i in order]


def rotate(vectors, cosine, sine_rows):
    half = vectors.shape[-1] // 2
    first, second = vectors[..., :half], vectors[..., half:]
    return jnp.concatenate(
        [first * cosine - second * sine_rows, second * cosine + first * sine_rows], axis=-1
    )


def product(one, two):
    return jnp.dot(one, two, preferred_element_type=F32)


def times_transposed(one, two):
    return lax.dot_general(one, two, (((1,), (1,)), ((), ())), preferred_element_type=F32)


def inner_rows(one, two):
    return lax.dot_general(one, two, (((0,), (0,)), ((), ())), preferred_element_type=F32)


def einsum(form, one, two):
    return jnp.einsum(form, one, two, preferred_element_type=F32)


def halves(weight):
    rows, columns = weight.shape
    return weight.reshape(rows, 2, columns // 2).transpose(1, 0, 2)


def joined(pair):
    return jnp.concatenate([pair[0], pair[1]], axis=1)


def local(
    dp,
    tokens,
    seg_ids,
    q_weight,
    k_weight,
    v_weight,
    o_weight,
    attn_gain,
    gate_weight,
    up_weight,
    down_weight,
    mlp_gain,
    out_grad,
):
    zn = dp // 4
    units = zn * 2
    count, width = tokens.shape
    rows = q_weight.shape[0]
    blocks, block_rows = 2 * seg_ids.shape[0], seg_ids.shape[1]
    q_half, kv_half = q_weight.shape[1] // 2, k_weight.shape[1] // 2
    ff_half = gate_weight.shape[1] // 2
    qkv_half = q_half + 2 * kv_half
    heads, groups = q_half // HEAD_DIM, kv_half // HEAD_DIM
    early = 2 * rows // 48 * 8
    early_sums = max(16, 2 * rows // 128 * 16)

    kv_shard = jnp.concatenate([halves(k_weight), halves(v_weight)], axis=2)
    gain_rows = jnp.zeros((8, 128), F32)
    gain_rows = gain_rows.at[0, :rows].set(attn_gain.astype(F32)).at[1, :rows].set(mlp_gain.astype(F32))
    gain_shard = jnp.stack([gain_rows, gain_rows])

    chip = 2 * count
    inverse = 1.0 / 10000.0 ** (jnp.arange(0, HEAD_DIM, 2, dtype=F32) / HEAD_DIM)
    inverse = jnp.tile(inverse, 4).reshape(1, 2 * HEAD_DIM)
    sign = jnp.tile(jnp.repeat(jnp.array([-1.0, 1.0], F32), HEAD_DIM // 2), 2).reshape(1, 2 * HEAD_DIM)
    (
        qkv_full,
        o_full,
        grads_chip,
        segment,
        down_full,
        mid,
        normed_two,
        activated,
        gate_grad,
        up_grad,
        back_term,
        normed,
        turned,
        context,
        cosines,
        sines,
        gain_rows,
    ) = call(
        functools.partial(forward, zn, early),
        "forward",
        0,
        (
            q_weight,
            kv_shard,
            o_weight.T,
            gain_shard,
            tokens,
            out_grad,
            seg_ids,
            gate_weight,
            up_weight,
            down_weight.T,
            inverse,
            sign,
        ),
        [VMEM] * 12,
        [
            ((width, qkv_half), BF16),
            ((width, q_half), BF16),
            ((units * 16, 128), F32),
            ((2, count, width), BF16),
            ((2, count, width), BF16),
            ((2,) + seg_ids.shape, jnp.int32),
        ]
        + [((width, ff_half), BF16)] * 3
        + [((count, width), F32), ((2, count, width), BF16)]
        + [((chip, ff_half), BF16)] * 3
        + [((2, count, width), BF16)] * 2
        + [((chip, width), BF16), ((chip, qkv_half), BF16), ((chip, q_half), BF16)]
        + [((chip, 2 * HEAD_DIM), F32)] * 2
        + [((8, width), F32)],
        [ANY] * 22,
        total_buffers(count, width)
        + [
            pltpu.VMEM((2, count, width), BF16),
            DMA((3,)),
            DMA((3,)),
            DMA((2,)),
            DMA((2,)),
            DMA((2, 3)),
            DMA((2,)),
            pltpu.VMEM((chip, 2 * HEAD_DIM), F32),
            pltpu.VMEM((chip, 2 * HEAD_DIM), F32),
            pltpu.VMEM((2,) + seg_ids.shape, jnp.int32),
            pltpu.VMEM((units * 16, 128), F32),
            pltpu.VMEM((8, width), F32),
            DMA((2, 3)),
            DMA((5,)),
        ]
        + gather_sems(6, 7, zn),
        order=(0, 1, 4, 5, 8, 9, 10, 11, 12, 13, 14, 16, 17, 18, 19, 20, 21),
    )
    gain_one, gain_two = gain_rows[0:1], gain_rows[1:2]
    grads_chip = grads_chip.reshape(chip, width)
    segment = segment.reshape(blocks, 1, block_rows)
    normed_two = normed_two.reshape(chip, width)

    gate_sum, down_sum, out, mid_grad, branch, gain_two_grad, qkv_back, in_term = call(
        functools.partial(scatter_feedforward, zn, early_sums),
        "scatter_feedforward",
        2,
        (
            normed_two,
            gate_grad,
            grads_chip,
            activated,
            back_term,
            down_full,
            mid,
            gain_two,
            turned,
            o_full,
            qkv_full,
            cosines,
            sines,
            segment,
        ),
        [ANY] * 7 + [VMEM] + [ANY] * 5 + [VMEM],
        [((rows, 2 * ff_half), F32)] * 2
        + [
            ((count, width), BF16),
            ((count, width), F32),
            ((2, count, width), BF16),
            ((1, width), F32),
            ((chip, qkv_half), BF16),
            ((2, count, width), BF16),
        ]
        + [((zn, 4 * rows, ff_half), BF16)] * 2
        + [((2, count, width), BF16)],
        [ANY] * 5 + [VMEM] + [ANY] * 5,
        scatter_buffers([(2 * rows, ff_half)] * 2, early_sums, zn)
        + total_buffers(count, width) * 2
        + [DMA((4,)), DMA((2,)), DMA((3,)), DMA((2,)), DMA((2, 2)), DMA((2, 4)), DMA((2, 2))]
        + scatter_sems(2, 2, zn),
        order=range(8),
    )
    branch = branch.reshape(chip, width)

    q_sum, kv_sum, o_sum, up_sum, in_grad, gain_sums = call(
        functools.partial(scatter_attention, zn, early_sums),
        "scatter_attention",
        3,
        (
            normed,
            qkv_back,
            branch,
            context,
            normed_two,
            up_grad,
            in_term,
            mid_grad,
            tokens,
            gain_one,
            gain_two_grad,
        ),
        [ANY] * 8 + [VMEM] * 3,
        [
            ((rows, 2 * q_half), F32),
            ((2, rows, 2 * kv_half), F32),
            ((rows, 2 * q_half), F32),
            ((rows, 2 * ff_half), F32),
            ((count, width), BF16),
            ((8, 4 * rows), F32),
            ((zn, 4 * rows, qkv_half), BF16),
            ((zn, 4 * rows, q_half), BF16),
            ((zn, 4 * rows, ff_half), BF16),
        ],
        [ANY] * 5 + [VMEM] + [ANY] * 3,
        scatter_buffers([(2 * rows, ff_half), (2 * rows, q_half), (2 * rows, qkv_half)], early_sums, zn)
        + total_buffers(count, width)
        + gain_buffers(zn, 4 * rows)
        + [DMA((6,)), DMA((1,)), pltpu.VMEM((1, width), F32)]
        + scatter_sems(3, 4, zn),
        order=range(6),
    )
    gain_grads = lax.dynamic_slice_in_dim(gain_sums, lax.rem(lax.axis_index("dp"), 4) * rows, rows, 1)
    return (
        out,
        in_grad,
        q_sum,
        joined(kv_sum[:, :, :kv_half]),
        joined(kv_sum[:, :, kv_half:]),
        o_sum.T,
        gain_grads[0],
        gate_sum,
        up_sum,
        down_sum.T,
        gain_grads[1],
    )


def solution(mesh):
    arguments = (
        P("dp", None),
        P("dp", None),
        P("dp", "tensor"),
        P("dp", "tensor"),
        P("dp", "tensor"),
        P("tensor", "dp"),
        P("dp"),
        P("dp", "tensor"),
        P("dp", "tensor"),
        P("tensor", "dp"),
        P("dp"),
        P("dp", None),
    )
    results = (
        P("dp", None),
        P("dp", None),
        P("dp", "tensor"),
        P("dp", "tensor"),
        P("dp", "tensor"),
        P("tensor", "dp"),
        P("dp"),
        P("dp", "tensor"),
        P("dp", "tensor"),
        P("tensor", "dp"),
        P("dp"),
    )
    return jax.shard_map(
        functools.partial(local, mesh.shape["dp"]),
        mesh=mesh,
        in_specs=arguments,
        out_specs=results,
        check_vma=False,
    )
```

```python
import functools

import jax
import jax.numpy as jnp
from jax import lax
from jax.experimental import pallas as pl
from jax.experimental.pallas import tpu as pltpu
from jax.sharding import PartitionSpec as P

HEAD_DIM = 64
norm_eps = 1e-05
MESH = pl.DeviceIdType.MESH
ANY = pl.BlockSpec(memory_space=pl.ANY)
VMEM = pl.BlockSpec(memory_space=pltpu.VMEM)
DMA = pltpu.SemaphoreType.DMA
F32 = jnp.float32
BF16 = jnp.bfloat16


def place():
    d = lax.axis_index("dp")
    t = lax.axis_index("tensor")
    return d, t, d // 4, lax.rem(d // 2, 2), lax.rem(d, 2)


def enter(zn, here):
    d, t, z, x, c = here
    bar = pltpu.get_barrier_semaphore()

    def hail(device):
        pl.semaphore_signal(bar, inc=1, device_id=device, device_id_type=MESH)

    hail((d + 1 - 2 * c, t))
    hail((d + 2 - 4 * x, t))
    hail((d, 1 - t))

    @pl.when(z > 0)
    def _():
        hail((d - 4, t))

    @pl.when(z < zn - 1)
    def _():
        hail((d + 4, t))

    pl.semaphore_wait(bar, 5 - (z == 0).astype(jnp.int32) - (z == zn - 1).astype(jnp.int32))


def farthest_first(zn, z, i):
    up = 1 - (2 * z) // zn
    longer = up * (zn - 1 - z) + (1 - up) * z
    shorter = zn - 1 - longer
    rest = i - (longer - shorter)
    return jnp.where(
        rest < 0,
        z + (2 * up - 1) * (longer - i),
        z + (1 - 2 * lax.rem(jnp.maximum(rest, 0), 2)) * (shorter - jnp.maximum(rest, 0) // 2),
    )


def loop(count, body):
    def step(i, carry):
        body(i)
        return carry

    lax.fori_loop(0, count, step, 0)


def remote(src, dst, send, recv, device):
    return pltpu.make_async_remote_copy(
        src_ref=src, dst_ref=dst, send_sem=send, recv_sem=recv, device_id=device, device_id_type=MESH
    )


def by_rows(count, body, block=16):
    def step(i, carry):
        body(pl.ds(pl.multiple_of(i * block, block), block))
        return carry

    lax.fori_loop(0, count // block, step, 0)


def gather_sems(n, sources, zn):
    return [
        DMA((sources,)),
        DMA((sources,)),
        DMA((sources,)),
        DMA((n, zn)),
        DMA((n, zn)),
        DMA((n,)),
        DMA((n,)),
        DMA((n, 2, zn)),
        DMA((n, zn)),
        DMA((n, 2, zn)),
        DMA((n, zn)),
    ]


def part(ref, core, paired):
    if paired:
        return ref.at[core]
    columns = ref.shape[1] // 2
    return ref.at[:, pl.ds(pl.multiple_of(core * columns, columns), columns)]


class Gather:
    def __init__(self, zn, here, arrays, sems):
        self.zn, self.here = zn, here
        self.full = [full for _, full, _ in arrays]
        self.early = [early for _, _, early in arrays]
        self.sources = [
            (j, i) + source for j, (sources, _, _) in enumerate(arrays) for i, source in enumerate(sources)
        ]
        (
            self.loc,
            self.cs,
            self.cr,
            self.xs,
            self.xr,
            self.es,
            self.er,
            self.zs,
            self.zr,
            self.bs,
            self.br,
        ) = sems

    def unit(self, j, unit, first, count):
        rows = self.full[j].shape[0] // (2 * self.zn)
        return pl.ds(pl.multiple_of(unit * rows + first, 8), count)

    def rows(self, j, unit, early):
        rows = self.full[j].shape[0] // (2 * self.zn)
        late = rows - self.early[j]
        first, count = {None: (0, rows), True: (late, rows - late), False: (0, late)}[early]
        return self.full[j].at[self.unit(j, unit, first, count)]

    def mine(self, s):
        d, t, z, x, c = self.here
        j, _, shard, paired, first, columns = self.sources[s]
        rows = self.full[j].shape[0] // (4 * self.zn)
        return self.full[j].at[self.unit(j, z * 2 + x, c * rows, rows), pl.ds(first, columns)]

    def keep(self, s):
        _, _, shard, paired, _, _ = self.sources[s]
        return pltpu.make_async_copy(part(shard, self.here[4], paired), self.mine(s), self.loc.at[s])

    def give(self, s):
        d, t, z, x, c = self.here
        _, _, shard, paired, _, _ = self.sources[s]
        return remote(
            part(shard, 1 - c, paired), self.mine(s), self.cs.at[s], self.cr.at[s], (d + 1 - 2 * c, t)
        )

    def x_late(self, j, o):
        d, t, z, x, c = self.here
        ref = self.rows(j, o * 2 + x, False)
        return remote(ref, ref, self.xs.at[j, o], self.xr.at[j, o], (d + 2 - 4 * x, t))

    def x_early(self, j):
        d, t, z, x, c = self.here
        ref = self.rows(j, z * 2 + x, True)
        return remote(ref, ref, self.es.at[j], self.er.at[j], (d + 2 - 4 * x, t))

    def along(self, j, o, down):
        d, t, z, x, c = self.here
        ref = self.rows(j, o * 2 + x, None)
        return remote(ref, ref, self.zs.at[j, down, o], self.zr.at[j, o], (d + 4 - 8 * down, t))

    def along_early(self, j, o, down):
        d, t, z, x, c = self.here
        ref = self.rows(j, o * 2 + 1 - x, True)
        return remote(ref, ref, self.bs.at[j, down, o], self.br.at[j, o], (d + 4 - 8 * down, t))

    def start(self):
        for s in range(len(self.sources)):
            self.give(s).start()
            self.keep(s).start()

    def ready(self, arrays):
        for j in arrays:
            for s, source in enumerate(self.sources):
                if source[0] == j:
                    self.keep(s).wait()
                    self.give(s).wait_recv()
            if self.early[j]:
                self.x_early(j).start()

    def start_own(self, arrays):
        z, zn = self.here[2], self.zn
        for j in arrays:
            self.x_late(j, z).start()

            @pl.when(z < zn - 1)
            def _():
                self.along(j, z, 0).start()

            @pl.when(z > 0)
            def _():
                self.along(j, z, 1).start()

    def start_early(self, arrays):
        z, zn = self.here[2], self.zn
        for j in arrays:
            if self.early[j]:
                self.x_early(j).wait_recv()

                @pl.when(z < zn - 1)
                def _():
                    self.along_early(j, z, 0).start()

                @pl.when(z > 0)
                def _():
                    self.along_early(j, z, 1).start()

    def relay(self, k, arrays):
        z, zn = self.here[2], self.zn
        o = farthest_first(zn, z, zn - 1 - k)
        down = (o > z).astype(jnp.int32)
        more = ((o < z) & (z < zn - 1)) | ((o > z) & (z > 0))
        for j in arrays:
            self.along(j, o, down).wait_recv()

            @pl.when(more)
            def _():
                self.along(j, o, down).start()

            self.x_late(j, o).start()
            if self.early[j]:
                self.along_early(j, o, down).wait_recv()

                @pl.when(more)
                def _():
                    self.along_early(j, o, down).start()

    def relays(self, first, arrays):
        loop(max(self.zn - first, 0), lambda i: self.relay(first + i, arrays))

    def arrived(self, j):
        loop(self.zn, lambda o: self.x_late(j, o).wait_recv())

    def finish(self):
        z, zn = self.here[2], self.zn
        for s in range(len(self.sources)):
            self.give(s).wait_send()
        for j in range(len(self.full)):
            if self.early[j]:
                self.x_early(j).wait_send()

            def step(o, j=j):
                self.x_late(j, o).wait_send()

                def sent(down):
                    self.along(j, o, down).wait_send()
                    if self.early[j]:
                        self.along_early(j, o, down).wait_send()

                @pl.when((o <= z) & (z < zn - 1))
                def _():
                    sent(0)

                @pl.when((o >= z) & (z > 0))
                def _():
                    sent(1)

            loop(zn, step)


def scatter_sems(n, outs, zn):
    return [
        DMA((n, zn)),
        DMA((n, zn)),
        DMA((n, zn)),
        DMA((n, zn)),
        DMA((n, zn)),
        DMA((n, zn + 1)),
        DMA((n, 2, zn)),
        DMA((n, zn)),
        DMA((n, zn + 1)),
        DMA((n,)),
        DMA((n,)),
        DMA((outs,)),
        DMA((outs,)),
        DMA((outs,)),
    ]


def scatter_buffers(shapes, early, zn):
    out = []
    for rows, columns in shapes:
        late = rows - early
        out += [
            pltpu.VMEM((zn, late, columns), BF16),
            pltpu.VMEM((zn, late, columns), BF16),
            pltpu.VMEM((zn + 1, late, columns), BF16),
            pltpu.VMEM((zn, 2, early, columns), BF16),
            pltpu.VMEM((zn + 1, 2, early, columns), BF16),
            pltpu.VMEM((early, columns), BF16),
            pltpu.VMEM((rows, columns), F32),
        ]
    return out


SCATTER_BUFFERS = 7


class Scatter:
    def __init__(self, zn, here, early, arrays, sems):
        self.zn, self.here, self.early = zn, here, early
        self.term = [term for term, _, _ in arrays]
        self.buffers = [buffers for _, buffers, _ in arrays]
        self.results = [(j,) + result for j, (_, _, results) in enumerate(arrays) for result in results]
        (
            self.st,
            self.ls,
            self.xs,
            self.xr,
            self.zs,
            self.zr,
            self.bls,
            self.bs,
            self.br,
            self.es,
            self.er,
            self.cs,
            self.cr,
            self.loc,
        ) = sems

    def unit(self, j, o, x, first, count):
        rows = self.term[j].shape[1] // 2
        return self.term[j].at[o, pl.ds(pl.multiple_of(x * rows + first, 16), count)]

    def late(self, j):
        return self.buffers[j][0].shape[1]

    def load(self, j, o):
        return pltpu.make_async_copy(
            self.unit(j, o, self.here[3], 0, self.late(j)), self.buffers[j][0].at[o], self.ls.at[j, o]
        )

    def load_early(self, j, o, other):
        x = self.here[3]
        return pltpu.make_async_copy(
            self.unit(j, o, 1 - x if other else x, self.late(j), self.early),
            self.buffers[j][3].at[o, other],
            self.bls.at[j, other, o],
        )

    def across(self, j, o):
        d, t, z, x, c = self.here
        return remote(
            self.unit(j, o, 1 - x, 0, self.late(j)),
            self.buffers[j][1].at[o],
            self.xs.at[j, o],
            self.xr.at[j, o],
            (d + 2 - 4 * x, t),
        )

    def across_early(self, j):
        d, t, z, x, c = self.here
        return remote(
            self.buffers[j][3].at[z, 1], self.buffers[j][5], self.es.at[j], self.er.at[j], (d + 2 - 4 * x, t)
        )

    def along(self, j, o, slot, down):
        d, t, z, x, c = self.here
        own, line = self.buffers[j][0], self.buffers[j][2]
        return remote(own.at[o], line.at[slot], self.zs.at[j, o], self.zr.at[j, slot], (d + 4 - 8 * down, t))

    def along_early(self, j, o, slot, down):
        d, t, z, x, c = self.here
        own, line = self.buffers[j][3], self.buffers[j][4]
        return remote(own.at[o], line.at[slot], self.bs.at[j, o], self.br.at[j, slot], (d + 4 - 8 * down, t))

    def give(self, r):
        d, t, z, x, c = self.here
        j, out, paired, first, columns = self.results[r]
        rows = out.shape[-2]
        ref = self.buffers[j][6].at[
            pl.ds(pl.multiple_of((1 - c) * rows, rows), rows), pl.ds(first, columns)
        ]
        return remote(ref, part(out, c, paired), self.cs.at[r], self.cr.at[r], (d + 1 - 2 * c, t))

    def keep(self, r):
        c = self.here[4]
        j, out, paired, first, columns = self.results[r]
        rows = out.shape[-2]
        ref = self.buffers[j][6].at[pl.ds(pl.multiple_of(c * rows, rows), rows), pl.ds(first, columns)]
        return pltpu.make_async_copy(ref, part(out, c, paired), self.loc.at[r])

    def store(self, j, o, stage, slot):
        columns = self.term[j].shape[2]
        return pltpu.make_async_copy(
            stage.at[slot, :, pl.ds(0, columns)], self.term[j].at[o], self.st.at[j, o]
        )

    def make(self, j, left, right, stage, between=None):
        z, zn = self.here[2], self.zn
        wide, columns = self.term[j].shape[1:]
        block = min(256, wide)

        def send(i):
            o = farthest_first(zn, z, i)
            self.store(j, o, stage, lax.rem(i, 2)).wait()
            self.across(j, o).start()
            for other in range(2):
                self.load_early(j, o, other).start()
            self.load(j, o).start()

        def compute(i):
            o = farthest_first(zn, z, i)
            slot = lax.rem(i, 2)

            def body(m):
                at = pl.multiple_of(o * wide + m * block, block)
                value = inner_rows(left[:, pl.ds(at, block)], right[...])
                stage[slot, pl.ds(pl.multiple_of(m * block, block), block), pl.ds(0, columns)] = value.astype(
                    BF16
                )

            loop(wide // block, body)
            self.store(j, o, stage, slot).start()

        def both(i):
            compute(i)
            send(i - 1)

        compute(0)
        if between is not None:
            between()
        loop(zn - 1, lambda i: both(i + 1))
        send(zn - 1)

    def add(self, j, o, slots):
        own, got, line = self.buffers[j][:3]

        def body(at):
            value = own[o, at].astype(F32) + got[o, at].astype(F32)
            for slot in slots:
                value = value + line[slot, at].astype(F32)
            own[o, at] = value.astype(BF16)

        by_rows(own.shape[1], body)

    def add_early(self, j, o, slots):
        own, line = self.buffers[j][3:5]
        for other in range(2):

            def body(at):
                value = own[o, other, at].astype(F32)
                for slot in slots:
                    value = value + line[slot, other, at].astype(F32)
                own[o, other, at] = value.astype(BF16)

            by_rows(own.shape[2], body)

    def route(self, i):
        z, zn = self.here[2], self.zn
        o = farthest_first(zn, z, i)
        down = (o < z).astype(jnp.int32)
        distance = jnp.maximum((o - z) * (1 - 2 * down), 1)
        slot = o + (zn - o) * down * (1 // distance)
        inner = ((o > z) & (z > 0)) | ((o < z) & (z < zn - 1))
        return o, slot, down, inner

    def hop_early(self, j, i):
        o, slot, down, inner = self.route(i)
        for other in range(2):
            self.load_early(j, o, other).wait()

        @pl.when(inner)
        def _():
            self.along_early(j, o, o, down).wait_recv()
            self.add_early(j, o, [o])

        self.along_early(j, o, slot, down).start()

    def hop(self, j, i):
        o, slot, down, inner = self.route(i)
        self.load(j, o).wait()
        self.across(j, o).wait_recv()

        @pl.when(inner)
        def _():
            self.along(j, o, o, down).wait_recv()
            self.add(j, o, [o])

        @pl.when(jnp.logical_not(inner))
        def _():
            self.add(j, o, [])

        self.along(j, o, slot, down).start()

    def third(self, hop, j, g):
        hops = self.zn - 1
        first = g * hops // 3
        loop((g + 1) * hops // 3 - first, lambda i: hop(j, first + i))

    def early_third(self, j, g):
        self.third(self.hop_early, j, g)

    def late_third(self, j, g):
        self.third(self.hop, j, g)

    def at_home(self, action):
        z, zn = self.here[2], self.zn

        @pl.when((z > 0) & (z < zn - 1))
        def _():
            action([z, zn])

        @pl.when(z == 0)
        def _():
            action([zn])

        @pl.when(z == zn - 1)
        def _():
            action([z])

    def early_home(self, j):
        z = self.here[2]
        for other in range(2):
            self.load_early(j, z, other).wait()

        def home(slots):
            for slot in slots:
                self.along_early(j, z, slot, 0).wait_recv()
            self.add_early(j, z, slots)

        self.at_home(home)
        self.across_early(j).start()

    def home(self, j):
        z = self.here[2]
        own, got, line, early, _, other_early, total = self.buffers[j]
        late = self.late(j)
        self.load(j, z).wait()
        self.across(j, z).wait_recv()

        def last(slots):
            for slot in slots:
                self.along(j, z, slot, 0).wait_recv()

            def body(at):
                value = own[z, at].astype(F32) + got[z, at].astype(F32)
                for slot in slots:
                    value = value + line[slot, at].astype(F32)
                total[at] = value

            by_rows(late, body)

        self.at_home(last)
        self.across_early(j).wait_recv()
        for i in range(self.early // 16):
            at = pl.ds(16 * i, 16)
            total[pl.ds(late + 16 * i, 16)] = early[z, 0, at].astype(F32) + other_early[at].astype(F32)
        for r, result in enumerate(self.results):
            if result[0] == j:
                self.give(r).start()
                self.keep(r).start()

    def done(self, j):
        z = self.here[2]
        for r, result in enumerate(self.results):
            if result[0] == j:
                self.give(r).wait()
                self.keep(r).wait()
        self.across_early(j).wait_send()

        def sent(o):
            self.across(j, o).wait_send()

            @pl.when(o != z)
            def _():
                self.along(j, o, 0, 0).wait_send()
                self.along_early(j, o, 0, 0).wait_send()

        loop(self.zn, sent)

    def lend(self, credit):
        d, t, z, x, c = self.here

        def tell(device):
            pl.semaphore_signal(credit, inc=1, device_id=device, device_id_type=MESH)

        tell((d + 2 - 4 * x, t))

        @pl.when(z > 0)
        def _():
            tell((d - 4, t))

        @pl.when(z < self.zn - 1)
        def _():
            tell((d + 4, t))

    def borrow(self, credit):
        z = self.here[2]
        pl.semaphore_wait(credit, 3 - (z == 0).astype(jnp.int32) - (z == self.zn - 1).astype(jnp.int32))


class Gains:
    def __init__(self, zn, here, own, got, line, sems):
        self.zn, self.here, self.own, self.got, self.line, self.sems = zn, here, own, got, line, sems

    def swap(self, i):
        d, t, z, x, c = self.here
        device = ((d + 1 - 2 * c, t), (d, 1 - t), (d + 2 - 4 * x, t))[i]
        return remote(self.own, self.got.at[i], self.sems.at[0, i], self.sems.at[1, i], device)

    def along(self, o, slot, down):
        d, t, z, x, c = self.here
        return remote(
            self.own.at[o], self.line.at[slot], self.sems.at[2, o], self.sems.at[3, slot], (d + 4 - 8 * down, t)
        )

    def start(self, rows):
        wide = self.own.shape[2]
        for o in range(self.zn):
            for i, row in enumerate(rows):
                self.own[o, pl.ds(i, 1)] = row[:, pl.ds(o * wide, wide)]
        self.swap(0).start()

    def swapped(self, i):
        self.swap(i).wait()
        self.own[...] += self.got[i]
        if i < 2:
            self.swap(i + 1).start()

    def hop(self, o, slot, down, inner):
        @pl.when(inner)
        def _():
            self.along(o, o, down).wait_recv()
            self.own[o] += self.line[o]

        self.along(o, slot, down).start()

    def steps(self, k, nearest):
        z, zn = self.here[2], self.zn

        @pl.when(z + k < zn)
        def _():
            self.hop(z + k, z + k, 0, z > 0)

        @pl.when(z - k >= 0)
        def _():
            self.hop(z - k, zn if nearest else z - k, 1, z < zn - 1)

    def run(self):
        zn = self.zn

        def step(i, carry):
            self.steps(zn - 1 - i, False)
            return carry

        lax.fori_loop(0, zn - 2, step, 0)
        self.steps(1, True)

    def finish(self, out):
        z, zn = self.here[2], self.zn
        value = self.own[z]

        @pl.when(z > 0)
        def _():
            self.along(z, z, 0).wait_recv()
            self.own[z] += self.line[z]

        @pl.when(z < zn - 1)
        def _():
            self.along(z, zn, 1).wait_recv()
            self.own[z] += self.line[zn]

        out[...] = self.own[z]

        def step(o, carry):
            @pl.when(o != z)
            def _():
                self.along(o, 0, 0).wait_send()

            return carry

        lax.fori_loop(0, zn, step, 0)


def gain_buffers(zn, wide):
    return [
        pltpu.VMEM((zn, 8, wide), F32),
        pltpu.VMEM((3, zn, 8, wide), F32),
        pltpu.VMEM((zn + 1, 8, wide), F32),
        DMA((4, zn + 1)),
    ]


class Total:
    def __init__(self, here, term, from_core, half, from_pair, sems):
        self.here, self.term, self.from_core, self.half, self.from_pair = here, term, from_core, half, from_pair
        self.sems = sems

    def core(self):
        d, t, z, x, c = self.here
        return remote(self.term.at[1 - c], self.from_core, self.sems.at[0], self.sems.at[1], (d + 1 - 2 * c, t))

    def load(self):
        return pltpu.make_async_copy(self.term.at[self.here[4]], self.half, self.sems.at[4])

    def start(self):
        self.core().start()
        self.load().start()

    def pair(self):
        d, t, z, x, c = self.here
        return remote(self.half, self.from_pair, self.sems.at[2], self.sems.at[3], (d, 1 - t))

    def meet(self, loaded=True, send=True):
        if loaded:
            self.load().wait()
        self.core().wait_recv()

        def body(at):
            self.half[at] = (self.half[at].astype(F32) + self.from_core[at].astype(F32)).astype(BF16)

        by_rows(self.half.shape[0], body)
        if send:
            self.pair().start()

    def rows(self, at):
        return self.half[at].astype(F32) + self.from_pair[at].astype(F32)

    def finish(self):
        self.core().wait_send()
        self.pair().wait_send()


def total_buffers(tokens, width):
    return [pltpu.VMEM((tokens, width), BF16)] * 3 + [DMA((5,))]


def share(here, src, dst, sems):
    d, t, z, x, c = here
    return (
        pltpu.make_async_copy(src, dst.at[c], sems.at[0]),
        remote(src, dst.at[c], sems.at[1], sems.at[2], (d + 1 - 2 * c, t)),
    )


def lanes(shape):
    return lax.broadcasted_iota(jnp.int32, shape, 1)


def partner(value):
    half = HEAD_DIM // 2
    wide = 2 * HEAD_DIM
    lower = lax.rem(lanes(value.shape), HEAD_DIM) < half
    return jnp.where(lower, pltpu.roll(value, wide - half, 1), pltpu.roll(value, half, 1))


def same_segment(row):
    count = row.shape[1]
    wide = jnp.broadcast_to(row, (count, count))
    before = lax.broadcasted_iota(jnp.int32, wide.shape, 1) < lax.broadcasted_iota(jnp.int32, wide.shape, 0)
    return wide == wide.T, before


def allowed_in(row):
    same, before = same_segment(row)
    here = lax.broadcasted_iota(jnp.int32, same.shape, 1) == lax.broadcasted_iota(jnp.int32, same.shape, 0)
    return same & (before | here)


def softmax_of(queries, keys, allowed):
    scores = jnp.where(allowed, times_transposed(queries, keys) * HEAD_DIM ** (-0.5), -1e30)
    shifted = jnp.exp(scores - jnp.max(scores, axis=-1, keepdims=True))
    return shifted / jnp.sum(shifted, axis=-1, keepdims=True)


def key_value_pairs(pair):
    pair = pair.astype(F32)
    first = lanes(pair.shape) < HEAD_DIM
    key, value = jnp.where(first, pair, 0.0), jnp.where(first, 0.0, pair)
    return [
        part.astype(BF16)
        for part in (key, pltpu.roll(key, HEAD_DIM, 1), pltpu.roll(value, HEAD_DIM, 1), value)
    ]


def attention_block(turned, context, queries_wide, row):
    wide = 2 * HEAD_DIM
    allowed = allowed_in(row)
    key_one, key_two, value_one, value_two = key_value_pairs(turned[:, queries_wide:])

    def heads(p):
        at = pl.ds(pl.multiple_of(p * wide, wide), wide)
        queries = turned[:, at]
        one = softmax_of(queries, key_one, allowed).astype(BF16)
        two = softmax_of(queries, key_two, allowed).astype(BF16)
        context[:, at] = (product(one, value_one) + product(two, value_two)).astype(BF16)

    loop(queries_wide // wide, heads)


def attention_block_back(turned, grads, back, sums, queries_wide, row, cosine, sine):
    wide = 2 * HEAD_DIM
    scale = HEAD_DIM ** (-0.5)
    allowed = allowed_in(row)
    key_one, key_two, value_one, value_two = key_value_pairs(turned[:, queries_wide:])
    sums[...] = jnp.zeros_like(sums)

    def heads(p):
        at = pl.ds(pl.multiple_of(p * wide, wide), wide)
        queries, grad = turned[:, at], grads[:, at]
        total = None
        for i, (key, value) in enumerate(((key_one, value_one), (key_two, value_two))):
            probs = softmax_of(queries, key, allowed)
            sums[i] += inner_rows(probs.astype(BF16), grad)
            prob_grad = times_transposed(grad, value)
            delta = jnp.sum(probs * prob_grad, axis=-1, keepdims=True)
            score_grad = (probs * (prob_grad - delta)).astype(BF16)
            term = product(score_grad, key)
            total = term if total is None else total + term
            sums[2 + i] += inner_rows(score_grad, queries)
        total = total * scale
        back[:, at] = (total * cosine - partner(total) * sine).astype(BF16)

    loop(queries_wide // wide, heads)
    value_grad = pltpu.roll(sums[0], HEAD_DIM, 1) + sums[1]
    key_grad = (sums[2] + pltpu.roll(sums[3], HEAD_DIM, 1)) * scale
    turned_back = key_grad * cosine - partner(key_grad) * sine
    back[:, pl.ds(queries_wide, wide)] = jnp.where(
        lanes(value_grad.shape) < HEAD_DIM, turned_back, value_grad
    ).astype(BF16)


def forward(zn, early, *refs):
    q, kv, o_shard, gains, tokens, grads, seg, gate, up, down, inverse, sign = refs[:12]
    qkv_all, o_all, gains_all, chip_tokens, chip_grads, seg_all = refs[12:18]
    gate_all, up_all, down_all, mid_out, normed_out, act_out, gate_grad_out, up_grad_out, back_out = refs[18:27]
    term, normed_one_out, turned_out, context_out, cosines_out, sines_out, gain_out = refs[27:34]
    total_refs = refs[34:38]
    normed, out_sems, pair_sems, load_sems, grad_sems, stage_sems, block_sems = refs[38:45]
    cosines, sines, seg_pair, gain_tiles, gain_rows, swap_sems, seg_sems = refs[45:52]
    here = place()
    c = here[4]
    enter(zn, here)
    total = Total(here, term, *total_refs)
    q_half = q.shape[1] // 2
    work = Gather(
        zn,
        here,
        [
            ([(gains, True, 0, gains.shape[2])], gains_all, 0),
            ([(q, False, 0, q_half), (kv, True, q_half, kv.shape[2])], qkv_all, early),
            ([(o_shard, False, 0, o_shard.shape[1] // 2)], o_all, early),
        ]
        + [
            ([(shard, False, 0, shard.shape[1] // 2)], full, early)
            for shard, full in ((down, down_all), (gate, gate_all), (up, up_all))
        ],
        refs[52:],
    )
    count, width = tokens.shape
    columns = gate_all.shape[1]
    block = seg.shape[1]
    blocks = 2 * count // block
    per = count // block
    attention_set = [0, 1, 2]
    swap = remote(seg, seg_pair.at[c], seg_sems.at[0], seg_sems.at[1], (here[0] + 1 - 2 * c, here[1]))
    swap.start()
    seg_pair[c] = seg[...]
    work.start()
    work.ready(attention_set)
    work.start_own(attention_set)
    shared = [
        share(here, src, dst, swap_sems.at[n])
        for n, (src, dst) in enumerate(((tokens, chip_tokens), (grads, chip_grads)))
    ]
    for copies in shared:
        for copy in copies:
            copy.start()
    work.ready([5])
    work.start_own([5])
    swap.wait()
    for i in range(blocks):
        row = seg_pair[i // per, pl.ds(i % per, 1)]
        same, before = same_segment(row)
        position = jnp.sum(jnp.where(same & before, 1.0, 0.0), axis=-1, keepdims=True)
        angles = position * inverse[...]
        cosines[pl.ds(i * block, block)] = jnp.cos(angles)
        sines[pl.ds(i * block, block)] = jnp.sin(angles) * sign[...]
    saves = [
        pltpu.make_async_copy(src, dst, seg_sems.at[2 + n])
        for n, (src, dst) in enumerate(((cosines, cosines_out), (sines, sines_out), (seg_pair, seg_all)))
    ]
    for copy in saves:
        copy.start()
    work.start_early([1, 2])
    work.relay(1, attention_set)
    work.start_early([5])
    work.ready([3])
    work.start_own([3])
    work.relay(2, attention_set)
    work.relays(3, attention_set)
    work.start_early([3])
    work.ready([4])
    work.start_own([4])
    work.arrived(0)
    load = pltpu.make_async_copy(gains_all, gain_tiles, load_sems.at[0])
    load.start()
    load.wait()
    features = width // (4 * zn)
    for owner in range(4 * zn):
        for i in range(2):
            gain_rows[pl.ds(i, 1), pl.ds(owner * features, features)] = gain_tiles[
                pl.ds(owner * 8 + i, 1), :features
            ]
    save_gains = pltpu.make_async_copy(gain_rows, gain_out, load_sems.at[1])
    save_gains.start()
    gain_one, gain = gain_rows[pl.ds(0, 1)], gain_rows[pl.ds(1, 1)]
    for copies in shared:
        for copy in copies:
            copy.wait()
    work.arrived(1)
    work.arrived(2)
    save_gains.wait()
    half = total_refs[1]

    def attention(qkv, o, inputs, normed_one, turned, context, attended):
        queries_wide = context.shape[2]
        wide = 2 * HEAD_DIM

        def place_of(i):
            return lax.rem((1 - c) * per + i, blocks)

        def rows_at(i):
            return pl.ds(pl.multiple_of(place_of(i) * block, block), block)

        def fetch_inputs(i, slot):
            which = place_of(i)
            return pltpu.make_async_copy(
                chip_tokens.at[which // per, pl.ds(pl.multiple_of(lax.rem(which, per) * block, block), block)],
                inputs.at[slot],
                grad_sems.at[slot],
            )

        def stores(i, slot):
            return [
                pltpu.make_async_copy(buffer.at[slot], out.at[rows_at(i)], stage_sems.at[slot, n])
                for n, (buffer, out) in enumerate(
                    ((normed_one, normed_one_out), (turned, turned_out), (context, context_out))
                )
            ]

        def store_term(i, slot):
            return pltpu.make_async_copy(
                attended.at[slot],
                term.at[1 - c, pl.ds(pl.multiple_of(i * block, block), block)],
                block_sems.at[slot],
            )

        fetch_inputs(0, 0).start()
        loads = [
            pltpu.make_async_copy(qkv_all, qkv, load_sems.at[0]),
            pltpu.make_async_copy(o_all, o, load_sems.at[1]),
        ]
        for load in loads:
            load.start()
        for load in loads:
            load.wait()

        def one_block(i):
            slot = lax.rem(i, 2)
            to = rows_at(i)
            fetch_inputs(i, slot).wait()

            @pl.when(i + 1 < blocks)
            def _():
                fetch_inputs(i + 1, 1 - slot).start()

            @pl.when(i > 1)
            def _():
                for copy in stores(i - 2, slot):
                    copy.wait()

            def norm(at):
                value = inputs[slot, at].astype(F32)
                factor = lax.rsqrt(jnp.mean(value * value, axis=-1, keepdims=True) + norm_eps)
                normed_one[slot, at] = (value * factor * gain_one).astype(BF16)

            by_rows(block, norm)
            cosine, sine = cosines[to], sines[to]
            raw = product(normed_one[slot], qkv[...])
            for first in range(0, queries_wide, wide):
                value = raw[:, first : first + wide]
                turned[slot, :, pl.ds(first, wide)] = (value * cosine + partner(value) * sine).astype(BF16)
            value = raw[:, queries_wide:]
            is_key = lanes(value.shape) < HEAD_DIM
            turned[slot, :, pl.ds(queries_wide, wide)] = jnp.where(
                is_key, value * cosine + partner(value) * sine, value
            ).astype(BF16)
            which = place_of(i)
            row = seg_pair[which // per, pl.ds(lax.rem(which, per), 1)]
            attention_block(turned.at[slot], context.at[slot], queries_wide, row)
            for copy in stores(i, slot):
                copy.start()
            return slot

        def other(i):
            slot = one_block(i)
            attended[slot] = times_transposed(context[slot], o[...]).astype(BF16)
            store_term(i, slot).start()

        def own(i):
            slot = one_block(per + i)
            half[pl.ds(pl.multiple_of(i * block, block), block)] = times_transposed(
                context[slot], o[...]
            ).astype(BF16)

        loop(per, other)
        for i in range(per):
            store_term(i, i % 2).wait()
        total.core().start()
        work.relay(1, [3])
        work.relay(2, [3])
        work.relay(1, [5])
        work.relay(2, [5])
        loop(per, own)
        for i in range(blocks - 2, blocks):
            for copy in stores(i, i % 2):
                copy.wait()

    pl.run_scoped(
        attention,
        pltpu.VMEM(qkv_all.shape, BF16),
        pltpu.VMEM(o_all.shape, BF16),
        pltpu.VMEM((2, block, width), BF16),
        pltpu.VMEM((2, block, width), BF16),
        pltpu.VMEM((2, block, qkv_all.shape[1]), BF16),
        pltpu.VMEM((2, block, o_all.shape[1]), BF16),
        pltpu.VMEM((2, block, width), BF16),
    )
    total.meet(False)
    work.start_early([4])
    work.relays(3, [3])
    work.relay(1, [4])
    work.relay(2, [4])

    def sums(mid):
        total.pair().wait_recv()

        def body(at):
            value = tokens[at].astype(F32) + total.rows(at)
            mid[at] = value
            factor = lax.rsqrt(jnp.mean(value * value, axis=-1, keepdims=True) + norm_eps)
            normed[c, at] = (value * factor * gain).astype(BF16)

        by_rows(count, body)
        save = pltpu.make_async_copy(mid, mid_out, out_sems.at[0])
        save.start()
        for copy in share(here, normed.at[c], normed, pair_sems)[1:]:
            copy.start()
        save.wait()

    def hidden(first, second, silu, slope, up_grad, inputs, result, stages, back_stage):
        def fetch_grads(i, slot):
            return pltpu.make_async_copy(
                chip_grads.at[i // per, pl.ds(pl.multiple_of(lax.rem(i, per) * block, block), block)],
                inputs.at[slot],
                grad_sems.at[slot],
            )

        def at_block(i):
            return pl.ds(pl.multiple_of(i * block, block), block)

        fetch_grads(0, 0).start()
        work.arrived(3)
        load = pltpu.make_async_copy(down_all, first, load_sems.at[0])
        load.start()
        load.wait()

        def hidden_block(i):
            slot = lax.rem(i, 2)
            fetch_grads(i, slot).wait()

            @pl.when(i + 1 < blocks)
            def _():
                fetch_grads(i + 1, 1 - slot).start()

            slope[at_block(i)] = product(inputs[slot], first[...])

        loop(blocks, hidden_block)
        work.relays(3, [4])
        pl.run_scoped(sums, pltpu.VMEM((count, width), F32))
        work.relays(3, [5])
        work.arrived(4)
        load = pltpu.make_async_copy(gate_all, second, load_sems.at[1])
        load.start()
        share(here, normed.at[c], normed, pair_sems)[1].wait()
        save = pltpu.make_async_copy(normed, normed_out, out_sems.at[1])
        save.start()
        load.wait()

        def gate_block(i):
            result[...] = product(normed[i // per, at_block(lax.rem(i, per))], second[...])

            def body(at):
                to = pl.ds(pl.multiple_of(i * block + at.start, 16), at.size)
                gated = result[at]
                grad = slope[to]
                sigmoid = 1.0 / (1.0 + jnp.exp(-gated))
                silu[to] = gated * sigmoid
                up_grad[to] = (grad * gated * sigmoid).astype(BF16)
                slope[to] = grad * (sigmoid * (1.0 + gated * (1.0 - sigmoid)))

            by_rows(block, body)

        loop(blocks, gate_block)
        save_up = pltpu.make_async_copy(up_grad, up_grad_out, out_sems.at[2])
        save_up.start()
        work.arrived(5)
        load = pltpu.make_async_copy(up_all, first, load_sems.at[0])
        load.start()
        load.wait()

        def stores(i, slot):
            to = at_block(i)
            return (
                pltpu.make_async_copy(stages.at[slot, 0], act_out.at[to], stage_sems.at[slot, 0]),
                pltpu.make_async_copy(stages.at[slot, 1], gate_grad_out.at[to], stage_sems.at[slot, 1]),
                pltpu.make_async_copy(
                    back_stage.at[slot], back_out.at[i // per, at_block(lax.rem(i, per))], stage_sems.at[slot, 2]
                ),
            )

        def up_block(i):
            slot = lax.rem(i, 2)

            @pl.when(i > 1)
            def _():
                for copy in stores(i - 2, slot):
                    copy.wait()

            result[...] = product(normed[i // per, at_block(lax.rem(i, per))], first[...])

            def body(at):
                to = pl.ds(pl.multiple_of(i * block + at.start, 16), at.size)
                upward = result[at]
                stages[slot, 0, at] = (silu[to] * upward).astype(BF16)
                stages[slot, 1, at] = (slope[to] * upward).astype(BF16)

            by_rows(block, body)
            value = times_transposed(stages[slot, 1], second[...]) + times_transposed(
                up_grad[at_block(i)], first[...]
            )
            back_stage[slot] = value.astype(BF16)
            for copy in stores(i, slot):
                copy.start()

        loop(blocks, up_block)
        for i in range(max(blocks - 2, 0), blocks):
            for copy in stores(i, i % 2):
                copy.wait()
        save.wait()
        save_up.wait()

    pl.run_scoped(
        hidden,
        pltpu.VMEM((width, columns), BF16),
        pltpu.VMEM((width, columns), BF16),
        pltpu.VMEM((2 * count, columns), F32),
        pltpu.VMEM((2 * count, columns), F32),
        pltpu.VMEM((2 * count, columns), BF16),
        pltpu.VMEM((2, block, width), BF16),
        pltpu.VMEM((block, columns), F32),
        pltpu.VMEM((2, 2, block, columns), BF16),
        pltpu.VMEM((2, block, width), BF16),
    )
    work.finish()
    total.finish()
    for copy in saves:
        copy.wait()


def fetch(pairs, sems):
    copies = [pltpu.make_async_copy(src, dst, sems.at[i]) for i, (src, dst) in enumerate(pairs)]
    for copy in copies:
        copy.start()
    return copies


def backward(zn, early, *refs):
    normed_two, gate_grad, chip_grads, activated, back_term, down_all, mid_in, up_grad, normed_one, context = refs[:10]
    turned_all, o_all, qkv_all, cosines, sines, tokens_in, rows_of, gain_rows = refs[10:18]
    down_out, gate_out, up_out, o_out, q_out, kv_out, out, in_grad, gain_out = refs[18:27]
    mid_grad_all, branch_all, qkv_back, in_term, out_term, down, gate, up, o_sums, qkv_sums = refs[27:37]
    n = SCATTER_BUFFERS
    buffers, refs = refs[37 : 37 + 4 * n], refs[37 + 4 * n :]
    back_refs, front_refs, in_refs = refs[:4], refs[4:8], refs[8:11]
    gain_refs, (one_sum, two_sum), refs = refs[11:15], refs[15:17], refs[17:]
    fetch_sems, out_sems, pair_sems, weight_sems, stage_sems, block_sems, back_sems, credit = refs[:8]
    here = place()
    z, c = here[2], here[4]
    chip, width = chip_grads.shape
    count = chip // 2
    block = rows_of.shape[2]
    blocks = chip // block
    per = blocks // 2
    qkv_wide, q_half = qkv_all.shape[1], o_all.shape[1]
    enter(zn, here)
    branch, out_rows, in_rows = back_refs[0], front_refs[0], in_refs[0]
    back = Total(here, back_term, *back_refs)
    front = Total(here, out_term, *front_refs)
    total = Total(here, in_term, in_refs[0], back_refs[1], in_refs[1], in_refs[2])
    gains = Gains(zn, here, *gain_refs)
    work = Scatter(
        zn,
        here,
        early,
        [
            (down, buffers[:n], [(down_out, False, 0, down_out.shape[1] // 2)]),
            (gate, buffers[n : 2 * n], [(gate_out, False, 0, gate_out.shape[1] // 2)]),
            (up, buffers[:n], [(up_out, False, 0, up_out.shape[1] // 2)]),
            (o_sums, buffers[2 * n : 3 * n], [(o_out, False, 0, q_half)]),
            (
                qkv_sums,
                buffers[3 * n :],
                [(q_out, False, 0, q_half), (kv_out, True, q_half, kv_out.shape[2])],
            ),
        ],
        refs[8:],
    )
    back.start()

    def out_terms(right_one, weights, stages):
        block = weights.shape[1]

        def fetch_weights(i, slot):
            return pltpu.make_async_copy(
                down_all.at[pl.ds(pl.multiple_of(i * block, block), block)], weights.at[slot], weight_sems.at[slot]
            )

        def stores(i, slot):
            to = pl.ds(pl.multiple_of(i * block, block), block)
            return [
                pltpu.make_async_copy(
                    stages.at[slot, pl.ds(half * (chip // 2), chip // 2)],
                    out_term.at[half, :, to],
                    stage_sems.at[slot, half],
                )
                for half in range(2)
            ]

        fetch_weights(0, 0).start()

        def step(i):
            slot = lax.rem(i, 2)
            fetch_weights(i, slot).wait()

            @pl.when(i + 1 < width // block)
            def _():
                fetch_weights(i + 1, 1 - slot).start()

            @pl.when(i > 1)
            def _():
                for copy in stores(i - 2, slot):
                    copy.wait()

            stages[slot] = times_transposed(right_one[...], weights[slot]).astype(BF16)
            for copy in stores(i, slot):
                copy.start()

        loop(width // block, step)
        for i in range(width // block - 2, width // block):
            for copy in stores(i, i % 2):
                copy.wait()

    def first_terms(left, right, stage, weights, stages):
        for load in fetch(((chip_grads, left), (activated, right)), fetch_sems):
            load.wait()
        work.make(0, left, right, stage, back.meet)
        load = fetch(((normed_two, left),), fetch_sems)[0]
        for g in range(3):
            work.early_third(0, g)
        work.late_third(0, 0)
        out_terms(right, weights, stages)
        front.start()
        load_right = pltpu.make_async_copy(gate_grad, right, fetch_sems.at[1])
        load_right.start()
        work.early_home(0)
        work.late_third(0, 1)
        work.late_third(0, 2)
        load.wait()
        load_right.wait()
        work.make(1, left, right, stage)

    wide = down.shape[2]
    operands = [pltpu.VMEM((chip, width), BF16), pltpu.VMEM((chip, wide), BF16), pltpu.VMEM((2,) + down.shape[1:], BF16)]
    pl.run_scoped(
        first_terms, *operands, pltpu.VMEM((2, 256, wide), BF16), pltpu.VMEM((2, chip, 256), BF16)
    )
    work.early_third(1, 0)
    work.early_third(1, 1)

    def sums(mid, mid_grad, grads):
        for load in fetch(
            (
                (mid_in, mid),
                (chip_grads.at[pl.ds(pl.multiple_of(c * count, 16), count)], grads),
            ),
            fetch_sems,
        ):
            load.wait()
        gain = gain_rows[pl.ds(1, 1)]
        two_sum[...] = jnp.zeros_like(two_sum)

        def body_gain(at):
            value = mid[at]
            factor = lax.rsqrt(jnp.mean(value * value, axis=-1, keepdims=True) + norm_eps)
            two_sum[...] += jnp.sum(back.half[at].astype(F32) * (value * factor), axis=0, keepdims=True)

        by_rows(count, body_gain)
        back.pair().wait_recv()

        def body(at):
            value = mid[at]
            factor = lax.rsqrt(jnp.mean(value * value, axis=-1, keepdims=True) + norm_eps)
            scaled = back.rows(at) * gain
            result = (
                grads[at].astype(F32)
                + factor * scaled
                - value * (factor * factor * factor) * jnp.mean(scaled * value, axis=-1, keepdims=True)
            )
            mid_grad[at] = result
            branch[at] = result.astype(BF16)

        by_rows(count, body)
        save = pltpu.make_async_copy(mid_grad, mid_grad_all, out_sems.at[0])
        save.start()
        for copy in share(here, branch, branch_all, pair_sems):
            copy.start()
        work.early_third(1, 2)
        save.wait()

    pl.run_scoped(
        sums, pltpu.VMEM((count, width), F32), pltpu.VMEM((count, width), F32), pltpu.VMEM((count, width), BF16)
    )
    work.home(0)
    work.late_third(1, 0)
    work.done(0)
    work.lend(credit)

    def middle_terms(left, right, stage):
        for copy in share(here, branch, branch_all, pair_sems):
            copy.wait()
        right_o = right.at[:, pl.ds(0, q_half)]
        loads = fetch(
            ((branch_all.at[0], left.at[pl.ds(0, count)]), (branch_all.at[1], left.at[pl.ds(count, count)])),
            fetch_sems,
        )
        loads.append(pltpu.make_async_copy(context, right_o, fetch_sems.at[2]))
        loads[2].start()
        for load in loads:
            load.wait()
        work.make(3, left, right_o, stage)
        loads = fetch(((normed_two, left), (up_grad, right)), fetch_sems)
        front.meet()
        work.late_third(1, 1)
        for load in loads:
            load.wait()
        work.borrow(credit)
        work.make(2, left, right, stage)

    pl.run_scoped(middle_terms, *operands)
    work.early_third(2, 0)
    work.late_third(1, 2)

    def attention(o, qkv, inputs, turned, grads, backs, terms_out, cosine, sine, accumulators):
        def which(i):
            return lax.rem((1 - c) * per + i, blocks)

        def rows_at(i):
            return pl.ds(pl.multiple_of(i * block, block), block)

        def fetches(i, slot):
            b = which(i)
            sources = (
                (branch_all.at[b // per, rows_at(lax.rem(b, per))], inputs),
                (turned_all.at[rows_at(b)], turned),
                (cosines.at[rows_at(b)], cosine),
                (sines.at[rows_at(b)], sine),
            )
            return [
                pltpu.make_async_copy(source, buffer.at[slot], block_sems.at[slot, k])
                for k, (source, buffer) in enumerate(sources)
            ]

        def stores(i, slot):
            b = which(i)
            return [
                pltpu.make_async_copy(backs.at[slot], qkv_back.at[rows_at(b)], back_sems.at[slot, 0]),
                pltpu.make_async_copy(
                    terms_out.at[slot], in_term.at[b // per, rows_at(lax.rem(b, per))], back_sems.at[slot, 1]
                ),
            ]

        loads = fetch(((o_all, o), (qkv_all, qkv)), fetch_sems)
        for copy in fetches(0, 0):
            copy.start()
        for load in loads:
            load.wait()

        def step(i):
            slot = lax.rem(i, 2)

            @pl.when(i == per)
            def _():
                for done in range(per):
                    for copy in stores(done, done % 2):
                        copy.wait()
                total.core().start()
                work.early_home(1)
                work.early_third(3, 0)
                work.late_third(3, 0)
                work.early_third(2, 1)

            @pl.when(i == blocks - 1)
            def _():
                work.early_third(2, 2)
                work.early_third(3, 1)

            for copy in fetches(i, slot):
                copy.wait()

            @pl.when(i + 1 < blocks)
            def _():
                for copy in fetches(i + 1, 1 - slot):
                    copy.start()

            grads[...] = product(inputs[slot], o[...]).astype(BF16)
            attention_block_back(
                turned.at[slot],
                grads,
                backs.at[slot],
                accumulators,
                q_half,
                rows_of[which(i)],
                cosine[slot],
                sine[slot],
            )
            terms_out[slot] = times_transposed(backs[slot], qkv[...]).astype(BF16)
            for copy in stores(i, slot):
                copy.start()

        loop(blocks, step)
        for i in range(per, blocks):
            for copy in stores(i, i % 2):
                copy.wait()

    pl.run_scoped(
        attention,
        pltpu.VMEM(o_all.shape, BF16),
        pltpu.VMEM(qkv_all.shape, BF16),
        pltpu.VMEM((2, block, width), BF16),
        pltpu.VMEM((2, block, qkv_wide), BF16),
        pltpu.VMEM((block, q_half), BF16),
        pltpu.VMEM((2, block, qkv_wide), BF16),
        pltpu.VMEM((2, block, width), BF16),
        pltpu.VMEM((2, block, 2 * HEAD_DIM), F32),
        pltpu.VMEM((2, block, 2 * HEAD_DIM), F32),
        pltpu.VMEM((4, block, 2 * HEAD_DIM), F32),
    )
    back.finish()
    total.load().start()

    def meeting(tokens):
        load = fetch(((tokens_in, tokens),), fetch_sems)[0]
        work.late_third(3, 1)
        total.meet(send=False)
        load.wait()
        one_sum[...] = jnp.zeros_like(one_sum)

        def body_gain(at):
            value = tokens[at].astype(F32)
            factor = lax.rsqrt(jnp.mean(value * value, axis=-1, keepdims=True) + norm_eps)
            one_sum[...] += jnp.sum(total.half[at].astype(F32) * (value * factor), axis=0, keepdims=True)

        by_rows(count, body_gain)

    pl.run_scoped(meeting, pltpu.VMEM((count, width), BF16))
    gains.start([one_sum, two_sum])
    gains.swapped(0)
    total.pair().start()
    work.late_third(3, 2)
    work.late_third(2, 0)

    def last_terms(left, right, stage):
        right_qkv = right.at[:, pl.ds(0, qkv_wide)]
        for load in fetch(((normed_one, left), (qkv_back, right_qkv)), fetch_sems):
            load.wait()
        gains.swapped(1)
        work.make(4, left, right_qkv, stage)

    pl.run_scoped(last_terms, *operands)
    work.early_third(4, 0)
    work.early_third(4, 1)
    work.late_third(2, 1)
    work.early_third(3, 2)
    work.late_third(2, 2)

    def output(mid):
        load = fetch(((mid_in, mid),), fetch_sems)[0]
        front.pair().wait_recv()
        load.wait()

        def body_out(at):
            out_rows[at] = (mid[at] + front.rows(at)).astype(BF16)

        by_rows(count, body_out)

    pl.run_scoped(output, pltpu.VMEM((count, width), F32))
    save_out = pltpu.make_async_copy(out_rows, out, out_sems.at[1])
    save_out.start()
    work.home(1)
    work.early_home(2)
    work.early_home(3)
    work.early_third(4, 2)
    work.late_third(4, 0)
    gains.swapped(2)
    gains.run()

    def inputs_back(mid_grad, tokens):
        loads = fetch(((mid_grad_all, mid_grad), (tokens_in, tokens)), fetch_sems)
        gain = gain_rows[pl.ds(0, 1)]
        total.pair().wait_recv()
        for load in loads:
            load.wait()

        def body(at):
            value = tokens[at].astype(F32)
            factor = lax.rsqrt(jnp.mean(value * value, axis=-1, keepdims=True) + norm_eps)
            scaled = total.rows(at) * gain
            in_rows[at] = (
                mid_grad[at]
                + factor * scaled
                - value * (factor * factor * factor) * jnp.mean(scaled * value, axis=-1, keepdims=True)
            ).astype(BF16)

        by_rows(count, body)

    pl.run_scoped(inputs_back, pltpu.VMEM((count, width), F32), pltpu.VMEM((count, width), BF16))
    save_in = pltpu.make_async_copy(in_rows, in_grad, out_sems.at[0])
    save_in.start()
    work.late_third(4, 1)
    work.late_third(4, 2)
    work.early_home(4)
    gains.finish(gain_out)
    for j in (2, 3, 4):
        work.home(j)
    for j in (1, 2, 3, 4):
        work.done(j)
    front.finish()
    total.finish()
    save_out.wait()
    save_in.wait()


def call(kernel, name, collective_id, operands, specs, outs, out_specs, scratch, order=None):
    results = pl.pallas_call(
        kernel,
        out_shape=[jax.ShapeDtypeStruct(shape, dtype) for shape, dtype in outs],
        in_specs=specs,
        out_specs=out_specs,
        scratch_shapes=scratch,
        name=name,
        compiler_params=pltpu.CompilerParams(
            collective_id=collective_id, has_side_effects=True, vmem_limit_bytes=63 << 20
        ),
    )(*operands)
    return results if order is None else [results[i] for i in order]


def rotate(vectors, cosine, sine_rows):
    half = vectors.shape[-1] // 2
    first, second = vectors[..., :half], vectors[..., half:]
    return jnp.concatenate(
        [first * cosine - second * sine_rows, second * cosine + first * sine_rows], axis=-1
    )


def product(one, two):
    return jnp.dot(one, two, preferred_element_type=F32)


def times_transposed(one, two):
    return lax.dot_general(one, two, (((1,), (1,)), ((), ())), preferred_element_type=F32)


def inner_rows(one, two):
    return lax.dot_general(one, two, (((0,), (0,)), ((), ())), preferred_element_type=F32)


def einsum(form, one, two):
    return jnp.einsum(form, one, two, preferred_element_type=F32)


def halves(weight):
    rows, columns = weight.shape
    return weight.reshape(rows, 2, columns // 2).transpose(1, 0, 2)


def joined(pair):
    return jnp.concatenate([pair[0], pair[1]], axis=1)


def local(
    dp,
    tokens,
    seg_ids,
    q_weight,
    k_weight,
    v_weight,
    o_weight,
    attn_gain,
    gate_weight,
    up_weight,
    down_weight,
    mlp_gain,
    out_grad,
):
    zn = dp // 4
    units = zn * 2
    count, width = tokens.shape
    rows = q_weight.shape[0]
    blocks, block_rows = 2 * seg_ids.shape[0], seg_ids.shape[1]
    q_half, kv_half = q_weight.shape[1] // 2, k_weight.shape[1] // 2
    ff_half = gate_weight.shape[1] // 2
    qkv_half = q_half + 2 * kv_half
    heads, groups = q_half // HEAD_DIM, kv_half // HEAD_DIM
    early = 2 * rows // 48 * 8
    early_sums = max(16, 2 * rows // 128 * 16)

    kv_shard = jnp.concatenate([halves(k_weight), halves(v_weight)], axis=2)
    gain_rows = jnp.zeros((8, 128), F32)
    gain_rows = gain_rows.at[0, :rows].set(attn_gain.astype(F32)).at[1, :rows].set(mlp_gain.astype(F32))
    gain_shard = jnp.stack([gain_rows, gain_rows])

    chip = 2 * count
    inverse = 1.0 / 10000.0 ** (jnp.arange(0, HEAD_DIM, 2, dtype=F32) / HEAD_DIM)
    inverse = jnp.tile(inverse, 4).reshape(1, 2 * HEAD_DIM)
    sign = jnp.tile(jnp.repeat(jnp.array([-1.0, 1.0], F32), HEAD_DIM // 2), 2).reshape(1, 2 * HEAD_DIM)
    (
        qkv_full,
        o_full,
        grads_chip,
        segment,
        down_full,
        mid,
        normed_two,
        activated,
        gate_grad,
        up_grad,
        back_term,
        normed,
        turned,
        context,
        cosines,
        sines,
        gain_rows,
    ) = call(
        functools.partial(forward, zn, early),
        "forward",
        0,
        (
            q_weight,
            kv_shard,
            o_weight.T,
            gain_shard,
            tokens,
            out_grad,
            seg_ids,
            gate_weight,
            up_weight,
            down_weight.T,
            inverse,
            sign,
        ),
        [VMEM] * 12,
        [
            ((width, qkv_half), BF16),
            ((width, q_half), BF16),
            ((units * 16, 128), F32),
            ((2, count, width), BF16),
            ((2, count, width), BF16),
            ((2,) + seg_ids.shape, jnp.int32),
        ]
        + [((width, ff_half), BF16)] * 3
        + [((count, width), F32), ((2, count, width), BF16)]
        + [((chip, ff_half), BF16)] * 3
        + [((2, count, width), BF16)] * 2
        + [((chip, width), BF16), ((chip, qkv_half), BF16), ((chip, q_half), BF16)]
        + [((chip, 2 * HEAD_DIM), F32)] * 2
        + [((8, width), F32)],
        [ANY] * 22,
        total_buffers(count, width)
        + [
            pltpu.VMEM((2, count, width), BF16),
            DMA((3,)),
            DMA((3,)),
            DMA((2,)),
            DMA((2,)),
            DMA((2, 3)),
            DMA((2,)),
            pltpu.VMEM((chip, 2 * HEAD_DIM), F32),
            pltpu.VMEM((chip, 2 * HEAD_DIM), F32),
            pltpu.VMEM((2,) + seg_ids.shape, jnp.int32),
            pltpu.VMEM((units * 16, 128), F32),
            pltpu.VMEM((8, width), F32),
            DMA((2, 3)),
            DMA((5,)),
        ]
        + gather_sems(6, 7, zn),
        order=(0, 1, 4, 5, 8, 9, 10, 11, 12, 13, 14, 16, 17, 18, 19, 20, 21),
    )
    grads_chip = grads_chip.reshape(chip, width)
    segment = segment.reshape(blocks, 1, block_rows)
    normed_two = normed_two.reshape(chip, width)

    down_sum, gate_sum, up_sum, o_sum, q_sum, kv_sum, out, in_grad, gain_sums = call(
        functools.partial(backward, zn, early_sums),
        "backward",
        1,
        (
            normed_two,
            gate_grad,
            grads_chip,
            activated,
            back_term,
            down_full,
            mid,
            up_grad,
            normed,
            context,
            turned,
            o_full,
            qkv_full,
            cosines,
            sines,
            tokens,
            segment,
            gain_rows,
        ),
        [ANY] * 16 + [VMEM] * 2,
        [((rows, 2 * ff_half), F32)] * 3
        + [
            ((rows, 2 * q_half), F32),
            ((rows, 2 * q_half), F32),
            ((2, rows, 2 * kv_half), F32),
            ((count, width), BF16),
            ((count, width), BF16),
            ((8, 4 * rows), F32),
            ((count, width), F32),
            ((2, count, width), BF16),
            ((chip, qkv_half), BF16),
            ((2, count, width), BF16),
            ((2, count, width), BF16),
        ]
        + [((zn, 4 * rows, ff_half), BF16)] * 3
        + [((zn, 4 * rows, q_half), BF16), ((zn, 4 * rows, qkv_half), BF16)],
        [ANY] * 8 + [VMEM] + [ANY] * 10,
        scatter_buffers(
            [(2 * rows, ff_half), (2 * rows, ff_half), (2 * rows, q_half), (2 * rows, qkv_half)], early_sums, zn
        )
        + total_buffers(count, width) * 2
        + [pltpu.VMEM((count, width), BF16)] * 2
        + [DMA((5,))]
        + gain_buffers(zn, 4 * rows)
        + [pltpu.VMEM((1, width), F32)] * 2
        + [
            DMA((4,)),
            DMA((2,)),
            DMA((3,)),
            DMA((2,)),
            DMA((2, 2)),
            DMA((2, 4)),
            DMA((2, 2)),
            pltpu.SemaphoreType.REGULAR,
        ]
        + scatter_sems(5, 6, zn),
        order=range(9),
    )
    gain_grads = lax.dynamic_slice_in_dim(gain_sums, lax.rem(lax.axis_index("dp"), 4) * rows, rows, 1)
    return (
        out,
        in_grad,
        q_sum,
        joined(kv_sum[:, :, :kv_half]),
        joined(kv_sum[:, :, kv_half:]),
        o_sum.T,
        gain_grads[0],
        gate_sum,
        up_sum,
        down_sum.T,
        gain_grads[1],
    )


def solution(mesh):
    arguments = (
        P("dp", None),
        P("dp", None),
        P("dp", "tensor"),
        P("dp", "tensor"),
        P("dp", "tensor"),
        P("tensor", "dp"),
        P("dp"),
        P("dp", "tensor"),
        P("dp", "tensor"),
        P("tensor", "dp"),
        P("dp"),
        P("dp", None),
    )
    results = (
        P("dp", None),
        P("dp", None),
        P("dp", "tensor"),
        P("dp", "tensor"),
        P("dp", "tensor"),
        P("tensor", "dp"),
        P("dp"),
        P("dp", "tensor"),
        P("dp", "tensor"),
        P("tensor", "dp"),
        P("dp"),
    )
    return jax.shard_map(
        functools.partial(local, mesh.shape["dp"]),
        mesh=mesh,
        in_specs=arguments,
        out_specs=results,
        check_vma=False,
    )
```

```python
import functools

import jax
import jax.numpy as jnp
import numpy as np
from jax import lax
from jax.experimental import pallas as pl
from jax.experimental.pallas import tpu as pltpu
from jax.sharding import PartitionSpec as P

HEAD_DIM = 64
norm_eps = 1e-05
MESH = pl.DeviceIdType.MESH
ANY = pl.BlockSpec(memory_space=pl.ANY)
VMEM = pl.BlockSpec(memory_space=pltpu.VMEM)
DMA = pltpu.SemaphoreType.DMA
F32 = jnp.float32
BF16 = jnp.bfloat16


def place():
    d = lax.axis_index("dp")
    t = lax.axis_index("tensor")
    return d, t, d // 4, lax.rem(d // 2, 2), lax.rem(d, 2)


def enter(zn, here):
    d, t, z, x, c = here
    bar = pltpu.get_barrier_semaphore()

    def hail(device):
        pl.semaphore_signal(bar, inc=1, device_id=device, device_id_type=MESH)

    hail((d + 1 - 2 * c, t))
    hail((d + 2 - 4 * x, t))
    hail((d, 1 - t))

    @pl.when(z > 0)
    def _():
        hail((d - 4, t))

    @pl.when(z < zn - 1)
    def _():
        hail((d + 4, t))

    pl.semaphore_wait(bar, 5 - (z == 0).astype(jnp.int32) - (z == zn - 1).astype(jnp.int32))


def farthest_first(zn, z, i):
    up = 1 - (2 * z) // zn
    longer = up * (zn - 1 - z) + (1 - up) * z
    shorter = zn - 1 - longer
    rest = i - (longer - shorter)
    return jnp.where(
        rest < 0,
        z + (2 * up - 1) * (longer - i),
        z + (1 - 2 * lax.rem(jnp.maximum(rest, 0), 2)) * (shorter - jnp.maximum(rest, 0) // 2),
    )


def loop(count, body):
    def step(i, carry):
        body(i)
        return carry

    lax.fori_loop(0, count, step, 0)


def remote(src, dst, send, recv, device):
    return pltpu.make_async_remote_copy(
        src_ref=src, dst_ref=dst, send_sem=send, recv_sem=recv, device_id=device, device_id_type=MESH
    )


def by_rows(count, body, block=16):
    def step(i, carry):
        body(pl.ds(pl.multiple_of(i * block, block), block))
        return carry

    lax.fori_loop(0, count // block, step, 0)


def gather_sems(n, sources, zn):
    return [
        DMA((sources,)),
        DMA((sources,)),
        DMA((sources,)),
        DMA((n, zn)),
        DMA((n, zn)),
        DMA((n,)),
        DMA((n,)),
        DMA((n, 2, zn)),
        DMA((n, zn)),
        DMA((n, 2, zn)),
        DMA((n, zn)),
    ]


def part(ref, core, paired):
    if paired:
        return ref.at[core]
    columns = ref.shape[1] // 2
    return ref.at[:, pl.ds(pl.multiple_of(core * columns, columns), columns)]


class Gather:
    def __init__(self, zn, here, arrays, sems):
        self.zn, self.here = zn, here
        self.full = [full for _, full, _ in arrays]
        self.early = [early for _, _, early in arrays]
        self.sources = [
            (j, i) + source for j, (sources, _, _) in enumerate(arrays) for i, source in enumerate(sources)
        ]
        (
            self.loc,
            self.cs,
            self.cr,
            self.xs,
            self.xr,
            self.es,
            self.er,
            self.zs,
            self.zr,
            self.bs,
            self.br,
        ) = sems

    def unit(self, j, unit, first, count):
        rows = self.full[j].shape[0] // (2 * self.zn)
        return pl.ds(pl.multiple_of(unit * rows + first, 8), count)

    def rows(self, j, unit, early):
        rows = self.full[j].shape[0] // (2 * self.zn)
        late = rows - self.early[j]
        first, count = {None: (0, rows), True: (late, rows - late), False: (0, late)}[early]
        return self.full[j].at[self.unit(j, unit, first, count)]

    def mine(self, s):
        d, t, z, x, c = self.here
        j, _, shard, paired, first, columns = self.sources[s]
        rows = self.full[j].shape[0] // (4 * self.zn)
        return self.full[j].at[self.unit(j, z * 2 + x, c * rows, rows), pl.ds(first, columns)]

    def keep(self, s):
        _, _, shard, paired, _, _ = self.sources[s]
        return pltpu.make_async_copy(part(shard, self.here[4], paired), self.mine(s), self.loc.at[s])

    def give(self, s):
        d, t, z, x, c = self.here
        _, _, shard, paired, _, _ = self.sources[s]
        return remote(
            part(shard, 1 - c, paired), self.mine(s), self.cs.at[s], self.cr.at[s], (d + 1 - 2 * c, t)
        )

    def x_late(self, j, o):
        d, t, z, x, c = self.here
        ref = self.rows(j, o * 2 + x, False)
        return remote(ref, ref, self.xs.at[j, o], self.xr.at[j, o], (d + 2 - 4 * x, t))

    def x_early(self, j):
        d, t, z, x, c = self.here
        ref = self.rows(j, z * 2 + x, True)
        return remote(ref, ref, self.es.at[j], self.er.at[j], (d + 2 - 4 * x, t))

    def along(self, j, o, down):
        d, t, z, x, c = self.here
        ref = self.rows(j, o * 2 + x, None)
        return remote(ref, ref, self.zs.at[j, down, o], self.zr.at[j, o], (d + 4 - 8 * down, t))

    def along_early(self, j, o, down):
        d, t, z, x, c = self.here
        ref = self.rows(j, o * 2 + 1 - x, True)
        return remote(ref, ref, self.bs.at[j, down, o], self.br.at[j, o], (d + 4 - 8 * down, t))

    def start(self, arrays):
        for s, source in enumerate(self.sources):
            if source[0] in arrays:
                self.give(s).start()
                self.keep(s).start()

    def ready(self, arrays):
        for j in arrays:
            for s, source in enumerate(self.sources):
                if source[0] == j:
                    self.keep(s).wait()
                    self.give(s).wait_recv()
            if self.early[j]:
                self.x_early(j).start()

    def start_own(self, arrays):
        z, zn = self.here[2], self.zn
        for j in arrays:
            self.x_late(j, z).start()

            @pl.when(z < zn - 1)
            def _():
                self.along(j, z, 0).start()

            @pl.when(z > 0)
            def _():
                self.along(j, z, 1).start()

    def start_early(self, arrays):
        z, zn = self.here[2], self.zn
        for j in arrays:
            if self.early[j]:
                self.x_early(j).wait_recv()

                @pl.when(z < zn - 1)
                def _():
                    self.along_early(j, z, 0).start()

                @pl.when(z > 0)
                def _():
                    self.along_early(j, z, 1).start()

    def relay(self, k, arrays):
        z, zn = self.here[2], self.zn
        o = farthest_first(zn, z, zn - 1 - k)
        down = (o > z).astype(jnp.int32)
        more = ((o < z) & (z < zn - 1)) | ((o > z) & (z > 0))
        for j in arrays:
            self.along(j, o, down).wait_recv()

            @pl.when(more)
            def _():
                self.along(j, o, down).start()

            self.x_late(j, o).start()
            if self.early[j]:
                self.along_early(j, o, down).wait_recv()

                @pl.when(more)
                def _():
                    self.along_early(j, o, down).start()

    def relays(self, first, arrays):
        loop(max(self.zn - first, 0), lambda i: self.relay(first + i, arrays))

    def arrived(self, j):
        loop(self.zn, lambda o: self.x_late(j, o).wait_recv())

    def finish(self):
        z, zn = self.here[2], self.zn
        for s in range(len(self.sources)):
            self.give(s).wait_send()
        for j in range(len(self.full)):
            if self.early[j]:
                self.x_early(j).wait_send()

            def step(o, j=j):
                self.x_late(j, o).wait_send()

                def sent(down):
                    self.along(j, o, down).wait_send()
                    if self.early[j]:
                        self.along_early(j, o, down).wait_send()

                @pl.when((o <= z) & (z < zn - 1))
                def _():
                    sent(0)

                @pl.when((o >= z) & (z > 0))
                def _():
                    sent(1)

            loop(zn, step)


def scatter_sems(n, outs, zn):
    return [
        DMA((n, zn)),
        DMA((n, zn)),
        DMA((n, zn)),
        DMA((n, zn)),
        DMA((n, zn)),
        DMA((n, zn + 1)),
        DMA((n, 2, zn)),
        DMA((n, zn)),
        DMA((n, zn + 1)),
        DMA((n,)),
        DMA((n,)),
        DMA((outs,)),
        DMA((outs,)),
        DMA((outs,)),
    ]


def scatter_buffers(shapes, early, zn):
    out = []
    for rows, columns in shapes:
        late = rows - early
        out += [
            pltpu.VMEM((zn, late, columns), BF16),
            pltpu.VMEM((zn, late, columns), BF16),
            pltpu.VMEM((zn + 1, late, columns), BF16),
            pltpu.VMEM((zn, 2, early, columns), BF16),
            pltpu.VMEM((zn + 1, 2, early, columns), BF16),
            pltpu.VMEM((early, columns), BF16),
            pltpu.VMEM((rows, columns), F32),
        ]
    return out


SCATTER_BUFFERS = 7


class Scatter:
    def __init__(self, zn, here, early, arrays, sems):
        self.zn, self.here, self.early = zn, here, early
        self.term = [term for term, _, _ in arrays]
        self.buffers = [buffers for _, buffers, _ in arrays]
        self.results = [(j,) + result for j, (_, _, results) in enumerate(arrays) for result in results]
        (
            self.st,
            self.ls,
            self.xs,
            self.xr,
            self.zs,
            self.zr,
            self.bls,
            self.bs,
            self.br,
            self.es,
            self.er,
            self.cs,
            self.cr,
            self.loc,
        ) = sems

    def unit(self, j, o, x, first, count):
        rows = self.term[j].shape[1] // 2
        return self.term[j].at[o, pl.ds(pl.multiple_of(x * rows + first, 16), count)]

    def late(self, j):
        return self.buffers[j][0].shape[1]

    def load(self, j, o):
        return pltpu.make_async_copy(
            self.unit(j, o, self.here[3], 0, self.late(j)), self.buffers[j][0].at[o], self.ls.at[j, o]
        )

    def load_early(self, j, o, other):
        x = self.here[3]
        return pltpu.make_async_copy(
            self.unit(j, o, 1 - x if other else x, self.late(j), self.early),
            self.buffers[j][3].at[o, other],
            self.bls.at[j, other, o],
        )

    def across(self, j, o):
        d, t, z, x, c = self.here
        return remote(
            self.unit(j, o, 1 - x, 0, self.late(j)),
            self.buffers[j][1].at[o],
            self.xs.at[j, o],
            self.xr.at[j, o],
            (d + 2 - 4 * x, t),
        )

    def across_early(self, j):
        d, t, z, x, c = self.here
        return remote(
            self.buffers[j][3].at[z, 1], self.buffers[j][5], self.es.at[j], self.er.at[j], (d + 2 - 4 * x, t)
        )

    def along(self, j, o, slot, down):
        d, t, z, x, c = self.here
        own, line = self.buffers[j][0], self.buffers[j][2]
        return remote(own.at[o], line.at[slot], self.zs.at[j, o], self.zr.at[j, slot], (d + 4 - 8 * down, t))

    def along_early(self, j, o, slot, down):
        d, t, z, x, c = self.here
        own, line = self.buffers[j][3], self.buffers[j][4]
        return remote(own.at[o], line.at[slot], self.bs.at[j, o], self.br.at[j, slot], (d + 4 - 8 * down, t))

    def give(self, r):
        d, t, z, x, c = self.here
        j, out, paired, first, columns = self.results[r]
        rows = out.shape[-2]
        ref = self.buffers[j][6].at[
            pl.ds(pl.multiple_of((1 - c) * rows, rows), rows), pl.ds(first, columns)
        ]
        return remote(ref, part(out, c, paired), self.cs.at[r], self.cr.at[r], (d + 1 - 2 * c, t))

    def keep(self, r):
        c = self.here[4]
        j, out, paired, first, columns = self.results[r]
        rows = out.shape[-2]
        ref = self.buffers[j][6].at[pl.ds(pl.multiple_of(c * rows, rows), rows), pl.ds(first, columns)]
        return pltpu.make_async_copy(ref, part(out, c, paired), self.loc.at[r])

    def store(self, j, o, stage, slot):
        columns = self.term[j].shape[2]
        return pltpu.make_async_copy(
            stage.at[slot, :, pl.ds(0, columns)], self.term[j].at[o], self.st.at[j, o]
        )

    def make(self, j, left, right, stage, between=None):
        z, zn = self.here[2], self.zn
        wide, columns = self.term[j].shape[1:]
        block = min(256, wide)

        def send(i):
            o = farthest_first(zn, z, i)
            self.store(j, o, stage, lax.rem(i, 2)).wait()
            self.across(j, o).start()
            for other in range(2):
                self.load_early(j, o, other).start()
            self.load(j, o).start()

        def compute(i):
            o = farthest_first(zn, z, i)
            slot = lax.rem(i, 2)

            def body(m):
                at = pl.multiple_of(o * wide + m * block, block)
                value = inner_rows(left[:, pl.ds(at, block)], right[...])
                stage[slot, pl.ds(pl.multiple_of(m * block, block), block), pl.ds(0, columns)] = value.astype(
                    BF16
                )

            loop(wide // block, body)
            self.store(j, o, stage, slot).start()

        def both(i):
            compute(i)
            send(i - 1)

        compute(0)
        if between is not None:
            between()
        loop(zn - 1, lambda i: both(i + 1))
        send(zn - 1)

    def add(self, j, o, slots):
        own, got, line = self.buffers[j][:3]

        def body(at):
            value = own[o, at].astype(F32) + got[o, at].astype(F32)
            for slot in slots:
                value = value + line[slot, at].astype(F32)
            own[o, at] = value.astype(BF16)

        by_rows(own.shape[1], body)

    def add_early(self, j, o, slots):
        own, line = self.buffers[j][3:5]
        for other in range(2):

            def body(at):
                value = own[o, other, at].astype(F32)
                for slot in slots:
                    value = value + line[slot, other, at].astype(F32)
                own[o, other, at] = value.astype(BF16)

            by_rows(own.shape[2], body)

    def route(self, i):
        z, zn = self.here[2], self.zn
        o = farthest_first(zn, z, i)
        down = (o < z).astype(jnp.int32)
        distance = jnp.maximum((o - z) * (1 - 2 * down), 1)
        slot = o + (zn - o) * down * (1 // distance)
        inner = ((o > z) & (z > 0)) | ((o < z) & (z < zn - 1))
        return o, slot, down, inner

    def hop_early(self, j, i):
        o, slot, down, inner = self.route(i)
        for other in range(2):
            self.load_early(j, o, other).wait()

        @pl.when(inner)
        def _():
            self.along_early(j, o, o, down).wait_recv()
            self.add_early(j, o, [o])

        self.along_early(j, o, slot, down).start()

    def hop(self, j, i):
        o, slot, down, inner = self.route(i)
        self.load(j, o).wait()
        self.across(j, o).wait_recv()

        @pl.when(inner)
        def _():
            self.along(j, o, o, down).wait_recv()
            self.add(j, o, [o])

        @pl.when(jnp.logical_not(inner))
        def _():
            self.add(j, o, [])

        self.along(j, o, slot, down).start()

    def third(self, hop, j, g):
        hops = self.zn - 1
        first = g * hops // 3
        loop((g + 1) * hops // 3 - first, lambda i: hop(j, first + i))

    def early_third(self, j, g):
        self.third(self.hop_early, j, g)

    def late_third(self, j, g):
        self.third(self.hop, j, g)

    def at_home(self, action):
        z, zn = self.here[2], self.zn

        @pl.when((z > 0) & (z < zn - 1))
        def _():
            action([z, zn])

        @pl.when(z == 0)
        def _():
            action([zn])

        @pl.when(z == zn - 1)
        def _():
            action([z])

    def early_home(self, j):
        z = self.here[2]
        for other in range(2):
            self.load_early(j, z, other).wait()

        def home(slots):
            for slot in slots:
                self.along_early(j, z, slot, 0).wait_recv()
            self.add_early(j, z, slots)

        self.at_home(home)
        self.across_early(j).start()

    def home(self, j):
        z = self.here[2]
        own, got, line, early, _, other_early, total = self.buffers[j]
        late = self.late(j)
        self.load(j, z).wait()
        self.across(j, z).wait_recv()

        def last(slots):
            for slot in slots:
                self.along(j, z, slot, 0).wait_recv()

            def body(at):
                value = own[z, at].astype(F32) + got[z, at].astype(F32)
                for slot in slots:
                    value = value + line[slot, at].astype(F32)
                total[at] = value

            by_rows(late, body)

        self.at_home(last)
        self.across_early(j).wait_recv()
        for i in range(self.early // 16):
            at = pl.ds(16 * i, 16)
            total[pl.ds(late + 16 * i, 16)] = early[z, 0, at].astype(F32) + other_early[at].astype(F32)
        for r, result in enumerate(self.results):
            if result[0] == j:
                self.give(r).start()
                self.keep(r).start()

    def done(self, j):
        z = self.here[2]
        for r, result in enumerate(self.results):
            if result[0] == j:
                self.give(r).wait()
                self.keep(r).wait()
        self.across_early(j).wait_send()

        def sent(o):
            self.across(j, o).wait_send()

            @pl.when(o != z)
            def _():
                self.along(j, o, 0, 0).wait_send()
                self.along_early(j, o, 0, 0).wait_send()

        loop(self.zn, sent)

    def lend(self, credit):
        d, t, z, x, c = self.here

        def tell(device):
            pl.semaphore_signal(credit, inc=1, device_id=device, device_id_type=MESH)

        tell((d + 2 - 4 * x, t))

        @pl.when(z > 0)
        def _():
            tell((d - 4, t))

        @pl.when(z < self.zn - 1)
        def _():
            tell((d + 4, t))

    def borrow(self, credit):
        z = self.here[2]
        pl.semaphore_wait(credit, 3 - (z == 0).astype(jnp.int32) - (z == self.zn - 1).astype(jnp.int32))


class Gains:
    def __init__(self, zn, here, own, got, line, sems):
        self.zn, self.here, self.own, self.got, self.line, self.sems = zn, here, own, got, line, sems

    def swap(self, i):
        d, t, z, x, c = self.here
        device = ((d + 1 - 2 * c, t), (d, 1 - t), (d + 2 - 4 * x, t))[i]
        return remote(self.own, self.got.at[i], self.sems.at[0, i], self.sems.at[1, i], device)

    def along(self, o, slot, down):
        d, t, z, x, c = self.here
        return remote(
            self.own.at[o], self.line.at[slot], self.sems.at[2, o], self.sems.at[3, slot], (d + 4 - 8 * down, t)
        )

    def start(self, rows):
        wide = self.own.shape[2]
        for o in range(self.zn):
            for i, row in enumerate(rows):
                self.own[o, pl.ds(i, 1)] = row[:, pl.ds(o * wide, wide)]
        self.swap(0).start()

    def swapped(self, i):
        self.swap(i).wait()
        self.own[...] += self.got[i]
        if i < 2:
            self.swap(i + 1).start()

    def hop(self, o, slot, down, inner):
        @pl.when(inner)
        def _():
            self.along(o, o, down).wait_recv()
            self.own[o] += self.line[o]

        self.along(o, slot, down).start()

    def steps(self, k, nearest):
        z, zn = self.here[2], self.zn

        @pl.when(z + k < zn)
        def _():
            self.hop(z + k, z + k, 0, z > 0)

        @pl.when(z - k >= 0)
        def _():
            self.hop(z - k, zn if nearest else z - k, 1, z < zn - 1)

    def run(self):
        zn = self.zn

        def step(i, carry):
            self.steps(zn - 1 - i, False)
            return carry

        lax.fori_loop(0, zn - 2, step, 0)
        self.steps(1, True)

    def finish(self, out):
        z, zn = self.here[2], self.zn
        value = self.own[z]

        @pl.when(z > 0)
        def _():
            self.along(z, z, 0).wait_recv()
            self.own[z] += self.line[z]

        @pl.when(z < zn - 1)
        def _():
            self.along(z, zn, 1).wait_recv()
            self.own[z] += self.line[zn]

        out[...] = self.own[z]

        def step(o, carry):
            @pl.when(o != z)
            def _():
                self.along(o, 0, 0).wait_send()

            return carry

        lax.fori_loop(0, zn, step, 0)


def gain_buffers(zn, wide):
    return [
        pltpu.VMEM((zn, 8, wide), F32),
        pltpu.VMEM((3, zn, 8, wide), F32),
        pltpu.VMEM((zn + 1, 8, wide), F32),
        DMA((4, zn + 1)),
    ]


class Total:
    def __init__(self, here, term, from_core, half, from_pair, sems):
        self.here, self.term, self.from_core, self.half, self.from_pair = here, term, from_core, half, from_pair
        self.sems = sems

    def core(self):
        d, t, z, x, c = self.here
        return remote(self.term.at[1 - c], self.from_core, self.sems.at[0], self.sems.at[1], (d + 1 - 2 * c, t))

    def load(self):
        return pltpu.make_async_copy(self.term.at[self.here[4]], self.half, self.sems.at[4])

    def start(self):
        self.core().start()
        self.load().start()

    def pair(self):
        d, t, z, x, c = self.here
        return remote(self.half, self.from_pair, self.sems.at[2], self.sems.at[3], (d, 1 - t))

    def meet(self, loaded=True, send=True):
        if loaded:
            self.load().wait()
        self.core().wait_recv()

        def body(at):
            self.half[at] = (self.half[at].astype(F32) + self.from_core[at].astype(F32)).astype(BF16)

        by_rows(self.half.shape[0], body)
        if send:
            self.pair().start()

    def rows(self, at):
        return self.half[at].astype(F32) + self.from_pair[at].astype(F32)

    def finish(self):
        self.core().wait_send()
        self.pair().wait_send()


def total_buffers(tokens, width):
    return [pltpu.VMEM((tokens, width), BF16)] * 3 + [DMA((5,))]


def share(here, src, dst, sems):
    d, t, z, x, c = here
    return (
        pltpu.make_async_copy(src, dst.at[c], sems.at[0]),
        remote(src, dst.at[c], sems.at[1], sems.at[2], (d + 1 - 2 * c, t)),
    )


def lanes(shape):
    return lax.broadcasted_iota(jnp.int32, shape, 1)


def partner(value):
    half = HEAD_DIM // 2
    wide = 2 * HEAD_DIM
    lower = lax.rem(lanes(value.shape), HEAD_DIM) < half
    return jnp.where(lower, pltpu.roll(value, wide - half, 1), pltpu.roll(value, half, 1))


def same_segment(row):
    count = row.shape[1]
    wide = jnp.broadcast_to(row, (count, count))
    before = lax.broadcasted_iota(jnp.int32, wide.shape, 1) < lax.broadcasted_iota(jnp.int32, wide.shape, 0)
    return wide == wide.T, before


def allowed_in(row):
    same, before = same_segment(row)
    here = lax.broadcasted_iota(jnp.int32, same.shape, 1) == lax.broadcasted_iota(jnp.int32, same.shape, 0)
    return same & (before | here)


def softmax_of(queries, keys, allowed):
    scores = jnp.where(allowed, times_transposed(queries, keys) * HEAD_DIM ** (-0.5), -1e30)
    shifted = jnp.exp(scores - jnp.max(scores, axis=-1, keepdims=True))
    return shifted / jnp.sum(shifted, axis=-1, keepdims=True)


def key_value_pairs(pair):
    pair = pair.astype(F32)
    first = lanes(pair.shape) < HEAD_DIM
    key, value = jnp.where(first, pair, 0.0), jnp.where(first, 0.0, pair)
    return [
        part.astype(BF16)
        for part in (key, pltpu.roll(key, HEAD_DIM, 1), pltpu.roll(value, HEAD_DIM, 1), value)
    ]


def attention_block(turned, context, queries_wide, row):
    wide = 2 * HEAD_DIM
    allowed = allowed_in(row)
    key_one, key_two, value_one, value_two = key_value_pairs(turned[:, queries_wide:])

    def heads(p):
        at = pl.ds(pl.multiple_of(p * wide, wide), wide)
        queries = turned[:, at]
        one = softmax_of(queries, key_one, allowed).astype(BF16)
        two = softmax_of(queries, key_two, allowed).astype(BF16)
        context[:, at] = (product(one, value_one) + product(two, value_two)).astype(BF16)

    loop(queries_wide // wide, heads)


def attention_block_back(turned, grads, back, sums, queries_wide, row, cosine, sine):
    wide = 2 * HEAD_DIM
    scale = HEAD_DIM ** (-0.5)
    allowed = allowed_in(row)
    key_one, key_two, value_one, value_two = key_value_pairs(turned[:, queries_wide:])
    sums[...] = jnp.zeros_like(sums)

    def heads(p):
        at = pl.ds(pl.multiple_of(p * wide, wide), wide)
        queries, grad = turned[:, at], grads[:, at]
        total = None
        for i, (key, value) in enumerate(((key_one, value_one), (key_two, value_two))):
            probs = softmax_of(queries, key, allowed)
            sums[i] += inner_rows(probs.astype(BF16), grad)
            prob_grad = times_transposed(grad, value)
            delta = jnp.sum(probs * prob_grad, axis=-1, keepdims=True)
            score_grad = (probs * (prob_grad - delta)).astype(BF16)
            term = product(score_grad, key)
            total = term if total is None else total + term
            sums[2 + i] += inner_rows(score_grad, queries)
        total = total * scale
        back[:, at] = (total * cosine - partner(total) * sine).astype(BF16)

    loop(queries_wide // wide, heads)
    value_grad = pltpu.roll(sums[0], HEAD_DIM, 1) + sums[1]
    key_grad = (sums[2] + pltpu.roll(sums[3], HEAD_DIM, 1)) * scale
    turned_back = key_grad * cosine - partner(key_grad) * sine
    back[:, pl.ds(queries_wide, wide)] = jnp.where(
        lanes(value_grad.shape) < HEAD_DIM, turned_back, value_grad
    ).astype(BF16)


def transposed(src, dst):
    def body(n):
        at = pl.ds(pl.multiple_of(n * 128, 128), 128)
        dst[:, at] = src[at, :].astype(F32).T.astype(BF16)

    loop(src.shape[0] // 128, body)


def forward(zn, early, *refs):
    q, k_shard, v_shard, o_turned, gain_shards, tokens_in, grads_in, seg, gate_in, up_in, down_in, inverse, sign = refs[:13]
    refs = refs[1:]
    qkv_all, o_all, gains_all, chip_tokens, chip_grads, seg_all = refs[12:18]
    gate_all, up_all, down_all, mid_out, normed_out, act_out, gate_grad_out, up_grad_out, back_out = refs[18:27]
    term, normed_one_out, turned_out, context_out, cosines_out, sines_out, gain_out = refs[27:34]
    total_refs = refs[34:38]
    normed, out_sems, pair_sems, load_sems, grad_sems, stage_sems, block_sems = refs[38:45]
    cosines, sines, seg_pair, gain_tiles, gain_rows, swap_sems, seg_sems = refs[45:52]
    kv, gains, o_shard, down, tokens, grads, gate, up, down_turned, first_sems = refs[52:62]
    here = place()
    z, c = here[2], here[4]
    firsts = [
        pltpu.make_async_copy(src, dst, first_sems.at[n])
        for n, (src, dst) in enumerate(
            ((down_in, down_turned), (tokens_in, tokens), (gate_in, gate), (up_in, up), (grads_in, grads))
        )
    ]
    for copy in firsts:
        copy.start()
    enter(zn, here)
    keys, values = k_shard[...].astype(F32), v_shard[...].astype(F32)
    is_key = lanes(keys.shape) < HEAD_DIM
    kv[0] = jnp.where(is_key, keys, pltpu.roll(values, HEAD_DIM, 1)).astype(BF16)
    kv[1] = jnp.where(is_key, pltpu.roll(keys, HEAD_DIM, 1), values).astype(BF16)
    for i in range(2):
        gains[i] = jnp.zeros(gains.shape[1:], F32)
        gains[i, pl.ds(0, 2), pl.ds(0, gain_shards.shape[1])] = gain_shards[...].astype(F32)
    transposed(o_turned, o_shard)
    total = Total(here, term, *total_refs)
    q_half = q.shape[1] // 2
    work = Gather(
        zn,
        here,
        [
            ([(gains, True, 0, gains.shape[2])], gains_all, 0),
            ([(q, False, 0, q_half), (kv, True, q_half, kv.shape[2])], qkv_all, early),
            ([(o_shard, False, 0, o_shard.shape[1] // 2)], o_all, early),
        ]
        + [
            ([(shard, False, 0, shard.shape[1] // 2)], full, early)
            for shard, full in ((down, down_all), (gate, gate_all), (up, up_all))
        ],
        refs[62:],
    )
    count, width = tokens.shape
    columns = gate_all.shape[1]
    block = seg.shape[1]
    blocks = 2 * count // block
    per = count // block
    attention_set = [0, 1, 2]
    swap = remote(seg, seg_pair.at[c], seg_sems.at[0], seg_sems.at[1], (here[0] + 1 - 2 * c, here[1]))
    swap.start()
    seg_pair[c] = seg[...]
    work.start(attention_set)
    firsts[0].wait()
    transposed(down_turned, down)
    work.start([3])
    work.ready(attention_set)
    work.start_own(attention_set)
    for copy in firsts[1:]:
        copy.wait()
    shared = [
        share(here, src, dst, swap_sems.at[n])
        for n, (src, dst) in enumerate(((tokens, chip_tokens), (grads, chip_grads)))
    ]
    for copy in shared[0]:
        copy.start()
    work.start([4, 5])
    for copy in shared[1]:
        copy.start()
    work.start_early([1, 2])
    work.ready([3])
    work.start_own([3])
    swap.wait()
    for i in range(blocks):
        row = seg_pair[i // per, pl.ds(i % per, 1)]
        same, before = same_segment(row)
        position = jnp.sum(jnp.where(same & before, 1.0, 0.0), axis=-1, keepdims=True)
        angles = position * inverse[...]
        cosines[pl.ds(i * block, block)] = jnp.cos(angles)
        sines[pl.ds(i * block, block)] = jnp.sin(angles) * sign[...]
    saves = [
        pltpu.make_async_copy(src, dst, seg_sems.at[2 + n])
        for n, (src, dst) in enumerate(((cosines, cosines_out), (sines, sines_out), (seg_pair, seg_all)))
    ]
    for copy in saves:
        copy.start()
    work.relay(1, attention_set)
    work.relay(2, attention_set)
    work.start_early([3])
    work.relays(3, attention_set)
    work.ready([4, 5])
    work.start_own([4, 5])
    work.start_early([4])
    work.arrived(0)
    load = pltpu.make_async_copy(gains_all, gain_tiles, load_sems.at[0])
    load.start()
    load.wait()
    features = width // (4 * zn)
    for owner in range(4 * zn):
        for i in range(2):
            gain_rows[pl.ds(i, 1), pl.ds(owner * features, features)] = gain_tiles[
                pl.ds(owner * 8 + i, 1), :features
            ]
    save_gains = pltpu.make_async_copy(gain_rows, gain_out, load_sems.at[1])
    save_gains.start()
    gain_one, gain = gain_rows[pl.ds(0, 1)], gain_rows[pl.ds(1, 1)]
    for copies in shared:
        for copy in copies:
            copy.wait()
    work.arrived(1)
    work.arrived(2)
    save_gains.wait()
    half = total_refs[1]

    def attention(qkv, o, inputs, normed_one, turned, context, attended):
        queries_wide = context.shape[2]
        wide = 2 * HEAD_DIM

        def place_of(i):
            return lax.rem((1 - c) * per + i, blocks)

        def rows_at(i):
            return pl.ds(pl.multiple_of(place_of(i) * block, block), block)

        def fetch_inputs(i, slot):
            which = place_of(i)
            return pltpu.make_async_copy(
                chip_tokens.at[which // per, pl.ds(pl.multiple_of(lax.rem(which, per) * block, block), block)],
                inputs.at[slot],
                grad_sems.at[slot],
            )

        def stores(i, slot):
            return [
                pltpu.make_async_copy(buffer.at[slot], out.at[rows_at(i)], stage_sems.at[slot, n])
                for n, (buffer, out) in enumerate(
                    ((normed_one, normed_one_out), (turned, turned_out), (context, context_out))
                )
            ]

        def store_term(i, slot):
            return pltpu.make_async_copy(
                attended.at[slot],
                term.at[1 - c, pl.ds(pl.multiple_of(i * block, block), block)],
                block_sems.at[slot],
            )

        fetch_inputs(0, 0).start()
        loads = [
            pltpu.make_async_copy(qkv_all, qkv, load_sems.at[0]),
            pltpu.make_async_copy(o_all, o, load_sems.at[1]),
        ]
        for load in loads:
            load.start()
        for load in loads:
            load.wait()

        def one_block(i):
            slot = lax.rem(i, 2)
            to = rows_at(i)
            fetch_inputs(i, slot).wait()

            @pl.when(i + 1 < blocks)
            def _():
                fetch_inputs(i + 1, 1 - slot).start()

            @pl.when(i > 1)
            def _():
                for copy in stores(i - 2, slot):
                    copy.wait()

            def norm(at):
                value = inputs[slot, at].astype(F32)
                factor = lax.rsqrt(jnp.mean(value * value, axis=-1, keepdims=True) + norm_eps)
                normed_one[slot, at] = (value * factor * gain_one).astype(BF16)

            by_rows(block, norm)
            cosine, sine = cosines[to], sines[to]
            raw = product(normed_one[slot], qkv[...])
            for first in range(0, queries_wide, wide):
                value = raw[:, first : first + wide]
                turned[slot, :, pl.ds(first, wide)] = (value * cosine + partner(value) * sine).astype(BF16)
            value = raw[:, queries_wide:]
            is_key = lanes(value.shape) < HEAD_DIM
            turned[slot, :, pl.ds(queries_wide, wide)] = jnp.where(
                is_key, value * cosine + partner(value) * sine, value
            ).astype(BF16)
            which = place_of(i)
            row = seg_pair[which // per, pl.ds(lax.rem(which, per), 1)]
            attention_block(turned.at[slot], context.at[slot], queries_wide, row)
            for copy in stores(i, slot):
                copy.start()
            return slot

        def other(i):
            slot = one_block(i)
            attended[slot] = times_transposed(context[slot], o[...]).astype(BF16)
            store_term(i, slot).start()

        def own(i):
            slot = one_block(per + i)
            half[pl.ds(pl.multiple_of(i * block, block), block)] = times_transposed(
                context[slot], o[...]
            ).astype(BF16)

        loop(per, other)
        for i in range(per):
            store_term(i, i % 2).wait()
        total.core().start()
        loop(per, own)
        for i in range(blocks - 2, blocks):
            for copy in stores(i, i % 2):
                copy.wait()

    pl.run_scoped(
        attention,
        pltpu.VMEM(qkv_all.shape, BF16),
        pltpu.VMEM(o_all.shape, BF16),
        pltpu.VMEM((2, block, width), BF16),
        pltpu.VMEM((2, block, width), BF16),
        pltpu.VMEM((2, block, qkv_all.shape[1]), BF16),
        pltpu.VMEM((2, block, o_all.shape[1]), BF16),
        pltpu.VMEM((2, block, width), BF16),
    )
    total.meet(False)
    for j in (3, 4):
        work.relay(1, [j])
        work.relay(2, [j])
    work.relays(3, [3])

    def sums(mid):
        total.pair().wait_recv()

        def body(at):
            value = tokens[at].astype(F32) + total.rows(at)
            mid[at] = value
            factor = lax.rsqrt(jnp.mean(value * value, axis=-1, keepdims=True) + norm_eps)
            normed[c, at] = (value * factor * gain).astype(BF16)

        by_rows(count, body)
        save = pltpu.make_async_copy(mid, mid_out, out_sems.at[0])
        save.start()
        for copy in share(here, normed.at[c], normed, pair_sems)[1:]:
            copy.start()
        save.wait()

    def hidden(first, second, silu, slope, upward, up_grad, inputs, result, stages, back_stage):
        def fetch_grads(i, slot):
            return pltpu.make_async_copy(
                chip_grads.at[i // per, pl.ds(pl.multiple_of(lax.rem(i, per) * block, block), block)],
                inputs.at[slot],
                grad_sems.at[slot],
            )

        def at_block(i):
            return pl.ds(pl.multiple_of(i * block, block), block)

        fetch_grads(0, 0).start()
        pl.run_scoped(sums, pltpu.VMEM((count, width), F32))
        work.relays(3, [4])
        work.start_early([5])
        work.arrived(3)
        load = pltpu.make_async_copy(down_all, first, load_sems.at[0])
        load.start()
        load.wait()

        def hidden_block(i):
            slot = lax.rem(i, 2)
            fetch_grads(i, slot).wait()

            @pl.when(i + 1 < blocks)
            def _():
                fetch_grads(i + 1, 1 - slot).start()

            slope[at_block(i)] = product(inputs[slot], first[...])

        loop(blocks, hidden_block)
        work.relay(1, [5])
        work.relay(2, [5])
        upward[...] = jnp.zeros_like(upward)
        work.arrived(4)
        load = pltpu.make_async_copy(gate_all, second, load_sems.at[1])
        load.start()
        share(here, normed.at[c], normed, pair_sems)[1].wait()
        save = pltpu.make_async_copy(normed, normed_out, out_sems.at[1])
        save.start()
        load.wait()

        def gate_block(i):
            result[...] = product(normed[i // per, at_block(lax.rem(i, per))], second[...])

            def body(at):
                to = pl.ds(pl.multiple_of(i * block + at.start, 16), at.size)
                gated = result[at]
                grad = slope[to]
                sigmoid = 1.0 / (1.0 + jnp.exp(-gated))
                silu[to] = gated * sigmoid
                up_grad[to] = (grad * gated * sigmoid).astype(BF16)
                slope[to] = grad * (sigmoid * (1.0 + gated * (1.0 - sigmoid)))

            by_rows(block, body)

        loop(blocks, gate_block)
        save_up = pltpu.make_async_copy(up_grad, up_grad_out, out_sems.at[2])
        save_up.start()
        work.relays(3, [5])
        group = width // zn

        def up_rows(k):
            o = farthest_first(zn, z, zn - 1 - k)
            at = pl.ds(pl.multiple_of(o * group, group), group)
            work.x_late(5, o).wait_recv()
            load = pltpu.make_async_copy(up_all.at[at], first.at[at], load_sems.at[0])
            load.start()
            load.wait()

            def up_part(i):
                rows = normed[i // per, at_block(lax.rem(i, per)), at]
                upward[at_block(i)] += product(rows, first[at])

            loop(blocks, up_part)

        loop(zn, up_rows)

        def stores(i, slot):
            to = at_block(i)
            return (
                pltpu.make_async_copy(stages.at[slot, 0], act_out.at[to], stage_sems.at[slot, 0]),
                pltpu.make_async_copy(stages.at[slot, 1], gate_grad_out.at[to], stage_sems.at[slot, 1]),
                pltpu.make_async_copy(
                    back_stage.at[slot], back_out.at[i // per, at_block(lax.rem(i, per))], stage_sems.at[slot, 2]
                ),
            )

        def up_block(i):
            slot = lax.rem(i, 2)

            @pl.when(i > 1)
            def _():
                for copy in stores(i - 2, slot):
                    copy.wait()

            def body(at):
                to = pl.ds(pl.multiple_of(i * block + at.start, 16), at.size)
                stages[slot, 0, at] = (silu[to] * upward[to]).astype(BF16)
                stages[slot, 1, at] = (slope[to] * upward[to]).astype(BF16)

            by_rows(block, body)
            value = times_transposed(stages[slot, 1], second[...]) + times_transposed(
                up_grad[at_block(i)], first[...]
            )
            back_stage[slot] = value.astype(BF16)
            for copy in stores(i, slot):
                copy.start()

        loop(blocks, up_block)
        for i in range(max(blocks - 2, 0), blocks):
            for copy in stores(i, i % 2):
                copy.wait()
        save.wait()
        save_up.wait()

    pl.run_scoped(
        hidden,
        pltpu.VMEM((width, columns), BF16),
        pltpu.VMEM((width, columns), BF16),
        pltpu.VMEM((2 * count, columns), F32),
        pltpu.VMEM((2 * count, columns), F32),
        pltpu.VMEM((2 * count, columns), F32),
        pltpu.VMEM((2 * count, columns), BF16),
        pltpu.VMEM((2, block, width), BF16),
        pltpu.VMEM((block, columns), F32),
        pltpu.VMEM((2, 2, block, columns), BF16),
        pltpu.VMEM((2, block, width), BF16),
    )
    work.finish()
    total.finish()
    for copy in saves:
        copy.wait()


def fetch(pairs, sems):
    copies = [pltpu.make_async_copy(src, dst, sems.at[i]) for i, (src, dst) in enumerate(pairs)]
    for copy in copies:
        copy.start()
    return copies


def backward(zn, early, *refs):
    normed_two, gate_grad, chip_grads, activated, back_term, down_all, mid_in, up_grad, normed_one, context = refs[:10]
    turned_all, o_all, qkv_all, cosines, sines, tokens_in, rows_of, gain_rows = refs[10:18]
    down_out, gate_out, up_out, o_out, q_out, kv_out, out, in_grad, gain_out = refs[18:27]
    mid_grad_all, branch_all, qkv_back, in_term, out_term, down, gate, up, o_sums, qkv_sums = refs[27:37]
    n = SCATTER_BUFFERS
    buffers, refs = refs[37 : 37 + 4 * n], refs[37 + 4 * n :]
    back_refs, front_refs, in_refs = refs[:4], refs[4:8], refs[8:11]
    gain_refs, (one_sum, two_sum), refs = refs[11:15], refs[15:17], refs[17:]
    fetch_sems, out_sems, pair_sems, weight_sems, stage_sems, block_sems, back_sems, credit = refs[:8]
    here = place()
    z, c = here[2], here[4]
    chip, width = chip_grads.shape
    count = chip // 2
    block = rows_of.shape[2]
    blocks = chip // block
    per = blocks // 2
    qkv_wide, q_half = qkv_all.shape[1], o_all.shape[1]
    enter(zn, here)
    branch, out_rows, in_rows = back_refs[0], front_refs[0], in_refs[0]
    back = Total(here, back_term, *back_refs)
    front = Total(here, out_term, *front_refs)
    total = Total(here, in_term, in_refs[0], back_refs[1], in_refs[1], in_refs[2])
    gains = Gains(zn, here, *gain_refs)
    work = Scatter(
        zn,
        here,
        early,
        [
            (down, buffers[:n], [(down_out, False, 0, down_out.shape[1] // 2)]),
            (gate, buffers[n : 2 * n], [(gate_out, False, 0, gate_out.shape[1] // 2)]),
            (up, buffers[:n], [(up_out, False, 0, up_out.shape[1] // 2)]),
            (o_sums, buffers[2 * n : 3 * n], [(o_out, False, 0, q_half)]),
            (
                qkv_sums,
                buffers[3 * n :],
                [(q_out, False, 0, q_half), (kv_out, True, q_half, kv_out.shape[2])],
            ),
        ],
        refs[8:],
    )
    back.start()

    def out_terms(right_one, weights, stages):
        block = weights.shape[1]

        def fetch_weights(i, slot):
            return pltpu.make_async_copy(
                down_all.at[pl.ds(pl.multiple_of(i * block, block), block)], weights.at[slot], weight_sems.at[slot]
            )

        def stores(i, slot):
            to = pl.ds(pl.multiple_of(i * block, block), block)
            return [
                pltpu.make_async_copy(
                    stages.at[slot, pl.ds(half * (chip // 2), chip // 2)],
                    out_term.at[half, :, to],
                    stage_sems.at[slot, half],
                )
                for half in range(2)
            ]

        fetch_weights(0, 0).start()

        def step(i):
            slot = lax.rem(i, 2)
            fetch_weights(i, slot).wait()

            @pl.when(i + 1 < width // block)
            def _():
                fetch_weights(i + 1, 1 - slot).start()

            @pl.when(i > 1)
            def _():
                for copy in stores(i - 2, slot):
                    copy.wait()

            stages[slot] = times_transposed(right_one[...], weights[slot]).astype(BF16)
            for copy in stores(i, slot):
                copy.start()

        loop(width // block, step)
        for i in range(width // block - 2, width // block):
            for copy in stores(i, i % 2):
                copy.wait()

    def first_terms(left, right, stage, weights, stages):
        for load in fetch(((chip_grads, left), (activated, right)), fetch_sems):
            load.wait()
        work.make(0, left, right, stage, back.meet)
        load = fetch(((normed_two, left),), fetch_sems)[0]
        for g in range(3):
            work.early_third(0, g)
        work.late_third(0, 0)
        out_terms(right, weights, stages)
        front.start()
        load_right = pltpu.make_async_copy(gate_grad, right, fetch_sems.at[1])
        load_right.start()
        work.early_home(0)
        work.late_third(0, 1)
        work.late_third(0, 2)
        load.wait()
        load_right.wait()
        work.make(1, left, right, stage)

    wide = down.shape[2]
    operands = [pltpu.VMEM((chip, width), BF16), pltpu.VMEM((chip, wide), BF16), pltpu.VMEM((2,) + down.shape[1:], BF16)]
    pl.run_scoped(
        first_terms, *operands, pltpu.VMEM((2, 256, wide), BF16), pltpu.VMEM((2, chip, 256), BF16)
    )
    work.early_third(1, 0)
    work.early_third(1, 1)

    def sums(mid, mid_grad, grads):
        for load in fetch(
            (
                (mid_in, mid),
                (chip_grads.at[pl.ds(pl.multiple_of(c * count, 16), count)], grads),
            ),
            fetch_sems,
        ):
            load.wait()
        gain = gain_rows[pl.ds(1, 1)]
        two_sum[...] = jnp.zeros_like(two_sum)

        def body_gain(at):
            value = mid[at]
            factor = lax.rsqrt(jnp.mean(value * value, axis=-1, keepdims=True) + norm_eps)
            two_sum[...] += jnp.sum(back.half[at].astype(F32) * (value * factor), axis=0, keepdims=True)

        by_rows(count, body_gain)
        back.pair().wait_recv()

        def body(at):
            value = mid[at]
            factor = lax.rsqrt(jnp.mean(value * value, axis=-1, keepdims=True) + norm_eps)
            scaled = back.rows(at) * gain
            result = (
                grads[at].astype(F32)
                + factor * scaled
                - value * (factor * factor * factor) * jnp.mean(scaled * value, axis=-1, keepdims=True)
            )
            mid_grad[at] = result
            branch[at] = result.astype(BF16)

        by_rows(count, body)
        save = pltpu.make_async_copy(mid_grad, mid_grad_all, out_sems.at[0])
        save.start()
        for copy in share(here, branch, branch_all, pair_sems):
            copy.start()
        work.early_third(1, 2)
        save.wait()

    pl.run_scoped(
        sums, pltpu.VMEM((count, width), F32), pltpu.VMEM((count, width), F32), pltpu.VMEM((count, width), BF16)
    )
    work.home(0)
    work.late_third(1, 0)
    work.done(0)
    work.lend(credit)

    def middle_terms(left, right, stage):
        for copy in share(here, branch, branch_all, pair_sems):
            copy.wait()
        right_o = right.at[:, pl.ds(0, q_half)]
        loads = fetch(
            ((branch_all.at[0], left.at[pl.ds(0, count)]), (branch_all.at[1], left.at[pl.ds(count, count)])),
            fetch_sems,
        )
        loads.append(pltpu.make_async_copy(context, right_o, fetch_sems.at[2]))
        loads[2].start()
        for load in loads:
            load.wait()
        work.make(3, left, right_o, stage)
        loads = fetch(((normed_two, left), (up_grad, right)), fetch_sems)
        front.meet()
        work.late_third(1, 1)
        for load in loads:
            load.wait()
        work.borrow(credit)
        work.make(2, left, right, stage)

    pl.run_scoped(middle_terms, *operands)
    work.early_third(2, 0)
    work.late_third(1, 2)

    def attention(o, qkv, inputs, turned, grads, backs, terms_out, cosine, sine, accumulators):
        def which(i):
            return lax.rem((1 - c) * per + i, blocks)

        def rows_at(i):
            return pl.ds(pl.multiple_of(i * block, block), block)

        def fetches(i, slot):
            b = which(i)
            sources = (
                (branch_all.at[b // per, rows_at(lax.rem(b, per))], inputs),
                (turned_all.at[rows_at(b)], turned),
                (cosines.at[rows_at(b)], cosine),
                (sines.at[rows_at(b)], sine),
            )
            return [
                pltpu.make_async_copy(source, buffer.at[slot], block_sems.at[slot, k])
                for k, (source, buffer) in enumerate(sources)
            ]

        def stores(i, slot):
            b = which(i)
            return [
                pltpu.make_async_copy(backs.at[slot], qkv_back.at[rows_at(b)], back_sems.at[slot, 0]),
                pltpu.make_async_copy(
                    terms_out.at[slot], in_term.at[b // per, rows_at(lax.rem(b, per))], back_sems.at[slot, 1]
                ),
            ]

        loads = fetch(((o_all, o), (qkv_all, qkv)), fetch_sems)
        for copy in fetches(0, 0):
            copy.start()
        for load in loads:
            load.wait()

        def step(i):
            slot = lax.rem(i, 2)

            @pl.when(i == per)
            def _():
                for done in range(per):
                    for copy in stores(done, done % 2):
                        copy.wait()
                total.core().start()
                work.early_home(1)
                work.early_third(3, 0)
                work.late_third(3, 0)
                work.early_third(2, 1)

            @pl.when(i == blocks - 1)
            def _():
                work.early_third(2, 2)
                work.early_third(3, 1)

            for copy in fetches(i, slot):
                copy.wait()

            @pl.when(i + 1 < blocks)
            def _():
                for copy in fetches(i + 1, 1 - slot):
                    copy.start()

            grads[...] = product(inputs[slot], o[...]).astype(BF16)
            attention_block_back(
                turned.at[slot],
                grads,
                backs.at[slot],
                accumulators,
                q_half,
                rows_of[which(i)],
                cosine[slot],
                sine[slot],
            )
            terms_out[slot] = times_transposed(backs[slot], qkv[...]).astype(BF16)
            for copy in stores(i, slot):
                copy.start()

        loop(blocks, step)
        for i in range(per, blocks):
            for copy in stores(i, i % 2):
                copy.wait()

    pl.run_scoped(
        attention,
        pltpu.VMEM(o_all.shape, BF16),
        pltpu.VMEM(qkv_all.shape, BF16),
        pltpu.VMEM((2, block, width), BF16),
        pltpu.VMEM((2, block, qkv_wide), BF16),
        pltpu.VMEM((block, q_half), BF16),
        pltpu.VMEM((2, block, qkv_wide), BF16),
        pltpu.VMEM((2, block, width), BF16),
        pltpu.VMEM((2, block, 2 * HEAD_DIM), F32),
        pltpu.VMEM((2, block, 2 * HEAD_DIM), F32),
        pltpu.VMEM((4, block, 2 * HEAD_DIM), F32),
    )
    back.finish()
    total.load().start()

    def meeting(tokens):
        load = fetch(((tokens_in, tokens),), fetch_sems)[0]
        work.late_third(3, 1)
        total.meet(send=False)
        load.wait()
        one_sum[...] = jnp.zeros_like(one_sum)

        def body_gain(at):
            value = tokens[at].astype(F32)
            factor = lax.rsqrt(jnp.mean(value * value, axis=-1, keepdims=True) + norm_eps)
            one_sum[...] += jnp.sum(total.half[at].astype(F32) * (value * factor), axis=0, keepdims=True)

        by_rows(count, body_gain)

    pl.run_scoped(meeting, pltpu.VMEM((count, width), BF16))
    gains.start([one_sum, two_sum])
    gains.swapped(0)
    total.pair().start()
    work.late_third(3, 2)
    work.late_third(2, 0)

    def last_terms(left, right, stage):
        right_qkv = right.at[:, pl.ds(0, qkv_wide)]
        for load in fetch(((normed_one, left), (qkv_back, right_qkv)), fetch_sems):
            load.wait()
        gains.swapped(1)
        work.make(4, left, right_qkv, stage)

    pl.run_scoped(last_terms, *operands)
    work.early_third(4, 0)
    work.early_third(4, 1)
    work.late_third(2, 1)
    work.early_third(3, 2)
    work.late_third(2, 2)

    def output(mid):
        load = fetch(((mid_in, mid),), fetch_sems)[0]
        front.pair().wait_recv()
        load.wait()

        def body_out(at):
            out_rows[at] = (mid[at] + front.rows(at)).astype(BF16)

        by_rows(count, body_out)

    pl.run_scoped(output, pltpu.VMEM((count, width), F32))
    save_out = pltpu.make_async_copy(out_rows, out, out_sems.at[1])
    save_out.start()
    work.home(1)
    work.early_home(2)
    work.early_home(3)
    work.early_third(4, 2)
    work.late_third(4, 0)
    gains.swapped(2)
    gains.run()

    def inputs_back(mid_grad, tokens):
        loads = fetch(((mid_grad_all, mid_grad), (tokens_in, tokens)), fetch_sems)
        gain = gain_rows[pl.ds(0, 1)]
        total.pair().wait_recv()
        for load in loads:
            load.wait()

        def body(at):
            value = tokens[at].astype(F32)
            factor = lax.rsqrt(jnp.mean(value * value, axis=-1, keepdims=True) + norm_eps)
            scaled = total.rows(at) * gain
            in_rows[at] = (
                mid_grad[at]
                + factor * scaled
                - value * (factor * factor * factor) * jnp.mean(scaled * value, axis=-1, keepdims=True)
            ).astype(BF16)

        by_rows(count, body)

    pl.run_scoped(inputs_back, pltpu.VMEM((count, width), F32), pltpu.VMEM((count, width), BF16))
    save_in = pltpu.make_async_copy(in_rows, in_grad, out_sems.at[0])
    save_in.start()
    work.late_third(4, 1)
    work.late_third(4, 2)
    work.early_home(4)
    gains.finish(gain_out)
    for j in (2, 3, 4):
        work.home(j)
    for j in (1, 2, 3, 4):
        work.done(j)
    front.finish()
    total.finish()
    save_out.wait()
    save_in.wait()


def call(kernel, name, collective_id, operands, specs, outs, out_specs, scratch, order=None):
    results = pl.pallas_call(
        kernel,
        out_shape=[jax.ShapeDtypeStruct(shape, dtype) for shape, dtype in outs],
        in_specs=specs,
        out_specs=out_specs,
        scratch_shapes=scratch,
        name=name,
        compiler_params=pltpu.CompilerParams(
            collective_id=collective_id, has_side_effects=True, vmem_limit_bytes=63 << 20
        ),
    )(*operands)
    return results if order is None else [results[i] for i in order]


def rotate(vectors, cosine, sine_rows):
    half = vectors.shape[-1] // 2
    first, second = vectors[..., :half], vectors[..., half:]
    return jnp.concatenate(
        [first * cosine - second * sine_rows, second * cosine + first * sine_rows], axis=-1
    )


def product(one, two):
    return jnp.dot(one, two, preferred_element_type=F32)


def times_transposed(one, two):
    return lax.dot_general(one, two, (((1,), (1,)), ((), ())), preferred_element_type=F32)


def inner_rows(one, two):
    return lax.dot_general(one, two, (((0,), (0,)), ((), ())), preferred_element_type=F32)


def einsum(form, one, two):
    return jnp.einsum(form, one, two, preferred_element_type=F32)


def halves(weight):
    rows, columns = weight.shape
    return weight.reshape(rows, 2, columns // 2).transpose(1, 0, 2)


def joined(pair):
    return jnp.concatenate([pair[0], pair[1]], axis=1)


def local(
    dp,
    tokens,
    seg_ids,
    q_weight,
    k_weight,
    v_weight,
    o_weight,
    attn_gain,
    gate_weight,
    up_weight,
    down_weight,
    mlp_gain,
    out_grad,
):
    zn = dp // 4
    units = zn * 2
    count, width = tokens.shape
    rows = q_weight.shape[0]
    blocks, block_rows = 2 * seg_ids.shape[0], seg_ids.shape[1]
    q_half, kv_half = q_weight.shape[1] // 2, k_weight.shape[1] // 2
    ff_half = gate_weight.shape[1] // 2
    qkv_half = q_half + 2 * kv_half
    heads, groups = q_half // HEAD_DIM, kv_half // HEAD_DIM
    early = 2 * rows // 48 * 8
    early_sums = max(16, 2 * rows // 128 * 16)

    chip = 2 * count
    inverse = 1.0 / 10000.0 ** (np.arange(0, HEAD_DIM, 2, dtype=np.float32) / HEAD_DIM)
    inverse = np.tile(inverse.astype(np.float32), 4)[None]
    sign = np.tile(np.repeat(np.array([-1.0, 1.0], np.float32), HEAD_DIM // 2), 2)[None]
    (
        qkv_full,
        o_full,
        grads_chip,
        segment,
        down_full,
        mid,
        normed_two,
        activated,
        gate_grad,
        up_grad,
        back_term,
        normed,
        turned,
        context,
        cosines,
        sines,
        gain_rows,
    ) = call(
        functools.partial(forward, zn, early),
        "forward",
        0,
        (
            q_weight,
            k_weight,
            v_weight,
            o_weight,
            jnp.stack([attn_gain, mlp_gain]),
            tokens,
            out_grad,
            seg_ids,
            gate_weight,
            up_weight,
            down_weight,
            inverse,
            sign,
        ),
        [VMEM] * 5 + [ANY] * 2 + [VMEM] + [ANY] * 3 + [VMEM] * 2,
        [
            ((width, qkv_half), BF16),
            ((width, q_half), BF16),
            ((units * 16, 128), F32),
            ((2, count, width), BF16),
            ((2, count, width), BF16),
            ((2,) + seg_ids.shape, jnp.int32),
        ]
        + [((width, ff_half), BF16)] * 3
        + [((count, width), F32), ((2, count, width), BF16)]
        + [((chip, ff_half), BF16)] * 3
        + [((2, count, width), BF16)] * 2
        + [((chip, width), BF16), ((chip, qkv_half), BF16), ((chip, q_half), BF16)]
        + [((chip, 2 * HEAD_DIM), F32)] * 2
        + [((8, width), F32)],
        [ANY] * 22,
        total_buffers(count, width)
        + [
            pltpu.VMEM((2, count, width), BF16),
            DMA((3,)),
            DMA((3,)),
            DMA((2,)),
            DMA((2,)),
            DMA((2, 3)),
            DMA((2,)),
            pltpu.VMEM((chip, 2 * HEAD_DIM), F32),
            pltpu.VMEM((chip, 2 * HEAD_DIM), F32),
            pltpu.VMEM((2,) + seg_ids.shape, jnp.int32),
            pltpu.VMEM((units * 16, 128), F32),
            pltpu.VMEM((8, width), F32),
            DMA((2, 3)),
            DMA((5,)),
            pltpu.VMEM((2, rows, 2 * kv_half), BF16),
            pltpu.VMEM((2, 8, 128), F32),
            pltpu.VMEM((rows, 2 * q_half), BF16),
            pltpu.VMEM((rows, 2 * ff_half), BF16),
            pltpu.VMEM((count, width), BF16),
            pltpu.VMEM((count, width), BF16),
            pltpu.VMEM((rows, 2 * ff_half), BF16),
            pltpu.VMEM((rows, 2 * ff_half), BF16),
            pltpu.VMEM((2 * ff_half, rows), BF16),
            DMA((5,)),
        ]
        + gather_sems(6, 7, zn),
        order=(0, 1, 4, 5, 8, 9, 10, 11, 12, 13, 14, 16, 17, 18, 19, 20, 21),
    )
    grads_chip = grads_chip.reshape(chip, width)
    segment = segment.reshape(blocks, 1, block_rows)
    normed_two = normed_two.reshape(chip, width)

    down_sum, gate_sum, up_sum, o_sum, q_sum, kv_sum, out, in_grad, gain_sums = call(
        functools.partial(backward, zn, early_sums),
        "backward",
        1,
        (
            normed_two,
            gate_grad,
            grads_chip,
            activated,
            back_term,
            down_full,
            mid,
            up_grad,
            normed,
            context,
            turned,
            o_full,
            qkv_full,
            cosines,
            sines,
            tokens,
            segment,
            gain_rows,
        ),
        [ANY] * 16 + [VMEM] * 2,
        [((rows, 2 * ff_half), F32)] * 3
        + [
            ((rows, 2 * q_half), F32),
            ((rows, 2 * q_half), F32),
            ((2, rows, 2 * kv_half), F32),
            ((count, width), BF16),
            ((count, width), BF16),
            ((8, 4 * rows), F32),
            ((count, width), F32),
            ((2, count, width), BF16),
            ((chip, qkv_half), BF16),
            ((2, count, width), BF16),
            ((2, count, width), BF16),
        ]
        + [((zn, 4 * rows, ff_half), BF16)] * 3
        + [((zn, 4 * rows, q_half), BF16), ((zn, 4 * rows, qkv_half), BF16)],
        [ANY] * 8 + [VMEM] + [ANY] * 10,
        scatter_buffers(
            [(2 * rows, ff_half), (2 * rows, ff_half), (2 * rows, q_half), (2 * rows, qkv_half)], early_sums, zn
        )
        + total_buffers(count, width) * 2
        + [pltpu.VMEM((count, width), BF16)] * 2
        + [DMA((5,))]
        + gain_buffers(zn, 4 * rows)
        + [pltpu.VMEM((1, width), F32)] * 2
        + [
            DMA((4,)),
            DMA((2,)),
            DMA((3,)),
            DMA((2,)),
            DMA((2, 2)),
            DMA((2, 4)),
            DMA((2, 2)),
            pltpu.SemaphoreType.REGULAR,
        ]
        + scatter_sems(5, 6, zn),
        order=range(9),
    )
    gain_grads = lax.dynamic_slice_in_dim(gain_sums, lax.rem(lax.axis_index("dp"), 4) * rows, rows, 1)
    return (
        out,
        in_grad,
        q_sum,
        joined(kv_sum[:, :, :kv_half]),
        joined(kv_sum[:, :, kv_half:]),
        o_sum.T,
        gain_grads[0],
        gate_sum,
        up_sum,
        down_sum.T,
        gain_grads[1],
    )


def solution(mesh):
    arguments = (
        P("dp", None),
        P("dp", None),
        P("dp", "tensor"),
        P("dp", "tensor"),
        P("dp", "tensor"),
        P("tensor", "dp"),
        P("dp"),
        P("dp", "tensor"),
        P("dp", "tensor"),
        P("tensor", "dp"),
        P("dp"),
        P("dp", None),
    )
    results = (
        P("dp", None),
        P("dp", None),
        P("dp", "tensor"),
        P("dp", "tensor"),
        P("dp", "tensor"),
        P("tensor", "dp"),
        P("dp"),
        P("dp", "tensor"),
        P("dp", "tensor"),
        P("tensor", "dp"),
        P("dp"),
    )
    return jax.shard_map(
        functools.partial(local, mesh.shape["dp"]),
        mesh=mesh,
        in_specs=arguments,
        out_specs=results,
        check_vma=False,
    )
```

```python
import functools

import jax
import jax.numpy as jnp
import numpy as np
from jax import lax
from jax.experimental import pallas as pl
from jax.experimental.pallas import tpu as pltpu
from jax.sharding import PartitionSpec as P

HEAD_DIM = 64
norm_eps = 1e-05
MESH = pl.DeviceIdType.MESH
ANY = pl.BlockSpec(memory_space=pl.ANY)
VMEM = pl.BlockSpec(memory_space=pltpu.VMEM)
DMA = pltpu.SemaphoreType.DMA
F32 = jnp.float32
BF16 = jnp.bfloat16


def place():
    d = lax.axis_index("dp")
    t = lax.axis_index("tensor")
    return d, t, d // 4, lax.rem(d // 2, 2), lax.rem(d, 2)


def enter(zn, here):
    d, t, z, x, c = here
    bar = pltpu.get_barrier_semaphore()

    def hail(device):
        pl.semaphore_signal(bar, inc=1, device_id=device, device_id_type=MESH)

    hail((d + 1 - 2 * c, t))
    hail((d + 2 - 4 * x, t))
    hail((d, 1 - t))

    @pl.when(z > 0)
    def _():
        hail((d - 4, t))

    @pl.when(z < zn - 1)
    def _():
        hail((d + 4, t))

    pl.semaphore_wait(bar, 5 - (z == 0).astype(jnp.int32) - (z == zn - 1).astype(jnp.int32))


def farthest_first(zn, z, i):
    up = 1 - (2 * z) // zn
    longer = up * (zn - 1 - z) + (1 - up) * z
    shorter = zn - 1 - longer
    rest = i - (longer - shorter)
    return jnp.where(
        rest < 0,
        z + (2 * up - 1) * (longer - i),
        z + (1 - 2 * lax.rem(jnp.maximum(rest, 0), 2)) * (shorter - jnp.maximum(rest, 0) // 2),
    )


def loop(count, body):
    def step(i, carry):
        body(i)
        return carry

    lax.fori_loop(0, count, step, 0)


def remote(src, dst, send, recv, device):
    return pltpu.make_async_remote_copy(
        src_ref=src, dst_ref=dst, send_sem=send, recv_sem=recv, device_id=device, device_id_type=MESH
    )


def by_rows(count, body, block=16):
    def step(i, carry):
        body(pl.ds(pl.multiple_of(i * block, block), block))
        return carry

    lax.fori_loop(0, count // block, step, 0)


def gather_sems(n, sources, zn):
    return [
        DMA((sources,)),
        DMA((sources,)),
        DMA((sources,)),
        DMA((n, zn)),
        DMA((n, zn)),
        DMA((n,)),
        DMA((n,)),
        DMA((n, 2, zn)),
        DMA((n, zn)),
        DMA((n, 2, zn)),
        DMA((n, zn)),
    ]


def part(ref, core, paired):
    if paired:
        return ref.at[core]
    columns = ref.shape[1] // 2
    return ref.at[:, pl.ds(pl.multiple_of(core * columns, columns), columns)]


class Gather:
    def __init__(self, zn, here, arrays, sems):
        self.zn, self.here = zn, here
        self.full = [full for _, full, _ in arrays]
        self.early = [early for _, _, early in arrays]
        self.sources = [
            (j, i) + source for j, (sources, _, _) in enumerate(arrays) for i, source in enumerate(sources)
        ]
        (
            self.loc,
            self.cs,
            self.cr,
            self.xs,
            self.xr,
            self.es,
            self.er,
            self.zs,
            self.zr,
            self.bs,
            self.br,
        ) = sems

    def unit(self, j, unit, first, count):
        rows = self.full[j].shape[0] // (2 * self.zn)
        return pl.ds(pl.multiple_of(unit * rows + first, 8), count)

    def rows(self, j, unit, early):
        rows = self.full[j].shape[0] // (2 * self.zn)
        late = rows - self.early[j]
        first, count = {None: (0, rows), True: (late, rows - late), False: (0, late)}[early]
        return self.full[j].at[self.unit(j, unit, first, count)]

    def mine(self, s):
        d, t, z, x, c = self.here
        j, _, shard, paired, first, columns = self.sources[s]
        rows = self.full[j].shape[0] // (4 * self.zn)
        return self.full[j].at[self.unit(j, z * 2 + x, c * rows, rows), pl.ds(first, columns)]

    def keep(self, s):
        _, _, shard, paired, _, _ = self.sources[s]
        return pltpu.make_async_copy(part(shard, self.here[4], paired), self.mine(s), self.loc.at[s])

    def give(self, s):
        d, t, z, x, c = self.here
        _, _, shard, paired, _, _ = self.sources[s]
        return remote(
            part(shard, 1 - c, paired), self.mine(s), self.cs.at[s], self.cr.at[s], (d + 1 - 2 * c, t)
        )

    def x_late(self, j, o):
        d, t, z, x, c = self.here
        ref = self.rows(j, o * 2 + x, False)
        return remote(ref, ref, self.xs.at[j, o], self.xr.at[j, o], (d + 2 - 4 * x, t))

    def x_early(self, j):
        d, t, z, x, c = self.here
        ref = self.rows(j, z * 2 + x, True)
        return remote(ref, ref, self.es.at[j], self.er.at[j], (d + 2 - 4 * x, t))

    def along(self, j, o, down):
        d, t, z, x, c = self.here
        ref = self.rows(j, o * 2 + x, None)
        return remote(ref, ref, self.zs.at[j, down, o], self.zr.at[j, o], (d + 4 - 8 * down, t))

    def along_early(self, j, o, down):
        d, t, z, x, c = self.here
        ref = self.rows(j, o * 2 + 1 - x, True)
        return remote(ref, ref, self.bs.at[j, down, o], self.br.at[j, o], (d + 4 - 8 * down, t))

    def start(self, arrays):
        for s, source in enumerate(self.sources):
            if source[0] in arrays:
                self.give(s).start()
                self.keep(s).start()

    def ready(self, arrays):
        for j in arrays:
            for s, source in enumerate(self.sources):
                if source[0] == j:
                    self.keep(s).wait()
                    self.give(s).wait_recv()
            if self.early[j]:
                self.x_early(j).start()

    def start_own(self, arrays):
        z, zn = self.here[2], self.zn
        for j in arrays:
            self.x_late(j, z).start()

            @pl.when(z < zn - 1)
            def _():
                self.along(j, z, 0).start()

            @pl.when(z > 0)
            def _():
                self.along(j, z, 1).start()

    def start_early(self, arrays):
        z, zn = self.here[2], self.zn
        for j in arrays:
            if self.early[j]:
                self.x_early(j).wait_recv()

                @pl.when(z < zn - 1)
                def _():
                    self.along_early(j, z, 0).start()

                @pl.when(z > 0)
                def _():
                    self.along_early(j, z, 1).start()

    def relay(self, k, arrays):
        z, zn = self.here[2], self.zn
        o = farthest_first(zn, z, zn - 1 - k)
        down = (o > z).astype(jnp.int32)
        more = ((o < z) & (z < zn - 1)) | ((o > z) & (z > 0))
        for j in arrays:
            self.along(j, o, down).wait_recv()

            @pl.when(more)
            def _():
                self.along(j, o, down).start()

            self.x_late(j, o).start()
            if self.early[j]:
                self.along_early(j, o, down).wait_recv()

                @pl.when(more)
                def _():
                    self.along_early(j, o, down).start()

    def relays(self, first, arrays):
        loop(max(self.zn - first, 0), lambda i: self.relay(first + i, arrays))

    def arrived(self, j):
        loop(self.zn, lambda o: self.x_late(j, o).wait_recv())

    def finish(self):
        z, zn = self.here[2], self.zn
        for s in range(len(self.sources)):
            self.give(s).wait_send()
        for j in range(len(self.full)):
            if self.early[j]:
                self.x_early(j).wait_send()

            def step(o, j=j):
                self.x_late(j, o).wait_send()

                def sent(down):
                    self.along(j, o, down).wait_send()
                    if self.early[j]:
                        self.along_early(j, o, down).wait_send()

                @pl.when((o <= z) & (z < zn - 1))
                def _():
                    sent(0)

                @pl.when((o >= z) & (z > 0))
                def _():
                    sent(1)

            loop(zn, step)


def scatter_sems(n, outs, zn):
    return [
        DMA((n, zn)),
        DMA((n, zn)),
        DMA((n, zn)),
        DMA((n, zn)),
        DMA((n, zn)),
        DMA((n, zn + 1)),
        DMA((n, 2, zn)),
        DMA((n, zn)),
        DMA((n, zn + 1)),
        DMA((n,)),
        DMA((n,)),
        DMA((outs,)),
        DMA((outs,)),
        DMA((outs,)),
    ]


def scatter_buffers(shapes, early, zn):
    out = []
    for rows, columns in shapes:
        late = rows - early
        out += [
            pltpu.VMEM((zn, late, columns), BF16),
            pltpu.VMEM((zn, late, columns), BF16),
            pltpu.VMEM((zn + 1, late, columns), BF16),
            pltpu.VMEM((zn, 2, early, columns), BF16),
            pltpu.VMEM((zn + 1, 2, early, columns), BF16),
            pltpu.VMEM((early, columns), BF16),
            pltpu.VMEM((rows, columns), F32),
        ]
    return out


SCATTER_BUFFERS = 7


class Scatter:
    def __init__(self, zn, here, early, arrays, sems):
        self.zn, self.here, self.early = zn, here, early
        self.term = [term for term, _, _ in arrays]
        self.buffers = [buffers for _, buffers, _ in arrays]
        self.results = [(j,) + result for j, (_, _, results) in enumerate(arrays) for result in results]
        (
            self.st,
            self.ls,
            self.xs,
            self.xr,
            self.zs,
            self.zr,
            self.bls,
            self.bs,
            self.br,
            self.es,
            self.er,
            self.cs,
            self.cr,
            self.loc,
        ) = sems

    def unit(self, j, o, x, first, count):
        rows = self.term[j].shape[1] // 2
        return self.term[j].at[o, pl.ds(pl.multiple_of(x * rows + first, 16), count)]

    def late(self, j):
        return self.buffers[j][0].shape[1]

    def load(self, j, o):
        return pltpu.make_async_copy(
            self.unit(j, o, self.here[3], 0, self.late(j)), self.buffers[j][0].at[o], self.ls.at[j, o]
        )

    def load_early(self, j, o, other):
        x = self.here[3]
        return pltpu.make_async_copy(
            self.unit(j, o, 1 - x if other else x, self.late(j), self.early),
            self.buffers[j][3].at[o, other],
            self.bls.at[j, other, o],
        )

    def across(self, j, o):
        d, t, z, x, c = self.here
        return remote(
            self.unit(j, o, 1 - x, 0, self.late(j)),
            self.buffers[j][1].at[o],
            self.xs.at[j, o],
            self.xr.at[j, o],
            (d + 2 - 4 * x, t),
        )

    def across_early(self, j):
        d, t, z, x, c = self.here
        return remote(
            self.buffers[j][3].at[z, 1], self.buffers[j][5], self.es.at[j], self.er.at[j], (d + 2 - 4 * x, t)
        )

    def along(self, j, o, slot, down):
        d, t, z, x, c = self.here
        own, line = self.buffers[j][0], self.buffers[j][2]
        return remote(own.at[o], line.at[slot], self.zs.at[j, o], self.zr.at[j, slot], (d + 4 - 8 * down, t))

    def along_early(self, j, o, slot, down):
        d, t, z, x, c = self.here
        own, line = self.buffers[j][3], self.buffers[j][4]
        return remote(own.at[o], line.at[slot], self.bs.at[j, o], self.br.at[j, slot], (d + 4 - 8 * down, t))

    def give(self, r):
        d, t, z, x, c = self.here
        j, out, paired, first, columns = self.results[r]
        rows = out.shape[-2]
        ref = self.buffers[j][6].at[
            pl.ds(pl.multiple_of((1 - c) * rows, rows), rows), pl.ds(first, columns)
        ]
        return remote(ref, part(out, c, paired), self.cs.at[r], self.cr.at[r], (d + 1 - 2 * c, t))

    def keep(self, r):
        c = self.here[4]
        j, out, paired, first, columns = self.results[r]
        rows = out.shape[-2]
        ref = self.buffers[j][6].at[pl.ds(pl.multiple_of(c * rows, rows), rows), pl.ds(first, columns)]
        return pltpu.make_async_copy(ref, part(out, c, paired), self.loc.at[r])

    def store(self, j, o, stage, slot):
        columns = self.term[j].shape[2]
        return pltpu.make_async_copy(
            stage.at[slot, :, pl.ds(0, columns)], self.term[j].at[o], self.st.at[j, o]
        )

    def make(self, j, left, right, stage, between=None):
        z, zn = self.here[2], self.zn
        wide, columns = self.term[j].shape[1:]
        block = min(256, wide)

        def send(i):
            o = farthest_first(zn, z, i)
            self.store(j, o, stage, lax.rem(i, 2)).wait()
            self.across(j, o).start()
            for other in range(2):
                self.load_early(j, o, other).start()
            self.load(j, o).start()

        def compute(i):
            o = farthest_first(zn, z, i)
            slot = lax.rem(i, 2)

            def body(m):
                at = pl.multiple_of(o * wide + m * block, block)
                value = inner_rows(left[:, pl.ds(at, block)], right[...])
                stage[slot, pl.ds(pl.multiple_of(m * block, block), block), pl.ds(0, columns)] = value.astype(
                    BF16
                )

            loop(wide // block, body)
            self.store(j, o, stage, slot).start()

        def both(i):
            compute(i)
            send(i - 1)

        compute(0)
        if between is not None:
            between()
        loop(zn - 1, lambda i: both(i + 1))
        send(zn - 1)

    def add(self, j, o, slots):
        own, got, line = self.buffers[j][:3]

        def body(at):
            value = own[o, at].astype(F32) + got[o, at].astype(F32)
            for slot in slots:
                value = value + line[slot, at].astype(F32)
            own[o, at] = value.astype(BF16)

        by_rows(own.shape[1], body)

    def add_early(self, j, o, slots):
        own, line = self.buffers[j][3:5]
        for other in range(2):

            def body(at):
                value = own[o, other, at].astype(F32)
                for slot in slots:
                    value = value + line[slot, other, at].astype(F32)
                own[o, other, at] = value.astype(BF16)

            by_rows(own.shape[2], body)

    def route(self, i):
        z, zn = self.here[2], self.zn
        o = farthest_first(zn, z, i)
        down = (o < z).astype(jnp.int32)
        distance = jnp.maximum((o - z) * (1 - 2 * down), 1)
        slot = o + (zn - o) * down * (1 // distance)
        inner = ((o > z) & (z > 0)) | ((o < z) & (z < zn - 1))
        return o, slot, down, inner

    def hop_early(self, j, i):
        o, slot, down, inner = self.route(i)
        for other in range(2):
            self.load_early(j, o, other).wait()

        @pl.when(inner)
        def _():
            self.along_early(j, o, o, down).wait_recv()
            self.add_early(j, o, [o])

        self.along_early(j, o, slot, down).start()

    def hop(self, j, i):
        o, slot, down, inner = self.route(i)
        self.load(j, o).wait()
        self.across(j, o).wait_recv()

        @pl.when(inner)
        def _():
            self.along(j, o, o, down).wait_recv()
            self.add(j, o, [o])

        @pl.when(jnp.logical_not(inner))
        def _():
            self.add(j, o, [])

        self.along(j, o, slot, down).start()

    def third(self, hop, j, g):
        hops = self.zn - 1
        first = g * hops // 3
        loop((g + 1) * hops // 3 - first, lambda i: hop(j, first + i))

    def early_third(self, j, g):
        self.third(self.hop_early, j, g)

    def late_third(self, j, g):
        self.third(self.hop, j, g)

    def at_home(self, action):
        z, zn = self.here[2], self.zn

        @pl.when((z > 0) & (z < zn - 1))
        def _():
            action([z, zn])

        @pl.when(z == 0)
        def _():
            action([zn])

        @pl.when(z == zn - 1)
        def _():
            action([z])

    def early_home(self, j):
        z = self.here[2]
        for other in range(2):
            self.load_early(j, z, other).wait()

        def home(slots):
            for slot in slots:
                self.along_early(j, z, slot, 0).wait_recv()
            self.add_early(j, z, slots)

        self.at_home(home)
        self.across_early(j).start()

    def home(self, j):
        z = self.here[2]
        own, got, line, early, _, other_early, total = self.buffers[j]
        late = self.late(j)
        self.load(j, z).wait()
        self.across(j, z).wait_recv()

        def last(slots):
            for slot in slots:
                self.along(j, z, slot, 0).wait_recv()

            def body(at):
                value = own[z, at].astype(F32) + got[z, at].astype(F32)
                for slot in slots:
                    value = value + line[slot, at].astype(F32)
                total[at] = value

            by_rows(late, body)

        self.at_home(last)
        self.across_early(j).wait_recv()
        for i in range(self.early // 16):
            at = pl.ds(16 * i, 16)
            total[pl.ds(late + 16 * i, 16)] = early[z, 0, at].astype(F32) + other_early[at].astype(F32)
        for r, result in enumerate(self.results):
            if result[0] == j:
                self.give(r).start()
                self.keep(r).start()

    def done(self, j):
        z = self.here[2]
        for r, result in enumerate(self.results):
            if result[0] == j:
                self.give(r).wait()
                self.keep(r).wait()
        self.across_early(j).wait_send()

        def sent(o):
            self.across(j, o).wait_send()

            @pl.when(o != z)
            def _():
                self.along(j, o, 0, 0).wait_send()
                self.along_early(j, o, 0, 0).wait_send()

        loop(self.zn, sent)

    def lend(self, credit):
        d, t, z, x, c = self.here

        def tell(device):
            pl.semaphore_signal(credit, inc=1, device_id=device, device_id_type=MESH)

        tell((d + 2 - 4 * x, t))

        @pl.when(z > 0)
        def _():
            tell((d - 4, t))

        @pl.when(z < self.zn - 1)
        def _():
            tell((d + 4, t))

    def borrow(self, credit):
        z = self.here[2]
        pl.semaphore_wait(credit, 3 - (z == 0).astype(jnp.int32) - (z == self.zn - 1).astype(jnp.int32))


class Gains:
    def __init__(self, zn, here, own, got, line, sems):
        self.zn, self.here, self.own, self.got, self.line, self.sems = zn, here, own, got, line, sems

    def swap(self, i):
        d, t, z, x, c = self.here
        device = ((d + 1 - 2 * c, t), (d, 1 - t), (d + 2 - 4 * x, t))[i]
        return remote(self.own, self.got.at[i], self.sems.at[0, i], self.sems.at[1, i], device)

    def along(self, o, slot, down):
        d, t, z, x, c = self.here
        return remote(
            self.own.at[o], self.line.at[slot], self.sems.at[2, o], self.sems.at[3, slot], (d + 4 - 8 * down, t)
        )

    def start(self, rows):
        wide = self.own.shape[2]
        for o in range(self.zn):
            for i, row in enumerate(rows):
                self.own[o, pl.ds(i, 1)] = row[:, pl.ds(o * wide, wide)]
        self.swap(0).start()

    def swapped(self, i):
        self.swap(i).wait()
        self.own[...] += self.got[i]
        if i < 2:
            self.swap(i + 1).start()

    def hop(self, o, slot, down, inner):
        @pl.when(inner)
        def _():
            self.along(o, o, down).wait_recv()
            self.own[o] += self.line[o]

        self.along(o, slot, down).start()

    def steps(self, k, nearest):
        z, zn = self.here[2], self.zn

        @pl.when(z + k < zn)
        def _():
            self.hop(z + k, z + k, 0, z > 0)

        @pl.when(z - k >= 0)
        def _():
            self.hop(z - k, zn if nearest else z - k, 1, z < zn - 1)

    def run(self):
        zn = self.zn

        def step(i, carry):
            self.steps(zn - 1 - i, False)
            return carry

        lax.fori_loop(0, zn - 2, step, 0)
        self.steps(1, True)

    def finish(self, out):
        z, zn = self.here[2], self.zn
        value = self.own[z]

        @pl.when(z > 0)
        def _():
            self.along(z, z, 0).wait_recv()
            self.own[z] += self.line[z]

        @pl.when(z < zn - 1)
        def _():
            self.along(z, zn, 1).wait_recv()
            self.own[z] += self.line[zn]

        out[...] = self.own[z]

        def step(o, carry):
            @pl.when(o != z)
            def _():
                self.along(o, 0, 0).wait_send()

            return carry

        lax.fori_loop(0, zn, step, 0)


def gain_buffers(zn, wide):
    return [
        pltpu.VMEM((zn, 8, wide), F32),
        pltpu.VMEM((3, zn, 8, wide), F32),
        pltpu.VMEM((zn + 1, 8, wide), F32),
        DMA((4, zn + 1)),
    ]


class Total:
    def __init__(self, here, term, from_core, half, from_pair, sems):
        self.here, self.term, self.from_core, self.half, self.from_pair = here, term, from_core, half, from_pair
        self.sems = sems

    def core(self):
        d, t, z, x, c = self.here
        return remote(self.term.at[1 - c], self.from_core, self.sems.at[0], self.sems.at[1], (d + 1 - 2 * c, t))

    def load(self):
        return pltpu.make_async_copy(self.term.at[self.here[4]], self.half, self.sems.at[4])

    def start(self):
        self.core().start()
        self.load().start()

    def pair(self):
        d, t, z, x, c = self.here
        return remote(self.half, self.from_pair, self.sems.at[2], self.sems.at[3], (d, 1 - t))

    def meet(self, loaded=True, send=True):
        if loaded:
            self.load().wait()
        self.core().wait_recv()

        def body(at):
            self.half[at] = (self.half[at].astype(F32) + self.from_core[at].astype(F32)).astype(BF16)

        by_rows(self.half.shape[0], body)
        if send:
            self.pair().start()

    def rows(self, at):
        return self.half[at].astype(F32) + self.from_pair[at].astype(F32)

    def finish(self):
        self.core().wait_send()
        self.pair().wait_send()


def total_buffers(tokens, width):
    return [pltpu.VMEM((tokens, width), BF16)] * 3 + [DMA((5,))]


def share(here, src, dst, sems):
    d, t, z, x, c = here
    return (
        pltpu.make_async_copy(src, dst.at[c], sems.at[0]),
        remote(src, dst.at[c], sems.at[1], sems.at[2], (d + 1 - 2 * c, t)),
    )


def lanes(shape):
    return lax.broadcasted_iota(jnp.int32, shape, 1)


def partner(value):
    half = HEAD_DIM // 2
    wide = 2 * HEAD_DIM
    lower = lax.rem(lanes(value.shape), HEAD_DIM) < half
    return jnp.where(lower, pltpu.roll(value, wide - half, 1), pltpu.roll(value, half, 1))


def same_segment(row):
    count = row.shape[1]
    wide = jnp.broadcast_to(row, (count, count))
    before = lax.broadcasted_iota(jnp.int32, wide.shape, 1) < lax.broadcasted_iota(jnp.int32, wide.shape, 0)
    return wide == wide.T, before


def allowed_in(row):
    same, before = same_segment(row)
    here = lax.broadcasted_iota(jnp.int32, same.shape, 1) == lax.broadcasted_iota(jnp.int32, same.shape, 0)
    return same & (before | here)


def softmax_of(queries, keys, allowed):
    scores = jnp.where(allowed, times_transposed(queries, keys) * HEAD_DIM ** (-0.5), -1e30)
    shifted = jnp.exp(scores - jnp.max(scores, axis=-1, keepdims=True))
    return shifted / jnp.sum(shifted, axis=-1, keepdims=True)


def key_value_pairs(pair):
    pair = pair.astype(F32)
    first = lanes(pair.shape) < HEAD_DIM
    key, value = jnp.where(first, pair, 0.0), jnp.where(first, 0.0, pair)
    return [
        part.astype(BF16)
        for part in (key, pltpu.roll(key, HEAD_DIM, 1), pltpu.roll(value, HEAD_DIM, 1), value)
    ]


def attention_block(turned, context, queries_wide, row):
    wide = 2 * HEAD_DIM
    allowed = allowed_in(row)
    key_one, key_two, value_one, value_two = key_value_pairs(turned[:, queries_wide:])

    def heads(p):
        at = pl.ds(pl.multiple_of(p * wide, wide), wide)
        queries = turned[:, at]
        one = softmax_of(queries, key_one, allowed).astype(BF16)
        two = softmax_of(queries, key_two, allowed).astype(BF16)
        context[:, at] = (product(one, value_one) + product(two, value_two)).astype(BF16)

    loop(queries_wide // wide, heads)


def attention_block_back(turned, grads, back, sums, queries_wide, row, cosine, sine):
    wide = 2 * HEAD_DIM
    scale = HEAD_DIM ** (-0.5)
    allowed = allowed_in(row)
    key_one, key_two, value_one, value_two = key_value_pairs(turned[:, queries_wide:])
    sums[...] = jnp.zeros_like(sums)

    def heads(p):
        at = pl.ds(pl.multiple_of(p * wide, wide), wide)
        queries, grad = turned[:, at], grads[:, at]
        total = None
        for i, (key, value) in enumerate(((key_one, value_one), (key_two, value_two))):
            probs = softmax_of(queries, key, allowed)
            sums[i] += inner_rows(probs.astype(BF16), grad)
            prob_grad = times_transposed(grad, value)
            delta = jnp.sum(probs * prob_grad, axis=-1, keepdims=True)
            score_grad = (probs * (prob_grad - delta)).astype(BF16)
            term = product(score_grad, key)
            total = term if total is None else total + term
            sums[2 + i] += inner_rows(score_grad, queries)
        total = total * scale
        back[:, at] = (total * cosine - partner(total) * sine).astype(BF16)

    loop(queries_wide // wide, heads)
    value_grad = pltpu.roll(sums[0], HEAD_DIM, 1) + sums[1]
    key_grad = (sums[2] + pltpu.roll(sums[3], HEAD_DIM, 1)) * scale
    turned_back = key_grad * cosine - partner(key_grad) * sine
    back[:, pl.ds(queries_wide, wide)] = jnp.where(
        lanes(value_grad.shape) < HEAD_DIM, turned_back, value_grad
    ).astype(BF16)


def transposed(src, dst):
    def body(n):
        at = pl.ds(pl.multiple_of(n * 128, 128), 128)
        dst[:, at] = src[at, :].astype(F32).T.astype(BF16)

    loop(src.shape[0] // 128, body)


def forward(zn, early, *refs):
    q, k_shard, v_shard, o_turned, gain_shards, tokens_in, grads_in, seg, gate_in, up_in, down_in, inverse, sign = refs[:13]
    refs = refs[1:]
    qkv_all, o_all, gains_all, chip_tokens, chip_grads, seg_all = refs[12:18]
    gate_all, up_all, down_all, mid_out, normed_out, act_out, gate_grad_out, up_grad_out = refs[18:26]
    term, normed_one_out, turned_out, context_out, cosines_out, sines_out, gain_out = refs[26:33]
    total_refs = refs[33:37]
    normed, out_sems, pair_sems, load_sems, grad_sems, stage_sems, block_sems = refs[37:44]
    cosines, sines, seg_pair, gain_tiles, gain_rows, swap_sems, seg_sems = refs[44:51]
    kv, gains, o_shard, down, tokens, grads, gate, up, down_turned, first_sems = refs[51:61]
    here = place()
    z, c = here[2], here[4]
    firsts = [
        pltpu.make_async_copy(src, dst, first_sems.at[n])
        for n, (src, dst) in enumerate(
            ((down_in, down_turned), (tokens_in, tokens), (gate_in, gate), (up_in, up), (grads_in, grads))
        )
    ]
    for copy in firsts:
        copy.start()
    enter(zn, here)
    keys, values = k_shard[...].astype(F32), v_shard[...].astype(F32)
    is_key = lanes(keys.shape) < HEAD_DIM
    kv[0] = jnp.where(is_key, keys, pltpu.roll(values, HEAD_DIM, 1)).astype(BF16)
    kv[1] = jnp.where(is_key, pltpu.roll(keys, HEAD_DIM, 1), values).astype(BF16)
    for i in range(2):
        gains[i] = jnp.zeros(gains.shape[1:], F32)
        gains[i, pl.ds(0, 2), pl.ds(0, gain_shards.shape[1])] = gain_shards[...].astype(F32)
    transposed(o_turned, o_shard)
    total = Total(here, term, *total_refs)
    q_half = q.shape[1] // 2
    work = Gather(
        zn,
        here,
        [
            ([(gains, True, 0, gains.shape[2])], gains_all, 0),
            ([(q, False, 0, q_half), (kv, True, q_half, kv.shape[2])], qkv_all, early),
            ([(o_shard, False, 0, o_shard.shape[1] // 2)], o_all, early),
        ]
        + [
            ([(shard, False, 0, shard.shape[1] // 2)], full, early)
            for shard, full in ((down, down_all), (gate, gate_all), (up, up_all))
        ],
        refs[61:],
    )
    count, width = tokens.shape
    columns = gate_all.shape[1]
    block = seg.shape[1]
    blocks = 2 * count // block
    per = count // block
    attention_set = [0, 1, 2]
    swap = remote(seg, seg_pair.at[c], seg_sems.at[0], seg_sems.at[1], (here[0] + 1 - 2 * c, here[1]))
    swap.start()
    seg_pair[c] = seg[...]
    work.start(attention_set)
    firsts[0].wait()
    transposed(down_turned, down)
    work.start([3])
    work.ready(attention_set)
    work.start_own(attention_set)
    for copy in firsts[1:]:
        copy.wait()
    shared = [
        share(here, src, dst, swap_sems.at[n])
        for n, (src, dst) in enumerate(((tokens, chip_tokens), (grads, chip_grads)))
    ]
    for copy in shared[0]:
        copy.start()
    work.start([4, 5])
    for copy in shared[1]:
        copy.start()
    work.start_early([1, 2])
    work.ready([3])
    work.start_own([3])
    swap.wait()
    for i in range(blocks):
        row = seg_pair[i // per, pl.ds(i % per, 1)]
        same, before = same_segment(row)
        position = jnp.sum(jnp.where(same & before, 1.0, 0.0), axis=-1, keepdims=True)
        angles = position * inverse[...]
        cosines[pl.ds(i * block, block)] = jnp.cos(angles)
        sines[pl.ds(i * block, block)] = jnp.sin(angles) * sign[...]
    saves = [
        pltpu.make_async_copy(src, dst, seg_sems.at[2 + n])
        for n, (src, dst) in enumerate(((cosines, cosines_out), (sines, sines_out), (seg_pair, seg_all)))
    ]
    for copy in saves:
        copy.start()
    work.relay(1, attention_set)
    work.relay(2, attention_set)
    work.start_early([3])
    work.relays(3, attention_set)
    work.ready([4, 5])
    work.start_own([4, 5])
    work.start_early([4])
    work.arrived(0)
    load = pltpu.make_async_copy(gains_all, gain_tiles, load_sems.at[0])
    load.start()
    load.wait()
    features = width // (4 * zn)
    for owner in range(4 * zn):
        for i in range(2):
            gain_rows[pl.ds(i, 1), pl.ds(owner * features, features)] = gain_tiles[
                pl.ds(owner * 8 + i, 1), :features
            ]
    save_gains = pltpu.make_async_copy(gain_rows, gain_out, load_sems.at[1])
    save_gains.start()
    gain_one, gain = gain_rows[pl.ds(0, 1)], gain_rows[pl.ds(1, 1)]
    for copies in shared:
        for copy in copies:
            copy.wait()
    work.arrived(1)
    work.arrived(2)
    save_gains.wait()
    half = total_refs[1]

    def attention(qkv, o, inputs, normed_one, turned, context, attended):
        queries_wide = context.shape[2]
        wide = 2 * HEAD_DIM

        def place_of(i):
            return lax.rem((1 - c) * per + i, blocks)

        def rows_at(i):
            return pl.ds(pl.multiple_of(place_of(i) * block, block), block)

        def fetch_inputs(i, slot):
            which = place_of(i)
            return pltpu.make_async_copy(
                chip_tokens.at[which // per, pl.ds(pl.multiple_of(lax.rem(which, per) * block, block), block)],
                inputs.at[slot],
                grad_sems.at[slot],
            )

        def stores(i, slot):
            return [
                pltpu.make_async_copy(buffer.at[slot], out.at[rows_at(i)], stage_sems.at[slot, n])
                for n, (buffer, out) in enumerate(
                    ((normed_one, normed_one_out), (turned, turned_out), (context, context_out))
                )
            ]

        def store_term(i, slot):
            return pltpu.make_async_copy(
                attended.at[slot],
                term.at[1 - c, pl.ds(pl.multiple_of(i * block, block), block)],
                block_sems.at[slot],
            )

        fetch_inputs(0, 0).start()
        loads = [
            pltpu.make_async_copy(qkv_all, qkv, load_sems.at[0]),
            pltpu.make_async_copy(o_all, o, load_sems.at[1]),
        ]
        for load in loads:
            load.start()
        for load in loads:
            load.wait()

        def one_block(i):
            slot = lax.rem(i, 2)
            to = rows_at(i)
            fetch_inputs(i, slot).wait()

            @pl.when(i + 1 < blocks)
            def _():
                fetch_inputs(i + 1, 1 - slot).start()

            @pl.when(i > 1)
            def _():
                for copy in stores(i - 2, slot):
                    copy.wait()

            def norm(at):
                value = inputs[slot, at].astype(F32)
                factor = lax.rsqrt(jnp.mean(value * value, axis=-1, keepdims=True) + norm_eps)
                normed_one[slot, at] = (value * factor * gain_one).astype(BF16)

            by_rows(block, norm)
            cosine, sine = cosines[to], sines[to]
            raw = product(normed_one[slot], qkv[...])
            for first in range(0, queries_wide, wide):
                value = raw[:, first : first + wide]
                turned[slot, :, pl.ds(first, wide)] = (value * cosine + partner(value) * sine).astype(BF16)
            value = raw[:, queries_wide:]
            is_key = lanes(value.shape) < HEAD_DIM
            turned[slot, :, pl.ds(queries_wide, wide)] = jnp.where(
                is_key, value * cosine + partner(value) * sine, value
            ).astype(BF16)
            which = place_of(i)
            row = seg_pair[which // per, pl.ds(lax.rem(which, per), 1)]
            attention_block(turned.at[slot], context.at[slot], queries_wide, row)
            for copy in stores(i, slot):
                copy.start()
            return slot

        def other(i):
            slot = one_block(i)
            attended[slot] = times_transposed(context[slot], o[...]).astype(BF16)
            store_term(i, slot).start()

        def own(i):
            slot = one_block(per + i)
            half[pl.ds(pl.multiple_of(i * block, block), block)] = times_transposed(
                context[slot], o[...]
            ).astype(BF16)

        loop(per, other)
        for i in range(per):
            store_term(i, i % 2).wait()
        total.core().start()
        loop(per, own)
        for i in range(blocks - 2, blocks):
            for copy in stores(i, i % 2):
                copy.wait()

    pl.run_scoped(
        attention,
        pltpu.VMEM(qkv_all.shape, BF16),
        pltpu.VMEM(o_all.shape, BF16),
        pltpu.VMEM((2, block, width), BF16),
        pltpu.VMEM((2, block, width), BF16),
        pltpu.VMEM((2, block, qkv_all.shape[1]), BF16),
        pltpu.VMEM((2, block, o_all.shape[1]), BF16),
        pltpu.VMEM((2, block, width), BF16),
    )
    total.meet(False)
    for j in (3, 4):
        work.relay(1, [j])
        work.relay(2, [j])
    work.relays(3, [3])

    def sums(mid):
        total.pair().wait_recv()

        def body(at):
            value = tokens[at].astype(F32) + total.rows(at)
            mid[at] = value
            factor = lax.rsqrt(jnp.mean(value * value, axis=-1, keepdims=True) + norm_eps)
            normed[c, at] = (value * factor * gain).astype(BF16)

        by_rows(count, body)
        save = pltpu.make_async_copy(mid, mid_out, out_sems.at[0])
        save.start()
        for copy in share(here, normed.at[c], normed, pair_sems)[1:]:
            copy.start()
        save.wait()

    def hidden(first, second, silu, slope, upward, up_grad, inputs, result, stages):
        def fetch_grads(i, slot):
            return pltpu.make_async_copy(
                chip_grads.at[i // per, pl.ds(pl.multiple_of(lax.rem(i, per) * block, block), block)],
                inputs.at[slot],
                grad_sems.at[slot],
            )

        def at_block(i):
            return pl.ds(pl.multiple_of(i * block, block), block)

        fetch_grads(0, 0).start()
        pl.run_scoped(sums, pltpu.VMEM((count, width), F32))
        work.relays(3, [4])
        work.start_early([5])
        work.arrived(3)
        load = pltpu.make_async_copy(down_all, first, load_sems.at[0])
        load.start()
        load.wait()

        def hidden_block(i):
            slot = lax.rem(i, 2)
            fetch_grads(i, slot).wait()

            @pl.when(i + 1 < blocks)
            def _():
                fetch_grads(i + 1, 1 - slot).start()

            slope[at_block(i)] = product(inputs[slot], first[...])

        loop(blocks, hidden_block)
        work.relay(1, [5])
        work.relay(2, [5])
        upward[...] = jnp.zeros_like(upward)
        work.arrived(4)
        load = pltpu.make_async_copy(gate_all, second, load_sems.at[1])
        load.start()
        share(here, normed.at[c], normed, pair_sems)[1].wait()
        save = pltpu.make_async_copy(normed, normed_out, out_sems.at[1])
        save.start()
        load.wait()

        def gate_block(i):
            result[...] = product(normed[i // per, at_block(lax.rem(i, per))], second[...])

            def body(at):
                to = pl.ds(pl.multiple_of(i * block + at.start, 16), at.size)
                gated = result[at]
                grad = slope[to]
                sigmoid = 1.0 / (1.0 + jnp.exp(-gated))
                silu[to] = gated * sigmoid
                up_grad[to] = (grad * gated * sigmoid).astype(BF16)
                slope[to] = grad * (sigmoid * (1.0 + gated * (1.0 - sigmoid)))

            by_rows(block, body)

        loop(blocks, gate_block)
        save_up = pltpu.make_async_copy(up_grad, up_grad_out, out_sems.at[2])
        save_up.start()
        work.relays(3, [5])
        group = width // zn

        def up_rows(k):
            o = farthest_first(zn, z, zn - 1 - k)
            at = pl.ds(pl.multiple_of(o * group, group), group)
            work.x_late(5, o).wait_recv()
            load = pltpu.make_async_copy(up_all.at[at], first.at[at], load_sems.at[0])
            load.start()
            load.wait()

            def up_part(i):
                rows = normed[i // per, at_block(lax.rem(i, per)), at]
                upward[at_block(i)] += product(rows, first[at])

            loop(blocks, up_part)

        loop(zn, up_rows)

        def stores(i, slot):
            to = at_block(i)
            return (
                pltpu.make_async_copy(stages.at[slot, 0], act_out.at[to], stage_sems.at[slot, 0]),
                pltpu.make_async_copy(stages.at[slot, 1], gate_grad_out.at[to], stage_sems.at[slot, 1]),
            )

        def up_block(i):
            slot = lax.rem(i, 2)

            @pl.when(i > 1)
            def _():
                for copy in stores(i - 2, slot):
                    copy.wait()

            def body(at):
                to = pl.ds(pl.multiple_of(i * block + at.start, 16), at.size)
                stages[slot, 0, at] = (silu[to] * upward[to]).astype(BF16)
                stages[slot, 1, at] = (slope[to] * upward[to]).astype(BF16)

            by_rows(block, body)
            for copy in stores(i, slot):
                copy.start()

        loop(blocks, up_block)
        for i in range(max(blocks - 2, 0), blocks):
            for copy in stores(i, i % 2):
                copy.wait()
        save.wait()
        save_up.wait()

    pl.run_scoped(
        hidden,
        pltpu.VMEM((width, columns), BF16),
        pltpu.VMEM((width, columns), BF16),
        pltpu.VMEM((2 * count, columns), F32),
        pltpu.VMEM((2 * count, columns), F32),
        pltpu.VMEM((2 * count, columns), F32),
        pltpu.VMEM((2 * count, columns), BF16),
        pltpu.VMEM((2, block, width), BF16),
        pltpu.VMEM((block, columns), F32),
        pltpu.VMEM((2, 2, block, columns), BF16),
    )
    work.finish()
    total.finish()
    for copy in saves:
        copy.wait()


def fetch(pairs, sems):
    copies = [pltpu.make_async_copy(src, dst, sems.at[i]) for i, (src, dst) in enumerate(pairs)]
    for copy in copies:
        copy.start()
    return copies


def backward(zn, early, *refs):
    normed_two, gate_grad, chip_grads, activated, gate_all, up_all, down_all, mid_in, up_grad = refs[:9]
    normed_one, context, turned_all, o_all, qkv_all, cosines, sines, tokens_in, rows_of, gain_rows = refs[9:19]
    down_out, gate_out, up_out, o_out, q_out, kv_out, out, in_grad, gain_out = refs[19:28]
    mid_grad_all, branch_all, qkv_back, in_term, out_term, back_term = refs[28:34]
    down, gate, up, o_sums, qkv_sums = refs[34:39]
    n = SCATTER_BUFFERS
    buffers, refs = refs[39 : 39 + 4 * n], refs[39 + 4 * n :]
    back_refs, front_refs, in_refs = refs[:4], refs[4:8], refs[8:11]
    gain_refs, (one_sum, two_sum), refs = refs[11:15], refs[15:17], refs[17:]
    fetch_sems, out_sems, pair_sems, weight_sems, stage_sems, block_sems, back_sems, credit = refs[:8]
    here = place()
    z, c = here[2], here[4]
    chip, width = chip_grads.shape
    count = chip // 2
    block = rows_of.shape[2]
    blocks = chip // block
    per = blocks // 2
    qkv_wide, q_half = qkv_all.shape[1], o_all.shape[1]
    enter(zn, here)
    branch, out_rows, in_rows = back_refs[0], front_refs[0], in_refs[0]
    back = Total(here, back_term, *back_refs)
    front = Total(here, out_term, *front_refs)
    total = Total(here, in_term, in_refs[0], back_refs[1], in_refs[1], in_refs[2])
    gains = Gains(zn, here, *gain_refs)
    work = Scatter(
        zn,
        here,
        early,
        [
            (down, buffers[:n], [(down_out, False, 0, down_out.shape[1] // 2)]),
            (gate, buffers[n : 2 * n], [(gate_out, False, 0, gate_out.shape[1] // 2)]),
            (up, buffers[:n], [(up_out, False, 0, up_out.shape[1] // 2)]),
            (o_sums, buffers[2 * n : 3 * n], [(o_out, False, 0, q_half)]),
            (
                qkv_sums,
                buffers[3 * n :],
                [(q_out, False, 0, q_half), (kv_out, True, q_half, kv_out.shape[2])],
            ),
        ],
        refs[8:],
    )
    def feature_terms(factors, term):
        def run(*refs):
            lefts, weights, stages = refs[:-2], refs[-2], refs[-1]
            group = weights.shape[2]
            loads = fetch([(left, ref) for (left, _), ref in zip(factors, lefts)], fetch_sems)

            def fetch_weights(i, slot):
                at = pl.ds(pl.multiple_of(i * group, group), group)
                return [
                    pltpu.make_async_copy(full.at[at], weights.at[slot, k], weight_sems.at[slot, k])
                    for k, (_, full) in enumerate(factors)
                ]

            def stores(i, slot):
                to = pl.ds(pl.multiple_of(i * group, group), group)
                return [
                    pltpu.make_async_copy(
                        stages.at[slot, pl.ds(half * count, count)], term.at[half, :, to], stage_sems.at[slot, half]
                    )
                    for half in range(2)
                ]

            for copy in fetch_weights(0, 0):
                copy.start()
            for load in loads:
                load.wait()

            def step(i):
                slot = lax.rem(i, 2)
                for copy in fetch_weights(i, slot):
                    copy.wait()

                @pl.when(i + 1 < width // group)
                def _():
                    for copy in fetch_weights(i + 1, 1 - slot):
                        copy.start()

                @pl.when(i > 1)
                def _():
                    for copy in stores(i - 2, slot):
                        copy.wait()

                value = times_transposed(lefts[0][...], weights[slot, 0])
                for k in range(1, len(lefts)):
                    value = value + times_transposed(lefts[k][...], weights[slot, k])
                stages[slot] = value.astype(BF16)
                for copy in stores(i, slot):
                    copy.start()

            loop(width // group, step)
            for i in range(width // group - 2, width // group):
                for copy in stores(i, i % 2):
                    copy.wait()

        pl.run_scoped(
            run,
            *[pltpu.VMEM((chip, wide), BF16)] * len(factors),
            pltpu.VMEM((2, len(factors), 256, wide), BF16),
            pltpu.VMEM((2, chip, 256), BF16),
        )

    wide = down.shape[2]
    operands = [pltpu.VMEM((chip, width), BF16), pltpu.VMEM((chip, wide), BF16), pltpu.VMEM((2,) + down.shape[1:], BF16)]

    def terms_of(j, left_all, right_all):
        def run(left, right, stage):
            for load in fetch(((left_all, left), (right_all, right)), fetch_sems):
                load.wait()
            work.make(j, left, right, stage)

        pl.run_scoped(run, *operands)

    terms_of(0, chip_grads, activated)
    for g in range(3):
        work.early_third(0, g)
    feature_terms([(gate_grad, gate_all), (up_grad, up_all)], back_term)
    back.start()
    work.late_third(0, 0)
    feature_terms([(activated, down_all)], out_term)
    back.meet()
    front.start()
    work.late_third(0, 1)
    work.early_home(0)
    work.late_third(0, 2)
    terms_of(1, normed_two, gate_grad)
    work.early_third(1, 0)

    def sums(mid, mid_grad, grads):
        for load in fetch(
            (
                (mid_in, mid),
                (chip_grads.at[pl.ds(pl.multiple_of(c * count, 16), count)], grads),
            ),
            fetch_sems,
        ):
            load.wait()
        gain = gain_rows[pl.ds(1, 1)]
        two_sum[...] = jnp.zeros_like(two_sum)

        def body_gain(at):
            value = mid[at]
            factor = lax.rsqrt(jnp.mean(value * value, axis=-1, keepdims=True) + norm_eps)
            two_sum[...] += jnp.sum(back.half[at].astype(F32) * (value * factor), axis=0, keepdims=True)

        by_rows(count, body_gain)
        work.late_third(1, 0)
        work.early_third(1, 1)
        work.early_third(1, 2)
        work.home(0)
        work.done(0)
        work.lend(credit)
        front.meet()
        back.pair().wait_recv()

        def body(at):
            value = mid[at]
            factor = lax.rsqrt(jnp.mean(value * value, axis=-1, keepdims=True) + norm_eps)
            scaled = back.rows(at) * gain
            result = (
                grads[at].astype(F32)
                + factor * scaled
                - value * (factor * factor * factor) * jnp.mean(scaled * value, axis=-1, keepdims=True)
            )
            mid_grad[at] = result
            branch[at] = result.astype(BF16)

        by_rows(count, body)
        save = pltpu.make_async_copy(mid_grad, mid_grad_all, out_sems.at[0])
        save.start()
        for copy in share(here, branch, branch_all, pair_sems):
            copy.start()
        work.late_third(1, 1)
        save.wait()

    pl.run_scoped(
        sums, pltpu.VMEM((count, width), F32), pltpu.VMEM((count, width), F32), pltpu.VMEM((count, width), BF16)
    )

    def middle_terms(left, right, stage):
        for copy in share(here, branch, branch_all, pair_sems):
            copy.wait()
        right_o = right.at[:, pl.ds(0, q_half)]
        loads = fetch(
            ((branch_all.at[0], left.at[pl.ds(0, count)]), (branch_all.at[1], left.at[pl.ds(count, count)])),
            fetch_sems,
        )
        loads.append(pltpu.make_async_copy(context, right_o, fetch_sems.at[2]))
        loads[2].start()
        for load in loads:
            load.wait()
        work.make(3, left, right_o, stage)
        loads = fetch(((normed_two, left), (up_grad, right)), fetch_sems)
        work.early_third(3, 0)
        work.late_third(1, 2)
        for load in loads:
            load.wait()
        work.borrow(credit)
        work.make(2, left, right, stage)

    pl.run_scoped(middle_terms, *operands)
    work.early_third(2, 0)

    def attention(o, qkv, inputs, turned, grads, backs, terms_out, cosine, sine, accumulators):
        def which(i):
            return lax.rem((1 - c) * per + i, blocks)

        def rows_at(i):
            return pl.ds(pl.multiple_of(i * block, block), block)

        def fetches(i, slot):
            b = which(i)
            sources = (
                (branch_all.at[b // per, rows_at(lax.rem(b, per))], inputs),
                (turned_all.at[rows_at(b)], turned),
                (cosines.at[rows_at(b)], cosine),
                (sines.at[rows_at(b)], sine),
            )
            return [
                pltpu.make_async_copy(source, buffer.at[slot], block_sems.at[slot, k])
                for k, (source, buffer) in enumerate(sources)
            ]

        def stores(i, slot):
            b = which(i)
            return [
                pltpu.make_async_copy(backs.at[slot], qkv_back.at[rows_at(b)], back_sems.at[slot, 0]),
                pltpu.make_async_copy(
                    terms_out.at[slot], in_term.at[b // per, rows_at(lax.rem(b, per))], back_sems.at[slot, 1]
                ),
            ]

        loads = fetch(((o_all, o), (qkv_all, qkv)), fetch_sems)
        for copy in fetches(0, 0):
            copy.start()
        for load in loads:
            load.wait()

        def step(i):
            slot = lax.rem(i, 2)

            @pl.when(i == per)
            def _():
                for done in range(per):
                    for copy in stores(done, done % 2):
                        copy.wait()
                total.core().start()
                work.early_third(2, 2)

            @pl.when(i == 1)
            def _():
                work.early_third(3, 1)
                work.early_third(2, 1)

            @pl.when(i == blocks - 1)
            def _():
                work.late_third(2, 0)

            for copy in fetches(i, slot):
                copy.wait()

            @pl.when(i + 1 < blocks)
            def _():
                for copy in fetches(i + 1, 1 - slot):
                    copy.start()

            grads[...] = product(inputs[slot], o[...]).astype(BF16)
            attention_block_back(
                turned.at[slot],
                grads,
                backs.at[slot],
                accumulators,
                q_half,
                rows_of[which(i)],
                cosine[slot],
                sine[slot],
            )
            terms_out[slot] = times_transposed(backs[slot], qkv[...]).astype(BF16)
            for copy in stores(i, slot):
                copy.start()

        loop(blocks, step)
        for i in range(per, blocks):
            for copy in stores(i, i % 2):
                copy.wait()

    pl.run_scoped(
        attention,
        pltpu.VMEM(o_all.shape, BF16),
        pltpu.VMEM(qkv_all.shape, BF16),
        pltpu.VMEM((2, block, width), BF16),
        pltpu.VMEM((2, block, qkv_wide), BF16),
        pltpu.VMEM((block, q_half), BF16),
        pltpu.VMEM((2, block, qkv_wide), BF16),
        pltpu.VMEM((2, block, width), BF16),
        pltpu.VMEM((2, block, 2 * HEAD_DIM), F32),
        pltpu.VMEM((2, block, 2 * HEAD_DIM), F32),
        pltpu.VMEM((4, block, 2 * HEAD_DIM), F32),
    )
    back.finish()
    total.load().start()

    def meeting(tokens):
        load = fetch(((tokens_in, tokens),), fetch_sems)[0]
        total.meet(send=False)
        load.wait()
        one_sum[...] = jnp.zeros_like(one_sum)

        def body_gain(at):
            value = tokens[at].astype(F32)
            factor = lax.rsqrt(jnp.mean(value * value, axis=-1, keepdims=True) + norm_eps)
            one_sum[...] += jnp.sum(total.half[at].astype(F32) * (value * factor), axis=0, keepdims=True)

        by_rows(count, body_gain)

    pl.run_scoped(meeting, pltpu.VMEM((count, width), BF16))
    gains.start([one_sum, two_sum])
    gains.swapped(0)
    total.pair().start()
    work.early_third(3, 2)
    work.late_third(2, 1)

    def output(mid):
        load = fetch(((mid_in, mid),), fetch_sems)[0]
        front.pair().wait_recv()
        load.wait()

        def body_out(at):
            out_rows[at] = (mid[at] + front.rows(at)).astype(BF16)

        by_rows(count, body_out)

    pl.run_scoped(output, pltpu.VMEM((count, width), F32))
    save_out = pltpu.make_async_copy(out_rows, out, out_sems.at[1])
    save_out.start()
    work.late_third(3, 0)
    work.late_third(2, 2)
    work.early_home(2)
    work.early_home(1)

    def last_terms(left, right, stage):
        right_qkv = right.at[:, pl.ds(0, qkv_wide)]
        for load in fetch(((normed_one, left), (qkv_back, right_qkv)), fetch_sems):
            load.wait()
        gains.swapped(1)
        work.make(4, left, right_qkv, stage)

    pl.run_scoped(last_terms, *operands)
    work.early_third(4, 0)
    work.home(1)
    work.late_third(4, 0)
    work.early_third(4, 1)
    work.early_third(4, 2)
    work.early_home(3)
    work.late_third(3, 1)
    work.home(2)
    gains.swapped(2)
    gains.run()
    work.late_third(4, 1)
    work.late_third(4, 2)
    work.late_third(3, 2)
    work.early_home(4)

    def inputs_back(mid_grad, tokens):
        loads = fetch(((mid_grad_all, mid_grad), (tokens_in, tokens)), fetch_sems)
        gain = gain_rows[pl.ds(0, 1)]
        total.pair().wait_recv()
        for load in loads:
            load.wait()

        def body(at):
            value = tokens[at].astype(F32)
            factor = lax.rsqrt(jnp.mean(value * value, axis=-1, keepdims=True) + norm_eps)
            scaled = total.rows(at) * gain
            in_rows[at] = (
                mid_grad[at]
                + factor * scaled
                - value * (factor * factor * factor) * jnp.mean(scaled * value, axis=-1, keepdims=True)
            ).astype(BF16)

        by_rows(count, body)

    pl.run_scoped(inputs_back, pltpu.VMEM((count, width), F32), pltpu.VMEM((count, width), BF16))
    save_in = pltpu.make_async_copy(in_rows, in_grad, out_sems.at[0])
    save_in.start()
    gains.finish(gain_out)
    work.home(4)
    work.home(3)
    for j in (1, 2, 3, 4):
        work.done(j)
    front.finish()
    total.finish()
    save_out.wait()
    save_in.wait()


def settle(*refs):
    turned, plain, kv = refs[:2], refs[2:7], refs[7]
    turned_out, plain_out, (k_out, v_out) = refs[8:10], refs[10:15], refs[15:17]
    turned_in, turned_to, plain_at, (kv_at, k_at, v_at) = refs[17:19], refs[19:21], refs[21:26], refs[26:29]
    load_sems, store_sems = refs[29:]

    def load(n, src, dst):
        return pltpu.make_async_copy(src, dst, load_sems.at[n])

    def store(n, src, dst):
        return pltpu.make_async_copy(src, dst, store_sems.at[n])

    loads = [load(0, turned[0], turned_in[0]), load(1, turned[1], turned_in[1]), load(2, kv, kv_at)]
    loads += [load(3 + n, src, dst) for n, (src, dst) in enumerate(zip(plain, plain_at))]
    for copy in loads[3:] + loads[:3]:
        copy.start()
    stores = []

    def send(n, src, dst):
        stores.append(store(n, src, dst))
        stores[-1].start()

    for n in range(5):
        loads[3 + n].wait()
        send(4 + n, plain_at[n], plain_out[n])
    for n in range(2):
        loads[n].wait()
        src, dst = turned_in[n], turned_to[n]

        def body(i, src=src, dst=dst):
            at = pl.ds(pl.multiple_of(i * 128, 128), 128)
            dst[at, :] = src[:, at].T

        loop(src.shape[1] // 128, body)
        send(n, dst, turned_out[n])
    loads[2].wait()
    one, two = kv_at[0], kv_at[1]
    is_key = lanes(one.shape) < HEAD_DIM
    k_at[...] = jnp.where(is_key, one, pltpu.roll(two, HEAD_DIM, 1))
    v_at[...] = jnp.where(is_key, pltpu.roll(one, HEAD_DIM, 1), two)
    send(2, k_at, k_out)
    send(3, v_at, v_out)
    for copy in stores:
        copy.wait()


def call(kernel, name, collective_id, operands, specs, outs, out_specs, scratch, order=None):
    results = pl.pallas_call(
        kernel,
        out_shape=[jax.ShapeDtypeStruct(shape, dtype) for shape, dtype in outs],
        in_specs=specs,
        out_specs=out_specs,
        scratch_shapes=scratch,
        name=name,
        compiler_params=pltpu.CompilerParams(
            collective_id=collective_id, has_side_effects=True, vmem_limit_bytes=255 << 18
        ),
    )(*operands)
    return results if order is None else [results[i] for i in order]


def rotate(vectors, cosine, sine_rows):
    half = vectors.shape[-1] // 2
    first, second = vectors[..., :half], vectors[..., half:]
    return jnp.concatenate(
        [first * cosine - second * sine_rows, second * cosine + first * sine_rows], axis=-1
    )


def product(one, two):
    return jnp.dot(one, two, preferred_element_type=F32)


def times_transposed(one, two):
    return lax.dot_general(one, two, (((1,), (1,)), ((), ())), preferred_element_type=F32)


def inner_rows(one, two):
    return lax.dot_general(one, two, (((0,), (0,)), ((), ())), preferred_element_type=F32)


def einsum(form, one, two):
    return jnp.einsum(form, one, two, preferred_element_type=F32)


def halves(weight):
    rows, columns = weight.shape
    return weight.reshape(rows, 2, columns // 2).transpose(1, 0, 2)


def joined(pair):
    return jnp.concatenate([pair[0], pair[1]], axis=1)


def local(
    dp,
    tokens,
    seg_ids,
    q_weight,
    k_weight,
    v_weight,
    o_weight,
    attn_gain,
    gate_weight,
    up_weight,
    down_weight,
    mlp_gain,
    out_grad,
):
    zn = dp // 4
    units = zn * 2
    count, width = tokens.shape
    rows = q_weight.shape[0]
    blocks, block_rows = 2 * seg_ids.shape[0], seg_ids.shape[1]
    q_half, kv_half = q_weight.shape[1] // 2, k_weight.shape[1] // 2
    ff_half = gate_weight.shape[1] // 2
    qkv_half = q_half + 2 * kv_half
    heads, groups = q_half // HEAD_DIM, kv_half // HEAD_DIM
    early = 2 * rows // 48 * 8
    early_sums = max(16, 2 * rows * 3 // 256 * 16)

    chip = 2 * count
    inverse = 1.0 / 10000.0 ** (np.arange(0, HEAD_DIM, 2, dtype=np.float32) / HEAD_DIM)
    inverse = np.tile(inverse.astype(np.float32), 4)[None]
    sign = np.tile(np.repeat(np.array([-1.0, 1.0], np.float32), HEAD_DIM // 2), 2)[None]
    (
        qkv_full,
        o_full,
        grads_chip,
        segment,
        gate_full,
        up_full,
        down_full,
        mid,
        normed_two,
        activated,
        gate_grad,
        up_grad,
        normed,
        turned,
        context,
        cosines,
        sines,
        gain_rows,
    ) = call(
        functools.partial(forward, zn, early),
        "forward",
        0,
        (
            q_weight,
            k_weight,
            v_weight,
            o_weight,
            jnp.stack([attn_gain, mlp_gain]),
            tokens,
            out_grad,
            seg_ids,
            gate_weight,
            up_weight,
            down_weight,
            inverse,
            sign,
        ),
        [VMEM] * 5 + [ANY] * 2 + [VMEM] + [ANY] * 3 + [VMEM] * 2,
        [
            ((width, qkv_half), BF16),
            ((width, q_half), BF16),
            ((units * 16, 128), F32),
            ((2, count, width), BF16),
            ((2, count, width), BF16),
            ((2,) + seg_ids.shape, jnp.int32),
        ]
        + [((width, ff_half), BF16)] * 3
        + [((count, width), F32), ((2, count, width), BF16)]
        + [((chip, ff_half), BF16)] * 3
        + [((2, count, width), BF16)]
        + [((chip, width), BF16), ((chip, qkv_half), BF16), ((chip, q_half), BF16)]
        + [((chip, 2 * HEAD_DIM), F32)] * 2
        + [((8, width), F32)],
        [ANY] * 21,
        total_buffers(count, width)
        + [
            pltpu.VMEM((2, count, width), BF16),
            DMA((3,)),
            DMA((3,)),
            DMA((2,)),
            DMA((2,)),
            DMA((2, 3)),
            DMA((2,)),
            pltpu.VMEM((chip, 2 * HEAD_DIM), F32),
            pltpu.VMEM((chip, 2 * HEAD_DIM), F32),
            pltpu.VMEM((2,) + seg_ids.shape, jnp.int32),
            pltpu.VMEM((units * 16, 128), F32),
            pltpu.VMEM((8, width), F32),
            DMA((2, 3)),
            DMA((5,)),
            pltpu.VMEM((2, rows, 2 * kv_half), BF16),
            pltpu.VMEM((2, 8, 128), F32),
            pltpu.VMEM((rows, 2 * q_half), BF16),
            pltpu.VMEM((rows, 2 * ff_half), BF16),
            pltpu.VMEM((count, width), BF16),
            pltpu.VMEM((count, width), BF16),
            pltpu.VMEM((rows, 2 * ff_half), BF16),
            pltpu.VMEM((rows, 2 * ff_half), BF16),
            pltpu.VMEM((2 * ff_half, rows), BF16),
            DMA((5,)),
        ]
        + gather_sems(6, 7, zn),
        order=(0, 1, 4, 5, 6, 7, 8, 9, 10, 11, 12, 13, 15, 16, 17, 18, 19, 20),
    )
    grads_chip = grads_chip.reshape(chip, width)
    segment = segment.reshape(blocks, 1, block_rows)
    normed_two = normed_two.reshape(chip, width)

    down_sum, gate_sum, up_sum, o_sum, q_sum, kv_sum, out, in_grad, gain_sums = call(
        functools.partial(backward, zn, early_sums),
        "backward",
        1,
        (
            normed_two,
            gate_grad,
            grads_chip,
            activated,
            gate_full,
            up_full,
            down_full,
            mid,
            up_grad,
            normed,
            context,
            turned,
            o_full,
            qkv_full,
            cosines,
            sines,
            tokens,
            segment,
            gain_rows,
        ),
        [ANY] * 17 + [VMEM] * 2,
        [((rows, 2 * ff_half), F32)] * 3
        + [
            ((rows, 2 * q_half), F32),
            ((rows, 2 * q_half), F32),
            ((2, rows, 2 * kv_half), F32),
            ((count, width), BF16),
            ((count, width), BF16),
            ((8, 4 * rows), F32),
            ((count, width), F32),
            ((2, count, width), BF16),
            ((chip, qkv_half), BF16),
            ((2, count, width), BF16),
            ((2, count, width), BF16),
            ((2, count, width), BF16),
        ]
        + [((zn, 4 * rows, ff_half), BF16)] * 3
        + [((zn, 4 * rows, q_half), BF16), ((zn, 4 * rows, qkv_half), BF16)],
        [ANY] * 8 + [VMEM] + [ANY] * 11,
        scatter_buffers(
            [(2 * rows, ff_half), (2 * rows, ff_half), (2 * rows, q_half), (2 * rows, qkv_half)], early_sums, zn
        )
        + total_buffers(count, width) * 2
        + [pltpu.VMEM((count, width), BF16)] * 2
        + [DMA((5,))]
        + gain_buffers(zn, 4 * rows)
        + [pltpu.VMEM((1, width), F32)] * 2
        + [
            DMA((4,)),
            DMA((2,)),
            DMA((3,)),
            DMA((2, 2)),
            DMA((2, 2)),
            DMA((2, 4)),
            DMA((2, 2)),
            pltpu.SemaphoreType.REGULAR,
        ]
        + scatter_sems(5, 6, zn),
        order=range(9),
    )
    gain_grads = lax.dynamic_slice_in_dim(gain_sums, lax.rem(lax.axis_index("dp"), 4) * rows, rows, 1)
    plain = (gate_sum, up_sum, q_sum, out, in_grad)
    turned = (down_sum, o_sum)
    shapes = [ref.shape[::-1] for ref in turned]
    results = pl.pallas_call(
        settle,
        out_shape=[jax.ShapeDtypeStruct(shape, F32) for shape in shapes]
        + [jax.ShapeDtypeStruct(ref.shape, ref.dtype) for ref in plain]
        + [jax.ShapeDtypeStruct((rows, 2 * kv_half), F32)] * 2,
        in_specs=[pl.BlockSpec(memory_space=pltpu.HBM)] * 8,
        out_specs=[pl.BlockSpec(memory_space=pltpu.HBM)] * 9,
        scratch_shapes=[pltpu.VMEM(ref.shape, F32) for ref in turned]
        + [pltpu.VMEM(shape, F32) for shape in shapes]
        + [pltpu.VMEM(ref.shape, ref.dtype) for ref in plain]
        + [pltpu.VMEM(kv_sum.shape, F32)]
        + [pltpu.VMEM((rows, 2 * kv_half), F32)] * 2
        + [DMA((8,)), DMA((9,))],
        name="settle",
        compiler_params=pltpu.CompilerParams(vmem_limit_bytes=62 << 20),
    )(*turned, *plain, kv_sum)
    down_final, o_final, gate_final, up_final, q_final, out, in_grad, k_final, v_final = results
    return (
        out,
        in_grad,
        q_final,
        k_final,
        v_final,
        o_final,
        gain_grads[0],
        gate_final,
        up_final,
        down_final,
        gain_grads[1],
    )


def solution(mesh):
    arguments = (
        P("dp", None),
        P("dp", None),
        P("dp", "tensor"),
        P("dp", "tensor"),
        P("dp", "tensor"),
        P("tensor", "dp"),
        P("dp"),
        P("dp", "tensor"),
        P("dp", "tensor"),
        P("tensor", "dp"),
        P("dp"),
        P("dp", None),
    )
    results = (
        P("dp", None),
        P("dp", None),
        P("dp", "tensor"),
        P("dp", "tensor"),
        P("dp", "tensor"),
        P("tensor", "dp"),
        P("dp"),
        P("dp", "tensor"),
        P("dp", "tensor"),
        P("tensor", "dp"),
        P("dp"),
    )
    return jax.shard_map(
        functools.partial(local, mesh.shape["dp"]),
        mesh=mesh,
        in_specs=arguments,
        out_specs=results,
        check_vma=False,
    )
```

```python
import functools

import jax
import jax.numpy as jnp
import numpy as np
from jax import lax
from jax.experimental import pallas as pl
from jax.experimental.pallas import tpu as pltpu
from jax.sharding import PartitionSpec as P

HEAD_DIM = 64
norm_eps = 1e-05
MESH = pl.DeviceIdType.MESH
ANY = pl.BlockSpec(memory_space=pl.ANY)
VMEM = pl.BlockSpec(memory_space=pltpu.VMEM)
DMA = pltpu.SemaphoreType.DMA
F32 = jnp.float32
BF16 = jnp.bfloat16


def place():
    d = lax.axis_index("dp")
    t = lax.axis_index("tensor")
    return d, t, d // 4, lax.rem(d // 2, 2), lax.rem(d, 2)


def enter(zn, here):
    d, t, z, x, c = here
    bar = pltpu.get_barrier_semaphore()

    def hail(device):
        pl.semaphore_signal(bar, inc=1, device_id=device, device_id_type=MESH)

    hail((d + 1 - 2 * c, t))
    hail((d + 2 - 4 * x, t))
    hail((d, 1 - t))

    @pl.when(z > 0)
    def _():
        hail((d - 4, t))

    @pl.when(z < zn - 1)
    def _():
        hail((d + 4, t))

    pl.semaphore_wait(bar, 5 - (z == 0).astype(jnp.int32) - (z == zn - 1).astype(jnp.int32))


def farthest_first(zn, z, i):
    up = 1 - (2 * z) // zn
    longer = up * (zn - 1 - z) + (1 - up) * z
    shorter = zn - 1 - longer
    rest = i - (longer - shorter)
    return jnp.where(
        rest < 0,
        z + (2 * up - 1) * (longer - i),
        z + (1 - 2 * lax.rem(jnp.maximum(rest, 0), 2)) * (shorter - jnp.maximum(rest, 0) // 2),
    )


def loop(count, body):
    def step(i, carry):
        body(i)
        return carry

    lax.fori_loop(0, count, step, 0)


def remote(src, dst, send, recv, device):
    return pltpu.make_async_remote_copy(
        src_ref=src, dst_ref=dst, send_sem=send, recv_sem=recv, device_id=device, device_id_type=MESH
    )


def by_rows(count, body, block=16):
    def step(i, carry):
        body(pl.ds(pl.multiple_of(i * block, block), block))
        return carry

    lax.fori_loop(0, count // block, step, 0)


def gather_sems(n, sources, zn):
    return [
        DMA((sources,)),
        DMA((sources,)),
        DMA((sources,)),
        DMA((n, zn)),
        DMA((n, zn)),
        DMA((n,)),
        DMA((n,)),
        DMA((n, 2, zn)),
        DMA((n, zn)),
        DMA((n, 2, zn)),
        DMA((n, zn)),
    ]


def part(ref, core, paired):
    if paired:
        return ref.at[core]
    columns = ref.shape[1] // 2
    return ref.at[:, pl.ds(pl.multiple_of(core * columns, columns), columns)]


class Gather:
    def __init__(self, zn, here, arrays, sems):
        self.zn, self.here = zn, here
        self.full = [full for _, full, _ in arrays]
        self.early = [early for _, _, early in arrays]
        self.sources = [
            (j, i) + source for j, (sources, _, _) in enumerate(arrays) for i, source in enumerate(sources)
        ]
        (
            self.loc,
            self.cs,
            self.cr,
            self.xs,
            self.xr,
            self.es,
            self.er,
            self.zs,
            self.zr,
            self.bs,
            self.br,
        ) = sems

    def unit(self, j, unit, first, count):
        rows = self.full[j].shape[0] // (2 * self.zn)
        return pl.ds(pl.multiple_of(unit * rows + first, 8), count)

    def rows(self, j, unit, early):
        rows = self.full[j].shape[0] // (2 * self.zn)
        late = rows - self.early[j]
        first, count = {None: (0, rows), True: (late, rows - late), False: (0, late)}[early]
        return self.full[j].at[self.unit(j, unit, first, count)]

    def mine(self, s):
        d, t, z, x, c = self.here
        j, _, shard, paired, first, columns = self.sources[s]
        rows = self.full[j].shape[0] // (4 * self.zn)
        return self.full[j].at[self.unit(j, z * 2 + x, c * rows, rows), pl.ds(first, columns)]

    def keep(self, s):
        _, _, shard, paired, _, _ = self.sources[s]
        return pltpu.make_async_copy(part(shard, self.here[4], paired), self.mine(s), self.loc.at[s])

    def give(self, s):
        d, t, z, x, c = self.here
        _, _, shard, paired, _, _ = self.sources[s]
        return remote(
            part(shard, 1 - c, paired), self.mine(s), self.cs.at[s], self.cr.at[s], (d + 1 - 2 * c, t)
        )

    def x_late(self, j, o):
        d, t, z, x, c = self.here
        ref = self.rows(j, o * 2 + x, False)
        return remote(ref, ref, self.xs.at[j, o], self.xr.at[j, o], (d + 2 - 4 * x, t))

    def x_early(self, j):
        d, t, z, x, c = self.here
        ref = self.rows(j, z * 2 + x, True)
        return remote(ref, ref, self.es.at[j], self.er.at[j], (d + 2 - 4 * x, t))

    def along(self, j, o, down):
        d, t, z, x, c = self.here
        ref = self.rows(j, o * 2 + x, None)
        return remote(ref, ref, self.zs.at[j, down, o], self.zr.at[j, o], (d + 4 - 8 * down, t))

    def along_early(self, j, o, down):
        d, t, z, x, c = self.here
        ref = self.rows(j, o * 2 + 1 - x, True)
        return remote(ref, ref, self.bs.at[j, down, o], self.br.at[j, o], (d + 4 - 8 * down, t))

    def start(self, arrays):
        for s, source in enumerate(self.sources):
            if source[0] in arrays:
                self.give(s).start()
                self.keep(s).start()

    def ready(self, arrays):
        for j in arrays:
            for s, source in enumerate(self.sources):
                if source[0] == j:
                    self.keep(s).wait()
                    self.give(s).wait_recv()
            if self.early[j]:
                self.x_early(j).start()

    def start_own(self, arrays):
        z, zn = self.here[2], self.zn
        for j in arrays:
            self.x_late(j, z).start()

            @pl.when(z < zn - 1)
            def _():
                self.along(j, z, 0).start()

            @pl.when(z > 0)
            def _():
                self.along(j, z, 1).start()

    def start_early(self, arrays):
        z, zn = self.here[2], self.zn
        for j in arrays:
            if self.early[j]:
                self.x_early(j).wait_recv()

                @pl.when(z < zn - 1)
                def _():
                    self.along_early(j, z, 0).start()

                @pl.when(z > 0)
                def _():
                    self.along_early(j, z, 1).start()

    def relay(self, k, arrays):
        z, zn = self.here[2], self.zn
        o = farthest_first(zn, z, zn - 1 - k)
        down = (o > z).astype(jnp.int32)
        more = ((o < z) & (z < zn - 1)) | ((o > z) & (z > 0))
        for j in arrays:
            self.along(j, o, down).wait_recv()

            @pl.when(more)
            def _():
                self.along(j, o, down).start()

            self.x_late(j, o).start()
            if self.early[j]:
                self.along_early(j, o, down).wait_recv()

                @pl.when(more)
                def _():
                    self.along_early(j, o, down).start()

    def relays(self, first, arrays):
        loop(max(self.zn - first, 0), lambda i: self.relay(first + i, arrays))

    def arrived(self, j):
        loop(self.zn, lambda o: self.x_late(j, o).wait_recv())

    def finish(self):
        z, zn = self.here[2], self.zn
        for s in range(len(self.sources)):
            self.give(s).wait_send()
        for j in range(len(self.full)):
            if self.early[j]:
                self.x_early(j).wait_send()

            def step(o, j=j):
                self.x_late(j, o).wait_send()

                def sent(down):
                    self.along(j, o, down).wait_send()
                    if self.early[j]:
                        self.along_early(j, o, down).wait_send()

                @pl.when((o <= z) & (z < zn - 1))
                def _():
                    sent(0)

                @pl.when((o >= z) & (z > 0))
                def _():
                    sent(1)

            loop(zn, step)


def scatter_sems(n, outs, zn):
    return [
        DMA((n, zn)),
        DMA((n, zn)),
        DMA((n, zn)),
        DMA((n, zn)),
        DMA((n, zn)),
        DMA((n, zn + 1)),
        DMA((n, 2, zn)),
        DMA((n, zn)),
        DMA((n, zn + 1)),
        DMA((n,)),
        DMA((n,)),
        DMA((outs,)),
        DMA((outs,)),
        DMA((outs,)),
    ]


def scatter_buffers(shapes, early, zn):
    out = []
    for rows, columns in shapes:
        late = rows - early
        out += [
            pltpu.VMEM((zn, late, columns), BF16),
            pltpu.VMEM((zn, late, columns), BF16),
            pltpu.VMEM((zn + 1, late, columns), BF16),
            pltpu.VMEM((zn, 2, early, columns), BF16),
            pltpu.VMEM((zn + 1, 2, early, columns), BF16),
            pltpu.VMEM((early, columns), BF16),
            pltpu.VMEM((rows, columns), F32),
        ]
    return out


SCATTER_BUFFERS = 7


class Scatter:
    def __init__(self, zn, here, early, arrays, sems):
        self.zn, self.here, self.early = zn, here, early
        self.term = [term for term, _, _ in arrays]
        self.buffers = [buffers for _, buffers, _ in arrays]
        self.results = [(j,) + result for j, (_, _, results) in enumerate(arrays) for result in results]
        (
            self.st,
            self.ls,
            self.xs,
            self.xr,
            self.zs,
            self.zr,
            self.bls,
            self.bs,
            self.br,
            self.es,
            self.er,
            self.cs,
            self.cr,
            self.loc,
        ) = sems

    def unit(self, j, o, x, first, count):
        rows = self.term[j].shape[1] // 2
        return self.term[j].at[o, pl.ds(pl.multiple_of(x * rows + first, 16), count)]

    def late(self, j):
        return self.buffers[j][0].shape[1]

    def load(self, j, o):
        return pltpu.make_async_copy(
            self.unit(j, o, self.here[3], 0, self.late(j)), self.buffers[j][0].at[o], self.ls.at[j, o]
        )

    def load_early(self, j, o, other):
        x = self.here[3]
        return pltpu.make_async_copy(
            self.unit(j, o, 1 - x if other else x, self.late(j), self.early),
            self.buffers[j][3].at[o, other],
            self.bls.at[j, other, o],
        )

    def across(self, j, o):
        d, t, z, x, c = self.here
        return remote(
            self.unit(j, o, 1 - x, 0, self.late(j)),
            self.buffers[j][1].at[o],
            self.xs.at[j, o],
            self.xr.at[j, o],
            (d + 2 - 4 * x, t),
        )

    def across_early(self, j):
        d, t, z, x, c = self.here
        return remote(
            self.buffers[j][3].at[z, 1], self.buffers[j][5], self.es.at[j], self.er.at[j], (d + 2 - 4 * x, t)
        )

    def along(self, j, o, slot, down):
        d, t, z, x, c = self.here
        own, line = self.buffers[j][0], self.buffers[j][2]
        return remote(own.at[o], line.at[slot], self.zs.at[j, o], self.zr.at[j, slot], (d + 4 - 8 * down, t))

    def along_early(self, j, o, slot, down):
        d, t, z, x, c = self.here
        own, line = self.buffers[j][3], self.buffers[j][4]
        return remote(own.at[o], line.at[slot], self.bs.at[j, o], self.br.at[j, slot], (d + 4 - 8 * down, t))

    def give(self, r):
        d, t, z, x, c = self.here
        j, out, paired, first, columns = self.results[r]
        rows = out.shape[-2]
        ref = self.buffers[j][6].at[
            pl.ds(pl.multiple_of((1 - c) * rows, rows), rows), pl.ds(first, columns)
        ]
        return remote(ref, part(out, c, paired), self.cs.at[r], self.cr.at[r], (d + 1 - 2 * c, t))

    def keep(self, r):
        c = self.here[4]
        j, out, paired, first, columns = self.results[r]
        rows = out.shape[-2]
        ref = self.buffers[j][6].at[pl.ds(pl.multiple_of(c * rows, rows), rows), pl.ds(first, columns)]
        return pltpu.make_async_copy(ref, part(out, c, paired), self.loc.at[r])

    def store(self, j, o, stage, slot):
        columns = self.term[j].shape[2]
        return pltpu.make_async_copy(
            stage.at[slot, :, pl.ds(0, columns)], self.term[j].at[o], self.st.at[j, o]
        )

    def make(self, j, left, right, stage, between=None):
        z, zn = self.here[2], self.zn
        wide, columns = self.term[j].shape[1:]
        block = min(256, wide)

        def send(i):
            o = farthest_first(zn, z, i)
            self.store(j, o, stage, lax.rem(i, 2)).wait()
            self.across(j, o).start()
            for other in range(2):
                self.load_early(j, o, other).start()
            self.load(j, o).start()

        def compute(i):
            o = farthest_first(zn, z, i)
            slot = lax.rem(i, 2)

            def body(m):
                at = pl.multiple_of(o * wide + m * block, block)
                value = inner_rows(left[:, pl.ds(at, block)], right[...])
                stage[slot, pl.ds(pl.multiple_of(m * block, block), block), pl.ds(0, columns)] = value.astype(
                    BF16
                )

            loop(wide // block, body)
            self.store(j, o, stage, slot).start()

        def both(i):
            compute(i)
            send(i - 1)

        compute(0)
        if between is not None:
            between()
        loop(zn - 1, lambda i: both(i + 1))
        send(zn - 1)

    def add(self, j, o, slots):
        own, got, line = self.buffers[j][:3]

        def body(at):
            value = own[o, at].astype(F32) + got[o, at].astype(F32)
            for slot in slots:
                value = value + line[slot, at].astype(F32)
            own[o, at] = value.astype(BF16)

        by_rows(own.shape[1], body)

    def add_early(self, j, o, slots):
        own, line = self.buffers[j][3:5]
        for other in range(2):

            def body(at):
                value = own[o, other, at].astype(F32)
                for slot in slots:
                    value = value + line[slot, other, at].astype(F32)
                own[o, other, at] = value.astype(BF16)

            by_rows(own.shape[2], body)

    def route(self, i):
        z, zn = self.here[2], self.zn
        o = farthest_first(zn, z, i)
        down = (o < z).astype(jnp.int32)
        distance = jnp.maximum((o - z) * (1 - 2 * down), 1)
        slot = o + (zn - o) * down * (1 // distance)
        inner = ((o > z) & (z > 0)) | ((o < z) & (z < zn - 1))
        return o, slot, down, inner

    def hop_early(self, j, i):
        o, slot, down, inner = self.route(i)
        for other in range(2):
            self.load_early(j, o, other).wait()

        @pl.when(inner)
        def _():
            self.along_early(j, o, o, down).wait_recv()
            self.add_early(j, o, [o])

        self.along_early(j, o, slot, down).start()

    def hop(self, j, i):
        o, slot, down, inner = self.route(i)
        self.load(j, o).wait()
        self.across(j, o).wait_recv()

        @pl.when(inner)
        def _():
            self.along(j, o, o, down).wait_recv()
            self.add(j, o, [o])

        @pl.when(jnp.logical_not(inner))
        def _():
            self.add(j, o, [])

        self.along(j, o, slot, down).start()

    def third(self, hop, j, g):
        hops = self.zn - 1
        first = g * hops // 3
        loop((g + 1) * hops // 3 - first, lambda i: hop(j, first + i))

    def early_third(self, j, g):
        self.third(self.hop_early, j, g)

    def late_third(self, j, g):
        self.third(self.hop, j, g)

    def at_home(self, action):
        z, zn = self.here[2], self.zn

        @pl.when((z > 0) & (z < zn - 1))
        def _():
            action([z, zn])

        @pl.when(z == 0)
        def _():
            action([zn])

        @pl.when(z == zn - 1)
        def _():
            action([z])

    def early_home(self, j):
        z = self.here[2]
        for other in range(2):
            self.load_early(j, z, other).wait()

        def home(slots):
            for slot in slots:
                self.along_early(j, z, slot, 0).wait_recv()
            self.add_early(j, z, slots)

        self.at_home(home)
        self.across_early(j).start()

    def home(self, j):
        z = self.here[2]
        own, got, line, early, _, other_early, total = self.buffers[j]
        late = self.late(j)
        self.load(j, z).wait()
        self.across(j, z).wait_recv()

        def last(slots):
            for slot in slots:
                self.along(j, z, slot, 0).wait_recv()

            def body(at):
                value = own[z, at].astype(F32) + got[z, at].astype(F32)
                for slot in slots:
                    value = value + line[slot, at].astype(F32)
                total[at] = value

            by_rows(late, body)

        self.at_home(last)
        self.across_early(j).wait_recv()
        for i in range(self.early // 16):
            at = pl.ds(16 * i, 16)
            total[pl.ds(late + 16 * i, 16)] = early[z, 0, at].astype(F32) + other_early[at].astype(F32)
        for r, result in enumerate(self.results):
            if result[0] == j:
                self.give(r).start()
                self.keep(r).start()

    def done(self, j):
        z = self.here[2]
        for r, result in enumerate(self.results):
            if result[0] == j:
                self.give(r).wait()
                self.keep(r).wait()
        self.across_early(j).wait_send()

        def sent(o):
            self.across(j, o).wait_send()

            @pl.when(o != z)
            def _():
                self.along(j, o, 0, 0).wait_send()
                self.along_early(j, o, 0, 0).wait_send()

        loop(self.zn, sent)

    def lend(self, credit):
        d, t, z, x, c = self.here

        def tell(device):
            pl.semaphore_signal(credit, inc=1, device_id=device, device_id_type=MESH)

        tell((d + 2 - 4 * x, t))

        @pl.when(z > 0)
        def _():
            tell((d - 4, t))

        @pl.when(z < self.zn - 1)
        def _():
            tell((d + 4, t))

    def borrow(self, credit):
        z = self.here[2]
        pl.semaphore_wait(credit, 3 - (z == 0).astype(jnp.int32) - (z == self.zn - 1).astype(jnp.int32))


class Gains:
    def __init__(self, zn, here, own, got, line, sems):
        self.zn, self.here, self.own, self.got, self.line, self.sems = zn, here, own, got, line, sems

    def swap(self, i):
        d, t, z, x, c = self.here
        device = ((d + 1 - 2 * c, t), (d, 1 - t), (d + 2 - 4 * x, t))[i]
        return remote(self.own, self.got.at[i], self.sems.at[0, i], self.sems.at[1, i], device)

    def along(self, o, slot, down):
        d, t, z, x, c = self.here
        return remote(
            self.own.at[o], self.line.at[slot], self.sems.at[2, o], self.sems.at[3, slot], (d + 4 - 8 * down, t)
        )

    def start(self, rows):
        wide = self.own.shape[2]
        for o in range(self.zn):
            for i, row in enumerate(rows):
                self.own[o, pl.ds(i, 1)] = row[:, pl.ds(o * wide, wide)]
        self.swap(0).start()

    def swapped(self, i):
        self.swap(i).wait()
        self.own[...] += self.got[i]
        if i < 2:
            self.swap(i + 1).start()

    def hop(self, o, slot, down, inner):
        @pl.when(inner)
        def _():
            self.along(o, o, down).wait_recv()
            self.own[o] += self.line[o]

        self.along(o, slot, down).start()

    def steps(self, k, nearest):
        z, zn = self.here[2], self.zn

        @pl.when(z + k < zn)
        def _():
            self.hop(z + k, z + k, 0, z > 0)

        @pl.when(z - k >= 0)
        def _():
            self.hop(z - k, zn if nearest else z - k, 1, z < zn - 1)

    def run(self):
        zn = self.zn

        def step(i, carry):
            self.steps(zn - 1 - i, False)
            return carry

        lax.fori_loop(0, zn - 2, step, 0)
        self.steps(1, True)

    def finish(self, out):
        z, zn = self.here[2], self.zn
        value = self.own[z]

        @pl.when(z > 0)
        def _():
            self.along(z, z, 0).wait_recv()
            self.own[z] += self.line[z]

        @pl.when(z < zn - 1)
        def _():
            self.along(z, zn, 1).wait_recv()
            self.own[z] += self.line[zn]

        out[...] = self.own[z]

        def step(o, carry):
            @pl.when(o != z)
            def _():
                self.along(o, 0, 0).wait_send()

            return carry

        lax.fori_loop(0, zn, step, 0)


def gain_buffers(zn, wide):
    return [
        pltpu.VMEM((zn, 8, wide), F32),
        pltpu.VMEM((3, zn, 8, wide), F32),
        pltpu.VMEM((zn + 1, 8, wide), F32),
        DMA((4, zn + 1)),
    ]


class Total:
    def __init__(self, here, term, from_core, half, from_pair, sems):
        self.here, self.term, self.from_core, self.half, self.from_pair = here, term, from_core, half, from_pair
        self.sems = sems

    def core(self):
        d, t, z, x, c = self.here
        return remote(self.term.at[1 - c], self.from_core, self.sems.at[0], self.sems.at[1], (d + 1 - 2 * c, t))

    def load(self):
        return pltpu.make_async_copy(self.term.at[self.here[4]], self.half, self.sems.at[4])

    def start(self):
        self.core().start()
        self.load().start()

    def pair(self):
        d, t, z, x, c = self.here
        return remote(self.half, self.from_pair, self.sems.at[2], self.sems.at[3], (d, 1 - t))

    def meet(self, loaded=True, send=True):
        if loaded:
            self.load().wait()
        self.core().wait_recv()

        def body(at):
            self.half[at] = (self.half[at].astype(F32) + self.from_core[at].astype(F32)).astype(BF16)

        by_rows(self.half.shape[0], body)
        if send:
            self.pair().start()

    def rows(self, at):
        return self.half[at].astype(F32) + self.from_pair[at].astype(F32)

    def finish(self):
        self.core().wait_send()
        self.pair().wait_send()


def total_buffers(tokens, width):
    return [pltpu.VMEM((tokens, width), BF16)] * 3 + [DMA((5,))]


def share(here, src, dst, sems):
    d, t, z, x, c = here
    return (
        pltpu.make_async_copy(src, dst.at[c], sems.at[0]),
        remote(src, dst.at[c], sems.at[1], sems.at[2], (d + 1 - 2 * c, t)),
    )


def lanes(shape):
    return lax.broadcasted_iota(jnp.int32, shape, 1)


def partner(value):
    half = HEAD_DIM // 2
    wide = 2 * HEAD_DIM
    lower = lax.rem(lanes(value.shape), HEAD_DIM) < half
    return jnp.where(lower, pltpu.roll(value, wide - half, 1), pltpu.roll(value, half, 1))


def same_segment(row):
    count = row.shape[1]
    wide = jnp.broadcast_to(row, (count, count))
    before = lax.broadcasted_iota(jnp.int32, wide.shape, 1) < lax.broadcasted_iota(jnp.int32, wide.shape, 0)
    return wide == wide.T, before


def allowed_in(row):
    same, before = same_segment(row)
    here = lax.broadcasted_iota(jnp.int32, same.shape, 1) == lax.broadcasted_iota(jnp.int32, same.shape, 0)
    return same & (before | here)


def softmax_of(queries, keys, allowed):
    scores = jnp.where(allowed, times_transposed(queries, keys) * HEAD_DIM ** (-0.5), -1e30)
    shifted = jnp.exp(scores - jnp.max(scores, axis=-1, keepdims=True))
    return shifted / jnp.sum(shifted, axis=-1, keepdims=True)


def key_value_pairs(pair):
    pair = pair.astype(F32)
    first = lanes(pair.shape) < HEAD_DIM
    key, value = jnp.where(first, pair, 0.0), jnp.where(first, 0.0, pair)
    return [
        part.astype(BF16)
        for part in (key, pltpu.roll(key, HEAD_DIM, 1), pltpu.roll(value, HEAD_DIM, 1), value)
    ]


def attention_block(turned, context, queries_wide, row):
    wide = 2 * HEAD_DIM
    allowed = allowed_in(row)
    key_one, key_two, value_one, value_two = key_value_pairs(turned[:, queries_wide:])

    def heads(p):
        at = pl.ds(pl.multiple_of(p * wide, wide), wide)
        queries = turned[:, at]
        one = softmax_of(queries, key_one, allowed).astype(BF16)
        two = softmax_of(queries, key_two, allowed).astype(BF16)
        context[:, at] = (product(one, value_one) + product(two, value_two)).astype(BF16)

    loop(queries_wide // wide, heads)


def attention_block_back(turned, grads, back, sums, queries_wide, row, cosine, sine):
    wide = 2 * HEAD_DIM
    scale = HEAD_DIM ** (-0.5)
    allowed = allowed_in(row)
    key_one, key_two, value_one, value_two = key_value_pairs(turned[:, queries_wide:])
    sums[...] = jnp.zeros_like(sums)

    def heads(p):
        at = pl.ds(pl.multiple_of(p * wide, wide), wide)
        queries, grad = turned[:, at], grads[:, at]
        total = None
        for i, (key, value) in enumerate(((key_one, value_one), (key_two, value_two))):
            probs = softmax_of(queries, key, allowed)
            sums[i] += inner_rows(probs.astype(BF16), grad)
            prob_grad = times_transposed(grad, value)
            delta = jnp.sum(probs * prob_grad, axis=-1, keepdims=True)
            score_grad = (probs * (prob_grad - delta)).astype(BF16)
            term = product(score_grad, key)
            total = term if total is None else total + term
            sums[2 + i] += inner_rows(score_grad, queries)
        total = total * scale
        back[:, at] = (total * cosine - partner(total) * sine).astype(BF16)

    loop(queries_wide // wide, heads)
    value_grad = pltpu.roll(sums[0], HEAD_DIM, 1) + sums[1]
    key_grad = (sums[2] + pltpu.roll(sums[3], HEAD_DIM, 1)) * scale
    turned_back = key_grad * cosine - partner(key_grad) * sine
    back[:, pl.ds(queries_wide, wide)] = jnp.where(
        lanes(value_grad.shape) < HEAD_DIM, turned_back, value_grad
    ).astype(BF16)


def transposed(src, dst):
    def body(n):
        at = pl.ds(pl.multiple_of(n * 128, 128), 128)
        dst[:, at] = src[at, :].astype(F32).T.astype(BF16)

    loop(src.shape[0] // 128, body)


def forward(zn, early, *refs):
    q, k_shard, v_shard, o_turned, one_shard, two_shard, tokens_in, grads_in, seg, gate_in, up_in, down_in, inverse, sign = refs[:14]
    refs = refs[2:]
    qkv_all, o_all, gains_all, chip_tokens, chip_grads, seg_all = refs[12:18]
    gate_all, up_all, down_all, mid_out, normed_out, act_out, gate_grad_out, up_grad_out = refs[18:26]
    term, normed_one_out, turned_out, context_out, cosines_out, sines_out, gain_out = refs[26:33]
    total_refs = refs[33:37]
    normed, out_sems, pair_sems, load_sems, grad_sems, stage_sems, block_sems = refs[37:44]
    cosines, sines, seg_pair, gain_tiles, gain_rows, swap_sems, seg_sems = refs[44:51]
    kv, gains, o_shard, down, tokens, grads, gate, up, down_turned, first_sems = refs[51:61]
    here = place()
    z, c = here[2], here[4]
    firsts = [
        pltpu.make_async_copy(src, dst, first_sems.at[n])
        for n, (src, dst) in enumerate(
            ((down_in, down_turned), (tokens_in, tokens), (gate_in, gate), (up_in, up), (grads_in, grads))
        )
    ]
    for copy in firsts:
        copy.start()
    enter(zn, here)
    keys, values = k_shard[...].astype(F32), v_shard[...].astype(F32)
    is_key = lanes(keys.shape) < HEAD_DIM
    kv[0] = jnp.where(is_key, keys, pltpu.roll(values, HEAD_DIM, 1)).astype(BF16)
    kv[1] = jnp.where(is_key, pltpu.roll(keys, HEAD_DIM, 1), values).astype(BF16)
    for i in range(2):
        gains[i] = jnp.zeros(gains.shape[1:], F32)
        for k, shard in enumerate((one_shard, two_shard)):
            gains[i, pl.ds(k, 1), pl.ds(0, shard.shape[1])] = shard[...].astype(F32)
    transposed(o_turned, o_shard)
    total = Total(here, term, *total_refs)
    q_half = q.shape[1] // 2
    work = Gather(
        zn,
        here,
        [
            ([(gains, True, 0, gains.shape[2])], gains_all, 0),
            ([(q, False, 0, q_half), (kv, True, q_half, kv.shape[2])], qkv_all, early),
            ([(o_shard, False, 0, o_shard.shape[1] // 2)], o_all, early),
        ]
        + [
            ([(shard, False, 0, shard.shape[1] // 2)], full, early)
            for shard, full in ((down, down_all), (gate, gate_all), (up, up_all))
        ],
        refs[61:],
    )
    count, width = tokens.shape
    columns = gate_all.shape[1]
    block = seg.shape[1]
    blocks = 2 * count // block
    per = count // block
    attention_set = [0, 1, 2]
    swap = remote(seg, seg_pair.at[c], seg_sems.at[0], seg_sems.at[1], (here[0] + 1 - 2 * c, here[1]))
    swap.start()
    seg_pair[c] = seg[...]
    work.start(attention_set)
    firsts[0].wait()
    transposed(down_turned, down)
    work.start([3])
    work.ready(attention_set)
    work.start_own(attention_set)
    for copy in firsts[1:]:
        copy.wait()
    shared = [
        share(here, src, dst, swap_sems.at[n])
        for n, (src, dst) in enumerate(((tokens, chip_tokens), (grads, chip_grads)))
    ]
    for copy in shared[0]:
        copy.start()
    work.start([4, 5])
    for copy in shared[1]:
        copy.start()
    work.start_early([1, 2])
    work.ready([3])
    work.start_own([3])
    swap.wait()
    for i in range(blocks):
        row = seg_pair[i // per, pl.ds(i % per, 1)]
        same, before = same_segment(row)
        position = jnp.sum(jnp.where(same & before, 1.0, 0.0), axis=-1, keepdims=True)
        angles = position * inverse[...]
        cosines[pl.ds(i * block, block)] = jnp.cos(angles)
        sines[pl.ds(i * block, block)] = jnp.sin(angles) * sign[...]
    saves = [
        pltpu.make_async_copy(src, dst, seg_sems.at[2 + n])
        for n, (src, dst) in enumerate(((cosines, cosines_out), (sines, sines_out), (seg_pair, seg_all)))
    ]
    for copy in saves:
        copy.start()
    work.relay(1, attention_set)
    work.relay(2, attention_set)
    work.start_early([3])
    work.relays(3, attention_set)
    work.ready([4, 5])
    work.start_own([4, 5])
    work.start_early([4])
    work.arrived(0)
    load = pltpu.make_async_copy(gains_all, gain_tiles, load_sems.at[0])
    load.start()
    load.wait()
    features = width // (4 * zn)
    for owner in range(4 * zn):
        for i in range(2):
            gain_rows[pl.ds(i, 1), pl.ds(owner * features, features)] = gain_tiles[
                pl.ds(owner * 8 + i, 1), :features
            ]
    save_gains = pltpu.make_async_copy(gain_rows, gain_out, load_sems.at[1])
    save_gains.start()
    gain_one, gain = gain_rows[pl.ds(0, 1)], gain_rows[pl.ds(1, 1)]
    for copies in shared:
        for copy in copies:
            copy.wait()
    work.arrived(1)
    work.arrived(2)
    save_gains.wait()
    half = total_refs[1]

    def attention(qkv, o, inputs, normed_one, turned, context, attended):
        queries_wide = context.shape[2]
        wide = 2 * HEAD_DIM

        def place_of(i):
            return lax.rem((1 - c) * per + i, blocks)

        def rows_at(i):
            return pl.ds(pl.multiple_of(place_of(i) * block, block), block)

        def fetch_inputs(i, slot):
            which = place_of(i)
            return pltpu.make_async_copy(
                chip_tokens.at[which // per, pl.ds(pl.multiple_of(lax.rem(which, per) * block, block), block)],
                inputs.at[slot],
                grad_sems.at[slot],
            )

        def stores(i, slot):
            return [
                pltpu.make_async_copy(buffer.at[slot], out.at[rows_at(i)], stage_sems.at[slot, n])
                for n, (buffer, out) in enumerate(
                    ((normed_one, normed_one_out), (turned, turned_out), (context, context_out))
                )
            ]

        def store_term(i, slot):
            return pltpu.make_async_copy(
                attended.at[slot],
                term.at[1 - c, pl.ds(pl.multiple_of(i * block, block), block)],
                block_sems.at[slot],
            )

        fetch_inputs(0, 0).start()
        loads = [
            pltpu.make_async_copy(qkv_all, qkv, load_sems.at[0]),
            pltpu.make_async_copy(o_all, o, load_sems.at[1]),
        ]
        for load in loads:
            load.start()
        for load in loads:
            load.wait()

        def one_block(i):
            slot = lax.rem(i, 2)
            to = rows_at(i)
            fetch_inputs(i, slot).wait()

            @pl.when(i + 1 < blocks)
            def _():
                fetch_inputs(i + 1, 1 - slot).start()

            @pl.when(i > 1)
            def _():
                for copy in stores(i - 2, slot):
                    copy.wait()

            def norm(at):
                value = inputs[slot, at].astype(F32)
                factor = lax.rsqrt(jnp.mean(value * value, axis=-1, keepdims=True) + norm_eps)
                normed_one[slot, at] = (value * factor * gain_one).astype(BF16)

            by_rows(block, norm)
            cosine, sine = cosines[to], sines[to]
            raw = product(normed_one[slot], qkv[...])
            for first in range(0, queries_wide, wide):
                value = raw[:, first : first + wide]
                turned[slot, :, pl.ds(first, wide)] = (value * cosine + partner(value) * sine).astype(BF16)
            value = raw[:, queries_wide:]
            is_key = lanes(value.shape) < HEAD_DIM
            turned[slot, :, pl.ds(queries_wide, wide)] = jnp.where(
                is_key, value * cosine + partner(value) * sine, value
            ).astype(BF16)
            which = place_of(i)
            row = seg_pair[which // per, pl.ds(lax.rem(which, per), 1)]
            attention_block(turned.at[slot], context.at[slot], queries_wide, row)
            for copy in stores(i, slot):
                copy.start()
            return slot

        def other(i):
            slot = one_block(i)
            attended[slot] = times_transposed(context[slot], o[...]).astype(BF16)
            store_term(i, slot).start()

        def own(i):
            slot = one_block(per + i)
            half[pl.ds(pl.multiple_of(i * block, block), block)] = times_transposed(
                context[slot], o[...]
            ).astype(BF16)

        loop(per, other)
        for i in range(per):
            store_term(i, i % 2).wait()
        total.core().start()
        loop(per, own)
        for i in range(blocks - 2, blocks):
            for copy in stores(i, i % 2):
                copy.wait()

    pl.run_scoped(
        attention,
        pltpu.VMEM(qkv_all.shape, BF16),
        pltpu.VMEM(o_all.shape, BF16),
        pltpu.VMEM((2, block, width), BF16),
        pltpu.VMEM((2, block, width), BF16),
        pltpu.VMEM((2, block, qkv_all.shape[1]), BF16),
        pltpu.VMEM((2, block, o_all.shape[1]), BF16),
        pltpu.VMEM((2, block, width), BF16),
    )
    total.meet(False)
    for j in (3, 4):
        work.relay(1, [j])
        work.relay(2, [j])
    work.relays(3, [3])

    def sums(mid):
        total.pair().wait_recv()

        def body(at):
            value = tokens[at].astype(F32) + total.rows(at)
            mid[at] = value
            factor = lax.rsqrt(jnp.mean(value * value, axis=-1, keepdims=True) + norm_eps)
            normed[c, at] = (value * factor * gain).astype(BF16)

        by_rows(count, body)
        save = pltpu.make_async_copy(mid, mid_out, out_sems.at[0])
        save.start()
        for copy in share(here, normed.at[c], normed, pair_sems)[1:]:
            copy.start()
        save.wait()

    def hidden(first, second, silu, slope, upward, up_grad, inputs, result, stages):
        def fetch_grads(i, slot):
            return pltpu.make_async_copy(
                chip_grads.at[i // per, pl.ds(pl.multiple_of(lax.rem(i, per) * block, block), block)],
                inputs.at[slot],
                grad_sems.at[slot],
            )

        def at_block(i):
            return pl.ds(pl.multiple_of(i * block, block), block)

        fetch_grads(0, 0).start()
        pl.run_scoped(sums, pltpu.VMEM((count, width), F32))
        work.relays(3, [4])
        work.start_early([5])
        work.arrived(3)
        load = pltpu.make_async_copy(down_all, first, load_sems.at[0])
        load.start()
        load.wait()

        def hidden_block(i):
            slot = lax.rem(i, 2)
            fetch_grads(i, slot).wait()

            @pl.when(i + 1 < blocks)
            def _():
                fetch_grads(i + 1, 1 - slot).start()

            slope[at_block(i)] = product(inputs[slot], first[...])

        loop(blocks, hidden_block)
        work.relay(1, [5])
        work.relay(2, [5])
        upward[...] = jnp.zeros_like(upward)
        work.arrived(4)
        load = pltpu.make_async_copy(gate_all, second, load_sems.at[1])
        load.start()
        share(here, normed.at[c], normed, pair_sems)[1].wait()
        save = pltpu.make_async_copy(normed, normed_out, out_sems.at[1])
        save.start()
        load.wait()

        def gate_block(i):
            result[...] = product(normed[i // per, at_block(lax.rem(i, per))], second[...])

            def body(at):
                to = pl.ds(pl.multiple_of(i * block + at.start, 16), at.size)
                gated = result[at]
                grad = slope[to]
                sigmoid = 1.0 / (1.0 + jnp.exp(-gated))
                silu[to] = gated * sigmoid
                up_grad[to] = (grad * gated * sigmoid).astype(BF16)
                slope[to] = grad * (sigmoid * (1.0 + gated * (1.0 - sigmoid)))

            by_rows(block, body)

        loop(blocks, gate_block)
        save_up = pltpu.make_async_copy(up_grad, up_grad_out, out_sems.at[2])
        save_up.start()
        work.relays(3, [5])
        group = width // zn

        def up_rows(k):
            o = farthest_first(zn, z, zn - 1 - k)
            at = pl.ds(pl.multiple_of(o * group, group), group)
            work.x_late(5, o).wait_recv()
            load = pltpu.make_async_copy(up_all.at[at], first.at[at], load_sems.at[0])
            load.start()
            load.wait()

            def up_part(i):
                rows = normed[i // per, at_block(lax.rem(i, per)), at]
                upward[at_block(i)] += product(rows, first[at])

            loop(blocks, up_part)

        loop(zn, up_rows)

        def stores(i, slot):
            to = at_block(i)
            return (
                pltpu.make_async_copy(stages.at[slot, 0], act_out.at[to], stage_sems.at[slot, 0]),
                pltpu.make_async_copy(stages.at[slot, 1], gate_grad_out.at[to], stage_sems.at[slot, 1]),
            )

        def up_block(i):
            slot = lax.rem(i, 2)

            @pl.when(i > 1)
            def _():
                for copy in stores(i - 2, slot):
                    copy.wait()

            def body(at):
                to = pl.ds(pl.multiple_of(i * block + at.start, 16), at.size)
                stages[slot, 0, at] = (silu[to] * upward[to]).astype(BF16)
                stages[slot, 1, at] = (slope[to] * upward[to]).astype(BF16)

            by_rows(block, body)
            for copy in stores(i, slot):
                copy.start()

        loop(blocks, up_block)
        for i in range(max(blocks - 2, 0), blocks):
            for copy in stores(i, i % 2):
                copy.wait()
        save.wait()
        save_up.wait()

    pl.run_scoped(
        hidden,
        pltpu.VMEM((width, columns), BF16),
        pltpu.VMEM((width, columns), BF16),
        pltpu.VMEM((2 * count, columns), F32),
        pltpu.VMEM((2 * count, columns), F32),
        pltpu.VMEM((2 * count, columns), F32),
        pltpu.VMEM((2 * count, columns), BF16),
        pltpu.VMEM((2, block, width), BF16),
        pltpu.VMEM((block, columns), F32),
        pltpu.VMEM((2, 2, block, columns), BF16),
    )
    work.finish()
    total.finish()
    for copy in saves:
        copy.wait()


def fetch(pairs, sems):
    copies = [pltpu.make_async_copy(src, dst, sems.at[i]) for i, (src, dst) in enumerate(pairs)]
    for copy in copies:
        copy.start()
    return copies


def backward(zn, early, *refs):
    normed_two, gate_grad, chip_grads, activated, gate_all, up_all, down_all, mid_in, up_grad = refs[:9]
    normed_one, context, turned_all, o_all, qkv_all, cosines, sines, tokens_in, rows_of, gain_rows = refs[9:19]
    down_out, gate_out, up_out, o_out, q_out, kv_out, out, in_grad, gain_out = refs[19:28]
    mid_grad_all, branch_all, qkv_back, in_term, out_term, back_term = refs[28:34]
    down, gate, up, o_sums, qkv_sums = refs[34:39]
    n = SCATTER_BUFFERS
    buffers, refs = refs[39 : 39 + 4 * n], refs[39 + 4 * n :]
    back_refs, front_refs, in_refs = refs[:4], refs[4:8], refs[8:11]
    gain_refs, (one_sum, two_sum), refs = refs[11:15], refs[15:17], refs[17:]
    fetch_sems, out_sems, pair_sems, weight_sems, stage_sems, block_sems, back_sems, credit = refs[:8]
    here = place()
    z, c = here[2], here[4]
    chip, width = chip_grads.shape
    count = chip // 2
    block = rows_of.shape[2]
    blocks = chip // block
    per = blocks // 2
    qkv_wide, q_half = qkv_all.shape[1], o_all.shape[1]
    enter(zn, here)
    branch, out_rows, in_rows = back_refs[0], front_refs[0], in_refs[0]
    back = Total(here, back_term, *back_refs)
    front = Total(here, out_term, *front_refs)
    total = Total(here, in_term, in_refs[0], back_refs[1], in_refs[1], in_refs[2])
    gains = Gains(zn, here, *gain_refs)
    work = Scatter(
        zn,
        here,
        early,
        [
            (down, buffers[:n], [(down_out, False, 0, down_out.shape[1] // 2)]),
            (gate, buffers[n : 2 * n], [(gate_out, False, 0, gate_out.shape[1] // 2)]),
            (up, buffers[:n], [(up_out, False, 0, up_out.shape[1] // 2)]),
            (o_sums, buffers[2 * n : 3 * n], [(o_out, False, 0, q_half)]),
            (
                qkv_sums,
                buffers[3 * n :],
                [(q_out, False, 0, q_half), (kv_out, True, q_half, kv_out.shape[2])],
            ),
        ],
        refs[8:],
    )
    def feature_terms(factors, term):
        def run(*refs):
            lefts, weights, stages = refs[:-2], refs[-2], refs[-1]
            group = weights.shape[2]
            loads = fetch([(left, ref) for (left, _), ref in zip(factors, lefts)], fetch_sems)

            def fetch_weights(i, slot):
                at = pl.ds(pl.multiple_of(i * group, group), group)
                return [
                    pltpu.make_async_copy(full.at[at], weights.at[slot, k], weight_sems.at[slot, k])
                    for k, (_, full) in enumerate(factors)
                ]

            def stores(i, slot):
                to = pl.ds(pl.multiple_of(i * group, group), group)
                return [
                    pltpu.make_async_copy(
                        stages.at[slot, pl.ds(half * count, count)], term.at[half, :, to], stage_sems.at[slot, half]
                    )
                    for half in range(2)
                ]

            for copy in fetch_weights(0, 0):
                copy.start()
            for load in loads:
                load.wait()

            def step(i):
                slot = lax.rem(i, 2)
                for copy in fetch_weights(i, slot):
                    copy.wait()

                @pl.when(i + 1 < width // group)
                def _():
                    for copy in fetch_weights(i + 1, 1 - slot):
                        copy.start()

                @pl.when(i > 1)
                def _():
                    for copy in stores(i - 2, slot):
                        copy.wait()

                value = times_transposed(lefts[0][...], weights[slot, 0])
                for k in range(1, len(lefts)):
                    value = value + times_transposed(lefts[k][...], weights[slot, k])
                stages[slot] = value.astype(BF16)
                for copy in stores(i, slot):
                    copy.start()

            loop(width // group, step)
            for i in range(width // group - 2, width // group):
                for copy in stores(i, i % 2):
                    copy.wait()

        pl.run_scoped(
            run,
            *[pltpu.VMEM((chip, wide), BF16)] * len(factors),
            pltpu.VMEM((2, len(factors), 256, wide), BF16),
            pltpu.VMEM((2, chip, 256), BF16),
        )

    wide = down.shape[2]
    operands = [pltpu.VMEM((chip, width), BF16), pltpu.VMEM((chip, wide), BF16), pltpu.VMEM((2,) + down.shape[1:], BF16)]

    def terms_of(j, left_all, right_all):
        def run(left, right, stage):
            for load in fetch(((left_all, left), (right_all, right)), fetch_sems):
                load.wait()
            work.make(j, left, right, stage)

        pl.run_scoped(run, *operands)

    terms_of(0, chip_grads, activated)
    for g in range(3):
        work.early_third(0, g)
    feature_terms([(gate_grad, gate_all), (up_grad, up_all)], back_term)
    back.start()
    work.late_third(0, 0)
    feature_terms([(activated, down_all)], out_term)
    back.meet()
    front.start()
    work.late_third(0, 1)
    work.early_home(0)
    work.late_third(0, 2)
    terms_of(1, normed_two, gate_grad)
    work.early_third(1, 0)

    def sums(mid, mid_grad, grads):
        for load in fetch(
            (
                (mid_in, mid),
                (chip_grads.at[pl.ds(pl.multiple_of(c * count, 16), count)], grads),
            ),
            fetch_sems,
        ):
            load.wait()
        gain = gain_rows[pl.ds(1, 1)]
        two_sum[...] = jnp.zeros_like(two_sum)

        def body_gain(at):
            value = mid[at]
            factor = lax.rsqrt(jnp.mean(value * value, axis=-1, keepdims=True) + norm_eps)
            two_sum[...] += jnp.sum(back.half[at].astype(F32) * (value * factor), axis=0, keepdims=True)

        by_rows(count, body_gain)
        work.late_third(1, 0)
        work.early_third(1, 1)
        work.early_third(1, 2)
        work.home(0)
        work.done(0)
        work.lend(credit)
        front.meet()
        back.pair().wait_recv()

        def body(at):
            value = mid[at]
            factor = lax.rsqrt(jnp.mean(value * value, axis=-1, keepdims=True) + norm_eps)
            scaled = back.rows(at) * gain
            result = (
                grads[at].astype(F32)
                + factor * scaled
                - value * (factor * factor * factor) * jnp.mean(scaled * value, axis=-1, keepdims=True)
            )
            mid_grad[at] = result
            branch[at] = result.astype(BF16)

        by_rows(count, body)
        save = pltpu.make_async_copy(mid_grad, mid_grad_all, out_sems.at[0])
        save.start()
        for copy in share(here, branch, branch_all, pair_sems):
            copy.start()
        work.late_third(1, 1)
        save.wait()

    pl.run_scoped(
        sums, pltpu.VMEM((count, width), F32), pltpu.VMEM((count, width), F32), pltpu.VMEM((count, width), BF16)
    )

    def middle_terms(left, right, stage):
        for copy in share(here, branch, branch_all, pair_sems):
            copy.wait()
        right_o = right.at[:, pl.ds(0, q_half)]
        loads = fetch(
            ((branch_all.at[0], left.at[pl.ds(0, count)]), (branch_all.at[1], left.at[pl.ds(count, count)])),
            fetch_sems,
        )
        loads.append(pltpu.make_async_copy(context, right_o, fetch_sems.at[2]))
        loads[2].start()
        for load in loads:
            load.wait()
        work.make(3, left, right_o, stage)
        loads = fetch(((normed_two, left), (up_grad, right)), fetch_sems)
        work.early_third(3, 0)
        work.late_third(1, 2)
        for load in loads:
            load.wait()
        work.borrow(credit)
        work.make(2, left, right, stage)

    pl.run_scoped(middle_terms, *operands)
    work.early_third(2, 0)

    def attention(o, qkv, inputs, turned, grads, backs, terms_out, cosine, sine, accumulators):
        def which(i):
            return lax.rem((1 - c) * per + i, blocks)

        def rows_at(i):
            return pl.ds(pl.multiple_of(i * block, block), block)

        def fetches(i, slot):
            b = which(i)
            sources = (
                (branch_all.at[b // per, rows_at(lax.rem(b, per))], inputs),
                (turned_all.at[rows_at(b)], turned),
                (cosines.at[rows_at(b)], cosine),
                (sines.at[rows_at(b)], sine),
            )
            return [
                pltpu.make_async_copy(source, buffer.at[slot], block_sems.at[slot, k])
                for k, (source, buffer) in enumerate(sources)
            ]

        def stores(i, slot):
            b = which(i)
            return [
                pltpu.make_async_copy(backs.at[slot], qkv_back.at[rows_at(b)], back_sems.at[slot, 0]),
                pltpu.make_async_copy(
                    terms_out.at[slot], in_term.at[b // per, rows_at(lax.rem(b, per))], back_sems.at[slot, 1]
                ),
            ]

        loads = fetch(((o_all, o), (qkv_all, qkv)), fetch_sems)
        for copy in fetches(0, 0):
            copy.start()
        for load in loads:
            load.wait()

        def step(i):
            slot = lax.rem(i, 2)

            @pl.when(i == per)
            def _():
                for done in range(per):
                    for copy in stores(done, done % 2):
                        copy.wait()
                total.core().start()
                work.early_third(2, 2)

            @pl.when(i == 1)
            def _():
                work.early_third(3, 1)
                work.early_third(2, 1)

            @pl.when(i == blocks - 1)
            def _():
                work.late_third(2, 0)

            for copy in fetches(i, slot):
                copy.wait()

            @pl.when(i + 1 < blocks)
            def _():
                for copy in fetches(i + 1, 1 - slot):
                    copy.start()

            grads[...] = product(inputs[slot], o[...]).astype(BF16)
            attention_block_back(
                turned.at[slot],
                grads,
                backs.at[slot],
                accumulators,
                q_half,
                rows_of[which(i) // per, pl.ds(lax.rem(which(i), per), 1)],
                cosine[slot],
                sine[slot],
            )
            terms_out[slot] = times_transposed(backs[slot], qkv[...]).astype(BF16)
            for copy in stores(i, slot):
                copy.start()

        loop(blocks, step)
        for i in range(per, blocks):
            for copy in stores(i, i % 2):
                copy.wait()

    pl.run_scoped(
        attention,
        pltpu.VMEM(o_all.shape, BF16),
        pltpu.VMEM(qkv_all.shape, BF16),
        pltpu.VMEM((2, block, width), BF16),
        pltpu.VMEM((2, block, qkv_wide), BF16),
        pltpu.VMEM((block, q_half), BF16),
        pltpu.VMEM((2, block, qkv_wide), BF16),
        pltpu.VMEM((2, block, width), BF16),
        pltpu.VMEM((2, block, 2 * HEAD_DIM), F32),
        pltpu.VMEM((2, block, 2 * HEAD_DIM), F32),
        pltpu.VMEM((4, block, 2 * HEAD_DIM), F32),
    )
    back.finish()
    total.load().start()

    def meeting(tokens):
        load = fetch(((tokens_in, tokens),), fetch_sems)[0]
        total.meet(send=False)
        load.wait()
        one_sum[...] = jnp.zeros_like(one_sum)

        def body_gain(at):
            value = tokens[at].astype(F32)
            factor = lax.rsqrt(jnp.mean(value * value, axis=-1, keepdims=True) + norm_eps)
            one_sum[...] += jnp.sum(total.half[at].astype(F32) * (value * factor), axis=0, keepdims=True)

        by_rows(count, body_gain)

    pl.run_scoped(meeting, pltpu.VMEM((count, width), BF16))
    gains.start([one_sum, two_sum])
    gains.swapped(0)
    total.pair().start()
    work.early_third(3, 2)
    work.late_third(2, 1)

    def output(mid):
        load = fetch(((mid_in, mid),), fetch_sems)[0]
        front.pair().wait_recv()
        load.wait()

        def body_out(at):
            out_rows[at] = (mid[at] + front.rows(at)).astype(BF16)

        by_rows(count, body_out)

    pl.run_scoped(output, pltpu.VMEM((count, width), F32))
    save_out = pltpu.make_async_copy(out_rows, out, out_sems.at[1])
    save_out.start()
    work.late_third(3, 0)
    work.late_third(2, 2)
    work.early_home(2)
    work.early_home(1)

    def last_terms(left, right, stage):
        right_qkv = right.at[:, pl.ds(0, qkv_wide)]
        for load in fetch(((normed_one, left), (qkv_back, right_qkv)), fetch_sems):
            load.wait()
        gains.swapped(1)
        work.make(4, left, right_qkv, stage)

    pl.run_scoped(last_terms, *operands)
    work.early_third(4, 0)
    work.home(1)
    work.late_third(4, 0)
    work.early_third(4, 1)
    work.early_third(4, 2)
    work.early_home(3)
    work.late_third(3, 1)
    work.home(2)
    gains.swapped(2)
    gains.run()
    work.late_third(4, 1)
    work.late_third(4, 2)
    work.late_third(3, 2)
    work.early_home(4)

    def inputs_back(mid_grad, tokens):
        loads = fetch(((mid_grad_all, mid_grad), (tokens_in, tokens)), fetch_sems)
        gain = gain_rows[pl.ds(0, 1)]
        total.pair().wait_recv()
        for load in loads:
            load.wait()

        def body(at):
            value = tokens[at].astype(F32)
            factor = lax.rsqrt(jnp.mean(value * value, axis=-1, keepdims=True) + norm_eps)
            scaled = total.rows(at) * gain
            in_rows[at] = (
                mid_grad[at]
                + factor * scaled
                - value * (factor * factor * factor) * jnp.mean(scaled * value, axis=-1, keepdims=True)
            ).astype(BF16)

        by_rows(count, body)

    pl.run_scoped(inputs_back, pltpu.VMEM((count, width), F32), pltpu.VMEM((count, width), BF16))
    save_in = pltpu.make_async_copy(in_rows, in_grad, out_sems.at[0])
    save_in.start()
    gains.finish(gain_out)
    work.home(4)
    work.home(3)
    for j in (1, 2, 3, 4):
        work.done(j)
    front.finish()
    total.finish()
    save_out.wait()
    save_in.wait()


def settle(*refs):
    turned, plain, kv, gains = refs[:2], refs[2:7], refs[7], refs[8]
    turned_out, plain_out, (k_out, v_out, one_out, two_out) = refs[9:11], refs[11:16], refs[16:20]
    turned_in, turned_to, plain_at, (kv_at, k_at, v_at) = refs[20:22], refs[22:24], refs[24:29], refs[29:32]
    load_sems, store_sems = refs[32:]
    pairs = list(zip(plain, plain_at)) + list(zip(turned, turned_in)) + [(kv, kv_at)]
    loads = [pltpu.make_async_copy(src, dst, load_sems.at[n]) for n, (src, dst) in enumerate(pairs)]
    for n in (0, 1, 5, 3, 4, 2, 6, 7):
        loads[n].start()
    stores = []

    def send(src, dst):
        stores.append(pltpu.make_async_copy(src, dst, store_sems.at[len(stores)]))
        stores[-1].start()

    def pass_on(n):
        loads[n].wait()
        send(plain_at[n], plain_out[n])

    def turn(n, first, last):
        src, dst = turned_in[n], turned_to[n]

        def body(i):
            at = pl.ds(pl.multiple_of((first + i) * 128, 128), 128)
            dst[at, :] = src[:, at].T

        loop(last - first, body)

    pass_on(0)
    pass_on(1)
    groups = turned_in[0].shape[1] // 128
    loads[5].wait()
    turn(0, 0, groups // 2)
    pass_on(3)
    pass_on(4)
    turn(0, groups // 2, groups)
    send(turned_to[0], turned_out[0])
    pass_on(2)
    loads[6].wait()
    turn(1, 0, turned_in[1].shape[1] // 128)
    send(turned_to[1], turned_out[1])
    loads[7].wait()
    one, two = kv_at[0], kv_at[1]
    is_key = lanes(one.shape) < HEAD_DIM
    k_at[...] = jnp.where(is_key, one, pltpu.roll(two, HEAD_DIM, 1))
    v_at[...] = jnp.where(is_key, pltpu.roll(one, HEAD_DIM, 1), two)
    send(k_at, k_out)
    send(v_at, v_out)
    features = one_out.shape[1]
    for owner in range(4):

        @pl.when(lax.rem(lax.axis_index("dp"), 4) == owner)
        def _():
            at = pl.ds(owner * features, features)
            one_out[...] = gains[pl.ds(0, 1), at]
            two_out[...] = gains[pl.ds(1, 1), at]

    for copy in stores:
        copy.wait()


def call(kernel, name, collective_id, operands, specs, outs, out_specs, scratch, order=None):
    results = pl.pallas_call(
        kernel,
        out_shape=[jax.ShapeDtypeStruct(shape, dtype) for shape, dtype in outs],
        in_specs=specs,
        out_specs=out_specs,
        scratch_shapes=scratch,
        name=name,
        compiler_params=pltpu.CompilerParams(
            collective_id=collective_id, has_side_effects=True, vmem_limit_bytes=255 << 18
        ),
    )(*operands)
    return results if order is None else [results[i] for i in order]


def rotate(vectors, cosine, sine_rows):
    half = vectors.shape[-1] // 2
    first, second = vectors[..., :half], vectors[..., half:]
    return jnp.concatenate(
        [first * cosine - second * sine_rows, second * cosine + first * sine_rows], axis=-1
    )


def product(one, two):
    return jnp.dot(one, two, preferred_element_type=F32)


def times_transposed(one, two):
    return lax.dot_general(one, two, (((1,), (1,)), ((), ())), preferred_element_type=F32)


def inner_rows(one, two):
    return lax.dot_general(one, two, (((0,), (0,)), ((), ())), preferred_element_type=F32)


def einsum(form, one, two):
    return jnp.einsum(form, one, two, preferred_element_type=F32)


def halves(weight):
    rows, columns = weight.shape
    return weight.reshape(rows, 2, columns // 2).transpose(1, 0, 2)


def joined(pair):
    return jnp.concatenate([pair[0], pair[1]], axis=1)


def local(
    dp,
    tokens,
    seg_ids,
    q_weight,
    k_weight,
    v_weight,
    o_weight,
    attn_gain,
    gate_weight,
    up_weight,
    down_weight,
    mlp_gain,
    out_grad,
):
    zn = dp // 4
    units = zn * 2
    count, width = tokens.shape
    rows = q_weight.shape[0]
    blocks, block_rows = 2 * seg_ids.shape[0], seg_ids.shape[1]
    q_half, kv_half = q_weight.shape[1] // 2, k_weight.shape[1] // 2
    ff_half = gate_weight.shape[1] // 2
    qkv_half = q_half + 2 * kv_half
    heads, groups = q_half // HEAD_DIM, kv_half // HEAD_DIM
    early = 2 * rows // 48 * 8
    early_sums = max(16, 2 * rows * 3 // 256 * 16)

    chip = 2 * count
    inverse = 1.0 / 10000.0 ** (np.arange(0, HEAD_DIM, 2, dtype=np.float32) / HEAD_DIM)
    inverse = np.tile(inverse.astype(np.float32), 4)[None]
    sign = np.tile(np.repeat(np.array([-1.0, 1.0], np.float32), HEAD_DIM // 2), 2)[None]
    (
        qkv_full,
        o_full,
        grads_chip,
        segment,
        gate_full,
        up_full,
        down_full,
        mid,
        normed_two,
        activated,
        gate_grad,
        up_grad,
        normed,
        turned,
        context,
        cosines,
        sines,
        gain_rows,
    ) = call(
        functools.partial(forward, zn, early),
        "forward",
        0,
        (
            q_weight,
            k_weight,
            v_weight,
            o_weight,
            attn_gain[None],
            mlp_gain[None],
            tokens,
            out_grad,
            seg_ids,
            gate_weight,
            up_weight,
            down_weight,
            inverse,
            sign,
        ),
        [VMEM] * 6 + [ANY] * 2 + [VMEM] + [ANY] * 3 + [VMEM] * 2,
        [
            ((width, qkv_half), BF16),
            ((width, q_half), BF16),
            ((units * 16, 128), F32),
            ((2, count, width), BF16),
            ((2, count, width), BF16),
            ((2,) + seg_ids.shape, jnp.int32),
        ]
        + [((width, ff_half), BF16)] * 3
        + [((count, width), F32), ((2, count, width), BF16)]
        + [((chip, ff_half), BF16)] * 3
        + [((2, count, width), BF16)]
        + [((chip, width), BF16), ((chip, qkv_half), BF16), ((chip, q_half), BF16)]
        + [((chip, 2 * HEAD_DIM), F32)] * 2
        + [((8, width), F32)],
        [ANY] * 21,
        total_buffers(count, width)
        + [
            pltpu.VMEM((2, count, width), BF16),
            DMA((3,)),
            DMA((3,)),
            DMA((2,)),
            DMA((2,)),
            DMA((2, 3)),
            DMA((2,)),
            pltpu.VMEM((chip, 2 * HEAD_DIM), F32),
            pltpu.VMEM((chip, 2 * HEAD_DIM), F32),
            pltpu.VMEM((2,) + seg_ids.shape, jnp.int32),
            pltpu.VMEM((units * 16, 128), F32),
            pltpu.VMEM((8, width), F32),
            DMA((2, 3)),
            DMA((5,)),
            pltpu.VMEM((2, rows, 2 * kv_half), BF16),
            pltpu.VMEM((2, 8, 128), F32),
            pltpu.VMEM((rows, 2 * q_half), BF16),
            pltpu.VMEM((rows, 2 * ff_half), BF16),
            pltpu.VMEM((count, width), BF16),
            pltpu.VMEM((count, width), BF16),
            pltpu.VMEM((rows, 2 * ff_half), BF16),
            pltpu.VMEM((rows, 2 * ff_half), BF16),
            pltpu.VMEM((2 * ff_half, rows), BF16),
            DMA((5,)),
        ]
        + gather_sems(6, 7, zn),
        order=(0, 1, 4, 5, 6, 7, 8, 9, 10, 11, 12, 13, 15, 16, 17, 18, 19, 20),
    )
    grads_chip = grads_chip.reshape(chip, width)
    normed_two = normed_two.reshape(chip, width)

    down_sum, gate_sum, up_sum, o_sum, q_sum, kv_sum, out, in_grad, gain_sums = call(
        functools.partial(backward, zn, early_sums),
        "backward",
        1,
        (
            normed_two,
            gate_grad,
            grads_chip,
            activated,
            gate_full,
            up_full,
            down_full,
            mid,
            up_grad,
            normed,
            context,
            turned,
            o_full,
            qkv_full,
            cosines,
            sines,
            tokens,
            segment,
            gain_rows,
        ),
        [ANY] * 17 + [VMEM] * 2,
        [((rows, 2 * ff_half), F32)] * 3
        + [
            ((rows, 2 * q_half), F32),
            ((rows, 2 * q_half), F32),
            ((2, rows, 2 * kv_half), F32),
            ((count, width), BF16),
            ((count, width), BF16),
            ((8, 4 * rows), F32),
            ((count, width), F32),
            ((2, count, width), BF16),
            ((chip, qkv_half), BF16),
            ((2, count, width), BF16),
            ((2, count, width), BF16),
            ((2, count, width), BF16),
        ]
        + [((zn, 4 * rows, ff_half), BF16)] * 3
        + [((zn, 4 * rows, q_half), BF16), ((zn, 4 * rows, qkv_half), BF16)],
        [ANY] * 8 + [VMEM] + [ANY] * 11,
        scatter_buffers(
            [(2 * rows, ff_half), (2 * rows, ff_half), (2 * rows, q_half), (2 * rows, qkv_half)], early_sums, zn
        )
        + total_buffers(count, width) * 2
        + [pltpu.VMEM((count, width), BF16)] * 2
        + [DMA((5,))]
        + gain_buffers(zn, 4 * rows)
        + [pltpu.VMEM((1, width), F32)] * 2
        + [
            DMA((4,)),
            DMA((2,)),
            DMA((3,)),
            DMA((2, 2)),
            DMA((2, 2)),
            DMA((2, 4)),
            DMA((2, 2)),
            pltpu.SemaphoreType.REGULAR,
        ]
        + scatter_sems(5, 6, zn),
        order=range(9),
    )
    plain = (gate_sum, up_sum, q_sum, out, in_grad)
    turned = (down_sum, o_sum)
    shapes = [ref.shape[::-1] for ref in turned]
    results = pl.pallas_call(
        settle,
        out_shape=[jax.ShapeDtypeStruct(shape, F32) for shape in shapes]
        + [jax.ShapeDtypeStruct(ref.shape, ref.dtype) for ref in plain]
        + [jax.ShapeDtypeStruct((rows, 2 * kv_half), F32)] * 2
        + [jax.ShapeDtypeStruct((1, rows), F32)] * 2,
        in_specs=[pl.BlockSpec(memory_space=pltpu.HBM)] * 8 + [VMEM],
        out_specs=[pl.BlockSpec(memory_space=pltpu.HBM)] * 9 + [VMEM] * 2,
        scratch_shapes=[pltpu.VMEM(ref.shape, F32) for ref in turned]
        + [pltpu.VMEM(shape, F32) for shape in shapes]
        + [pltpu.VMEM(ref.shape, ref.dtype) for ref in plain]
        + [pltpu.VMEM(kv_sum.shape, F32)]
        + [pltpu.VMEM((rows, 2 * kv_half), F32)] * 2
        + [DMA((8,)), DMA((9,))],
        name="settle",
        compiler_params=pltpu.CompilerParams(vmem_limit_bytes=62 << 20),
    )(*turned, *plain, kv_sum, gain_sums)
    down_final, o_final, gate_final, up_final, q_final, out, in_grad, k_final, v_final, one, two = results
    return (
        out,
        in_grad,
        q_final,
        k_final,
        v_final,
        o_final,
        one.reshape(rows),
        gate_final,
        up_final,
        down_final,
        two.reshape(rows),
    )


def solution(mesh):
    arguments = (
        P("dp", None),
        P("dp", None),
        P("dp", "tensor"),
        P("dp", "tensor"),
        P("dp", "tensor"),
        P("tensor", "dp"),
        P("dp"),
        P("dp", "tensor"),
        P("dp", "tensor"),
        P("tensor", "dp"),
        P("dp"),
        P("dp", None),
    )
    results = (
        P("dp", None),
        P("dp", None),
        P("dp", "tensor"),
        P("dp", "tensor"),
        P("dp", "tensor"),
        P("tensor", "dp"),
        P("dp"),
        P("dp", "tensor"),
        P("dp", "tensor"),
        P("tensor", "dp"),
        P("dp"),
    )
    return jax.shard_map(
        functools.partial(local, mesh.shape["dp"]),
        mesh=mesh,
        in_specs=arguments,
        out_specs=results,
        check_vma=False,
    )
```

```python
import functools

import jax
import jax.numpy as jnp
import numpy as np
from jax import lax
from jax.experimental import pallas as pl
from jax.experimental.pallas import tpu as pltpu
from jax.sharding import PartitionSpec as P

HEAD_DIM = 64
norm_eps = 1e-05
MESH = pl.DeviceIdType.MESH
ANY = pl.BlockSpec(memory_space=pl.ANY)
VMEM = pl.BlockSpec(memory_space=pltpu.VMEM)
DMA = pltpu.SemaphoreType.DMA
F32 = jnp.float32
BF16 = jnp.bfloat16


def place():
    d = lax.axis_index("dp")
    t = lax.axis_index("tensor")
    return d, t, d // 4, lax.rem(d // 2, 2), lax.rem(d, 2)


def enter(zn, here):
    d, t, z, x, c = here
    bar = pltpu.get_barrier_semaphore()

    def hail(device):
        pl.semaphore_signal(bar, inc=1, device_id=device, device_id_type=MESH)

    hail((d + 1 - 2 * c, t))
    hail((d + 2 - 4 * x, t))
    hail((d, 1 - t))

    @pl.when(z > 0)
    def _():
        hail((d - 4, t))

    @pl.when(z < zn - 1)
    def _():
        hail((d + 4, t))

    pl.semaphore_wait(bar, 5 - (z == 0).astype(jnp.int32) - (z == zn - 1).astype(jnp.int32))


def farthest_first(zn, z, i):
    up = 1 - (2 * z) // zn
    longer = up * (zn - 1 - z) + (1 - up) * z
    shorter = zn - 1 - longer
    rest = i - (longer - shorter)
    return jnp.where(
        rest < 0,
        z + (2 * up - 1) * (longer - i),
        z + (1 - 2 * lax.rem(jnp.maximum(rest, 0), 2)) * (shorter - jnp.maximum(rest, 0) // 2),
    )


def loop(count, body):
    def step(i, carry):
        body(i)
        return carry

    lax.fori_loop(0, count, step, 0)


def remote(src, dst, send, recv, device):
    return pltpu.make_async_remote_copy(
        src_ref=src, dst_ref=dst, send_sem=send, recv_sem=recv, device_id=device, device_id_type=MESH
    )


def by_rows(count, body, block=16):
    def step(i, carry):
        body(pl.ds(pl.multiple_of(i * block, block), block))
        return carry

    lax.fori_loop(0, count // block, step, 0)


def gather_sems(n, sources, zn):
    return [
        DMA((sources,)),
        DMA((sources,)),
        DMA((sources,)),
        DMA((n, zn)),
        DMA((n, zn)),
        DMA((n,)),
        DMA((n,)),
        DMA((n, 2, zn)),
        DMA((n, zn)),
        DMA((n, 2, zn)),
        DMA((n, zn)),
    ]


def part(ref, core, paired):
    if paired:
        return ref.at[core]
    columns = ref.shape[1] // 2
    return ref.at[:, pl.ds(pl.multiple_of(core * columns, columns), columns)]


class Gather:
    def __init__(self, zn, here, arrays, sems):
        self.zn, self.here = zn, here
        self.full = [full for _, full, _ in arrays]
        self.early = [early for _, _, early in arrays]
        self.sources = [
            (j, i) + source for j, (sources, _, _) in enumerate(arrays) for i, source in enumerate(sources)
        ]
        (
            self.loc,
            self.cs,
            self.cr,
            self.xs,
            self.xr,
            self.es,
            self.er,
            self.zs,
            self.zr,
            self.bs,
            self.br,
        ) = sems

    def unit(self, j, unit, first, count):
        rows = self.full[j].shape[0] // (2 * self.zn)
        return pl.ds(pl.multiple_of(unit * rows + first, 8), count)

    def rows(self, j, unit, early):
        rows = self.full[j].shape[0] // (2 * self.zn)
        late = rows - self.early[j]
        first, count = {None: (0, rows), True: (late, rows - late), False: (0, late)}[early]
        return self.full[j].at[self.unit(j, unit, first, count)]

    def mine(self, s):
        d, t, z, x, c = self.here
        j, _, shard, paired, first, columns = self.sources[s]
        rows = self.full[j].shape[0] // (4 * self.zn)
        return self.full[j].at[self.unit(j, z * 2 + x, c * rows, rows), pl.ds(first, columns)]

    def keep(self, s):
        _, _, shard, paired, _, _ = self.sources[s]
        return pltpu.make_async_copy(part(shard, self.here[4], paired), self.mine(s), self.loc.at[s])

    def give(self, s):
        d, t, z, x, c = self.here
        _, _, shard, paired, _, _ = self.sources[s]
        return remote(
            part(shard, 1 - c, paired), self.mine(s), self.cs.at[s], self.cr.at[s], (d + 1 - 2 * c, t)
        )

    def x_late(self, j, o):
        d, t, z, x, c = self.here
        ref = self.rows(j, o * 2 + x, False)
        return remote(ref, ref, self.xs.at[j, o], self.xr.at[j, o], (d + 2 - 4 * x, t))

    def x_early(self, j):
        d, t, z, x, c = self.here
        ref = self.rows(j, z * 2 + x, True)
        return remote(ref, ref, self.es.at[j], self.er.at[j], (d + 2 - 4 * x, t))

    def along(self, j, o, down):
        d, t, z, x, c = self.here
        ref = self.rows(j, o * 2 + x, None)
        return remote(ref, ref, self.zs.at[j, down, o], self.zr.at[j, o], (d + 4 - 8 * down, t))

    def along_early(self, j, o, down):
        d, t, z, x, c = self.here
        ref = self.rows(j, o * 2 + 1 - x, True)
        return remote(ref, ref, self.bs.at[j, down, o], self.br.at[j, o], (d + 4 - 8 * down, t))

    def start(self, arrays):
        for s, source in enumerate(self.sources):
            if source[0] in arrays:
                self.give(s).start()
                self.keep(s).start()

    def ready(self, arrays):
        for j in arrays:
            for s, source in enumerate(self.sources):
                if source[0] == j:
                    self.keep(s).wait()
                    self.give(s).wait_recv()
            if self.early[j]:
                self.x_early(j).start()

    def start_own(self, arrays):
        z, zn = self.here[2], self.zn
        for j in arrays:
            self.x_late(j, z).start()

            @pl.when(z < zn - 1)
            def _():
                self.along(j, z, 0).start()

            @pl.when(z > 0)
            def _():
                self.along(j, z, 1).start()

    def start_early(self, arrays):
        z, zn = self.here[2], self.zn
        for j in arrays:
            if self.early[j]:
                self.x_early(j).wait_recv()

                @pl.when(z < zn - 1)
                def _():
                    self.along_early(j, z, 0).start()

                @pl.when(z > 0)
                def _():
                    self.along_early(j, z, 1).start()

    def relay(self, k, arrays):
        z, zn = self.here[2], self.zn
        o = farthest_first(zn, z, zn - 1 - k)
        down = (o > z).astype(jnp.int32)
        more = ((o < z) & (z < zn - 1)) | ((o > z) & (z > 0))
        for j in arrays:
            self.along(j, o, down).wait_recv()

            @pl.when(more)
            def _():
                self.along(j, o, down).start()

            self.x_late(j, o).start()
            if self.early[j]:
                self.along_early(j, o, down).wait_recv()

                @pl.when(more)
                def _():
                    self.along_early(j, o, down).start()

    def relays(self, first, arrays):
        loop(max(self.zn - first, 0), lambda i: self.relay(first + i, arrays))

    def arrived(self, j):
        loop(self.zn, lambda o: self.x_late(j, o).wait_recv())

    def finish(self):
        z, zn = self.here[2], self.zn
        for s in range(len(self.sources)):
            self.give(s).wait_send()
        for j in range(len(self.full)):
            if self.early[j]:
                self.x_early(j).wait_send()

            def step(o, j=j):
                self.x_late(j, o).wait_send()

                def sent(down):
                    self.along(j, o, down).wait_send()
                    if self.early[j]:
                        self.along_early(j, o, down).wait_send()

                @pl.when((o <= z) & (z < zn - 1))
                def _():
                    sent(0)

                @pl.when((o >= z) & (z > 0))
                def _():
                    sent(1)

            loop(zn, step)


def scatter_sems(n, outs, zn):
    return [
        DMA((n, zn)),
        DMA((n, zn)),
        DMA((n, zn)),
        DMA((n, zn)),
        DMA((n, zn)),
        DMA((n, zn + 1)),
        DMA((n, 2, zn)),
        DMA((n, zn)),
        DMA((n, zn + 1)),
        DMA((n,)),
        DMA((n,)),
        DMA((outs,)),
        DMA((outs,)),
        DMA((outs,)),
    ]


def scatter_buffers(shapes, early, zn):
    out = []
    for rows, columns in shapes:
        late = rows - early
        out += [
            pltpu.VMEM((zn, late, columns), BF16),
            pltpu.VMEM((zn, late, columns), BF16),
            pltpu.VMEM((zn + 1, late, columns), BF16),
            pltpu.VMEM((zn, 2, early, columns), BF16),
            pltpu.VMEM((zn + 1, 2, early, columns), BF16),
            pltpu.VMEM((early, columns), BF16),
            pltpu.VMEM((rows, columns), F32),
        ]
    return out


SCATTER_BUFFERS = 7


class Scatter:
    def __init__(self, zn, here, early, arrays, sems):
        self.zn, self.here, self.early = zn, here, early
        self.term = [term for term, _, _ in arrays]
        self.buffers = [buffers for _, buffers, _ in arrays]
        self.results = [(j,) + result for j, (_, _, results) in enumerate(arrays) for result in results]
        (
            self.st,
            self.ls,
            self.xs,
            self.xr,
            self.zs,
            self.zr,
            self.bls,
            self.bs,
            self.br,
            self.es,
            self.er,
            self.cs,
            self.cr,
            self.loc,
        ) = sems

    def unit(self, j, o, x, first, count):
        rows = self.term[j].shape[1] // 2
        return self.term[j].at[o, pl.ds(pl.multiple_of(x * rows + first, 16), count)]

    def late(self, j):
        return self.buffers[j][0].shape[1]

    def load(self, j, o):
        return pltpu.make_async_copy(
            self.unit(j, o, self.here[3], 0, self.late(j)), self.buffers[j][0].at[o], self.ls.at[j, o]
        )

    def load_early(self, j, o, other):
        x = self.here[3]
        return pltpu.make_async_copy(
            self.unit(j, o, 1 - x if other else x, self.late(j), self.early),
            self.buffers[j][3].at[o, other],
            self.bls.at[j, other, o],
        )

    def across(self, j, o):
        d, t, z, x, c = self.here
        return remote(
            self.unit(j, o, 1 - x, 0, self.late(j)),
            self.buffers[j][1].at[o],
            self.xs.at[j, o],
            self.xr.at[j, o],
            (d + 2 - 4 * x, t),
        )

    def across_early(self, j):
        d, t, z, x, c = self.here
        return remote(
            self.buffers[j][3].at[z, 1], self.buffers[j][5], self.es.at[j], self.er.at[j], (d + 2 - 4 * x, t)
        )

    def along(self, j, o, slot, down):
        d, t, z, x, c = self.here
        own, line = self.buffers[j][0], self.buffers[j][2]
        return remote(own.at[o], line.at[slot], self.zs.at[j, o], self.zr.at[j, slot], (d + 4 - 8 * down, t))

    def along_early(self, j, o, slot, down):
        d, t, z, x, c = self.here
        own, line = self.buffers[j][3], self.buffers[j][4]
        return remote(own.at[o], line.at[slot], self.bs.at[j, o], self.br.at[j, slot], (d + 4 - 8 * down, t))

    def give(self, r):
        d, t, z, x, c = self.here
        j, out, paired, first, columns = self.results[r]
        rows = out.shape[-2]
        ref = self.buffers[j][6].at[
            pl.ds(pl.multiple_of((1 - c) * rows, rows), rows), pl.ds(first, columns)
        ]
        return remote(ref, part(out, c, paired), self.cs.at[r], self.cr.at[r], (d + 1 - 2 * c, t))

    def keep(self, r):
        c = self.here[4]
        j, out, paired, first, columns = self.results[r]
        rows = out.shape[-2]
        ref = self.buffers[j][6].at[pl.ds(pl.multiple_of(c * rows, rows), rows), pl.ds(first, columns)]
        return pltpu.make_async_copy(ref, part(out, c, paired), self.loc.at[r])

    def store(self, j, o, stage, slot):
        columns = self.term[j].shape[2]
        return pltpu.make_async_copy(
            stage.at[slot, :, pl.ds(0, columns)], self.term[j].at[o], self.st.at[j, o]
        )

    def make(self, j, left, right, stage, between=None):
        z, zn = self.here[2], self.zn
        wide, columns = self.term[j].shape[1:]
        block = min(256, wide)

        def send(i):
            o = farthest_first(zn, z, i)
            self.store(j, o, stage, lax.rem(i, 2)).wait()
            self.across(j, o).start()
            for other in range(2):
                self.load_early(j, o, other).start()
            self.load(j, o).start()

        def compute(i):
            o = farthest_first(zn, z, i)
            slot = lax.rem(i, 2)

            def body(m):
                at = pl.multiple_of(o * wide + m * block, block)
                value = inner_rows(left[:, pl.ds(at, block)], right[...])
                stage[slot, pl.ds(pl.multiple_of(m * block, block), block), pl.ds(0, columns)] = value.astype(
                    BF16
                )

            loop(wide // block, body)
            self.store(j, o, stage, slot).start()

        def both(i):
            compute(i)
            send(i - 1)

        compute(0)
        if between is not None:
            between()
        loop(zn - 1, lambda i: both(i + 1))
        send(zn - 1)

    def add(self, j, o, slots):
        own, got, line = self.buffers[j][:3]

        def body(at):
            value = own[o, at].astype(F32) + got[o, at].astype(F32)
            for slot in slots:
                value = value + line[slot, at].astype(F32)
            own[o, at] = value.astype(BF16)

        by_rows(own.shape[1], body)

    def add_early(self, j, o, slots):
        own, line = self.buffers[j][3:5]
        for other in range(2):

            def body(at):
                value = own[o, other, at].astype(F32)
                for slot in slots:
                    value = value + line[slot, other, at].astype(F32)
                own[o, other, at] = value.astype(BF16)

            by_rows(own.shape[2], body)

    def route(self, i):
        z, zn = self.here[2], self.zn
        o = farthest_first(zn, z, i)
        down = (o < z).astype(jnp.int32)
        distance = jnp.maximum((o - z) * (1 - 2 * down), 1)
        slot = o + (zn - o) * down * (1 // distance)
        inner = ((o > z) & (z > 0)) | ((o < z) & (z < zn - 1))
        return o, slot, down, inner

    def hop_early(self, j, i):
        o, slot, down, inner = self.route(i)
        for other in range(2):
            self.load_early(j, o, other).wait()

        @pl.when(inner)
        def _():
            self.along_early(j, o, o, down).wait_recv()
            self.add_early(j, o, [o])

        self.along_early(j, o, slot, down).start()

    def hop(self, j, i):
        o, slot, down, inner = self.route(i)
        self.load(j, o).wait()
        self.across(j, o).wait_recv()

        @pl.when(inner)
        def _():
            self.along(j, o, o, down).wait_recv()
            self.add(j, o, [o])

        @pl.when(jnp.logical_not(inner))
        def _():
            self.add(j, o, [])

        self.along(j, o, slot, down).start()

    def third(self, hop, j, g):
        hops = self.zn - 1
        first = g * hops // 3
        loop((g + 1) * hops // 3 - first, lambda i: hop(j, first + i))

    def early_third(self, j, g):
        self.third(self.hop_early, j, g)

    def late_third(self, j, g):
        self.third(self.hop, j, g)

    def at_home(self, action):
        z, zn = self.here[2], self.zn

        @pl.when((z > 0) & (z < zn - 1))
        def _():
            action([z, zn])

        @pl.when(z == 0)
        def _():
            action([zn])

        @pl.when(z == zn - 1)
        def _():
            action([z])

    def early_home(self, j):
        z = self.here[2]
        for other in range(2):
            self.load_early(j, z, other).wait()

        def home(slots):
            for slot in slots:
                self.along_early(j, z, slot, 0).wait_recv()
            self.add_early(j, z, slots)

        self.at_home(home)
        self.across_early(j).start()

    def home(self, j):
        z = self.here[2]
        own, got, line, early, _, other_early, total = self.buffers[j]
        late = self.late(j)
        self.load(j, z).wait()
        self.across(j, z).wait_recv()

        def last(slots):
            for slot in slots:
                self.along(j, z, slot, 0).wait_recv()

            def body(at):
                value = own[z, at].astype(F32) + got[z, at].astype(F32)
                for slot in slots:
                    value = value + line[slot, at].astype(F32)
                total[at] = value

            by_rows(late, body)

        self.at_home(last)
        self.across_early(j).wait_recv()
        for i in range(self.early // 16):
            at = pl.ds(16 * i, 16)
            total[pl.ds(late + 16 * i, 16)] = early[z, 0, at].astype(F32) + other_early[at].astype(F32)
        for r, result in enumerate(self.results):
            if result[0] == j:
                self.give(r).start()
                self.keep(r).start()

    def done(self, j):
        z = self.here[2]
        for r, result in enumerate(self.results):
            if result[0] == j:
                self.give(r).wait()
                self.keep(r).wait()
        self.across_early(j).wait_send()

        def sent(o):
            self.across(j, o).wait_send()

            @pl.when(o != z)
            def _():
                self.along(j, o, 0, 0).wait_send()
                self.along_early(j, o, 0, 0).wait_send()

        loop(self.zn, sent)

    def lend(self, credit):
        d, t, z, x, c = self.here

        def tell(device):
            pl.semaphore_signal(credit, inc=1, device_id=device, device_id_type=MESH)

        tell((d + 2 - 4 * x, t))

        @pl.when(z > 0)
        def _():
            tell((d - 4, t))

        @pl.when(z < self.zn - 1)
        def _():
            tell((d + 4, t))

    def borrow(self, credit):
        z = self.here[2]
        pl.semaphore_wait(credit, 3 - (z == 0).astype(jnp.int32) - (z == self.zn - 1).astype(jnp.int32))


class Gains:
    def __init__(self, zn, here, own, got, line, sems):
        self.zn, self.here, self.own, self.got, self.line, self.sems = zn, here, own, got, line, sems

    def swap(self, i):
        d, t, z, x, c = self.here
        device = ((d + 1 - 2 * c, t), (d, 1 - t), (d + 2 - 4 * x, t))[i]
        return remote(self.own, self.got.at[i], self.sems.at[0, i], self.sems.at[1, i], device)

    def along(self, o, slot, down):
        d, t, z, x, c = self.here
        return remote(
            self.own.at[o], self.line.at[slot], self.sems.at[2, o], self.sems.at[3, slot], (d + 4 - 8 * down, t)
        )

    def start(self, rows):
        wide = self.own.shape[2]
        for o in range(self.zn):
            for i, row in enumerate(rows):
                self.own[o, pl.ds(i, 1)] = row[:, pl.ds(o * wide, wide)]
        self.swap(0).start()

    def swapped(self, i):
        self.swap(i).wait()
        self.own[...] += self.got[i]
        if i < 2:
            self.swap(i + 1).start()

    def hop(self, o, slot, down, inner):
        @pl.when(inner)
        def _():
            self.along(o, o, down).wait_recv()
            self.own[o] += self.line[o]

        self.along(o, slot, down).start()

    def steps(self, k, nearest):
        z, zn = self.here[2], self.zn

        @pl.when(z + k < zn)
        def _():
            self.hop(z + k, z + k, 0, z > 0)

        @pl.when(z - k >= 0)
        def _():
            self.hop(z - k, zn if nearest else z - k, 1, z < zn - 1)

    def run(self):
        zn = self.zn

        def step(i, carry):
            self.steps(zn - 1 - i, False)
            return carry

        lax.fori_loop(0, zn - 2, step, 0)
        self.steps(1, True)

    def finish(self, out):
        z, zn = self.here[2], self.zn
        value = self.own[z]

        @pl.when(z > 0)
        def _():
            self.along(z, z, 0).wait_recv()
            self.own[z] += self.line[z]

        @pl.when(z < zn - 1)
        def _():
            self.along(z, zn, 1).wait_recv()
            self.own[z] += self.line[zn]

        out[...] = self.own[z]

        def step(o, carry):
            @pl.when(o != z)
            def _():
                self.along(o, 0, 0).wait_send()

            return carry

        lax.fori_loop(0, zn, step, 0)


def gain_buffers(zn, wide):
    return [
        pltpu.VMEM((zn, 8, wide), F32),
        pltpu.VMEM((3, zn, 8, wide), F32),
        pltpu.VMEM((zn + 1, 8, wide), F32),
        DMA((4, zn + 1)),
    ]


class Total:
    def __init__(self, here, term, from_core, half, from_pair, sems):
        self.here, self.term, self.from_core, self.half, self.from_pair = here, term, from_core, half, from_pair
        self.sems = sems

    def core(self):
        d, t, z, x, c = self.here
        return remote(self.term.at[1 - c], self.from_core, self.sems.at[0], self.sems.at[1], (d + 1 - 2 * c, t))

    def load(self):
        return pltpu.make_async_copy(self.term.at[self.here[4]], self.half, self.sems.at[4])

    def start(self):
        self.core().start()
        self.load().start()

    def pair(self):
        d, t, z, x, c = self.here
        return remote(self.half, self.from_pair, self.sems.at[2], self.sems.at[3], (d, 1 - t))

    def meet(self, loaded=True, send=True):
        if loaded:
            self.load().wait()
        self.core().wait_recv()

        def body(at):
            self.half[at] = (self.half[at].astype(F32) + self.from_core[at].astype(F32)).astype(BF16)

        by_rows(self.half.shape[0], body)
        if send:
            self.pair().start()

    def rows(self, at):
        return self.half[at].astype(F32) + self.from_pair[at].astype(F32)

    def finish(self):
        self.core().wait_send()
        self.pair().wait_send()


def total_buffers(tokens, width):
    return [pltpu.VMEM((tokens, width), BF16)] * 3 + [DMA((5,))]


def share(here, src, dst, sems):
    d, t, z, x, c = here
    return (
        pltpu.make_async_copy(src, dst.at[c], sems.at[0]),
        remote(src, dst.at[c], sems.at[1], sems.at[2], (d + 1 - 2 * c, t)),
    )


def lanes(shape):
    return lax.broadcasted_iota(jnp.int32, shape, 1)


def partner(value):
    half = HEAD_DIM // 2
    wide = 2 * HEAD_DIM
    lower = lax.rem(lanes(value.shape), HEAD_DIM) < half
    return jnp.where(lower, pltpu.roll(value, wide - half, 1), pltpu.roll(value, half, 1))


def same_segment(row):
    count = row.shape[1]
    wide = jnp.broadcast_to(row, (count, count))
    before = lax.broadcasted_iota(jnp.int32, wide.shape, 1) < lax.broadcasted_iota(jnp.int32, wide.shape, 0)
    return wide == wide.T, before


def allowed_in(row):
    same, before = same_segment(row)
    here = lax.broadcasted_iota(jnp.int32, same.shape, 1) == lax.broadcasted_iota(jnp.int32, same.shape, 0)
    return same & (before | here)


def softmax_of(queries, keys, allowed):
    scores = jnp.where(allowed, times_transposed(queries, keys) * HEAD_DIM ** (-0.5), -1e30)
    shifted = jnp.exp(scores - jnp.max(scores, axis=-1, keepdims=True))
    return shifted / jnp.sum(shifted, axis=-1, keepdims=True)


def key_value_pairs(pair):
    pair = pair.astype(F32)
    first = lanes(pair.shape) < HEAD_DIM
    key, value = jnp.where(first, pair, 0.0), jnp.where(first, 0.0, pair)
    return [
        part.astype(BF16)
        for part in (key, pltpu.roll(key, HEAD_DIM, 1), pltpu.roll(value, HEAD_DIM, 1), value)
    ]


def attention_block(turned, context, queries_wide, row):
    wide = 2 * HEAD_DIM
    allowed = allowed_in(row)
    key_one, key_two, value_one, value_two = key_value_pairs(turned[:, queries_wide:])

    def heads(p):
        at = pl.ds(pl.multiple_of(p * wide, wide), wide)
        queries = turned[:, at]
        one = softmax_of(queries, key_one, allowed).astype(BF16)
        two = softmax_of(queries, key_two, allowed).astype(BF16)
        context[:, at] = (product(one, value_one) + product(two, value_two)).astype(BF16)

    loop(queries_wide // wide, heads)


def attention_block_back(turned, grads, back, sums, queries_wide, row, cosine, sine):
    wide = 2 * HEAD_DIM
    scale = HEAD_DIM ** (-0.5)
    allowed = allowed_in(row)
    key_one, key_two, value_one, value_two = key_value_pairs(turned[:, queries_wide:])
    sums[...] = jnp.zeros_like(sums)

    def heads(p):
        at = pl.ds(pl.multiple_of(p * wide, wide), wide)
        queries, grad = turned[:, at], grads[:, at]
        total = None
        for i, (key, value) in enumerate(((key_one, value_one), (key_two, value_two))):
            probs = softmax_of(queries, key, allowed)
            sums[i] += inner_rows(probs.astype(BF16), grad)
            prob_grad = times_transposed(grad, value)
            delta = jnp.sum(probs * prob_grad, axis=-1, keepdims=True)
            score_grad = (probs * (prob_grad - delta)).astype(BF16)
            term = product(score_grad, key)
            total = term if total is None else total + term
            sums[2 + i] += inner_rows(score_grad, queries)
        total = total * scale
        back[:, at] = (total * cosine - partner(total) * sine).astype(BF16)

    loop(queries_wide // wide, heads)
    value_grad = pltpu.roll(sums[0], HEAD_DIM, 1) + sums[1]
    key_grad = (sums[2] + pltpu.roll(sums[3], HEAD_DIM, 1)) * scale
    turned_back = key_grad * cosine - partner(key_grad) * sine
    back[:, pl.ds(queries_wide, wide)] = jnp.where(
        lanes(value_grad.shape) < HEAD_DIM, turned_back, value_grad
    ).astype(BF16)


def transposed(src, dst):
    def body(n):
        at = pl.ds(pl.multiple_of(n * 128, 128), 128)
        dst[:, at] = src[at, :].astype(F32).T.astype(BF16)

    loop(src.shape[0] // 128, body)


def forward(zn, early, *refs):
    q, k_shard, v_shard, o_turned, one_shard, two_shard, tokens_in, grads_in, seg, gate_in, up_in, down_in, inverse, sign = refs[:14]
    refs = refs[2:]
    qkv_all, o_all, gains_all, chip_tokens, chip_grads, seg_all = refs[12:18]
    gate_all, up_all, down_all, mid_out, normed_out, act_out, gate_grad_out, up_grad_out = refs[18:26]
    term, normed_one_out, turned_out, context_out, cosines_out, sines_out, gain_out = refs[26:33]
    total_refs = refs[33:37]
    normed, out_sems, pair_sems, load_sems, grad_sems, stage_sems, block_sems = refs[37:44]
    cosines, sines, seg_pair, gain_tiles, gain_rows, swap_sems, seg_sems = refs[44:51]
    kv, gains, o_shard, down, tokens, grads, gate, up, down_turned, first_sems = refs[51:61]
    here = place()
    z, c = here[2], here[4]
    firsts = [
        pltpu.make_async_copy(src, dst, first_sems.at[n])
        for n, (src, dst) in enumerate(
            ((down_in, down_turned), (tokens_in, tokens), (gate_in, gate), (up_in, up), (grads_in, grads))
        )
    ]
    for copy in firsts:
        copy.start()
    enter(zn, here)
    keys, values = k_shard[...].astype(F32), v_shard[...].astype(F32)
    is_key = lanes(keys.shape) < HEAD_DIM
    kv[0] = jnp.where(is_key, keys, pltpu.roll(values, HEAD_DIM, 1)).astype(BF16)
    kv[1] = jnp.where(is_key, pltpu.roll(keys, HEAD_DIM, 1), values).astype(BF16)
    for i in range(2):
        gains[i] = jnp.zeros(gains.shape[1:], F32)
        for k, shard in enumerate((one_shard, two_shard)):
            gains[i, pl.ds(k, 1), pl.ds(0, shard.shape[1])] = shard[...].astype(F32)
    transposed(o_turned, o_shard)
    total = Total(here, term, *total_refs)
    q_half = q.shape[1] // 2
    work = Gather(
        zn,
        here,
        [
            ([(gains, True, 0, gains.shape[2])], gains_all, 0),
            ([(q, False, 0, q_half), (kv, True, q_half, kv.shape[2])], qkv_all, early[0]),
            ([(o_shard, False, 0, o_shard.shape[1] // 2)], o_all, early[0]),
        ]
        + [
            ([(shard, False, 0, shard.shape[1] // 2)], full, rows_early)
            for shard, full, rows_early in zip((down, gate, up), (down_all, gate_all, up_all), early[1:])
        ],
        refs[61:],
    )
    count, width = tokens.shape
    columns = gate_all.shape[1]
    block = seg.shape[1]
    blocks = 2 * count // block
    per = count // block
    attention_set = [0, 1, 2]
    swap = remote(seg, seg_pair.at[c], seg_sems.at[0], seg_sems.at[1], (here[0] + 1 - 2 * c, here[1]))
    swap.start()
    seg_pair[c] = seg[...]
    work.start(attention_set)
    firsts[0].wait()
    transposed(down_turned, down)
    work.start([3])
    work.ready(attention_set)
    work.start_own(attention_set)
    for copy in firsts[1:]:
        copy.wait()
    shared = [
        share(here, src, dst, swap_sems.at[n])
        for n, (src, dst) in enumerate(((tokens, chip_tokens), (grads, chip_grads)))
    ]
    for copy in shared[0]:
        copy.start()
    work.start([4, 5])
    for copy in shared[1]:
        copy.start()
    work.start_early([1, 2])
    work.ready([3])
    work.start_own([3])
    swap.wait()
    for i in range(blocks):
        row = seg_pair[i // per, pl.ds(i % per, 1)]
        same, before = same_segment(row)
        position = jnp.sum(jnp.where(same & before, 1.0, 0.0), axis=-1, keepdims=True)
        angles = position * inverse[...]
        cosines[pl.ds(i * block, block)] = jnp.cos(angles)
        sines[pl.ds(i * block, block)] = jnp.sin(angles) * sign[...]
    saves = [
        pltpu.make_async_copy(src, dst, seg_sems.at[2 + n])
        for n, (src, dst) in enumerate(((cosines, cosines_out), (sines, sines_out), (seg_pair, seg_all)))
    ]
    for copy in saves:
        copy.start()
    work.relay(1, attention_set)
    work.relay(2, attention_set)
    work.start_early([3])
    work.relays(3, attention_set)
    work.ready([4, 5])
    work.start_own([4, 5])
    work.start_early([4])
    work.arrived(0)
    load = pltpu.make_async_copy(gains_all, gain_tiles, load_sems.at[0])
    load.start()
    load.wait()
    features = width // (4 * zn)
    for owner in range(4 * zn):
        for i in range(2):
            gain_rows[pl.ds(i, 1), pl.ds(owner * features, features)] = gain_tiles[
                pl.ds(owner * 8 + i, 1), :features
            ]
    save_gains = pltpu.make_async_copy(gain_rows, gain_out, load_sems.at[1])
    save_gains.start()
    gain_one, gain = gain_rows[pl.ds(0, 1)], gain_rows[pl.ds(1, 1)]
    for copies in shared:
        for copy in copies:
            copy.wait()
    work.arrived(1)
    work.arrived(2)
    save_gains.wait()
    half = total_refs[1]

    def attention(qkv, o, inputs, normed_one, turned, context, attended):
        queries_wide = context.shape[2]
        wide = 2 * HEAD_DIM

        def place_of(i):
            return lax.rem((1 - c) * per + i, blocks)

        def rows_at(i):
            return pl.ds(pl.multiple_of(place_of(i) * block, block), block)

        def fetch_inputs(i, slot):
            which = place_of(i)
            return pltpu.make_async_copy(
                chip_tokens.at[which // per, pl.ds(pl.multiple_of(lax.rem(which, per) * block, block), block)],
                inputs.at[slot],
                grad_sems.at[slot],
            )

        def stores(i, slot):
            return [
                pltpu.make_async_copy(buffer.at[slot], out.at[rows_at(i)], stage_sems.at[slot, n])
                for n, (buffer, out) in enumerate(
                    ((normed_one, normed_one_out), (turned, turned_out), (context, context_out))
                )
            ]

        def store_term(i, slot):
            return pltpu.make_async_copy(
                attended.at[slot],
                term.at[1 - c, pl.ds(pl.multiple_of(i * block, block), block)],
                block_sems.at[slot],
            )

        fetch_inputs(0, 0).start()
        loads = [
            pltpu.make_async_copy(qkv_all, qkv, load_sems.at[0]),
            pltpu.make_async_copy(o_all, o, load_sems.at[1]),
        ]
        for load in loads:
            load.start()
        for load in loads:
            load.wait()

        def one_block(i):
            slot = lax.rem(i, 2)
            to = rows_at(i)
            fetch_inputs(i, slot).wait()

            @pl.when(i + 1 < blocks)
            def _():
                fetch_inputs(i + 1, 1 - slot).start()

            @pl.when(i > 1)
            def _():
                for copy in stores(i - 2, slot):
                    copy.wait()

            def norm(at):
                value = inputs[slot, at].astype(F32)
                factor = lax.rsqrt(jnp.mean(value * value, axis=-1, keepdims=True) + norm_eps)
                normed_one[slot, at] = (value * factor * gain_one).astype(BF16)

            by_rows(block, norm)
            cosine, sine = cosines[to], sines[to]
            raw = product(normed_one[slot], qkv[...])
            for first in range(0, queries_wide, wide):
                value = raw[:, first : first + wide]
                turned[slot, :, pl.ds(first, wide)] = (value * cosine + partner(value) * sine).astype(BF16)
            value = raw[:, queries_wide:]
            is_key = lanes(value.shape) < HEAD_DIM
            turned[slot, :, pl.ds(queries_wide, wide)] = jnp.where(
                is_key, value * cosine + partner(value) * sine, value
            ).astype(BF16)
            which = place_of(i)
            row = seg_pair[which // per, pl.ds(lax.rem(which, per), 1)]
            attention_block(turned.at[slot], context.at[slot], queries_wide, row)
            for copy in stores(i, slot):
                copy.start()
            return slot

        def other(i):
            slot = one_block(i)
            attended[slot] = times_transposed(context[slot], o[...]).astype(BF16)
            store_term(i, slot).start()

        def own(i):
            slot = one_block(per + i)
            half[pl.ds(pl.multiple_of(i * block, block), block)] = times_transposed(
                context[slot], o[...]
            ).astype(BF16)

        loop(per, other)
        for i in range(per):
            store_term(i, i % 2).wait()
        total.core().start()
        loop(per, own)
        for i in range(blocks - 2, blocks):
            for copy in stores(i, i % 2):
                copy.wait()

    pl.run_scoped(
        attention,
        pltpu.VMEM(qkv_all.shape, BF16),
        pltpu.VMEM(o_all.shape, BF16),
        pltpu.VMEM((2, block, width), BF16),
        pltpu.VMEM((2, block, width), BF16),
        pltpu.VMEM((2, block, qkv_all.shape[1]), BF16),
        pltpu.VMEM((2, block, o_all.shape[1]), BF16),
        pltpu.VMEM((2, block, width), BF16),
    )
    total.meet(False)
    for j in (3, 4):
        work.relay(1, [j])
        work.relay(2, [j])
    work.relays(3, [3])

    def sums(mid):
        total.pair().wait_recv()

        def body(at):
            value = tokens[at].astype(F32) + total.rows(at)
            mid[at] = value
            factor = lax.rsqrt(jnp.mean(value * value, axis=-1, keepdims=True) + norm_eps)
            normed[c, at] = (value * factor * gain).astype(BF16)

        by_rows(count, body)
        save = pltpu.make_async_copy(mid, mid_out, out_sems.at[0])
        save.start()
        for copy in share(here, normed.at[c], normed, pair_sems)[1:]:
            copy.start()
        save.wait()

    def hidden(first, second, silu, slope, upward, up_grad, inputs, result, stages):
        def fetch_grads(i, slot):
            return pltpu.make_async_copy(
                chip_grads.at[i // per, pl.ds(pl.multiple_of(lax.rem(i, per) * block, block), block)],
                inputs.at[slot],
                grad_sems.at[slot],
            )

        def at_block(i):
            return pl.ds(pl.multiple_of(i * block, block), block)

        fetch_grads(0, 0).start()
        pl.run_scoped(sums, pltpu.VMEM((count, width), F32))
        work.relays(3, [4])
        work.start_early([5])
        work.arrived(3)
        load = pltpu.make_async_copy(down_all, first, load_sems.at[0])
        load.start()
        load.wait()

        def hidden_block(i):
            slot = lax.rem(i, 2)
            fetch_grads(i, slot).wait()

            @pl.when(i + 1 < blocks)
            def _():
                fetch_grads(i + 1, 1 - slot).start()

            slope[at_block(i)] = product(inputs[slot], first[...])

        loop(blocks, hidden_block)
        work.relay(1, [5])
        work.relay(2, [5])
        upward[...] = jnp.zeros_like(upward)
        work.arrived(4)
        load = pltpu.make_async_copy(gate_all, second, load_sems.at[1])
        load.start()
        share(here, normed.at[c], normed, pair_sems)[1].wait()
        save = pltpu.make_async_copy(normed, normed_out, out_sems.at[1])
        save.start()
        load.wait()

        def gate_block(i):
            result[...] = product(normed[i // per, at_block(lax.rem(i, per))], second[...])

            def body(at):
                to = pl.ds(pl.multiple_of(i * block + at.start, 16), at.size)
                gated = result[at]
                grad = slope[to]
                sigmoid = 1.0 / (1.0 + jnp.exp(-gated))
                silu[to] = gated * sigmoid
                up_grad[to] = (grad * gated * sigmoid).astype(BF16)
                slope[to] = grad * (sigmoid * (1.0 + gated * (1.0 - sigmoid)))

            by_rows(block, body)

        loop(blocks, gate_block)
        save_up = pltpu.make_async_copy(up_grad, up_grad_out, out_sems.at[2])
        save_up.start()
        work.relays(3, [5])
        group = width // zn

        def up_rows(k):
            o = farthest_first(zn, z, zn - 1 - k)
            at = pl.ds(pl.multiple_of(o * group, group), group)
            work.x_late(5, o).wait_recv()
            load = pltpu.make_async_copy(up_all.at[at], first.at[at], load_sems.at[0])
            load.start()
            load.wait()

            def up_part(i):
                rows = normed[i // per, at_block(lax.rem(i, per)), at]
                upward[at_block(i)] += product(rows, first[at])

            loop(blocks, up_part)

        loop(zn, up_rows)

        def stores(i, slot):
            to = at_block(i)
            return (
                pltpu.make_async_copy(stages.at[slot, 0], act_out.at[to], stage_sems.at[slot, 0]),
                pltpu.make_async_copy(stages.at[slot, 1], gate_grad_out.at[to], stage_sems.at[slot, 1]),
            )

        def up_block(i):
            slot = lax.rem(i, 2)

            @pl.when(i > 1)
            def _():
                for copy in stores(i - 2, slot):
                    copy.wait()

            def body(at):
                to = pl.ds(pl.multiple_of(i * block + at.start, 16), at.size)
                stages[slot, 0, at] = (silu[to] * upward[to]).astype(BF16)
                stages[slot, 1, at] = (slope[to] * upward[to]).astype(BF16)

            by_rows(block, body)
            for copy in stores(i, slot):
                copy.start()

        loop(blocks, up_block)
        for i in range(max(blocks - 2, 0), blocks):
            for copy in stores(i, i % 2):
                copy.wait()
        save.wait()
        save_up.wait()

    pl.run_scoped(
        hidden,
        pltpu.VMEM((width, columns), BF16),
        pltpu.VMEM((width, columns), BF16),
        pltpu.VMEM((2 * count, columns), F32),
        pltpu.VMEM((2 * count, columns), F32),
        pltpu.VMEM((2 * count, columns), F32),
        pltpu.VMEM((2 * count, columns), BF16),
        pltpu.VMEM((2, block, width), BF16),
        pltpu.VMEM((block, columns), F32),
        pltpu.VMEM((2, 2, block, columns), BF16),
    )
    work.finish()
    total.finish()
    for copy in saves:
        copy.wait()


def fetch(pairs, sems):
    copies = [pltpu.make_async_copy(src, dst, sems.at[i]) for i, (src, dst) in enumerate(pairs)]
    for copy in copies:
        copy.start()
    return copies


def backward(zn, early, *refs):
    normed_two, gate_grad, chip_grads, activated, gate_all, up_all, down_all, mid_in, up_grad = refs[:9]
    normed_one, context, turned_all, o_all, qkv_all, cosines, sines, tokens_in, rows_of, gain_rows = refs[9:19]
    down_out, gate_out, up_out, o_out, q_out, kv_out, out, in_grad, gain_out = refs[19:28]
    mid_grad_all, branch_all, qkv_back, in_term, out_term, back_term = refs[28:34]
    down, gate, up, o_sums, qkv_sums = refs[34:39]
    n = SCATTER_BUFFERS
    buffers, refs = refs[39 : 39 + 4 * n], refs[39 + 4 * n :]
    back_refs, front_refs, in_refs = refs[:4], refs[4:8], refs[8:11]
    gain_refs, (one_sum, two_sum), refs = refs[11:15], refs[15:17], refs[17:]
    fetch_sems, out_sems, pair_sems, weight_sems, stage_sems, block_sems, back_sems, credit = refs[:8]
    here = place()
    z, c = here[2], here[4]
    chip, width = chip_grads.shape
    count = chip // 2
    block = rows_of.shape[2]
    blocks = chip // block
    per = blocks // 2
    qkv_wide, q_half = qkv_all.shape[1], o_all.shape[1]
    enter(zn, here)
    branch, out_rows, in_rows = back_refs[0], front_refs[0], in_refs[0]
    back = Total(here, back_term, *back_refs)
    front = Total(here, out_term, *front_refs)
    total = Total(here, in_term, in_refs[0], back_refs[1], in_refs[1], in_refs[2])
    gains = Gains(zn, here, *gain_refs)
    work = Scatter(
        zn,
        here,
        early,
        [
            (down, buffers[:n], [(down_out, False, 0, down_out.shape[1] // 2)]),
            (gate, buffers[n : 2 * n], [(gate_out, False, 0, gate_out.shape[1] // 2)]),
            (up, buffers[:n], [(up_out, False, 0, up_out.shape[1] // 2)]),
            (o_sums, buffers[2 * n : 3 * n], [(o_out, False, 0, q_half)]),
            (
                qkv_sums,
                buffers[3 * n :],
                [(q_out, False, 0, q_half), (kv_out, True, q_half, kv_out.shape[2])],
            ),
        ],
        refs[8:],
    )
    def feature_terms(factors, term):
        def run(*refs):
            lefts, weights, stages = refs[:-2], refs[-2], refs[-1]
            group = weights.shape[2]
            loads = fetch([(left, ref) for (left, _), ref in zip(factors, lefts)], fetch_sems)

            def fetch_weights(i, slot):
                at = pl.ds(pl.multiple_of(i * group, group), group)
                return [
                    pltpu.make_async_copy(full.at[at], weights.at[slot, k], weight_sems.at[slot, k])
                    for k, (_, full) in enumerate(factors)
                ]

            def stores(i, slot):
                to = pl.ds(pl.multiple_of(i * group, group), group)
                return [
                    pltpu.make_async_copy(
                        stages.at[slot, pl.ds(half * count, count)], term.at[half, :, to], stage_sems.at[slot, half]
                    )
                    for half in range(2)
                ]

            for copy in fetch_weights(0, 0):
                copy.start()
            for load in loads:
                load.wait()

            def step(i):
                slot = lax.rem(i, 2)
                for copy in fetch_weights(i, slot):
                    copy.wait()

                @pl.when(i + 1 < width // group)
                def _():
                    for copy in fetch_weights(i + 1, 1 - slot):
                        copy.start()

                @pl.when(i > 1)
                def _():
                    for copy in stores(i - 2, slot):
                        copy.wait()

                value = times_transposed(lefts[0][...], weights[slot, 0])
                for k in range(1, len(lefts)):
                    value = value + times_transposed(lefts[k][...], weights[slot, k])
                stages[slot] = value.astype(BF16)
                for copy in stores(i, slot):
                    copy.start()

            loop(width // group, step)
            for i in range(width // group - 2, width // group):
                for copy in stores(i, i % 2):
                    copy.wait()

        pl.run_scoped(
            run,
            *[pltpu.VMEM((chip, wide), BF16)] * len(factors),
            pltpu.VMEM((2, len(factors), 256, wide), BF16),
            pltpu.VMEM((2, chip, 256), BF16),
        )

    wide = down.shape[2]
    operands = [pltpu.VMEM((chip, width), BF16), pltpu.VMEM((chip, wide), BF16), pltpu.VMEM((2,) + down.shape[1:], BF16)]

    def terms_of(j, left_all, right_all):
        def run(left, right, stage):
            for load in fetch(((left_all, left), (right_all, right)), fetch_sems):
                load.wait()
            work.make(j, left, right, stage)

        pl.run_scoped(run, *operands)

    terms_of(0, chip_grads, activated)
    for g in range(3):
        work.early_third(0, g)
    feature_terms([(gate_grad, gate_all), (up_grad, up_all)], back_term)
    back.start()
    work.late_third(0, 0)
    feature_terms([(activated, down_all)], out_term)
    back.meet()
    front.start()
    work.late_third(0, 1)
    work.early_home(0)
    work.late_third(0, 2)
    terms_of(1, normed_two, gate_grad)
    work.early_third(1, 0)

    def sums(mid, mid_grad, grads):
        for load in fetch(
            (
                (mid_in, mid),
                (chip_grads.at[pl.ds(pl.multiple_of(c * count, 16), count)], grads),
            ),
            fetch_sems,
        ):
            load.wait()
        gain = gain_rows[pl.ds(1, 1)]
        two_sum[...] = jnp.zeros_like(two_sum)

        def body_gain(at):
            value = mid[at]
            factor = lax.rsqrt(jnp.mean(value * value, axis=-1, keepdims=True) + norm_eps)
            two_sum[...] += jnp.sum(back.half[at].astype(F32) * (value * factor), axis=0, keepdims=True)

        by_rows(count, body_gain)
        work.late_third(1, 0)
        work.early_third(1, 1)
        work.early_third(1, 2)
        work.home(0)
        work.done(0)
        work.lend(credit)
        front.meet()
        back.pair().wait_recv()

        def body(at):
            value = mid[at]
            factor = lax.rsqrt(jnp.mean(value * value, axis=-1, keepdims=True) + norm_eps)
            scaled = back.rows(at) * gain
            result = (
                grads[at].astype(F32)
                + factor * scaled
                - value * (factor * factor * factor) * jnp.mean(scaled * value, axis=-1, keepdims=True)
            )
            mid_grad[at] = result
            branch[at] = result.astype(BF16)

        by_rows(count, body)
        save = pltpu.make_async_copy(mid_grad, mid_grad_all, out_sems.at[0])
        save.start()
        for copy in share(here, branch, branch_all, pair_sems):
            copy.start()
        work.late_third(1, 1)
        save.wait()

    pl.run_scoped(
        sums, pltpu.VMEM((count, width), F32), pltpu.VMEM((count, width), F32), pltpu.VMEM((count, width), BF16)
    )

    def middle_terms(left, right, stage):
        for copy in share(here, branch, branch_all, pair_sems):
            copy.wait()
        right_o = right.at[:, pl.ds(0, q_half)]
        loads = fetch(
            ((branch_all.at[0], left.at[pl.ds(0, count)]), (branch_all.at[1], left.at[pl.ds(count, count)])),
            fetch_sems,
        )
        loads.append(pltpu.make_async_copy(context, right_o, fetch_sems.at[2]))
        loads[2].start()
        for load in loads:
            load.wait()
        work.make(3, left, right_o, stage)
        loads = fetch(((normed_two, left), (up_grad, right)), fetch_sems)
        work.early_third(3, 0)
        work.late_third(1, 2)
        for load in loads:
            load.wait()
        work.borrow(credit)
        work.make(2, left, right, stage)

    pl.run_scoped(middle_terms, *operands)
    work.early_third(2, 0)

    def attention(o, qkv, inputs, turned, grads, backs, terms_out, cosine, sine, accumulators):
        def which(i):
            return lax.rem((1 - c) * per + i, blocks)

        def rows_at(i):
            return pl.ds(pl.multiple_of(i * block, block), block)

        def fetches(i, slot):
            b = which(i)
            sources = (
                (branch_all.at[b // per, rows_at(lax.rem(b, per))], inputs),
                (turned_all.at[rows_at(b)], turned),
                (cosines.at[rows_at(b)], cosine),
                (sines.at[rows_at(b)], sine),
            )
            return [
                pltpu.make_async_copy(source, buffer.at[slot], block_sems.at[slot, k])
                for k, (source, buffer) in enumerate(sources)
            ]

        def stores(i, slot):
            b = which(i)
            return [
                pltpu.make_async_copy(backs.at[slot], qkv_back.at[rows_at(b)], back_sems.at[slot, 0]),
                pltpu.make_async_copy(
                    terms_out.at[slot], in_term.at[b // per, rows_at(lax.rem(b, per))], back_sems.at[slot, 1]
                ),
            ]

        loads = fetch(((o_all, o), (qkv_all, qkv)), fetch_sems)
        for copy in fetches(0, 0):
            copy.start()
        for load in loads:
            load.wait()

        def step(i):
            slot = lax.rem(i, 2)

            @pl.when(i == per)
            def _():
                for done in range(per):
                    for copy in stores(done, done % 2):
                        copy.wait()
                total.core().start()
                work.early_third(2, 2)

            @pl.when(i == 1)
            def _():
                work.early_third(3, 1)
                work.early_third(2, 1)

            @pl.when(i == blocks - 1)
            def _():
                work.late_third(2, 0)

            for copy in fetches(i, slot):
                copy.wait()

            @pl.when(i + 1 < blocks)
            def _():
                for copy in fetches(i + 1, 1 - slot):
                    copy.start()

            grads[...] = product(inputs[slot], o[...]).astype(BF16)
            attention_block_back(
                turned.at[slot],
                grads,
                backs.at[slot],
                accumulators,
                q_half,
                rows_of[which(i) // per, pl.ds(lax.rem(which(i), per), 1)],
                cosine[slot],
                sine[slot],
            )
            terms_out[slot] = times_transposed(backs[slot], qkv[...]).astype(BF16)
            for copy in stores(i, slot):
                copy.start()

        loop(blocks, step)
        for i in range(per, blocks):
            for copy in stores(i, i % 2):
                copy.wait()

    pl.run_scoped(
        attention,
        pltpu.VMEM(o_all.shape, BF16),
        pltpu.VMEM(qkv_all.shape, BF16),
        pltpu.VMEM((2, block, width), BF16),
        pltpu.VMEM((2, block, qkv_wide), BF16),
        pltpu.VMEM((block, q_half), BF16),
        pltpu.VMEM((2, block, qkv_wide), BF16),
        pltpu.VMEM((2, block, width), BF16),
        pltpu.VMEM((2, block, 2 * HEAD_DIM), F32),
        pltpu.VMEM((2, block, 2 * HEAD_DIM), F32),
        pltpu.VMEM((4, block, 2 * HEAD_DIM), F32),
    )
    back.finish()
    total.load().start()

    def meeting(tokens):
        load = fetch(((tokens_in, tokens),), fetch_sems)[0]
        total.meet(send=False)
        load.wait()
        one_sum[...] = jnp.zeros_like(one_sum)

        def body_gain(at):
            value = tokens[at].astype(F32)
            factor = lax.rsqrt(jnp.mean(value * value, axis=-1, keepdims=True) + norm_eps)
            one_sum[...] += jnp.sum(total.half[at].astype(F32) * (value * factor), axis=0, keepdims=True)

        by_rows(count, body_gain)

    pl.run_scoped(meeting, pltpu.VMEM((count, width), BF16))
    gains.start([one_sum, two_sum])
    gains.swapped(0)
    total.pair().start()
    work.early_third(3, 2)
    work.late_third(2, 1)

    def output(mid):
        load = fetch(((mid_in, mid),), fetch_sems)[0]
        front.pair().wait_recv()
        load.wait()

        def body_out(at):
            out_rows[at] = (mid[at] + front.rows(at)).astype(BF16)

        by_rows(count, body_out)

    pl.run_scoped(output, pltpu.VMEM((count, width), F32))
    save_out = pltpu.make_async_copy(out_rows, out, out_sems.at[1])
    save_out.start()
    work.late_third(3, 0)
    work.late_third(2, 2)
    work.early_home(2)
    work.early_home(1)

    def last_terms(left, right, stage):
        right_qkv = right.at[:, pl.ds(0, qkv_wide)]
        for load in fetch(((normed_one, left), (qkv_back, right_qkv)), fetch_sems):
            load.wait()
        gains.swapped(1)
        work.make(4, left, right_qkv, stage)

    pl.run_scoped(last_terms, *operands)
    work.early_third(4, 0)
    work.home(1)
    work.late_third(4, 0)
    work.early_third(4, 1)
    work.early_third(4, 2)
    work.early_home(3)
    work.late_third(3, 1)
    work.home(2)
    gains.swapped(2)
    gains.run()
    work.late_third(4, 1)
    work.late_third(4, 2)
    work.late_third(3, 2)
    work.early_home(4)

    def inputs_back(mid_grad, tokens):
        loads = fetch(((mid_grad_all, mid_grad), (tokens_in, tokens)), fetch_sems)
        gain = gain_rows[pl.ds(0, 1)]
        total.pair().wait_recv()
        for load in loads:
            load.wait()

        def body(at):
            value = tokens[at].astype(F32)
            factor = lax.rsqrt(jnp.mean(value * value, axis=-1, keepdims=True) + norm_eps)
            scaled = total.rows(at) * gain
            in_rows[at] = (
                mid_grad[at]
                + factor * scaled
                - value * (factor * factor * factor) * jnp.mean(scaled * value, axis=-1, keepdims=True)
            ).astype(BF16)

        by_rows(count, body)

    pl.run_scoped(inputs_back, pltpu.VMEM((count, width), F32), pltpu.VMEM((count, width), BF16))
    save_in = pltpu.make_async_copy(in_rows, in_grad, out_sems.at[0])
    save_in.start()
    gains.finish(gain_out)
    work.home(4)
    work.home(3)
    for j in (1, 2, 3, 4):
        work.done(j)
    front.finish()
    total.finish()
    save_out.wait()
    save_in.wait()


def settle(*refs):
    turned, plain, kv, gains = refs[:2], refs[2:7], refs[7], refs[8]
    turned_out, plain_out, (k_out, v_out, one_out, two_out) = refs[9:11], refs[11:16], refs[16:20]
    turned_in, turned_to, plain_at, (kv_at, k_at, v_at) = refs[20:22], refs[22:24], refs[24:29], refs[29:32]
    load_sems, store_sems = refs[32:]
    pairs = list(zip(plain, plain_at)) + list(zip(turned, turned_in)) + [(kv, kv_at)]
    loads = [pltpu.make_async_copy(src, dst, load_sems.at[n]) for n, (src, dst) in enumerate(pairs)]
    for n in (0, 1, 5, 3, 4, 2, 6, 7):
        loads[n].start()
    stores = []

    def send(src, dst):
        stores.append(pltpu.make_async_copy(src, dst, store_sems.at[len(stores)]))
        stores[-1].start()

    def pass_on(n):
        loads[n].wait()
        send(plain_at[n], plain_out[n])

    def turn(n, first, last):
        src, dst = turned_in[n], turned_to[n]

        def body(i):
            at = pl.ds(pl.multiple_of((first + i) * 128, 128), 128)
            dst[at, :] = src[:, at].T

        loop(last - first, body)

    pass_on(0)
    pass_on(1)
    groups = turned_in[0].shape[1] // 128
    loads[5].wait()
    turn(0, 0, groups // 2)
    pass_on(3)
    pass_on(4)
    turn(0, groups // 2, groups)
    send(turned_to[0], turned_out[0])
    pass_on(2)
    loads[6].wait()
    turn(1, 0, turned_in[1].shape[1] // 128)
    send(turned_to[1], turned_out[1])
    loads[7].wait()
    one, two = kv_at[0], kv_at[1]
    is_key = lanes(one.shape) < HEAD_DIM
    k_at[...] = jnp.where(is_key, one, pltpu.roll(two, HEAD_DIM, 1))
    v_at[...] = jnp.where(is_key, pltpu.roll(one, HEAD_DIM, 1), two)
    send(k_at, k_out)
    send(v_at, v_out)
    features = one_out.shape[1]
    for owner in range(4):

        @pl.when(lax.rem(lax.axis_index("dp"), 4) == owner)
        def _():
            at = pl.ds(owner * features, features)
            one_out[...] = gains[pl.ds(0, 1), at]
            two_out[...] = gains[pl.ds(1, 1), at]

    for copy in stores:
        copy.wait()


def call(kernel, name, collective_id, operands, specs, outs, out_specs, scratch, order=None):
    results = pl.pallas_call(
        kernel,
        out_shape=[jax.ShapeDtypeStruct(shape, dtype) for shape, dtype in outs],
        in_specs=specs,
        out_specs=out_specs,
        scratch_shapes=scratch,
        name=name,
        compiler_params=pltpu.CompilerParams(
            collective_id=collective_id, has_side_effects=True, vmem_limit_bytes=255 << 18
        ),
    )(*operands)
    return results if order is None else [results[i] for i in order]


def rotate(vectors, cosine, sine_rows):
    half = vectors.shape[-1] // 2
    first, second = vectors[..., :half], vectors[..., half:]
    return jnp.concatenate(
        [first * cosine - second * sine_rows, second * cosine + first * sine_rows], axis=-1
    )


def product(one, two):
    return jnp.dot(one, two, preferred_element_type=F32)


def times_transposed(one, two):
    return lax.dot_general(one, two, (((1,), (1,)), ((), ())), preferred_element_type=F32)


def inner_rows(one, two):
    return lax.dot_general(one, two, (((0,), (0,)), ((), ())), preferred_element_type=F32)


def einsum(form, one, two):
    return jnp.einsum(form, one, two, preferred_element_type=F32)


def halves(weight):
    rows, columns = weight.shape
    return weight.reshape(rows, 2, columns // 2).transpose(1, 0, 2)


def joined(pair):
    return jnp.concatenate([pair[0], pair[1]], axis=1)


def local(
    dp,
    tokens,
    seg_ids,
    q_weight,
    k_weight,
    v_weight,
    o_weight,
    attn_gain,
    gate_weight,
    up_weight,
    down_weight,
    mlp_gain,
    out_grad,
):
    zn = dp // 4
    units = zn * 2
    count, width = tokens.shape
    rows = q_weight.shape[0]
    blocks, block_rows = 2 * seg_ids.shape[0], seg_ids.shape[1]
    q_half, kv_half = q_weight.shape[1] // 2, k_weight.shape[1] // 2
    ff_half = gate_weight.shape[1] // 2
    qkv_half = q_half + 2 * kv_half
    heads, groups = q_half // HEAD_DIM, kv_half // HEAD_DIM
    early = [2 * rows * part // 256 // 8 * 8 for part in (32, 40, 32, 48)]
    early_sums = max(16, 2 * rows * 3 // 256 * 16)

    chip = 2 * count
    inverse = 1.0 / 10000.0 ** (np.arange(0, HEAD_DIM, 2, dtype=np.float32) / HEAD_DIM)
    inverse = np.tile(inverse.astype(np.float32), 4)[None]
    sign = np.tile(np.repeat(np.array([-1.0, 1.0], np.float32), HEAD_DIM // 2), 2)[None]
    (
        qkv_full,
        o_full,
        grads_chip,
        segment,
        gate_full,
        up_full,
        down_full,
        mid,
        normed_two,
        activated,
        gate_grad,
        up_grad,
        normed,
        turned,
        context,
        cosines,
        sines,
        gain_rows,
    ) = call(
        functools.partial(forward, zn, early),
        "forward",
        0,
        (
            q_weight,
            k_weight,
            v_weight,
            o_weight,
            attn_gain[None],
            mlp_gain[None],
            tokens,
            out_grad,
            seg_ids,
            gate_weight,
            up_weight,
            down_weight,
            inverse,
            sign,
        ),
        [VMEM] * 6 + [ANY] * 2 + [VMEM] + [ANY] * 3 + [VMEM] * 2,
        [
            ((width, qkv_half), BF16),
            ((width, q_half), BF16),
            ((units * 16, 128), F32),
            ((2, count, width), BF16),
            ((2, count, width), BF16),
            ((2,) + seg_ids.shape, jnp.int32),
        ]
        + [((width, ff_half), BF16)] * 3
        + [((count, width), F32), ((2, count, width), BF16)]
        + [((chip, ff_half), BF16)] * 3
        + [((2, count, width), BF16)]
        + [((chip, width), BF16), ((chip, qkv_half), BF16), ((chip, q_half), BF16)]
        + [((chip, 2 * HEAD_DIM), F32)] * 2
        + [((8, width), F32)],
        [ANY] * 21,
        total_buffers(count, width)
        + [
            pltpu.VMEM((2, count, width), BF16),
            DMA((3,)),
            DMA((3,)),
            DMA((2,)),
            DMA((2,)),
            DMA((2, 3)),
            DMA((2,)),
            pltpu.VMEM((chip, 2 * HEAD_DIM), F32),
            pltpu.VMEM((chip, 2 * HEAD_DIM), F32),
            pltpu.VMEM((2,) + seg_ids.shape, jnp.int32),
            pltpu.VMEM((units * 16, 128), F32),
            pltpu.VMEM((8, width), F32),
            DMA((2, 3)),
            DMA((5,)),
            pltpu.VMEM((2, rows, 2 * kv_half), BF16),
            pltpu.VMEM((2, 8, 128), F32),
            pltpu.VMEM((rows, 2 * q_half), BF16),
            pltpu.VMEM((rows, 2 * ff_half), BF16),
            pltpu.VMEM((count, width), BF16),
            pltpu.VMEM((count, width), BF16),
            pltpu.VMEM((rows, 2 * ff_half), BF16),
            pltpu.VMEM((rows, 2 * ff_half), BF16),
            pltpu.VMEM((2 * ff_half, rows), BF16),
            DMA((5,)),
        ]
        + gather_sems(6, 7, zn),
        order=(0, 1, 4, 5, 6, 7, 8, 9, 10, 11, 12, 13, 15, 16, 17, 18, 19, 20),
    )
    grads_chip = grads_chip.reshape(chip, width)
    normed_two = normed_two.reshape(chip, width)

    down_sum, gate_sum, up_sum, o_sum, q_sum, kv_sum, out, in_grad, gain_sums = call(
        functools.partial(backward, zn, early_sums),
        "backward",
        1,
        (
            normed_two,
            gate_grad,
            grads_chip,
            activated,
            gate_full,
            up_full,
            down_full,
            mid,
            up_grad,
            normed,
            context,
            turned,
            o_full,
            qkv_full,
            cosines,
            sines,
            tokens,
            segment,
            gain_rows,
        ),
        [ANY] * 17 + [VMEM] * 2,
        [((rows, 2 * ff_half), F32)] * 3
        + [
            ((rows, 2 * q_half), F32),
            ((rows, 2 * q_half), F32),
            ((2, rows, 2 * kv_half), F32),
            ((count, width), BF16),
            ((count, width), BF16),
            ((8, 4 * rows), F32),
            ((count, width), F32),
            ((2, count, width), BF16),
            ((chip, qkv_half), BF16),
            ((2, count, width), BF16),
            ((2, count, width), BF16),
            ((2, count, width), BF16),
        ]
        + [((zn, 4 * rows, ff_half), BF16)] * 3
        + [((zn, 4 * rows, q_half), BF16), ((zn, 4 * rows, qkv_half), BF16)],
        [ANY] * 8 + [VMEM] + [ANY] * 11,
        scatter_buffers(
            [(2 * rows, ff_half), (2 * rows, ff_half), (2 * rows, q_half), (2 * rows, qkv_half)], early_sums, zn
        )
        + total_buffers(count, width) * 2
        + [pltpu.VMEM((count, width), BF16)] * 2
        + [DMA((5,))]
        + gain_buffers(zn, 4 * rows)
        + [pltpu.VMEM((1, width), F32)] * 2
        + [
            DMA((4,)),
            DMA((2,)),
            DMA((3,)),
            DMA((2, 2)),
            DMA((2, 2)),
            DMA((2, 4)),
            DMA((2, 2)),
            pltpu.SemaphoreType.REGULAR,
        ]
        + scatter_sems(5, 6, zn),
        order=range(9),
    )
    plain = (gate_sum, up_sum, q_sum, out, in_grad)
    turned = (down_sum, o_sum)
    shapes = [ref.shape[::-1] for ref in turned]
    results = pl.pallas_call(
        settle,
        out_shape=[jax.ShapeDtypeStruct(shape, F32) for shape in shapes]
        + [jax.ShapeDtypeStruct(ref.shape, ref.dtype) for ref in plain]
        + [jax.ShapeDtypeStruct((rows, 2 * kv_half), F32)] * 2
        + [jax.ShapeDtypeStruct((1, rows), F32)] * 2,
        in_specs=[pl.BlockSpec(memory_space=pltpu.HBM)] * 8 + [VMEM],
        out_specs=[pl.BlockSpec(memory_space=pltpu.HBM)] * 9 + [VMEM] * 2,
        scratch_shapes=[pltpu.VMEM(ref.shape, F32) for ref in turned]
        + [pltpu.VMEM(shape, F32) for shape in shapes]
        + [pltpu.VMEM(ref.shape, ref.dtype) for ref in plain]
        + [pltpu.VMEM(kv_sum.shape, F32)]
        + [pltpu.VMEM((rows, 2 * kv_half), F32)] * 2
        + [DMA((8,)), DMA((9,))],
        name="settle",
        compiler_params=pltpu.CompilerParams(vmem_limit_bytes=62 << 20),
    )(*turned, *plain, kv_sum, gain_sums)
    down_final, o_final, gate_final, up_final, q_final, out, in_grad, k_final, v_final, one, two = results
    return (
        out,
        in_grad,
        q_final,
        k_final,
        v_final,
        o_final,
        one.reshape(rows),
        gate_final,
        up_final,
        down_final,
        two.reshape(rows),
    )


def solution(mesh):
    arguments = (
        P("dp", None),
        P("dp", None),
        P("dp", "tensor"),
        P("dp", "tensor"),
        P("dp", "tensor"),
        P("tensor", "dp"),
        P("dp"),
        P("dp", "tensor"),
        P("dp", "tensor"),
        P("tensor", "dp"),
        P("dp"),
        P("dp", None),
    )
    results = (
        P("dp", None),
        P("dp", None),
        P("dp", "tensor"),
        P("dp", "tensor"),
        P("dp", "tensor"),
        P("tensor", "dp"),
        P("dp"),
        P("dp", "tensor"),
        P("dp", "tensor"),
        P("tensor", "dp"),
        P("dp"),
    )
    return jax.shard_map(
        functools.partial(local, mesh.shape["dp"]),
        mesh=mesh,
        in_specs=arguments,
        out_specs=results,
        check_vma=False,
    )
```

```python
import functools

import jax
import jax.numpy as jnp
import numpy as np
from jax import lax
from jax.experimental import pallas as pl
from jax.experimental.pallas import tpu as pltpu
from jax.sharding import PartitionSpec as P

HEAD_DIM = 64
norm_eps = 1e-05
MESH = pl.DeviceIdType.MESH
ANY = pl.BlockSpec(memory_space=pl.ANY)
VMEM = pl.BlockSpec(memory_space=pltpu.VMEM)
DMA = pltpu.SemaphoreType.DMA
F32 = jnp.float32
BF16 = jnp.bfloat16


def place():
    d = lax.axis_index("dp")
    t = lax.axis_index("tensor")
    return d, t, d // 4, lax.rem(d // 2, 2), lax.rem(d, 2)


def enter(zn, here):
    d, t, z, x, c = here
    bar = pltpu.get_barrier_semaphore()

    def hail(device):
        pl.semaphore_signal(bar, inc=1, device_id=device, device_id_type=MESH)

    hail((d + 1 - 2 * c, t))
    hail((d + 2 - 4 * x, t))
    hail((d, 1 - t))

    @pl.when(z > 0)
    def _():
        hail((d - 4, t))

    @pl.when(z < zn - 1)
    def _():
        hail((d + 4, t))

    pl.semaphore_wait(bar, 5 - (z == 0).astype(jnp.int32) - (z == zn - 1).astype(jnp.int32))


def farthest_first(zn, z, i):
    up = 1 - (2 * z) // zn
    longer = up * (zn - 1 - z) + (1 - up) * z
    shorter = zn - 1 - longer
    rest = i - (longer - shorter)
    return jnp.where(
        rest < 0,
        z + (2 * up - 1) * (longer - i),
        z + (1 - 2 * lax.rem(jnp.maximum(rest, 0), 2)) * (shorter - jnp.maximum(rest, 0) // 2),
    )


def loop(count, body):
    def step(i, carry):
        body(i)
        return carry

    lax.fori_loop(0, count, step, 0)


def remote(src, dst, send, recv, device):
    return pltpu.make_async_remote_copy(
        src_ref=src, dst_ref=dst, send_sem=send, recv_sem=recv, device_id=device, device_id_type=MESH
    )


def by_rows(count, body, block=16):
    block = 2 * block if count % (2 * block) == 0 else block

    def step(i, carry):
        body(pl.ds(pl.multiple_of(i * block, block), block))
        return carry

    lax.fori_loop(0, count // block, step, 0)


def gather_sems(n, sources, zn):
    return [
        DMA((sources,)),
        DMA((sources,)),
        DMA((sources,)),
        DMA((n, zn)),
        DMA((n, zn)),
        DMA((n,)),
        DMA((n,)),
        DMA((n, 2, zn)),
        DMA((n, zn)),
        DMA((n, 2, zn)),
        DMA((n, zn)),
    ]


def part(ref, core, paired):
    if paired:
        return ref.at[core]
    columns = ref.shape[1] // 2
    return ref.at[:, pl.ds(pl.multiple_of(core * columns, columns), columns)]


class Gather:
    def __init__(self, zn, here, arrays, sems):
        self.zn, self.here = zn, here
        self.full = [full for _, full, _ in arrays]
        self.early = [early for _, _, early in arrays]
        self.sources = [
            (j, i) + source for j, (sources, _, _) in enumerate(arrays) for i, source in enumerate(sources)
        ]
        (
            self.loc,
            self.cs,
            self.cr,
            self.xs,
            self.xr,
            self.es,
            self.er,
            self.zs,
            self.zr,
            self.bs,
            self.br,
        ) = sems

    def unit(self, j, unit, first, count):
        rows = self.full[j].shape[0] // (2 * self.zn)
        return pl.ds(pl.multiple_of(unit * rows + first, 8), count)

    def rows(self, j, unit, early):
        rows = self.full[j].shape[0] // (2 * self.zn)
        late = rows - self.early[j]
        first, count = {None: (0, rows), True: (late, rows - late), False: (0, late)}[early]
        return self.full[j].at[self.unit(j, unit, first, count)]

    def mine(self, s):
        d, t, z, x, c = self.here
        j, _, shard, paired, first, columns = self.sources[s]
        rows = self.full[j].shape[0] // (4 * self.zn)
        return self.full[j].at[self.unit(j, z * 2 + x, c * rows, rows), pl.ds(first, columns)]

    def keep(self, s):
        _, _, shard, paired, _, _ = self.sources[s]
        return pltpu.make_async_copy(part(shard, self.here[4], paired), self.mine(s), self.loc.at[s])

    def give(self, s):
        d, t, z, x, c = self.here
        _, _, shard, paired, _, _ = self.sources[s]
        return remote(
            part(shard, 1 - c, paired), self.mine(s), self.cs.at[s], self.cr.at[s], (d + 1 - 2 * c, t)
        )

    def x_late(self, j, o):
        d, t, z, x, c = self.here
        ref = self.rows(j, o * 2 + x, False)
        return remote(ref, ref, self.xs.at[j, o], self.xr.at[j, o], (d + 2 - 4 * x, t))

    def x_early(self, j):
        d, t, z, x, c = self.here
        ref = self.rows(j, z * 2 + x, True)
        return remote(ref, ref, self.es.at[j], self.er.at[j], (d + 2 - 4 * x, t))

    def along(self, j, o, down):
        d, t, z, x, c = self.here
        ref = self.rows(j, o * 2 + x, None)
        return remote(ref, ref, self.zs.at[j, down, o], self.zr.at[j, o], (d + 4 - 8 * down, t))

    def along_early(self, j, o, down):
        d, t, z, x, c = self.here
        ref = self.rows(j, o * 2 + 1 - x, True)
        return remote(ref, ref, self.bs.at[j, down, o], self.br.at[j, o], (d + 4 - 8 * down, t))

    def start(self, arrays):
        for s, source in enumerate(self.sources):
            if source[0] in arrays:
                self.give(s).start()
                self.keep(s).start()

    def ready(self, arrays):
        for j in arrays:
            for s, source in enumerate(self.sources):
                if source[0] == j:
                    self.keep(s).wait()
                    self.give(s).wait_recv()
            if self.early[j]:
                self.x_early(j).start()

    def start_own(self, arrays):
        z, zn = self.here[2], self.zn
        for j in arrays:
            self.x_late(j, z).start()

            @pl.when(z < zn - 1)
            def _():
                self.along(j, z, 0).start()

            @pl.when(z > 0)
            def _():
                self.along(j, z, 1).start()

    def start_early(self, arrays):
        z, zn = self.here[2], self.zn
        for j in arrays:
            if self.early[j]:
                self.x_early(j).wait_recv()

                @pl.when(z < zn - 1)
                def _():
                    self.along_early(j, z, 0).start()

                @pl.when(z > 0)
                def _():
                    self.along_early(j, z, 1).start()

    def relay(self, k, arrays):
        z, zn = self.here[2], self.zn
        o = farthest_first(zn, z, zn - 1 - k)
        down = (o > z).astype(jnp.int32)
        more = ((o < z) & (z < zn - 1)) | ((o > z) & (z > 0))
        for j in arrays:
            self.along(j, o, down).wait_recv()

            @pl.when(more)
            def _():
                self.along(j, o, down).start()

            self.x_late(j, o).start()
            if self.early[j]:
                self.along_early(j, o, down).wait_recv()

                @pl.when(more)
                def _():
                    self.along_early(j, o, down).start()

    def relays(self, first, arrays):
        loop(max(self.zn - first, 0), lambda i: self.relay(first + i, arrays))

    def arrived(self, j):
        loop(self.zn, lambda o: self.x_late(j, o).wait_recv())

    def finish(self):
        z, zn = self.here[2], self.zn
        for s in range(len(self.sources)):
            self.give(s).wait_send()
        for j in range(len(self.full)):
            if self.early[j]:
                self.x_early(j).wait_send()

            def step(o, j=j):
                self.x_late(j, o).wait_send()

                def sent(down):
                    self.along(j, o, down).wait_send()
                    if self.early[j]:
                        self.along_early(j, o, down).wait_send()

                @pl.when((o <= z) & (z < zn - 1))
                def _():
                    sent(0)

                @pl.when((o >= z) & (z > 0))
                def _():
                    sent(1)

            loop(zn, step)


def scatter_sems(n, outs, zn):
    return [
        DMA((n, zn)),
        DMA((n, zn)),
        DMA((n, zn)),
        DMA((n, zn)),
        DMA((n, zn)),
        DMA((n, zn + 1)),
        DMA((n, 2, zn)),
        DMA((n, zn)),
        DMA((n, zn + 1)),
        DMA((n,)),
        DMA((n,)),
        DMA((outs,)),
        DMA((outs,)),
        DMA((outs,)),
    ]


def scatter_buffers(shapes, early, zn):
    out = []
    for rows, columns in shapes:
        late = rows - early
        out += [
            pltpu.VMEM((zn, late, columns), BF16),
            pltpu.VMEM((zn, late, columns), BF16),
            pltpu.VMEM((zn + 1, late, columns), BF16),
            pltpu.VMEM((zn, 2, early, columns), BF16),
            pltpu.VMEM((zn + 1, 2, early, columns), BF16),
            pltpu.VMEM((early, columns), BF16),
            pltpu.VMEM((rows, columns), F32),
        ]
    return out


SCATTER_BUFFERS = 7


class Scatter:
    def __init__(self, zn, here, early, arrays, sems):
        self.zn, self.here, self.early = zn, here, early
        self.term = [term for term, _, _ in arrays]
        self.buffers = [buffers for _, buffers, _ in arrays]
        self.results = [(j,) + result for j, (_, _, results) in enumerate(arrays) for result in results]
        (
            self.st,
            self.ls,
            self.xs,
            self.xr,
            self.zs,
            self.zr,
            self.bls,
            self.bs,
            self.br,
            self.es,
            self.er,
            self.cs,
            self.cr,
            self.loc,
        ) = sems

    def unit(self, j, o, x, first, count):
        rows = self.term[j].shape[1] // 2
        return self.term[j].at[o, pl.ds(pl.multiple_of(x * rows + first, 16), count)]

    def late(self, j):
        return self.buffers[j][0].shape[1]

    def load(self, j, o):
        return pltpu.make_async_copy(
            self.unit(j, o, self.here[3], 0, self.late(j)), self.buffers[j][0].at[o], self.ls.at[j, o]
        )

    def load_early(self, j, o, other):
        x = self.here[3]
        return pltpu.make_async_copy(
            self.unit(j, o, 1 - x if other else x, self.late(j), self.early),
            self.buffers[j][3].at[o, other],
            self.bls.at[j, other, o],
        )

    def across(self, j, o):
        d, t, z, x, c = self.here
        return remote(
            self.unit(j, o, 1 - x, 0, self.late(j)),
            self.buffers[j][1].at[o],
            self.xs.at[j, o],
            self.xr.at[j, o],
            (d + 2 - 4 * x, t),
        )

    def across_early(self, j):
        d, t, z, x, c = self.here
        return remote(
            self.buffers[j][3].at[z, 1], self.buffers[j][5], self.es.at[j], self.er.at[j], (d + 2 - 4 * x, t)
        )

    def along(self, j, o, slot, down):
        d, t, z, x, c = self.here
        own, line = self.buffers[j][0], self.buffers[j][2]
        return remote(own.at[o], line.at[slot], self.zs.at[j, o], self.zr.at[j, slot], (d + 4 - 8 * down, t))

    def along_early(self, j, o, slot, down):
        d, t, z, x, c = self.here
        own, line = self.buffers[j][3], self.buffers[j][4]
        return remote(own.at[o], line.at[slot], self.bs.at[j, o], self.br.at[j, slot], (d + 4 - 8 * down, t))

    def give(self, r):
        d, t, z, x, c = self.here
        j, out, paired, first, columns = self.results[r]
        rows = out.shape[-2]
        ref = self.buffers[j][6].at[
            pl.ds(pl.multiple_of((1 - c) * rows, rows), rows), pl.ds(first, columns)
        ]
        return remote(ref, part(out, c, paired), self.cs.at[r], self.cr.at[r], (d + 1 - 2 * c, t))

    def keep(self, r):
        c = self.here[4]
        j, out, paired, first, columns = self.results[r]
        rows = out.shape[-2]
        ref = self.buffers[j][6].at[pl.ds(pl.multiple_of(c * rows, rows), rows), pl.ds(first, columns)]
        return pltpu.make_async_copy(ref, part(out, c, paired), self.loc.at[r])

    def store(self, j, o, stage, slot):
        columns = self.term[j].shape[2]
        return pltpu.make_async_copy(
            stage.at[slot, :, pl.ds(0, columns)], self.term[j].at[o], self.st.at[j, o]
        )

    def make(self, j, left, right, stage, between=None):
        z, zn = self.here[2], self.zn
        wide, columns = self.term[j].shape[1:]
        block = min(256, wide)

        def send(i):
            o = farthest_first(zn, z, i)
            self.store(j, o, stage, lax.rem(i, 2)).wait()
            self.across(j, o).start()
            for other in range(2):
                self.load_early(j, o, other).start()
            self.load(j, o).start()

        def compute(i):
            o = farthest_first(zn, z, i)
            slot = lax.rem(i, 2)

            def body(m):
                at = pl.multiple_of(o * wide + m * block, block)
                value = inner_rows(left[:, pl.ds(at, block)], right[...])
                stage[slot, pl.ds(pl.multiple_of(m * block, block), block), pl.ds(0, columns)] = value.astype(
                    BF16
                )

            loop(wide // block, body)
            self.store(j, o, stage, slot).start()

        def both(i):
            compute(i)
            send(i - 1)

        compute(0)
        if between is not None:
            between()
        loop(zn - 1, lambda i: both(i + 1))
        send(zn - 1)

    def add(self, j, o, slots):
        own, got, line = self.buffers[j][:3]

        def body(at):
            value = own[o, at].astype(F32) + got[o, at].astype(F32)
            for slot in slots:
                value = value + line[slot, at].astype(F32)
            own[o, at] = value.astype(BF16)

        by_rows(own.shape[1], body)

    def add_early(self, j, o, slots):
        own, line = self.buffers[j][3:5]
        for other in range(2):

            def body(at):
                value = own[o, other, at].astype(F32)
                for slot in slots:
                    value = value + line[slot, other, at].astype(F32)
                own[o, other, at] = value.astype(BF16)

            by_rows(own.shape[2], body)

    def route(self, i):
        z, zn = self.here[2], self.zn
        o = farthest_first(zn, z, i)
        down = (o < z).astype(jnp.int32)
        distance = jnp.maximum((o - z) * (1 - 2 * down), 1)
        slot = o + (zn - o) * down * (1 // distance)
        inner = ((o > z) & (z > 0)) | ((o < z) & (z < zn - 1))
        return o, slot, down, inner

    def hop_early(self, j, i):
        o, slot, down, inner = self.route(i)
        for other in range(2):
            self.load_early(j, o, other).wait()

        @pl.when(inner)
        def _():
            self.along_early(j, o, o, down).wait_recv()
            self.add_early(j, o, [o])

        self.along_early(j, o, slot, down).start()

    def hop(self, j, i):
        o, slot, down, inner = self.route(i)
        self.load(j, o).wait()
        self.across(j, o).wait_recv()

        @pl.when(inner)
        def _():
            self.along(j, o, o, down).wait_recv()
            self.add(j, o, [o])

        @pl.when(jnp.logical_not(inner))
        def _():
            self.add(j, o, [])

        self.along(j, o, slot, down).start()

    def third(self, hop, j, g):
        hops = self.zn - 1
        first = g * hops // 3
        loop((g + 1) * hops // 3 - first, lambda i: hop(j, first + i))

    def early_third(self, j, g):
        self.third(self.hop_early, j, g)

    def late_third(self, j, g):
        self.third(self.hop, j, g)

    def at_home(self, action):
        z, zn = self.here[2], self.zn

        @pl.when((z > 0) & (z < zn - 1))
        def _():
            action([z, zn])

        @pl.when(z == 0)
        def _():
            action([zn])

        @pl.when(z == zn - 1)
        def _():
            action([z])

    def early_home(self, j):
        z = self.here[2]
        for other in range(2):
            self.load_early(j, z, other).wait()

        def home(slots):
            for slot in slots:
                self.along_early(j, z, slot, 0).wait_recv()
            self.add_early(j, z, slots)

        self.at_home(home)
        self.across_early(j).start()

    def home(self, j):
        z = self.here[2]
        own, got, line, early, _, other_early, total = self.buffers[j]
        late = self.late(j)
        self.load(j, z).wait()
        self.across(j, z).wait_recv()

        def last(slots):
            for slot in slots:
                self.along(j, z, slot, 0).wait_recv()

            def body(at):
                value = own[z, at].astype(F32) + got[z, at].astype(F32)
                for slot in slots:
                    value = value + line[slot, at].astype(F32)
                total[at] = value

            by_rows(late, body)

        self.at_home(last)
        self.across_early(j).wait_recv()
        for i in range(self.early // 16):
            at = pl.ds(16 * i, 16)
            total[pl.ds(late + 16 * i, 16)] = early[z, 0, at].astype(F32) + other_early[at].astype(F32)
        for r, result in enumerate(self.results):
            if result[0] == j:
                self.give(r).start()
                self.keep(r).start()

    def done(self, j):
        z = self.here[2]
        for r, result in enumerate(self.results):
            if result[0] == j:
                self.give(r).wait()
                self.keep(r).wait()
        self.across_early(j).wait_send()

        def sent(o):
            self.across(j, o).wait_send()

            @pl.when(o != z)
            def _():
                self.along(j, o, 0, 0).wait_send()
                self.along_early(j, o, 0, 0).wait_send()

        loop(self.zn, sent)

    def lend(self, credit):
        d, t, z, x, c = self.here

        def tell(device):
            pl.semaphore_signal(credit, inc=1, device_id=device, device_id_type=MESH)

        tell((d + 2 - 4 * x, t))

        @pl.when(z > 0)
        def _():
            tell((d - 4, t))

        @pl.when(z < self.zn - 1)
        def _():
            tell((d + 4, t))

    def borrow(self, credit):
        z = self.here[2]
        pl.semaphore_wait(credit, 3 - (z == 0).astype(jnp.int32) - (z == self.zn - 1).astype(jnp.int32))


class Gains:
    def __init__(self, zn, here, own, got, line, sems):
        self.zn, self.here, self.own, self.got, self.line, self.sems = zn, here, own, got, line, sems

    def swap(self, i):
        d, t, z, x, c = self.here
        device = ((d + 1 - 2 * c, t), (d, 1 - t), (d + 2 - 4 * x, t))[i]
        return remote(self.own, self.got.at[i], self.sems.at[0, i], self.sems.at[1, i], device)

    def along(self, o, slot, down):
        d, t, z, x, c = self.here
        return remote(
            self.own.at[o], self.line.at[slot], self.sems.at[2, o], self.sems.at[3, slot], (d + 4 - 8 * down, t)
        )

    def start(self, rows):
        wide = self.own.shape[2]
        for o in range(self.zn):
            for i, row in enumerate(rows):
                self.own[o, pl.ds(i, 1)] = row[:, pl.ds(o * wide, wide)]
        self.swap(0).start()

    def swapped(self, i):
        self.swap(i).wait()
        self.own[...] += self.got[i]
        if i < 2:
            self.swap(i + 1).start()

    def hop(self, o, slot, down, inner):
        @pl.when(inner)
        def _():
            self.along(o, o, down).wait_recv()
            self.own[o] += self.line[o]

        self.along(o, slot, down).start()

    def steps(self, k, nearest):
        z, zn = self.here[2], self.zn

        @pl.when(z + k < zn)
        def _():
            self.hop(z + k, z + k, 0, z > 0)

        @pl.when(z - k >= 0)
        def _():
            self.hop(z - k, zn if nearest else z - k, 1, z < zn - 1)

    def run(self):
        zn = self.zn

        def step(i, carry):
            self.steps(zn - 1 - i, False)
            return carry

        lax.fori_loop(0, zn - 2, step, 0)
        self.steps(1, True)

    def finish(self, out):
        z, zn = self.here[2], self.zn
        value = self.own[z]

        @pl.when(z > 0)
        def _():
            self.along(z, z, 0).wait_recv()
            self.own[z] += self.line[z]

        @pl.when(z < zn - 1)
        def _():
            self.along(z, zn, 1).wait_recv()
            self.own[z] += self.line[zn]

        out[...] = self.own[z]

        def step(o, carry):
            @pl.when(o != z)
            def _():
                self.along(o, 0, 0).wait_send()

            return carry

        lax.fori_loop(0, zn, step, 0)


def gain_buffers(zn, wide):
    return [
        pltpu.VMEM((zn, 8, wide), F32),
        pltpu.VMEM((3, zn, 8, wide), F32),
        pltpu.VMEM((zn + 1, 8, wide), F32),
        DMA((4, zn + 1)),
    ]


class Total:
    def __init__(self, here, term, from_core, half, from_pair, sems):
        self.here, self.term, self.from_core, self.half, self.from_pair = here, term, from_core, half, from_pair
        self.sems = sems

    def core(self):
        d, t, z, x, c = self.here
        return remote(self.term.at[1 - c], self.from_core, self.sems.at[0], self.sems.at[1], (d + 1 - 2 * c, t))

    def load(self):
        return pltpu.make_async_copy(self.term.at[self.here[4]], self.half, self.sems.at[4])

    def start(self):
        self.core().start()
        self.load().start()

    def pair(self):
        d, t, z, x, c = self.here
        return remote(self.half, self.from_pair, self.sems.at[2], self.sems.at[3], (d, 1 - t))

    def meet(self, loaded=True, send=True):
        if loaded:
            self.load().wait()
        self.core().wait_recv()

        def body(at):
            self.half[at] = (self.half[at].astype(F32) + self.from_core[at].astype(F32)).astype(BF16)

        by_rows(self.half.shape[0], body)
        if send:
            self.pair().start()

    def rows(self, at):
        return self.half[at].astype(F32) + self.from_pair[at].astype(F32)

    def finish(self):
        self.core().wait_send()
        self.pair().wait_send()


def total_buffers(tokens, width):
    return [pltpu.VMEM((tokens, width), BF16)] * 3 + [DMA((5,))]


def share(here, src, dst, sems):
    d, t, z, x, c = here
    return (
        pltpu.make_async_copy(src, dst.at[c], sems.at[0]),
        remote(src, dst.at[c], sems.at[1], sems.at[2], (d + 1 - 2 * c, t)),
    )


def lanes(shape):
    return lax.broadcasted_iota(jnp.int32, shape, 1)


def partner(value):
    half = HEAD_DIM // 2
    wide = 2 * HEAD_DIM
    lower = lax.rem(lanes(value.shape), HEAD_DIM) < half
    return jnp.where(lower, pltpu.roll(value, wide - half, 1), pltpu.roll(value, half, 1))


def same_segment(row):
    count = row.shape[1]
    wide = jnp.broadcast_to(row, (count, count))
    before = lax.broadcasted_iota(jnp.int32, wide.shape, 1) < lax.broadcasted_iota(jnp.int32, wide.shape, 0)
    return wide == wide.T, before


def allowed_in(row):
    same, before = same_segment(row)
    here = lax.broadcasted_iota(jnp.int32, same.shape, 1) == lax.broadcasted_iota(jnp.int32, same.shape, 0)
    return same & (before | here)


def softmax_of(queries, keys, allowed):
    scores = jnp.where(allowed, times_transposed(queries, keys) * HEAD_DIM ** (-0.5), -1e30)
    shifted = jnp.exp(scores - jnp.max(scores, axis=-1, keepdims=True))
    return shifted / jnp.sum(shifted, axis=-1, keepdims=True)


def key_value_pairs(pair):
    pair = pair.astype(F32)
    first = lanes(pair.shape) < HEAD_DIM
    key, value = jnp.where(first, pair, 0.0), jnp.where(first, 0.0, pair)
    return [
        part.astype(BF16)
        for part in (key, pltpu.roll(key, HEAD_DIM, 1), pltpu.roll(value, HEAD_DIM, 1), value)
    ]


def attention_block(turned, context, queries_wide, row):
    wide = 2 * HEAD_DIM
    allowed = allowed_in(row)
    key_one, key_two, value_one, value_two = key_value_pairs(turned[:, queries_wide:])

    def heads(p):
        at = pl.ds(pl.multiple_of(p * wide, wide), wide)
        queries = turned[:, at]
        one = softmax_of(queries, key_one, allowed).astype(BF16)
        two = softmax_of(queries, key_two, allowed).astype(BF16)
        context[:, at] = (product(one, value_one) + product(two, value_two)).astype(BF16)

    loop(queries_wide // wide, heads)


def attention_block_back(turned, grads, back, sums, queries_wide, row, cosine, sine):
    wide = 2 * HEAD_DIM
    scale = HEAD_DIM ** (-0.5)
    allowed = allowed_in(row)
    key_one, key_two, value_one, value_two = key_value_pairs(turned[:, queries_wide:])
    sums[...] = jnp.zeros_like(sums)

    def heads(p):
        at = pl.ds(pl.multiple_of(p * wide, wide), wide)
        queries, grad = turned[:, at], grads[:, at]
        total = None
        for i, (key, value) in enumerate(((key_one, value_one), (key_two, value_two))):
            probs = softmax_of(queries, key, allowed)
            sums[i] += inner_rows(probs.astype(BF16), grad)
            prob_grad = times_transposed(grad, value)
            delta = jnp.sum(probs * prob_grad, axis=-1, keepdims=True)
            score_grad = (probs * (prob_grad - delta)).astype(BF16)
            term = product(score_grad, key)
            total = term if total is None else total + term
            sums[2 + i] += inner_rows(score_grad, queries)
        total = total * scale
        back[:, at] = (total * cosine - partner(total) * sine).astype(BF16)

    loop(queries_wide // wide, heads)
    value_grad = pltpu.roll(sums[0], HEAD_DIM, 1) + sums[1]
    key_grad = (sums[2] + pltpu.roll(sums[3], HEAD_DIM, 1)) * scale
    turned_back = key_grad * cosine - partner(key_grad) * sine
    back[:, pl.ds(queries_wide, wide)] = jnp.where(
        lanes(value_grad.shape) < HEAD_DIM, turned_back, value_grad
    ).astype(BF16)


def transposed(src, dst):
    def body(n):
        at = pl.ds(pl.multiple_of(n * 128, 128), 128)
        dst[:, at] = src[at, :].astype(F32).T.astype(BF16)

    loop(src.shape[0] // 128, body)


def forward(zn, early, *refs):
    q, k_shard, v_shard, o_turned, one_shard, two_shard, tokens_in, grads_in, seg, gate_in, up_in, down_in, inverse, sign = refs[:14]
    refs = refs[2:]
    qkv_all, o_all, gains_all, chip_tokens, chip_grads, seg_all = refs[12:18]
    gate_all, up_all, down_all, mid_out, normed_out, act_out, gate_grad_out, up_grad_out = refs[18:26]
    term, normed_one_out, turned_out, context_out, cosines_out, sines_out, gain_out = refs[26:33]
    total_refs = refs[33:37]
    normed, out_sems, pair_sems, load_sems, grad_sems, stage_sems, block_sems = refs[37:44]
    cosines, sines, seg_pair, gain_tiles, gain_rows, swap_sems, seg_sems = refs[44:51]
    kv, gains, o_shard, down, tokens, grads, gate, up, down_turned, first_sems = refs[51:61]
    here = place()
    z, c = here[2], here[4]
    firsts = [
        pltpu.make_async_copy(src, dst, first_sems.at[n])
        for n, (src, dst) in enumerate(
            ((down_in, down_turned), (tokens_in, tokens), (gate_in, gate), (up_in, up), (grads_in, grads))
        )
    ]
    for copy in firsts:
        copy.start()
    enter(zn, here)
    keys, values = k_shard[...].astype(F32), v_shard[...].astype(F32)
    is_key = lanes(keys.shape) < HEAD_DIM
    kv[0] = jnp.where(is_key, keys, pltpu.roll(values, HEAD_DIM, 1)).astype(BF16)
    kv[1] = jnp.where(is_key, pltpu.roll(keys, HEAD_DIM, 1), values).astype(BF16)
    for i in range(2):
        gains[i] = jnp.zeros(gains.shape[1:], F32)
        for k, shard in enumerate((one_shard, two_shard)):
            gains[i, pl.ds(k, 1), pl.ds(0, shard.shape[1])] = shard[...].astype(F32)
    transposed(o_turned, o_shard)
    total = Total(here, term, *total_refs)
    q_half = q.shape[1] // 2
    work = Gather(
        zn,
        here,
        [
            ([(gains, True, 0, gains.shape[2])], gains_all, 0),
            ([(q, False, 0, q_half), (kv, True, q_half, kv.shape[2])], qkv_all, early[0]),
            ([(o_shard, False, 0, o_shard.shape[1] // 2)], o_all, early[0]),
        ]
        + [
            ([(shard, False, 0, shard.shape[1] // 2)], full, rows_early)
            for shard, full, rows_early in zip((down, gate, up), (down_all, gate_all, up_all), early[1:])
        ],
        refs[61:],
    )
    count, width = tokens.shape
    columns = gate_all.shape[1]
    block = seg.shape[1]
    blocks = 2 * count // block
    per = count // block
    attention_set = [0, 1, 2]
    swap = remote(seg, seg_pair.at[c], seg_sems.at[0], seg_sems.at[1], (here[0] + 1 - 2 * c, here[1]))
    swap.start()
    seg_pair[c] = seg[...]
    work.start(attention_set)
    firsts[0].wait()
    transposed(down_turned, down)
    work.start([3])
    work.ready(attention_set)
    work.start_own(attention_set)
    for copy in firsts[1:]:
        copy.wait()
    shared = [
        share(here, src, dst, swap_sems.at[n])
        for n, (src, dst) in enumerate(((tokens, chip_tokens), (grads, chip_grads)))
    ]
    for copy in shared[0]:
        copy.start()
    work.start([4, 5])
    for copy in shared[1]:
        copy.start()
    work.start_early([1, 2])
    work.ready([3])
    work.start_own([3])
    swap.wait()
    for i in range(blocks):
        row = seg_pair[i // per, pl.ds(i % per, 1)]
        same, before = same_segment(row)
        position = jnp.sum(jnp.where(same & before, 1.0, 0.0), axis=-1, keepdims=True)
        angles = position * inverse[...]
        cosines[pl.ds(i * block, block)] = jnp.cos(angles)
        sines[pl.ds(i * block, block)] = jnp.sin(angles) * sign[...]
    saves = [
        pltpu.make_async_copy(src, dst, seg_sems.at[2 + n])
        for n, (src, dst) in enumerate(((cosines, cosines_out), (sines, sines_out), (seg_pair, seg_all)))
    ]
    for copy in saves:
        copy.start()
    work.relay(1, attention_set)
    work.relay(2, attention_set)
    work.start_early([3])
    work.relays(3, attention_set)
    work.ready([4, 5])
    work.start_own([4, 5])
    work.start_early([4])
    work.arrived(0)
    load = pltpu.make_async_copy(gains_all, gain_tiles, load_sems.at[0])
    load.start()
    load.wait()
    features = width // (4 * zn)
    for owner in range(4 * zn):
        for i in range(2):
            gain_rows[pl.ds(i, 1), pl.ds(owner * features, features)] = gain_tiles[
                pl.ds(owner * 8 + i, 1), :features
            ]
    save_gains = pltpu.make_async_copy(gain_rows, gain_out, load_sems.at[1])
    save_gains.start()
    gain_one, gain = gain_rows[pl.ds(0, 1)], gain_rows[pl.ds(1, 1)]
    for copies in shared:
        for copy in copies:
            copy.wait()
    work.arrived(1)
    work.arrived(2)
    save_gains.wait()
    half = total_refs[1]

    def attention(qkv, o, inputs, normed_one, turned, context, attended):
        queries_wide = context.shape[2]
        wide = 2 * HEAD_DIM

        def place_of(i):
            return lax.rem((1 - c) * per + i, blocks)

        def rows_at(i):
            return pl.ds(pl.multiple_of(place_of(i) * block, block), block)

        def fetch_inputs(i, slot):
            which = place_of(i)
            return pltpu.make_async_copy(
                chip_tokens.at[which // per, pl.ds(pl.multiple_of(lax.rem(which, per) * block, block), block)],
                inputs.at[slot],
                grad_sems.at[slot],
            )

        def stores(i, slot):
            return [
                pltpu.make_async_copy(buffer.at[slot], out.at[rows_at(i)], stage_sems.at[slot, n])
                for n, (buffer, out) in enumerate(
                    ((normed_one, normed_one_out), (turned, turned_out), (context, context_out))
                )
            ]

        def store_term(i, slot):
            return pltpu.make_async_copy(
                attended.at[slot],
                term.at[1 - c, pl.ds(pl.multiple_of(i * block, block), block)],
                block_sems.at[slot],
            )

        fetch_inputs(0, 0).start()
        loads = [
            pltpu.make_async_copy(qkv_all, qkv, load_sems.at[0]),
            pltpu.make_async_copy(o_all, o, load_sems.at[1]),
        ]
        for load in loads:
            load.start()
        for load in loads:
            load.wait()

        def one_block(i):
            slot = lax.rem(i, 2)
            to = rows_at(i)
            fetch_inputs(i, slot).wait()

            @pl.when(i + 1 < blocks)
            def _():
                fetch_inputs(i + 1, 1 - slot).start()

            @pl.when(i > 1)
            def _():
                for copy in stores(i - 2, slot):
                    copy.wait()

            def norm(at):
                value = inputs[slot, at].astype(F32)
                factor = lax.rsqrt(jnp.mean(value * value, axis=-1, keepdims=True) + norm_eps)
                normed_one[slot, at] = (value * factor * gain_one).astype(BF16)

            by_rows(block, norm)
            cosine, sine = cosines[to], sines[to]
            raw = product(normed_one[slot], qkv[...])
            for first in range(0, queries_wide, wide):
                value = raw[:, first : first + wide]
                turned[slot, :, pl.ds(first, wide)] = (value * cosine + partner(value) * sine).astype(BF16)
            value = raw[:, queries_wide:]
            is_key = lanes(value.shape) < HEAD_DIM
            turned[slot, :, pl.ds(queries_wide, wide)] = jnp.where(
                is_key, value * cosine + partner(value) * sine, value
            ).astype(BF16)
            which = place_of(i)
            row = seg_pair[which // per, pl.ds(lax.rem(which, per), 1)]
            attention_block(turned.at[slot], context.at[slot], queries_wide, row)
            for copy in stores(i, slot):
                copy.start()
            return slot

        def other(i):
            slot = one_block(i)
            attended[slot] = times_transposed(context[slot], o[...]).astype(BF16)
            store_term(i, slot).start()

        def own(i):
            slot = one_block(per + i)
            half[pl.ds(pl.multiple_of(i * block, block), block)] = times_transposed(
                context[slot], o[...]
            ).astype(BF16)

        loop(per, other)
        for i in range(per):
            store_term(i, i % 2).wait()
        total.core().start()
        loop(per, own)
        for i in range(blocks - 2, blocks):
            for copy in stores(i, i % 2):
                copy.wait()

    pl.run_scoped(
        attention,
        pltpu.VMEM(qkv_all.shape, BF16),
        pltpu.VMEM(o_all.shape, BF16),
        pltpu.VMEM((2, block, width), BF16),
        pltpu.VMEM((2, block, width), BF16),
        pltpu.VMEM((2, block, qkv_all.shape[1]), BF16),
        pltpu.VMEM((2, block, o_all.shape[1]), BF16),
        pltpu.VMEM((2, block, width), BF16),
    )
    total.meet(False)
    for j in (3, 4):
        work.relay(1, [j])
        work.relay(2, [j])
    work.relays(3, [3])

    def sums(mid):
        total.pair().wait_recv()

        def body(at):
            value = tokens[at].astype(F32) + total.rows(at)
            mid[at] = value
            factor = lax.rsqrt(jnp.mean(value * value, axis=-1, keepdims=True) + norm_eps)
            normed[c, at] = (value * factor * gain).astype(BF16)

        by_rows(count, body)
        save = pltpu.make_async_copy(mid, mid_out, out_sems.at[0])
        save.start()
        for copy in share(here, normed.at[c], normed, pair_sems)[1:]:
            copy.start()
        save.wait()

    def hidden(first, second, silu, slope, upward, up_grad, inputs, result, stages):
        def fetch_grads(i, slot):
            return pltpu.make_async_copy(
                chip_grads.at[i // per, pl.ds(pl.multiple_of(lax.rem(i, per) * block, block), block)],
                inputs.at[slot],
                grad_sems.at[slot],
            )

        def at_block(i):
            return pl.ds(pl.multiple_of(i * block, block), block)

        fetch_grads(0, 0).start()
        pl.run_scoped(sums, pltpu.VMEM((count, width), F32))
        work.relays(3, [4])
        work.start_early([5])
        work.arrived(3)
        load = pltpu.make_async_copy(down_all, first, load_sems.at[0])
        load.start()
        load.wait()

        def hidden_block(i):
            slot = lax.rem(i, 2)
            fetch_grads(i, slot).wait()

            @pl.when(i + 1 < blocks)
            def _():
                fetch_grads(i + 1, 1 - slot).start()

            slope[at_block(i)] = product(inputs[slot], first[...])

        loop(blocks, hidden_block)
        work.relay(1, [5])
        work.relay(2, [5])
        upward[...] = jnp.zeros_like(upward)
        work.arrived(4)
        load = pltpu.make_async_copy(gate_all, second, load_sems.at[1])
        load.start()
        share(here, normed.at[c], normed, pair_sems)[1].wait()
        save = pltpu.make_async_copy(normed, normed_out, out_sems.at[1])
        save.start()
        load.wait()

        def gate_block(i):
            result[...] = product(normed[i // per, at_block(lax.rem(i, per))], second[...])

            def body(at):
                to = pl.ds(pl.multiple_of(i * block + at.start, 16), at.size)
                gated = result[at]
                grad = slope[to]
                sigmoid = 1.0 / (1.0 + jnp.exp(-gated))
                silu[to] = gated * sigmoid
                up_grad[to] = (grad * gated * sigmoid).astype(BF16)
                slope[to] = grad * (sigmoid * (1.0 + gated * (1.0 - sigmoid)))

            by_rows(block, body)

        loop(blocks, gate_block)
        save_up = pltpu.make_async_copy(up_grad, up_grad_out, out_sems.at[2])
        save_up.start()
        work.relays(3, [5])
        group = width // zn

        def up_rows(k):
            o = farthest_first(zn, z, zn - 1 - k)
            at = pl.ds(pl.multiple_of(o * group, group), group)
            work.x_late(5, o).wait_recv()
            load = pltpu.make_async_copy(up_all.at[at], first.at[at], load_sems.at[0])
            load.start()
            load.wait()

            def up_part(i):
                rows = normed[i // per, at_block(lax.rem(i, per)), at]
                upward[at_block(i)] += product(rows, first[at])

            loop(blocks, up_part)

        loop(zn, up_rows)

        def stores(i, slot):
            to = at_block(i)
            return (
                pltpu.make_async_copy(stages.at[slot, 0], act_out.at[to], stage_sems.at[slot, 0]),
                pltpu.make_async_copy(stages.at[slot, 1], gate_grad_out.at[to], stage_sems.at[slot, 1]),
            )

        def up_block(i):
            slot = lax.rem(i, 2)

            @pl.when(i > 1)
            def _():
                for copy in stores(i - 2, slot):
                    copy.wait()

            def body(at):
                to = pl.ds(pl.multiple_of(i * block + at.start, 16), at.size)
                stages[slot, 0, at] = (silu[to] * upward[to]).astype(BF16)
                stages[slot, 1, at] = (slope[to] * upward[to]).astype(BF16)

            by_rows(block, body)
            for copy in stores(i, slot):
                copy.start()

        loop(blocks, up_block)
        for i in range(max(blocks - 2, 0), blocks):
            for copy in stores(i, i % 2):
                copy.wait()
        save.wait()
        save_up.wait()

    pl.run_scoped(
        hidden,
        pltpu.VMEM((width, columns), BF16),
        pltpu.VMEM((width, columns), BF16),
        pltpu.VMEM((2 * count, columns), F32),
        pltpu.VMEM((2 * count, columns), F32),
        pltpu.VMEM((2 * count, columns), F32),
        pltpu.VMEM((2 * count, columns), BF16),
        pltpu.VMEM((2, block, width), BF16),
        pltpu.VMEM((block, columns), F32),
        pltpu.VMEM((2, 2, block, columns), BF16),
    )
    work.finish()
    total.finish()
    for copy in saves:
        copy.wait()


def fetch(pairs, sems):
    copies = [pltpu.make_async_copy(src, dst, sems.at[i]) for i, (src, dst) in enumerate(pairs)]
    for copy in copies:
        copy.start()
    return copies


def backward(zn, early, *refs):
    normed_two, gate_grad, chip_grads, activated, gate_all, up_all, down_all, mid_in, up_grad = refs[:9]
    normed_one, context, turned_all, o_all, qkv_all, cosines, sines, tokens_in, rows_of, gain_rows = refs[9:19]
    down_out, gate_out, up_out, o_out, q_out, kv_out, out, in_grad, gain_out = refs[19:28]
    mid_grad_all, branch_all, qkv_back, in_term, out_term, back_term = refs[28:34]
    down, gate, up, o_sums, qkv_sums = refs[34:39]
    n = SCATTER_BUFFERS
    buffers, refs = refs[39 : 39 + 4 * n], refs[39 + 4 * n :]
    back_refs, front_refs, in_refs = refs[:4], refs[4:8], refs[8:11]
    gain_refs, (one_sum, two_sum), refs = refs[11:15], refs[15:17], refs[17:]
    fetch_sems, out_sems, pair_sems, weight_sems, stage_sems, block_sems, back_sems, credit = refs[:8]
    here = place()
    z, c = here[2], here[4]
    chip, width = chip_grads.shape
    count = chip // 2
    block = rows_of.shape[2]
    blocks = chip // block
    per = blocks // 2
    qkv_wide, q_half = qkv_all.shape[1], o_all.shape[1]
    enter(zn, here)
    branch, out_rows, in_rows = back_refs[0], front_refs[0], in_refs[0]
    back = Total(here, back_term, *back_refs)
    front = Total(here, out_term, *front_refs)
    total = Total(here, in_term, in_refs[0], back_refs[1], in_refs[1], in_refs[2])
    gains = Gains(zn, here, *gain_refs)
    work = Scatter(
        zn,
        here,
        early,
        [
            (down, buffers[:n], [(down_out, False, 0, down_out.shape[1] // 2)]),
            (gate, buffers[n : 2 * n], [(gate_out, False, 0, gate_out.shape[1] // 2)]),
            (up, buffers[:n], [(up_out, False, 0, up_out.shape[1] // 2)]),
            (o_sums, buffers[2 * n : 3 * n], [(o_out, False, 0, q_half)]),
            (
                qkv_sums,
                buffers[3 * n :],
                [(q_out, False, 0, q_half), (kv_out, True, q_half, kv_out.shape[2])],
            ),
        ],
        refs[8:],
    )
    def feature_terms(factors, term):
        def run(*refs):
            lefts, weights, stages = refs[:-2], refs[-2], refs[-1]
            group = weights.shape[2]
            loads = fetch([(left, ref) for (left, _), ref in zip(factors, lefts)], fetch_sems)

            def fetch_weights(i, slot):
                at = pl.ds(pl.multiple_of(i * group, group), group)
                return [
                    pltpu.make_async_copy(full.at[at], weights.at[slot, k], weight_sems.at[slot, k])
                    for k, (_, full) in enumerate(factors)
                ]

            def stores(i, slot):
                to = pl.ds(pl.multiple_of(i * group, group), group)
                return [
                    pltpu.make_async_copy(
                        stages.at[slot, pl.ds(half * count, count)], term.at[half, :, to], stage_sems.at[slot, half]
                    )
                    for half in range(2)
                ]

            for copy in fetch_weights(0, 0):
                copy.start()
            for load in loads:
                load.wait()

            def step(i):
                slot = lax.rem(i, 2)
                for copy in fetch_weights(i, slot):
                    copy.wait()

                @pl.when(i + 1 < width // group)
                def _():
                    for copy in fetch_weights(i + 1, 1 - slot):
                        copy.start()

                @pl.when(i > 1)
                def _():
                    for copy in stores(i - 2, slot):
                        copy.wait()

                value = times_transposed(lefts[0][...], weights[slot, 0])
                for k in range(1, len(lefts)):
                    value = value + times_transposed(lefts[k][...], weights[slot, k])
                stages[slot] = value.astype(BF16)
                for copy in stores(i, slot):
                    copy.start()

            loop(width // group, step)
            for i in range(width // group - 2, width // group):
                for copy in stores(i, i % 2):
                    copy.wait()

        pl.run_scoped(
            run,
            *[pltpu.VMEM((chip, wide), BF16)] * len(factors),
            pltpu.VMEM((2, len(factors), 256, wide), BF16),
            pltpu.VMEM((2, chip, 256), BF16),
        )

    wide = down.shape[2]
    operands = [pltpu.VMEM((chip, width), BF16), pltpu.VMEM((chip, wide), BF16), pltpu.VMEM((2,) + down.shape[1:], BF16)]

    def terms_of(j, left_all, right_all):
        def run(left, right, stage):
            for load in fetch(((left_all, left), (right_all, right)), fetch_sems):
                load.wait()
            work.make(j, left, right, stage)

        pl.run_scoped(run, *operands)

    terms_of(0, chip_grads, activated)
    for g in range(3):
        work.early_third(0, g)
    feature_terms([(gate_grad, gate_all), (up_grad, up_all)], back_term)
    back.start()
    work.late_third(0, 0)
    feature_terms([(activated, down_all)], out_term)
    back.meet()
    front.start()
    work.late_third(0, 1)
    work.early_home(0)
    work.late_third(0, 2)
    terms_of(1, normed_two, gate_grad)
    work.early_third(1, 0)

    def sums(mid, mid_grad, grads):
        for load in fetch(
            (
                (mid_in, mid),
                (chip_grads.at[pl.ds(pl.multiple_of(c * count, 16), count)], grads),
            ),
            fetch_sems,
        ):
            load.wait()
        gain = gain_rows[pl.ds(1, 1)]
        two_sum[...] = jnp.zeros_like(two_sum)

        def body_gain(at):
            value = mid[at]
            factor = lax.rsqrt(jnp.mean(value * value, axis=-1, keepdims=True) + norm_eps)
            two_sum[...] += jnp.sum(back.half[at].astype(F32) * (value * factor), axis=0, keepdims=True)

        by_rows(count, body_gain)
        work.late_third(1, 0)
        work.early_third(1, 1)
        work.early_third(1, 2)
        work.home(0)
        work.done(0)
        work.lend(credit)
        front.meet()
        back.pair().wait_recv()

        def body(at):
            value = mid[at]
            factor = lax.rsqrt(jnp.mean(value * value, axis=-1, keepdims=True) + norm_eps)
            scaled = back.rows(at) * gain
            result = (
                grads[at].astype(F32)
                + factor * scaled
                - value * (factor * factor * factor) * jnp.mean(scaled * value, axis=-1, keepdims=True)
            )
            mid_grad[at] = result
            branch[at] = result.astype(BF16)

        by_rows(count, body)
        save = pltpu.make_async_copy(mid_grad, mid_grad_all, out_sems.at[0])
        save.start()
        for copy in share(here, branch, branch_all, pair_sems):
            copy.start()
        work.late_third(1, 1)
        save.wait()

    pl.run_scoped(
        sums, pltpu.VMEM((count, width), F32), pltpu.VMEM((count, width), F32), pltpu.VMEM((count, width), BF16)
    )

    def middle_terms(left, right, stage):
        for copy in share(here, branch, branch_all, pair_sems):
            copy.wait()
        right_o = right.at[:, pl.ds(0, q_half)]
        loads = fetch(
            ((branch_all.at[0], left.at[pl.ds(0, count)]), (branch_all.at[1], left.at[pl.ds(count, count)])),
            fetch_sems,
        )
        loads.append(pltpu.make_async_copy(context, right_o, fetch_sems.at[2]))
        loads[2].start()
        for load in loads:
            load.wait()
        work.make(3, left, right_o, stage)
        loads = fetch(((normed_two, left), (up_grad, right)), fetch_sems)
        work.early_third(3, 0)
        work.late_third(1, 2)
        for load in loads:
            load.wait()
        work.borrow(credit)
        work.make(2, left, right, stage)

    pl.run_scoped(middle_terms, *operands)
    work.early_third(2, 0)

    def attention(o, qkv, inputs, turned, grads, backs, terms_out, cosine, sine, accumulators):
        def which(i):
            return lax.rem((1 - c) * per + i, blocks)

        def rows_at(i):
            return pl.ds(pl.multiple_of(i * block, block), block)

        def fetches(i, slot):
            b = which(i)
            sources = (
                (branch_all.at[b // per, rows_at(lax.rem(b, per))], inputs),
                (turned_all.at[rows_at(b)], turned),
                (cosines.at[rows_at(b)], cosine),
                (sines.at[rows_at(b)], sine),
            )
            return [
                pltpu.make_async_copy(source, buffer.at[slot], block_sems.at[slot, k])
                for k, (source, buffer) in enumerate(sources)
            ]

        def stores(i, slot):
            b = which(i)
            return [
                pltpu.make_async_copy(backs.at[slot], qkv_back.at[rows_at(b)], back_sems.at[slot, 0]),
                pltpu.make_async_copy(
                    terms_out.at[slot], in_term.at[b // per, rows_at(lax.rem(b, per))], back_sems.at[slot, 1]
                ),
            ]

        loads = fetch(((o_all, o), (qkv_all, qkv)), fetch_sems)
        for copy in fetches(0, 0):
            copy.start()
        for load in loads:
            load.wait()

        def step(i):
            slot = lax.rem(i, 2)

            @pl.when(i == per)
            def _():
                for done in range(per):
                    for copy in stores(done, done % 2):
                        copy.wait()
                total.core().start()
                work.early_third(2, 2)

            @pl.when(i == 1)
            def _():
                work.early_third(3, 1)
                work.early_third(2, 1)

            @pl.when(i == blocks - 1)
            def _():
                work.late_third(2, 0)

            for copy in fetches(i, slot):
                copy.wait()

            @pl.when(i + 1 < blocks)
            def _():
                for copy in fetches(i + 1, 1 - slot):
                    copy.start()

            grads[...] = product(inputs[slot], o[...]).astype(BF16)
            attention_block_back(
                turned.at[slot],
                grads,
                backs.at[slot],
                accumulators,
                q_half,
                rows_of[which(i) // per, pl.ds(lax.rem(which(i), per), 1)],
                cosine[slot],
                sine[slot],
            )
            terms_out[slot] = times_transposed(backs[slot], qkv[...]).astype(BF16)
            for copy in stores(i, slot):
                copy.start()

        loop(blocks, step)
        for i in range(per, blocks):
            for copy in stores(i, i % 2):
                copy.wait()

    pl.run_scoped(
        attention,
        pltpu.VMEM(o_all.shape, BF16),
        pltpu.VMEM(qkv_all.shape, BF16),
        pltpu.VMEM((2, block, width), BF16),
        pltpu.VMEM((2, block, qkv_wide), BF16),
        pltpu.VMEM((block, q_half), BF16),
        pltpu.VMEM((2, block, qkv_wide), BF16),
        pltpu.VMEM((2, block, width), BF16),
        pltpu.VMEM((2, block, 2 * HEAD_DIM), F32),
        pltpu.VMEM((2, block, 2 * HEAD_DIM), F32),
        pltpu.VMEM((4, block, 2 * HEAD_DIM), F32),
    )
    back.finish()
    total.load().start()

    def meeting(tokens):
        load = fetch(((tokens_in, tokens),), fetch_sems)[0]
        total.meet(send=False)
        load.wait()
        one_sum[...] = jnp.zeros_like(one_sum)

        def body_gain(at):
            value = tokens[at].astype(F32)
            factor = lax.rsqrt(jnp.mean(value * value, axis=-1, keepdims=True) + norm_eps)
            one_sum[...] += jnp.sum(total.half[at].astype(F32) * (value * factor), axis=0, keepdims=True)

        by_rows(count, body_gain)

    pl.run_scoped(meeting, pltpu.VMEM((count, width), BF16))
    gains.start([one_sum, two_sum])
    gains.swapped(0)
    total.pair().start()
    work.early_third(3, 2)
    work.late_third(2, 1)

    def output(mid):
        load = fetch(((mid_in, mid),), fetch_sems)[0]
        front.pair().wait_recv()
        load.wait()

        def body_out(at):
            out_rows[at] = (mid[at] + front.rows(at)).astype(BF16)

        by_rows(count, body_out)

    pl.run_scoped(output, pltpu.VMEM((count, width), F32))
    save_out = pltpu.make_async_copy(out_rows, out, out_sems.at[1])
    save_out.start()
    work.late_third(3, 0)
    work.late_third(2, 2)
    work.early_home(2)
    work.early_home(1)

    def last_terms(left, right, stage):
        right_qkv = right.at[:, pl.ds(0, qkv_wide)]
        for load in fetch(((normed_one, left), (qkv_back, right_qkv)), fetch_sems):
            load.wait()
        gains.swapped(1)
        work.make(4, left, right_qkv, stage)

    pl.run_scoped(last_terms, *operands)
    work.early_third(4, 0)
    work.home(1)
    work.late_third(4, 0)
    work.early_third(4, 1)
    work.early_third(4, 2)
    work.early_home(3)
    work.late_third(3, 1)
    work.home(2)
    gains.swapped(2)
    gains.run()
    work.late_third(4, 1)
    work.late_third(4, 2)
    work.late_third(3, 2)
    work.early_home(4)

    def inputs_back(mid_grad, tokens):
        loads = fetch(((mid_grad_all, mid_grad), (tokens_in, tokens)), fetch_sems)
        gain = gain_rows[pl.ds(0, 1)]
        total.pair().wait_recv()
        for load in loads:
            load.wait()

        def body(at):
            value = tokens[at].astype(F32)
            factor = lax.rsqrt(jnp.mean(value * value, axis=-1, keepdims=True) + norm_eps)
            scaled = total.rows(at) * gain
            in_rows[at] = (
                mid_grad[at]
                + factor * scaled
                - value * (factor * factor * factor) * jnp.mean(scaled * value, axis=-1, keepdims=True)
            ).astype(BF16)

        by_rows(count, body)

    pl.run_scoped(inputs_back, pltpu.VMEM((count, width), F32), pltpu.VMEM((count, width), BF16))
    save_in = pltpu.make_async_copy(in_rows, in_grad, out_sems.at[0])
    save_in.start()
    gains.finish(gain_out)
    work.home(4)
    work.home(3)
    for j in (1, 2, 3, 4):
        work.done(j)
    front.finish()
    total.finish()
    save_out.wait()
    save_in.wait()


def settle(*refs):
    turned, plain, kv, gains = refs[:2], refs[2:7], refs[7], refs[8]
    turned_out, plain_out, (k_out, v_out, one_out, two_out) = refs[9:11], refs[11:16], refs[16:20]
    turned_in, turned_to, plain_at, (kv_at, k_at, v_at) = refs[20:22], refs[22:24], refs[24:29], refs[29:32]
    load_sems, store_sems = refs[32:]
    pairs = list(zip(plain, plain_at)) + list(zip(turned, turned_in)) + [(kv, kv_at)]
    loads = [pltpu.make_async_copy(src, dst, load_sems.at[n]) for n, (src, dst) in enumerate(pairs)]
    for n in (0, 1, 5, 3, 4, 2, 6, 7):
        loads[n].start()
    stores = []

    def send(src, dst):
        stores.append(pltpu.make_async_copy(src, dst, store_sems.at[len(stores)]))
        stores[-1].start()

    def pass_on(n):
        loads[n].wait()
        send(plain_at[n], plain_out[n])

    def turn(n, first, last):
        src, dst = turned_in[n], turned_to[n]

        def body(i):
            at = pl.ds(pl.multiple_of((first + i) * 128, 128), 128)
            dst[at, :] = src[:, at].T

        loop(last - first, body)

    pass_on(0)
    pass_on(1)
    groups = turned_in[0].shape[1] // 128
    loads[5].wait()
    turn(0, 0, groups // 2)
    pass_on(3)
    pass_on(4)
    turn(0, groups // 2, groups)
    send(turned_to[0], turned_out[0])
    pass_on(2)
    loads[6].wait()
    turn(1, 0, turned_in[1].shape[1] // 128)
    send(turned_to[1], turned_out[1])
    loads[7].wait()
    one, two = kv_at[0], kv_at[1]
    is_key = lanes(one.shape) < HEAD_DIM
    k_at[...] = jnp.where(is_key, one, pltpu.roll(two, HEAD_DIM, 1))
    v_at[...] = jnp.where(is_key, pltpu.roll(one, HEAD_DIM, 1), two)
    send(k_at, k_out)
    send(v_at, v_out)
    features = one_out.shape[1]
    for owner in range(4):

        @pl.when(lax.rem(lax.axis_index("dp"), 4) == owner)
        def _():
            at = pl.ds(owner * features, features)
            one_out[...] = gains[pl.ds(0, 1), at]
            two_out[...] = gains[pl.ds(1, 1), at]

    for copy in stores:
        copy.wait()


def call(kernel, name, collective_id, operands, specs, outs, out_specs, scratch, order=None):
    results = pl.pallas_call(
        kernel,
        out_shape=[jax.ShapeDtypeStruct(shape, dtype) for shape, dtype in outs],
        in_specs=specs,
        out_specs=out_specs,
        scratch_shapes=scratch,
        name=name,
        compiler_params=pltpu.CompilerParams(
            collective_id=collective_id, has_side_effects=True, vmem_limit_bytes=255 << 18
        ),
    )(*operands)
    return results if order is None else [results[i] for i in order]


def rotate(vectors, cosine, sine_rows):
    half = vectors.shape[-1] // 2
    first, second = vectors[..., :half], vectors[..., half:]
    return jnp.concatenate(
        [first * cosine - second * sine_rows, second * cosine + first * sine_rows], axis=-1
    )


def product(one, two):
    return jnp.dot(one, two, preferred_element_type=F32)


def times_transposed(one, two):
    return lax.dot_general(one, two, (((1,), (1,)), ((), ())), preferred_element_type=F32)


def inner_rows(one, two):
    return lax.dot_general(one, two, (((0,), (0,)), ((), ())), preferred_element_type=F32)


def einsum(form, one, two):
    return jnp.einsum(form, one, two, preferred_element_type=F32)


def halves(weight):
    rows, columns = weight.shape
    return weight.reshape(rows, 2, columns // 2).transpose(1, 0, 2)


def joined(pair):
    return jnp.concatenate([pair[0], pair[1]], axis=1)


def local(
    dp,
    tokens,
    seg_ids,
    q_weight,
    k_weight,
    v_weight,
    o_weight,
    attn_gain,
    gate_weight,
    up_weight,
    down_weight,
    mlp_gain,
    out_grad,
):
    zn = dp // 4
    units = zn * 2
    count, width = tokens.shape
    rows = q_weight.shape[0]
    blocks, block_rows = 2 * seg_ids.shape[0], seg_ids.shape[1]
    q_half, kv_half = q_weight.shape[1] // 2, k_weight.shape[1] // 2
    ff_half = gate_weight.shape[1] // 2
    qkv_half = q_half + 2 * kv_half
    heads, groups = q_half // HEAD_DIM, kv_half // HEAD_DIM
    early = [2 * rows * part // 256 // 8 * 8 for part in (32, 40, 32, 48)]
    early_sums = max(16, 2 * rows * 3 // 256 * 16)

    chip = 2 * count
    inverse = 1.0 / 10000.0 ** (np.arange(0, HEAD_DIM, 2, dtype=np.float32) / HEAD_DIM)
    inverse = np.tile(inverse.astype(np.float32), 4)[None]
    sign = np.tile(np.repeat(np.array([-1.0, 1.0], np.float32), HEAD_DIM // 2), 2)[None]
    (
        qkv_full,
        o_full,
        grads_chip,
        segment,
        gate_full,
        up_full,
        down_full,
        mid,
        normed_two,
        activated,
        gate_grad,
        up_grad,
        normed,
        turned,
        context,
        cosines,
        sines,
        gain_rows,
    ) = call(
        functools.partial(forward, zn, early),
        "forward",
        0,
        (
            q_weight,
            k_weight,
            v_weight,
            o_weight,
            attn_gain[None],
            mlp_gain[None],
            tokens,
            out_grad,
            seg_ids,
            gate_weight,
            up_weight,
            down_weight,
            inverse,
            sign,
        ),
        [VMEM] * 6 + [ANY] * 2 + [VMEM] + [ANY] * 3 + [VMEM] * 2,
        [
            ((width, qkv_half), BF16),
            ((width, q_half), BF16),
            ((units * 16, 128), F32),
            ((2, count, width), BF16),
            ((2, count, width), BF16),
            ((2,) + seg_ids.shape, jnp.int32),
        ]
        + [((width, ff_half), BF16)] * 3
        + [((count, width), F32), ((2, count, width), BF16)]
        + [((chip, ff_half), BF16)] * 3
        + [((2, count, width), BF16)]
        + [((chip, width), BF16), ((chip, qkv_half), BF16), ((chip, q_half), BF16)]
        + [((chip, 2 * HEAD_DIM), F32)] * 2
        + [((8, width), F32)],
        [ANY] * 21,
        total_buffers(count, width)
        + [
            pltpu.VMEM((2, count, width), BF16),
            DMA((3,)),
            DMA((3,)),
            DMA((2,)),
            DMA((2,)),
            DMA((2, 3)),
            DMA((2,)),
            pltpu.VMEM((chip, 2 * HEAD_DIM), F32),
            pltpu.VMEM((chip, 2 * HEAD_DIM), F32),
            pltpu.VMEM((2,) + seg_ids.shape, jnp.int32),
            pltpu.VMEM((units * 16, 128), F32),
            pltpu.VMEM((8, width), F32),
            DMA((2, 3)),
            DMA((5,)),
            pltpu.VMEM((2, rows, 2 * kv_half), BF16),
            pltpu.VMEM((2, 8, 128), F32),
            pltpu.VMEM((rows, 2 * q_half), BF16),
            pltpu.VMEM((rows, 2 * ff_half), BF16),
            pltpu.VMEM((count, width), BF16),
            pltpu.VMEM((count, width), BF16),
            pltpu.VMEM((rows, 2 * ff_half), BF16),
            pltpu.VMEM((rows, 2 * ff_half), BF16),
            pltpu.VMEM((2 * ff_half, rows), BF16),
            DMA((5,)),
        ]
        + gather_sems(6, 7, zn),
        order=(0, 1, 4, 5, 6, 7, 8, 9, 10, 11, 12, 13, 15, 16, 17, 18, 19, 20),
    )
    grads_chip = grads_chip.reshape(chip, width)
    normed_two = normed_two.reshape(chip, width)

    down_sum, gate_sum, up_sum, o_sum, q_sum, kv_sum, out, in_grad, gain_sums = call(
        functools.partial(backward, zn, early_sums),
        "backward",
        1,
        (
            normed_two,
            gate_grad,
            grads_chip,
            activated,
            gate_full,
            up_full,
            down_full,
            mid,
            up_grad,
            normed,
            context,
            turned,
            o_full,
            qkv_full,
            cosines,
            sines,
            tokens,
            segment,
            gain_rows,
        ),
        [ANY] * 17 + [VMEM] * 2,
        [((rows, 2 * ff_half), F32)] * 3
        + [
            ((rows, 2 * q_half), F32),
            ((rows, 2 * q_half), F32),
            ((2, rows, 2 * kv_half), F32),
            ((count, width), BF16),
            ((count, width), BF16),
            ((8, 4 * rows), F32),
            ((count, width), F32),
            ((2, count, width), BF16),
            ((chip, qkv_half), BF16),
            ((2, count, width), BF16),
            ((2, count, width), BF16),
            ((2, count, width), BF16),
        ]
        + [((zn, 4 * rows, ff_half), BF16)] * 3
        + [((zn, 4 * rows, q_half), BF16), ((zn, 4 * rows, qkv_half), BF16)],
        [ANY] * 8 + [VMEM] + [ANY] * 11,
        scatter_buffers(
            [(2 * rows, ff_half), (2 * rows, ff_half), (2 * rows, q_half), (2 * rows, qkv_half)], early_sums, zn
        )
        + total_buffers(count, width) * 2
        + [pltpu.VMEM((count, width), BF16)] * 2
        + [DMA((5,))]
        + gain_buffers(zn, 4 * rows)
        + [pltpu.VMEM((1, width), F32)] * 2
        + [
            DMA((4,)),
            DMA((2,)),
            DMA((3,)),
            DMA((2, 2)),
            DMA((2, 2)),
            DMA((2, 4)),
            DMA((2, 2)),
            pltpu.SemaphoreType.REGULAR,
        ]
        + scatter_sems(5, 6, zn),
        order=range(9),
    )
    plain = (gate_sum, up_sum, q_sum, out, in_grad)
    turned = (down_sum, o_sum)
    shapes = [ref.shape[::-1] for ref in turned]
    results = pl.pallas_call(
        settle,
        out_shape=[jax.ShapeDtypeStruct(shape, F32) for shape in shapes]
        + [jax.ShapeDtypeStruct(ref.shape, ref.dtype) for ref in plain]
        + [jax.ShapeDtypeStruct((rows, 2 * kv_half), F32)] * 2
        + [jax.ShapeDtypeStruct((1, rows), F32)] * 2,
        in_specs=[pl.BlockSpec(memory_space=pltpu.HBM)] * 8 + [VMEM],
        out_specs=[pl.BlockSpec(memory_space=pltpu.HBM)] * 9 + [VMEM] * 2,
        scratch_shapes=[pltpu.VMEM(ref.shape, F32) for ref in turned]
        + [pltpu.VMEM(shape, F32) for shape in shapes]
        + [pltpu.VMEM(ref.shape, ref.dtype) for ref in plain]
        + [pltpu.VMEM(kv_sum.shape, F32)]
        + [pltpu.VMEM((rows, 2 * kv_half), F32)] * 2
        + [DMA((8,)), DMA((9,))],
        name="settle",
        compiler_params=pltpu.CompilerParams(vmem_limit_bytes=62 << 20),
    )(*turned, *plain, kv_sum, gain_sums)
    down_final, o_final, gate_final, up_final, q_final, out, in_grad, k_final, v_final, one, two = results
    return (
        out,
        in_grad,
        q_final,
        k_final,
        v_final,
        o_final,
        one.reshape(rows),
        gate_final,
        up_final,
        down_final,
        two.reshape(rows),
    )


def solution(mesh):
    arguments = (
        P("dp", None),
        P("dp", None),
        P("dp", "tensor"),
        P("dp", "tensor"),
        P("dp", "tensor"),
        P("tensor", "dp"),
        P("dp"),
        P("dp", "tensor"),
        P("dp", "tensor"),
        P("tensor", "dp"),
        P("dp"),
        P("dp", None),
    )
    results = (
        P("dp", None),
        P("dp", None),
        P("dp", "tensor"),
        P("dp", "tensor"),
        P("dp", "tensor"),
        P("tensor", "dp"),
        P("dp"),
        P("dp", "tensor"),
        P("dp", "tensor"),
        P("tensor", "dp"),
        P("dp"),
    )
    return jax.shard_map(
        functools.partial(local, mesh.shape["dp"]),
        mesh=mesh,
        in_specs=arguments,
        out_specs=results,
        check_vma=False,
    )
```
